32 devices in a mesh: dp: 8 (over z, y), tensor: 4 (over x, core).
Axes of the slice: x: 2, y: 2, z: 4, core: 2. Of those that a mesh axis runs over, the one named last changes fastest.
Arguments:
- hidden: bfloat16 [8, 832, 1024], P('dp'), may hold values from -6 to 6
- text_states: bfloat16 [8, 256, 1024], P('dp'), may hold values from -6 to 6
- text_len: int32 [8], P('dp'), may hold values from 1 to 256, as said below
- ln1_gain: float32 [1024], replicated, may hold values from 0.5 to 1.5
- ln1_bias: float32 [1024], replicated, may hold values from -3 to 3
- self_q: bfloat16 [1024, 1024], P(None, 'tensor'), may hold values from -0.1875 to 0.1875
- self_k: bfloat16 [1024, 1024], P(None, 'tensor'), may hold values from -0.1875 to 0.1875
- self_v: bfloat16 [1024, 1024], P(None, 'tensor'), may hold values from -0.1875 to 0.1875
- self_o: bfloat16 [1024, 1024], P('tensor'), may hold values from -1.5 to 1.5
- ln2_gain: float32 [1024], replicated, may hold values from 0.5 to 1.5
- ln2_bias: float32 [1024], replicated, may hold values from -3 to 3
- cross_q: bfloat16 [1024, 1024], P(None, 'tensor'), may hold values from -0.1875 to 0.1875
- cross_k: bfloat16 [1024, 1024], P(None, 'tensor'), may hold values from -0.1875 to 0.1875
- cross_v: bfloat16 [1024, 1024], P(None, 'tensor'), may hold values from -0.1875 to 0.1875
- cross_o: bfloat16 [1024, 1024], P('tensor'), may hold values from -0.75 to 0.75
- ln3_gain: float32 [1024], replicated, may hold values from 0.5 to 1.5
- ln3_bias: float32 [1024], replicated, may hold values from -3 to 3
- ffn_up: bfloat16 [1024, 4096], P(None, 'tensor'), may hold values from -0.1875 to 0.1875
- ffn_down: bfloat16 [4096, 1024], P('tensor'), may hold values from -0.09375 to 0.09375
- cotangent: bfloat16 [8, 832, 1024], P('dp'), may hold values from -6 to 6
Outputs:
- output: bfloat16 [8, 832, 1024], P('dp')
- hidden_grad: bfloat16 [8, 832, 1024], P('dp')
- text_grad: float32 [8, 256, 1024], P('dp')
- ln1_gain_grad: float32 [1024], P('dp')
- ln1_bias_grad: float32 [1024], P('dp')
- self_q_grad: float32 [1024, 1024], P('dp', 'tensor')
- self_k_grad: float32 [1024, 1024], P('dp', 'tensor')
- self_v_grad: float32 [1024, 1024], P('dp', 'tensor')
- self_o_grad: float32 [1024, 1024], P('tensor', 'dp')
- ln2_gain_grad: float32 [1024], P('dp')
- ln2_bias_grad: float32 [1024], P('dp')
- cross_q_grad: float32 [1024, 1024], P('dp', 'tensor')
- cross_k_grad: float32 [1024, 1024], P('dp', 'tensor')
- cross_v_grad: float32 [1024, 1024], P('dp', 'tensor')
- cross_o_grad: float32 [1024, 1024], P('tensor', 'dp')
- ln3_gain_grad: float32 [1024], P('dp')
- ln3_bias_grad: float32 [1024], P('dp')
- ffn_up_grad: float32 [1024, 4096], P('dp', 'tensor')
- ffn_down_grad: float32 [4096, 1024], P('tensor', 'dp')
The draws below stay inside these ranges and needn't reach their ends.
Inputs may be any that keep to these rules, and one draw needn't show every extreme that they name: Clip c attends to text slots below text_len[c]; the other slots of its 256 are padding. Some clip uses all 256.
All inputs are finite; a program needn't handle non-finite values.
Results may differ from the reference program's by a relative error of at most 0.019.
Values sent between devices are 32-bit elements; how exact they have to be, the bound alone decides.
No kernel may reach another device: no remote copies, remote signals or barrier semaphores. Data moves between devices by JAX's collectives and lax.ppermute only.
A program may use at most 192 MiB of HBM per device.

```python
import jax
import jax.numpy as jnp
from jax import lax

D = 1024
HEADS = 16
HD = 64
FF = 4096
TXT = 256
FRAMES = 832
CLIPS = 8


def draw_text_len(key, part):
    first_key, second_key, third_key = jax.random.split(key, 3)
    short_len = jax.random.randint(first_key, (CLIPS,), 1, TXT // 4 + 1)
    long_len = jax.random.randint(second_key, (CLIPS,), 1, TXT + 1)
    picker = jax.random.randint(third_key, (CLIPS,), 0, 4)
    lengths = jnp.where(picker == 0, long_len, short_len)
    fullest = jax.random.randint(jax.random.fold_in(key, 7), (), 0, CLIPS)
    lengths = jnp.where(jnp.arange(CLIPS) == fullest, TXT, lengths)
    return lengths.astype(jnp.int32)


def spiked(values, own_key, source, target, shards_of, factor):
    owner, partner = [(jnp.arange(values.shape[dim]) // (values.shape[dim] // shards_of)).reshape([-1 if axis == dim else 1 for axis in range(values.ndim)]) for dim in (source, target)]
    chosen = jax.random.permutation(own_key, shards_of)[partner]
    strong = (owner == chosen) | (owner == (partner + shards_of // 2) % shards_of)
    return jnp.where(strong, factor * values, values)


def shard_levels(own_key, shape, cuts, least, high):
    level = 1.0
    for axis_at, parts in cuts:
        steps = jax.random.uniform(jax.random.fold_in(jax.random.fold_in(own_key, 6), axis_at), (parts,), jnp.float32, least / len(cuts), high / len(cuts))
        level = level * jnp.repeat(jnp.exp(steps), shape[axis_at] // parts).reshape((-1,) + (1,) * (len(shape) - 1 - axis_at))
    return level


def bell_draw(stream_key, dims, width, limit, cuts=(), kind=jnp.bfloat16):
    values = jax.random.normal(stream_key, dims, jnp.float32) * width
    if len(cuts) > 0:
        values = shard_levels(stream_key, dims, cuts, -0.22, 0.18) * values
    return jnp.clip(values, min=-limit, max=limit).astype(kind)


def noise_with(key, extent, deviation, reach, cuts, heavy, dtype=jnp.bfloat16):
    drawn = deviation * jax.random.normal(key, extent, jnp.float32)
    if cuts:
        drawn = drawn * shard_levels(key, extent, cuts, -0.22, 0.18)
    return jnp.clip(spiked(drawn, jax.random.fold_in(key, 3), *heavy), -reach, reach).astype(dtype)


def setup_inputs(seed: int = 0) -> dict:
    key_list = jax.random.split(jax.random.key(seed), 21)
    return {
        "hidden": bell_draw(key_list[0], (CLIPS, FRAMES, D), 1.0, 6.0, ((0, 8),)),
        "text_states": bell_draw(key_list[1], (CLIPS, TXT, D), 1.0, 6.0, ((0, 8),)),
        "text_len": draw_text_len(jax.random.fold_in(key_list[20], 71), 0),
        "ln1_gain": jnp.clip(1.0 + 0.1 * jax.random.normal(key_list[3], (D,), jnp.float32), 0.5, 1.5),
        "ln1_bias": bell_draw(key_list[4], (D,), 0.3, 3.0, (), jnp.float32),
        "self_q": bell_draw(key_list[5], (D, D), D ** -0.5, 0.1875, ((1, 4),)),
        "self_k": bell_draw(key_list[6], (D, D), D ** -0.5, 0.1875, ((1, 4),)),
        "self_v": bell_draw(key_list[7], (D, D), D ** -0.5, 0.1875, ((1, 4),)),
        "self_o": bell_draw(key_list[8], (D, D), (D // 64) ** -0.5, 1.5, ((0, 4),)),
        "ln2_gain": jnp.clip(1.0 + 0.1 * jax.random.normal(key_list[9], (D,), jnp.float32), 0.5, 1.5),
        "ln2_bias": bell_draw(key_list[10], (D,), 0.3, 3.0, (), jnp.float32),
        "cross_q": bell_draw(key_list[11], (D, D), D ** -0.5, 0.1875, ((1, 4),)),
        "cross_k": bell_draw(key_list[12], (D, D), D ** -0.5, 0.1875, ((1, 4),)),
        "cross_v": bell_draw(key_list[13], (D, D), D ** -0.5, 0.1875, ((1, 4),)),
        "cross_o": bell_draw(key_list[14], (D, D), (D // 16) ** -0.5, 0.75, ((0, 4),)),
        "ln3_gain": jnp.clip(1.0 + 0.1 * jax.random.normal(key_list[15], (D,), jnp.float32), 0.5, 1.5),
        "ln3_bias": bell_draw(key_list[16], (D,), 0.3, 3.0, (), jnp.float32),
        "ffn_up": bell_draw(key_list[17], (D, FF), D ** -0.5, 0.1875, ((1, 4),)),
        "ffn_down": bell_draw(key_list[18], (FF, D), FF ** -0.5, 0.09375, ((0, 4),)),
        "cotangent": noise_with(key_list[19], (CLIPS, FRAMES, D), 1.0, 6.0, ((0, 8),), (0, 2, 8, 2.0)),
    }


EPS = 1e-05
NEG = -1e+30

@jax.custom_vjp
def low(v):
    return lax.optimization_barrier(v.astype(jnp.bfloat16)).astype(jnp.float32)

@jax.custom_vjp
def low_back(v):
    return v

def low_keep(v):
    return (low(v), None)

def low_pass(kept, grad):
    return (grad,)

def back_keep(v):
    return (v, None)

def back_low(kept, grad):
    return (low(grad),)
low.defvjp(low_keep, low_pass)
low_back.defvjp(back_keep, back_low)

def layer_norm(values, gain_vec, shift_vec):
    row_mean = lax.optimization_barrier(jnp.mean(values, -1, keepdims=True))
    centred = values - row_mean
    variance = lax.optimization_barrier(jnp.mean(centred * centred, -1, keepdims=True))
    return centred * lax.rsqrt(variance + EPS) * gain_vec + shift_vec

def matmul(left_op, right_op):
    return jnp.dot(left_op, right_op, precision=lax.Precision.HIGHEST)

def project(row_block, weight):
    return low_back(low(matmul(row_block, weight)))

def attention(query_rows, key_rows, value_rows, allowed):
    count_q = query_rows.shape[0]
    count_k = key_rows.shape[0]
    query_heads = query_rows.reshape(count_q, HEADS, HD)
    key_heads = key_rows.reshape(count_k, HEADS, HD)
    value_heads = value_rows.reshape(count_k, HEADS, HD)
    scores = jnp.einsum('qhd,khd->hqk', query_heads, key_heads, precision=lax.Precision.HIGHEST) * HD ** (-0.5)
    scores = jnp.where(allowed[None], low_back(scores), NEG)
    probs_low = low(jax.nn.softmax(scores, axis=-1))
    mixed_out = jnp.einsum('hqk,khd->qhd', probs_low, value_heads, precision=lax.Precision.HIGHEST)
    return low_back(low(mixed_out.reshape(count_q, HEADS * HD)))

def clip_layer(hidden_rows, text_rows, length, params):
    ln1_gain, ln1_bias, self_q, self_k, self_v, self_o, ln2_gain, ln2_bias, cross_q, cross_k, cross_v, cross_o, ln3_gain, ln3_bias, ffn_up, ffn_down = params
    frames = hidden_rows.shape[0]
    position = jnp.arange(frames)
    causal = position[:, None] >= position[None, :]
    text_mask = jnp.broadcast_to(jnp.arange(text_rows.shape[0])[None, :] < length, (frames, text_rows.shape[0]))
    normed = low(layer_norm(hidden_rows, ln1_gain, ln1_bias))
    attended = attention(project(normed, self_q), project(normed, self_k), project(normed, self_v), causal)
    first_sum = hidden_rows + low_back(matmul(attended, self_o))
    normed = low(layer_norm(first_sum, ln2_gain, ln2_bias))
    attended = attention(project(normed, cross_q), project(text_rows, cross_k), project(text_rows, cross_v), text_mask)
    second_sum = first_sum + low_back(matmul(attended, cross_o))
    normed = low(layer_norm(second_sum, ln3_gain, ln3_bias))
    inner_pre = low_back(matmul(normed, ffn_up))
    active = low_back(low(jax.nn.gelu(inner_pre, approximate=False)))
    return second_sum + low_back(matmul(active, ffn_down))

def reference(hidden, text_states, text_len, ln1_gain, ln1_bias, self_q, self_k, self_v, self_o, ln2_gain, ln2_bias, cross_q, cross_k, cross_v, cross_o, ln3_gain, ln3_bias, ffn_up, ffn_down, cotangent):
    weights = tuple((weight.astype(jnp.float32) for weight in (ln1_gain, ln1_bias, self_q, self_k, self_v, self_o, ln2_gain, ln2_bias, cross_q, cross_k, cross_v, cross_o, ln3_gain, ln3_bias, ffn_up, ffn_down)))

    def run_clip(running, clip_data):
        hidden_clip, text_clip, length, grad_clip = clip_data

        def forward(hidden_f32, text_f32, *params):
            return clip_layer(hidden_f32, text_f32, length, params)
        result, pullback = jax.vjp(forward, hidden_clip.astype(jnp.float32), text_clip.astype(jnp.float32), *weights)
        grads = pullback(grad_clip.astype(jnp.float32))
        updated = tuple((total_now + fresh for total_now, fresh in zip(running, grads[2:])))
        return (updated, (result.astype(jnp.bfloat16), grads[0].astype(jnp.bfloat16), grads[1]))
    zeros = tuple((jnp.zeros(weight.shape, jnp.float32) for weight in weights))
    totals, (output, hidden_grad, text_grad) = lax.scan(run_clip, zeros, (hidden, text_states, text_len, cotangent))
    return (output, hidden_grad, text_grad, totals[0], totals[1], totals[2], totals[3], totals[4], totals[5], totals[6], totals[7], totals[8], totals[9], totals[10], totals[11], totals[12], totals[13], totals[14], totals[15])
```

```python
import jax
import jax.numpy as jnp
from jax import lax
from jax.sharding import PartitionSpec as P

HD = 64


EPS = 1e-05
NEG = -1e30


def norm_forward(values, gain_vec, shift_vec):
    row_mean = jnp.mean(values, -1, keepdims=True)
    centred = values - row_mean
    variance = jnp.mean(centred * centred, -1, keepdims=True)
    inverse = lax.rsqrt(variance + EPS)
    scaled = centred * inverse
    return (scaled * gain_vec + shift_vec, scaled, inverse)


def norm_backward(grad_out, scaled, inverse, gain_vec):
    weighted = grad_out * gain_vec
    first_mean = jnp.mean(weighted, -1, keepdims=True)
    second_mean = jnp.mean(weighted * scaled, -1, keepdims=True)
    grad_in = inverse * (weighted - first_mean - scaled * second_mean)
    return (grad_in, jnp.sum(grad_out * scaled, 0), jnp.sum(grad_out, 0))


def over_rows(left_op, right_op):
    return lax.dot_general(
        left_op, right_op, (((0,), (0,)), ((), ())), preferred_element_type=jnp.float32
    )


def against(left_op, right_op):
    return lax.dot_general(
        left_op, right_op, (((1,), (1,)), ((), ())), preferred_element_type=jnp.float32
    )


def project(row_block, weight):
    return jnp.dot(row_block, weight, preferred_element_type=jnp.float32).astype(jnp.bfloat16)


def split_heads(values, clip_count):
    return values.reshape(clip_count, -1, values.shape[-1] // HD, HD)


def masked_scores(query_heads, key_heads, allowed):
    scores = jnp.einsum(
        "cqhd,ckhd->chqk", query_heads, key_heads, preferred_element_type=jnp.float32
    ) * HD ** (-0.5)
    return jnp.where(allowed[:, None], scores, NEG)


def attend_forward(query_heads, key_heads, value_heads, allowed):
    scores = masked_scores(query_heads, key_heads, allowed)
    row_top = jnp.max(scores, -1, keepdims=True)
    exp_total = jnp.sum(jnp.exp(scores - row_top), -1, keepdims=True)
    log_total = row_top + jnp.log(exp_total)
    probs_low = jnp.exp(scores - log_total).astype(jnp.bfloat16)
    mixed_out = jnp.einsum(
        "chqk,ckhd->cqhd", probs_low, value_heads, preferred_element_type=jnp.float32
    )
    return (mixed_out.astype(jnp.bfloat16), log_total)


def attend_backward(query_heads, key_heads, value_heads, allowed, log_total, mixed_grad):
    scores = masked_scores(query_heads, key_heads, allowed)
    prob_f32 = jnp.exp(scores - log_total)
    value_grad = jnp.einsum(
        "chqk,cqhd->ckhd",
        prob_f32.astype(jnp.bfloat16),
        mixed_grad,
        preferred_element_type=jnp.float32,
    )
    prob_grad = jnp.einsum(
        "cqhd,ckhd->chqk", mixed_grad, value_heads, preferred_element_type=jnp.float32
    )
    score_grad = prob_f32 * (prob_grad - jnp.sum(prob_f32 * prob_grad, -1, keepdims=True))
    score_low = score_grad.astype(jnp.bfloat16)
    query_grad = jnp.einsum(
        "chqk,ckhd->cqhd", score_low, key_heads, preferred_element_type=jnp.float32
    ) * HD ** (-0.5)
    key_grad = jnp.einsum(
        "chqk,cqhd->ckhd", score_low, query_heads, preferred_element_type=jnp.float32
    ) * HD ** (-0.5)
    return (
        query_grad.astype(jnp.bfloat16),
        key_grad.astype(jnp.bfloat16),
        value_grad.astype(jnp.bfloat16),
    )


FLIPS = {"y": 1, "a": 2, "b": 6}


def swap(value, axis, size, flip):
    return lax.ppermute(value, axis, [(i, i ^ flip) for i in range(size)])


def tensor_sum(value):
    half = value.shape[0] // 2
    core = lax.axis_index("tensor") & 1
    keep = lax.dynamic_slice_in_dim(value, core * half, half)
    send = lax.dynamic_slice_in_dim(value, (1 - core) * half, half)
    mine = keep + swap(send, "tensor", 4, 1)
    mine = mine + swap(mine, "tensor", 4, 2)
    other = swap(mine, "tensor", 4, 1)
    both = jnp.concatenate([mine, other, mine])
    return lax.dynamic_slice_in_dim(both, core * half, 2 * half)


def scatter_sum(value, dp_size, order):
    if dp_size != 8:
        return lax.psum_scatter(value, "dp", scatter_dimension=0, tiled=True)
    rows = value.shape[0] // 8
    me = lax.axis_index("dp")
    parts = [
        lax.dynamic_slice_in_dim(value, (me ^ m) * rows, rows) for m in (0, 1, 2, 3, 6, 7, 4, 5)
    ]
    left = jnp.stack(parts).reshape(2, 2, 2, rows, value.shape[1])
    axes = ["b", "a", "y"]
    for name in order:
        at = axes.index(name)
        axes.pop(at)
        keep = lax.index_in_dim(left, 0, at, keepdims=False)
        send = lax.index_in_dim(left, 1, at, keepdims=False)
        left = keep + swap(send, "dp", 8, FLIPS[name])
    return left


def gelu_exact(values):
    return jax.nn.gelu(values, approximate=False)


def body(
    hidden,
    text_states,
    text_len,
    ln1_gain,
    ln1_bias,
    self_q,
    self_k,
    self_v,
    self_o,
    ln2_gain,
    ln2_bias,
    cross_q,
    cross_k,
    cross_v,
    cross_o,
    ln3_gain,
    ln3_bias,
    ffn_up,
    ffn_down,
    cotangent,
):
    clip_count, frames, model_width = hidden.shape
    text_rows = text_states.shape[1]
    row_count = clip_count * frames
    position = jnp.arange(frames)
    causal = jnp.broadcast_to(position[:, None] >= position[None, :], (clip_count, frames, frames))
    text_mask = jnp.broadcast_to(
        jnp.arange(text_rows)[None, None, :] < text_len[:, None, None],
        (clip_count, frames, text_rows),
    )
    resid_in = hidden.astype(jnp.float32).reshape(row_count, model_width)
    norm_one, scaled_one, inverse_one = norm_forward(resid_in, ln1_gain, ln1_bias)
    norm_one_low = norm_one.astype(jnp.bfloat16)
    query_one = split_heads(project(norm_one_low, self_q), clip_count)
    key_one = split_heads(project(norm_one_low, self_k), clip_count)
    value_one = split_heads(project(norm_one_low, self_v), clip_count)
    mixed_one, total_one = attend_forward(query_one, key_one, value_one, causal)
    mixed_one_rows = mixed_one.reshape(row_count, -1)
    first_sum = resid_in + tensor_sum(jnp.dot(mixed_one_rows, self_o, preferred_element_type=jnp.float32))
    norm_two, scaled_two, inverse_two = norm_forward(first_sum, ln2_gain, ln2_bias)
    norm_two_low = norm_two.astype(jnp.bfloat16)
    text_flat = text_states.reshape(clip_count * text_rows, model_width)
    query_two = split_heads(project(norm_two_low, cross_q), clip_count)
    key_two = split_heads(project(text_flat, cross_k), clip_count)
    value_two = split_heads(project(text_flat, cross_v), clip_count)
    mixed_two, total_two = attend_forward(query_two, key_two, value_two, text_mask)
    mixed_two_rows = mixed_two.reshape(row_count, -1)
    second_sum = first_sum + tensor_sum(jnp.dot(mixed_two_rows, cross_o, preferred_element_type=jnp.float32))
    norm_three, scaled_three, inverse_three = norm_forward(second_sum, ln3_gain, ln3_bias)
    norm_three_low = norm_three.astype(jnp.bfloat16)
    inner_pre = jnp.dot(norm_three_low, ffn_up, preferred_element_type=jnp.float32)
    active, gelu_pull = jax.vjp(gelu_exact, inner_pre)
    active_low = active.astype(jnp.bfloat16)
    final_sum = second_sum + tensor_sum(jnp.dot(active_low, ffn_down, preferred_element_type=jnp.float32))
    output = final_sum.astype(jnp.bfloat16).reshape(clip_count, frames, model_width)
    out_grad = cotangent.reshape(row_count, model_width)
    down_grad = over_rows(out_grad, active_low)
    active_grad = against(out_grad, ffn_down).astype(jnp.bfloat16)
    inner_grad = gelu_pull(active_grad.astype(jnp.float32))[0].astype(jnp.bfloat16)
    up_grad = over_rows(norm_three_low, inner_grad)
    norm_three_grad = tensor_sum(against(inner_grad, ffn_up))
    delta_in, gain3_grad, bias3_grad = norm_backward(
        norm_three_grad, scaled_three, inverse_three, ln3_gain
    )
    grad_resid = out_grad.astype(jnp.float32) + delta_in
    resid_low = grad_resid.astype(jnp.bfloat16)
    co_grad = over_rows(resid_low, mixed_two_rows)
    mixed_two_grad = split_heads(against(resid_low, cross_o).astype(jnp.bfloat16), clip_count)
    query_two_grad, key_two_grad, value_two_grad = attend_backward(
        query_two, key_two, value_two, text_mask, total_two, mixed_two_grad
    )
    query_two_rows = query_two_grad.reshape(row_count, -1)
    key_two_rows = key_two_grad.reshape(clip_count * text_rows, -1)
    value_two_rows = value_two_grad.reshape(clip_count * text_rows, -1)
    cq_grad = over_rows(norm_two_low, query_two_rows)
    ck_grad = over_rows(text_flat, key_two_rows)
    cv_grad = over_rows(text_flat, value_two_rows)
    norm_two_part = against(query_two_rows, cross_q)
    text_part = against(key_two_rows, cross_k) + against(value_two_rows, cross_v)
    norm_two_grad, text_sum = (tensor_sum(norm_two_part), tensor_sum(text_part))
    text_grad = text_sum.reshape(clip_count, text_rows, model_width)
    delta_in, gain2_grad, bias2_grad = norm_backward(
        norm_two_grad, scaled_two, inverse_two, ln2_gain
    )
    grad_resid = grad_resid + delta_in
    resid_low = grad_resid.astype(jnp.bfloat16)
    so_grad = over_rows(resid_low, mixed_one_rows)
    mixed_one_grad = split_heads(against(resid_low, self_o).astype(jnp.bfloat16), clip_count)
    query_one_grad, key_one_grad, value_one_grad = attend_backward(
        query_one, key_one, value_one, causal, total_one, mixed_one_grad
    )
    query_one_rows = query_one_grad.reshape(row_count, -1)
    key_one_rows = key_one_grad.reshape(row_count, -1)
    value_one_rows = value_one_grad.reshape(row_count, -1)
    sq_grad = over_rows(norm_one_low, query_one_rows)
    sk_grad = over_rows(norm_one_low, key_one_rows)
    sv_grad = over_rows(norm_one_low, value_one_rows)
    norm_one_part = (
        against(query_one_rows, self_q)
        + against(key_one_rows, self_k)
        + against(value_one_rows, self_v)
    )
    norm_one_grad = tensor_sum(norm_one_part)
    delta_in, gain1_grad, bias1_grad = norm_backward(
        norm_one_grad, scaled_one, inverse_one, ln1_gain
    )
    hidden_grad = (
        (grad_resid + delta_in).astype(jnp.bfloat16).reshape(clip_count, frames, model_width)
    )
    dp_size = lax.axis_size("dp")
    up_grad = scatter_sum(up_grad, dp_size, "yab")
    down_grad = scatter_sum(down_grad, dp_size, "aby").T
    cross = scatter_sum(
        jnp.concatenate([co_grad, cq_grad, ck_grad, cv_grad], 1), dp_size, "bya"
    )
    attn = scatter_sum(jnp.concatenate([sq_grad, sk_grad, so_grad], 1), dp_size, "yab")
    vectors = jnp.stack(
        [gain1_grad, bias1_grad, gain2_grad, bias2_grad, gain3_grad, bias3_grad] * 1, 1
    )
    last = scatter_sum(jnp.concatenate([sv_grad, jnp.pad(vectors, ((0, 0), (0, 122)))], 1), dp_size, "aby")
    width = sq_grad.shape[1]
    co_grad, cq_grad, ck_grad, cv_grad = (cross[:, i * width : (i + 1) * width] for i in range(4))
    sq_grad, sk_grad, so_grad = (attn[:, i * width : (i + 1) * width] for i in range(3))
    sv_grad = last[:, :width]
    co_grad, so_grad = co_grad.T, so_grad.T
    gain1_grad, bias1_grad, gain2_grad, bias2_grad, gain3_grad, bias3_grad = (
        last[:, width + i] for i in range(6)
    )
    return (
        output,
        hidden_grad,
        text_grad,
        gain1_grad,
        bias1_grad,
        sq_grad,
        sk_grad,
        sv_grad,
        so_grad,
        gain2_grad,
        bias2_grad,
        cq_grad,
        ck_grad,
        cv_grad,
        co_grad,
        gain3_grad,
        bias3_grad,
        up_grad,
        down_grad,
    )


def solution(mesh):
    in_specs = (
        P("dp", None, None),
        P("dp", None, None),
        P("dp"),
        P(),
        P(),
        P(None, "tensor"),
        P(None, "tensor"),
        P(None, "tensor"),
        P("tensor", None),
        P(),
        P(),
        P(None, "tensor"),
        P(None, "tensor"),
        P(None, "tensor"),
        P("tensor", None),
        P(),
        P(),
        P(None, "tensor"),
        P("tensor", None),
        P("dp", None, None),
    )
    out_specs = (
        P("dp", None, None),
        P("dp", None, None),
        P("dp", None, None),
        P("dp"),
        P("dp"),
        P("dp", "tensor"),
        P("dp", "tensor"),
        P("dp", "tensor"),
        P("tensor", "dp"),
        P("dp"),
        P("dp"),
        P("dp", "tensor"),
        P("dp", "tensor"),
        P("dp", "tensor"),
        P("tensor", "dp"),
        P("dp"),
        P("dp"),
        P("dp", "tensor"),
        P("tensor", "dp"),
    )
    return jax.shard_map(body, mesh=mesh, in_specs=in_specs, out_specs=out_specs, check_vma=False)
```

```python
import functools

import jax
import jax.numpy as jnp
import numpy as np
from jax import lax
from jax.experimental import pallas as pl
from jax.experimental.pallas import tpu as pltpu
from jax.sharding import PartitionSpec as P

HD = 64
EPS = 1e-05
NEG = -1e30
SCALE = HD ** (-0.5)
BF = jnp.bfloat16
F32 = jnp.float32
PAIR = 2 * HD

FLIPS = {"y": 1, "a": 2, "b": 6}
WEIGHT = {"y": 1, "a": 2, "b": 4}
RELATIVE = (0, 1, 2, 3, 6, 7, 4, 5)

CORE, PEER, Y, LABEL, TABLE = 0, 1, 2, 3, 8


def index_table(dp_size):
    rows = []
    for me in range(dp_size):
        for t in range(4):
            row = [t & 1, 1 - (t & 1), me & 1, me & 3, 0, 0, 0, 0]
            row += [(me ^ m) if dp_size == 8 else i for i, m in enumerate(RELATIVE)]
            rows.append(row)
    return np.array(rows, np.int32)


def dot(left, right):
    return lax.dot_general(left, right, (((1,), (0,)), ((), ())), preferred_element_type=F32)


def against(left, right):
    return lax.dot_general(left, right, (((1,), (1,)), ((), ())), preferred_element_type=F32)


def over_rows(left, right):
    return lax.dot_general(left, right, (((0,), (0,)), ((), ())), preferred_element_type=F32)


def swap(value, axis, size, flip):
    return lax.ppermute(value, axis, [(i, i ^ flip) for i in range(size)])


def core_swap(value):
    return swap(value, "tensor", 4, 1)


def x_swap(value):
    return swap(value, "tensor", 4, 2)


def cross_swap(value):
    return swap(value, "tensor", 4, 3)


def after(value, *others):
    return lax.optimization_barrier((value, *others))[0]


def full(shape):
    return pl.BlockSpec(shape, lambda *_: (0,) * len(shape))


def launch(body, info, args, in_specs, outs, out_specs, grid=(1,), scratch=(), flops=0, exps=0, grant=20, cost=0):
    specs = [full(a.shape) if s is None else s for a, s in zip(args, in_specs)]
    ospecs = [full(o.shape) if s is None else s for o, s in zip(outs, out_specs)]
    return pl.pallas_call(
        body,
        out_shape=list(outs),
        grid_spec=pltpu.PrefetchScalarGridSpec(
            num_scalar_prefetch=1,
            grid=grid,
            in_specs=specs,
            out_specs=ospecs,
            scratch_shapes=list(scratch),
        ),
        compiler_params=pltpu.CompilerParams(vmem_limit_bytes=grant << 20),
        cost_estimate=pl.CostEstimate(
            flops=1 + cost * 10**9, bytes_accessed=1, transcendentals=0
        ),
        name=body.__name__ if hasattr(body, "__name__") else body.func.__name__,
    )(info, *args)


def arr(shape, dtype=F32):
    return jax.ShapeDtypeStruct(shape, dtype)


def normed(values):
    centred = values - jnp.mean(values, -1, keepdims=True)
    inverse = lax.rsqrt(jnp.mean(centred * centred, -1, keepdims=True) + EPS)
    return centred * inverse, inverse


def norm_back(grad, scaled, inverse, gain):
    weighted = grad * gain
    first = jnp.mean(weighted, -1, keepdims=True)
    second = jnp.mean(weighted * scaled, -1, keepdims=True)
    return inverse * (weighted - first - scaled * second)


def head_lanes(odd, dtype):
    lane = lax.broadcasted_iota(jnp.int32, (1, PAIR), 1)
    return ((lane // HD) == odd).astype(dtype)


def norm_project(info, hid, gain, bias, wq, wk, wv, a1, q, k, v):
    scaled, _ = normed(hid[...].astype(F32))
    low = (scaled * gain[...] + bias[...]).astype(BF)
    a1[...] = low
    q[...] = (dot(low, wq[...]) * SCALE).astype(BF)
    k[...] = dot(low, wk[...]).astype(BF)
    v[...] = dot(low, wv[...]).astype(BF)


def text_project(info, text, wk, wv, k, v):
    k[...] = dot(text[...], wk[...]).astype(BF)
    v[...] = dot(text[...], wv[...]).astype(BF)


def blocks_of(rows, step=256):
    return [(s, min(step, rows - s)) for s in range(0, rows, step)]


def causal(scores):
    key = lax.broadcasted_iota(jnp.int32, scores.shape, 0)
    query = lax.broadcasted_iota(jnp.int32, scores.shape, 1)
    return jnp.where(key <= query, scores, NEG)


def self_forward(info, q, k, v, keep, send, total, mixed):
    rows = q.shape[0]
    half = rows // 2
    odd = lax.rem(pl.program_id(0), 2)
    lanes = head_lanes(odd, BF)
    lanes_on = head_lanes(odd, F32) > 0
    for start, size in blocks_of(rows):
        here = slice(start, start + size)
        query = q[here, :] * lanes
        near = causal(against(k[here, :], query))
        top = jnp.max(near, 0, keepdims=True)
        if start:
            far = against(k[:start, :], query)
            top = jnp.maximum(top, jnp.max(far, 0, keepdims=True))
        near = jnp.exp(near - top)
        count = jnp.sum(near, 0, keepdims=True)
        if start:
            far = jnp.exp(far - top)
            count = count + jnp.sum(far, 0, keepdims=True)
        scale = 1.0 / count
        out = over_rows(v[here, :], (near * scale).astype(BF))
        if start:
            out = out + over_rows(v[:start, :], (far * scale).astype(BF))
        total[0, :, here] = top + jnp.log(count)
        mixed[here, :] = jnp.where(lanes_on, out.T, mixed[here, :])

    @pl.when(odd == 1)
    def _():
        keep[...] = mixed[pl.ds(pl.multiple_of(info[CORE] * half, 8), half), :]
        send[...] = mixed[pl.ds(pl.multiple_of(info[PEER] * half, 8), half), :]


def prepare(info, so, co, cq, own, first):
    own[0:256, :] = so[...].astype(F32)
    own[256:512, :] = co[...].astype(F32)
    own[512:768, :] = cq[...].astype(F32).T
    first[0:128, :] = own[pl.ds(pl.multiple_of(info[Y] * 128, 8), 128), :]
    for i in range(2):
        at = pl.multiple_of(256 + i * 256 + info[LABEL] * 64, 8)
        first[128 + i * 64 : 192 + i * 64, :] = own[pl.ds(at, 64), :]


def mix(info, one, two, w_one, w_two, out):
    out[...] = dot(one[...].astype(BF), w_one[...].astype(BF)) + dot(
        two[...].astype(BF), w_two[...].astype(BF)
    )


def gather_halves(info, far, weights):
    for s in range(2):
        for p in range(2):

            @pl.when(info[Y] == p)
            def _(s=s, p=p):
                weights[s * 256 + p * 128 : s * 256 + p * 128 + 128, :] = far[2 * s][
                    :128, :
                ].astype(BF)

            @pl.when(info[Y] != p)
            def _(s=s, p=p):
                weights[s * 256 + p * 128 : s * 256 + p * 128 + 128, :] = far[2 * s + 1][
                    :128, :
                ].astype(BF)


def gather_quarters(info, far, weights, first):
    for s in range(2):
        over_x, over_y, over_z = far[3 * s : 3 * s + 3]
        pieces = (
            over_x[128 + first : 192 + first, :],
            over_y[128 + first : 192 + first, :],
            over_z[:64, :],
            over_z[64:, :],
        )
        for j, piece in enumerate(pieces):
            at = pl.multiple_of(s * 256 + (info[LABEL] ^ j) * 64, 64)
            weights[pl.ds(at, 64), :] = piece.astype(BF)


def mix_far(info, pre, one, two, far, weights, which):
    if which is None:
        gather_halves(info, far, weights)
    else:
        gather_quarters(info, far, weights, which)
    far_part = dot(one[...].astype(BF), weights[:256, :]) + dot(
        two[...].astype(BF), weights[256:, :]
    )
    return pre[...] + far_part


def mix_norm(which, info, base, pre, one, two, *refs):
    n = 7 if which is None else 5
    far, (gain, bias, resid, low, *packs, weights) = refs[:-n], refs[-n:]
    for i, pack in enumerate(packs):
        for j in range(2):
            pack[j * 64 : j * 64 + 64, :] = far[j][128 + i * 64 : 192 + i * 64, :]
    part = mix_far(info, pre, one, two, far, weights, which)
    total = base[...].astype(F32) + part
    resid[...] = total
    scaled, _ = normed(total)
    low[...] = scaled * gain[...] + bias[...]


def mix_norm_back(info, pre, one, two, *refs):
    far, (gain, resid, e_in, e_out, grads, weights) = refs[:-6], refs[-6:]
    grad = mix_far(info, pre, one, two, far, weights, 64)
    scaled, inverse = normed(resid[...])
    e_out[...] = e_in[...] + norm_back(grad, scaled, inverse, gain[...])
    grads[0:1, :] = jnp.sum(grad * scaled, 0, keepdims=True) * 0.5
    grads[1:2, :] = jnp.sum(grad, 0, keepdims=True) * 0.5


def sum_norm_back(info, mine, far, gain, resid, e_in, e_out, grads):
    grad = mine[...] + far[...]
    scaled, inverse = normed(resid[...])
    e_out[...] = e_in[...].astype(F32) + norm_back(grad, scaled, inverse, gain[...])
    grads[0:1, :] = jnp.sum(grad * scaled, 0, keepdims=True) * 0.5
    grads[1:2, :] = jnp.sum(grad, 0, keepdims=True) * 0.5


def sum_first_grads(info, mine, recv, hid, out, grads):
    grad = mine[...] + recv[...]
    out[...] = grad
    scaled, _ = normed(hid[...].astype(F32))
    grads[0:1, :] = jnp.sum(grad * scaled, 0, keepdims=True)
    grads[1:2, :] = jnp.sum(grad, 0, keepdims=True)


def last_norm_back(info, mine, far, gain, hid, e_in, out):
    grad = mine[...] + far[...]
    scaled, inverse = normed(hid[...].astype(F32))
    out[...] = e_in[...] + norm_back(grad, scaled, inverse, gain[...])


def cross_forward(info, length, a2, wq, k, v, q, mixed, total):
    query_rows = (dot(a2[...].astype(BF), wq[...]) * SCALE).astype(BF)
    q[...] = query_rows
    for pair in range(2):
        cols = slice(pair * PAIR, (pair + 1) * PAIR)
        pair_out = None
        for odd in range(2):
            query = query_rows[:, cols] * head_lanes(odd, BF)
            scores = against(k[:, cols], query)
            slot = lax.broadcasted_iota(jnp.int32, scores.shape, 0)
            scores = jnp.where(slot < length[0], scores, NEG)
            top = jnp.max(scores, 0, keepdims=True)
            scores = jnp.exp(scores - top)
            count = jnp.sum(scores, 0, keepdims=True)
            out = over_rows(v[:, cols], (scores * (1.0 / count)).astype(BF)).T
            total[pair * 2 + odd] = top + jnp.log(count)
            pair_out = out if odd == 0 else jnp.where(head_lanes(1, F32) > 0, out, pair_out)
        mixed[:, cols] = pair_out


def feed_forward(info, a3, cot, up, down, g, du, da3):
    n = pl.program_id(0)
    u = dot(a3[...].astype(BF), up[...])
    cdf = 0.5 + 0.5 * lax.erf(u * (0.5**0.5))
    g[...] = (u * cdf).astype(BF)
    slope = cdf + u * jnp.exp(-0.5 * u * u) * (1.0 / (2.0 * np.pi) ** 0.5)
    dg = against(cot[...], down[...]).astype(BF).astype(F32)
    low = (dg * slope).astype(BF)
    du[...] = low
    part = against(low, up[...])

    @pl.when(n == 0)
    def _():
        da3[...] = part

    @pl.when(n > 0)
    def _():
        da3[...] += part


def down_project(info, own, sib, down, out_own, out_sib):
    out_own[...] = dot(own[...], down[...])
    out_sib[...] = dot(sib[...], down[...])


def cross_backward(second, info, length, e1, wo, q, k, v, total, *rest):
    if second:
        dk_in, dv_in, dq, dk_out, dv_out = rest
    else:
        dq, dk_out, dv_out = rest
    mixed_grad = against(e1[...].astype(BF), wo[...]).astype(BF)
    for pair in range(2):
        cols = slice(pair * PAIR, (pair + 1) * PAIR)
        dk = dk_in[:, cols] if second else None
        dv = dv_in[:, cols] if second else None
        pair_dq = None
        for odd in range(2):
            lanes = head_lanes(odd, BF)
            query = q[:, cols] * lanes
            grad = mixed_grad[:, cols] * lanes
            scores = against(k[:, cols], query)
            slot = lax.broadcasted_iota(jnp.int32, scores.shape, 0)
            scores = jnp.where(slot < length[0], scores, NEG)
            probs = jnp.exp(scores - total[pair * 2 + odd])
            prob_grad = against(v[:, cols], grad)
            part = dot(probs.astype(BF), grad)
            dv = part if dv is None else dv + part
            delta = jnp.sum(probs * prob_grad, 0, keepdims=True)
            low = (probs * (prob_grad - delta)).astype(BF)
            part = dot(low, query)
            dk = part if dk is None else dk + part
            out = over_rows(k[:, cols], low).T
            pair_dq = out if odd == 0 else jnp.where(head_lanes(1, F32) > 0, out, pair_dq)
        dq[:, cols] = pair_dq * SCALE
        dk_out[:, cols] = dk.astype(dk_out.dtype)
        dv_out[:, cols] = dv.astype(dv_out.dtype)


def text_back(info, dk, dv, wk, wv, own, send, scratch):
    half = own.shape[0]
    scratch[...] = against(dk[...], wk[...]) + against(dv[...], wv[...])
    own[...] = scratch[pl.ds(pl.multiple_of(info[CORE] * half, 8), half), :]
    send[...] = scratch[pl.ds(pl.multiple_of(info[PEER] * half, 8), half), :]


def mixed_back(info, own, sib, wo, out):
    half = own.shape[0]
    out[pl.ds(pl.multiple_of(info[CORE] * half, 16), half), :] = against(
        own[...].astype(BF), wo[...]
    ).astype(BF)
    out[pl.ds(pl.multiple_of(info[PEER] * half, 16), half), :] = against(
        sib[...].astype(BF), wo[...]
    ).astype(BF)


def self_backward(info, q, k, v, grad_in, total, dq, dk, dv, dq_sum, dk_sum, dv_sum):
    rows = q.shape[0]
    odd = lax.rem(pl.program_id(0), 2)
    lanes = head_lanes(odd, BF)
    lanes_on = head_lanes(odd, F32) > 0

    @pl.when(odd == 0)
    def _():
        dk_sum[...] = jnp.zeros_like(dk_sum)
        dv_sum[...] = jnp.zeros_like(dv_sum)

    for start, size in blocks_of(rows):
        here = slice(start, start + size)
        query = q[here, :] * lanes
        grad = grad_in[here, :] * lanes
        level = total[0, :, here]
        near = jnp.exp(causal(against(k[here, :], query)) - level)
        near_grad = against(v[here, :], grad)
        delta = jnp.sum(near * near_grad, 0, keepdims=True)
        dv_sum[here, :] += dot(near.astype(BF), grad)
        if start:
            far = jnp.exp(against(k[:start, :], query) - level)
            far_grad = against(v[:start, :], grad)
            delta = delta + jnp.sum(far * far_grad, 0, keepdims=True)
            dv_sum[:start, :] += dot(far.astype(BF), grad)
        near_low = (near * (near_grad - delta)).astype(BF)
        dk_sum[here, :] += dot(near_low, query)
        out = over_rows(k[here, :], near_low)
        if start:
            far_low = (far * (far_grad - delta)).astype(BF)
            dk_sum[:start, :] += dot(far_low, query)
            out = out + over_rows(k[:start, :], far_low)
        dq_sum[here, :] = jnp.where(lanes_on, out.T * SCALE, dq_sum[here, :])

    @pl.when(odd == 1)
    def _():
        dq[...] = dq_sum[...].astype(BF)
        dk[...] = dk_sum[...].astype(BF)
        dv[...] = dv_sum[...].astype(BF)


def first_back(info, dq, dk, dv, wq, wk, wv, own, send):
    half = own.shape[0]
    for at, out in ((PEER, send), (CORE, own)):
        here = pl.ds(pl.multiple_of(info[at] * half, 16), half)
        out[...] = (
            against(dq[here, :], wq[...])
            + against(dk[here, :], wk[...])
            + against(dv[here, :], wv[...])
        )


def weight_grad(plan, shapes, n_v, info, *refs):
    at = 0
    groups = []
    for n_left, n_right in shapes:
        groups.append((refs[at : at + n_left], refs[at + n_left : at + n_left + n_right]))
        at += n_left + n_right
    vectors = refs[at : at + n_v]
    outs = refs[at + n_v : at + n_v + 2 * len(plan)]
    lhs, rhs = refs[-2:]
    for g, (lefts, rights) in enumerate(groups):
        row = 0
        per = len(rights) // len(lefts)
        for i, left in enumerate(lefts):
            rows = left.shape[0]
            for j in range(8):
                block = left[:, pl.ds(pl.multiple_of(info[TABLE + j] * 128, 128), 128)]
                lhs[row : row + rows, j * 128 : (j + 1) * 128] = block.astype(BF)
            col = 0
            for right in rights[i * per : (i + 1) * per]:
                rhs[row : row + rows, col : col + right.shape[1]] = right[...].astype(BF)
                col += right.shape[1]
            row += rows
        for s, (order, segments) in enumerate(plan):
            put = 0
            for group, first, width in segments:
                if group == g:
                    for half in range(2):
                        value = over_rows(
                            lhs[:row, half * 512 : half * 512 + 512],
                            rhs[:row, first : first + width],
                        )
                        for q in range(4):
                            j = half * 4 + q
                            sent, pos = spot(order, j)
                            outs[2 * s + sent][pos, :128, put : put + width] = value[
                                q * 128 : (q + 1) * 128, :
                            ]
                put += width
    if n_v:
        for j in range(8):
            sent, pos = spot(plan[-1][0], j)
            out = outs[2 * len(plan) - 2 + sent]
            out[pos, 128:, :] = jnp.zeros((8, out.shape[2]), F32)
            for i, ref in enumerate(vectors):
                block = ref[:, pl.ds(pl.multiple_of(info[TABLE + j] * 128, 128), 128)]
                out[pos, 128 + 2 * i : 130 + 2 * i, :128] = block


def spot(order, j):
    bits = [(j // WEIGHT[name]) & 1 for name in order]
    return bits[0], bits[1] * 2 + bits[2]


def weight_grads(info, groups, plan, vectors=()):
    args, shapes, flops = [], [], 0
    for lefts, rights in groups:
        flat = [r for group in rights for r in group]
        args += [*lefts, *flat]
        shapes.append((len(lefts), len(flat)))
        flops += 2 * sum(a.shape[0] for a in lefts) * 1024 * sum(r.shape[1] for r in rights[0])
    args += vectors
    outs = []
    for s, (order, segments) in enumerate(plan):
        tall = 136 if vectors and s == len(plan) - 1 else 128
        outs += [arr((4, tall, sum(w for _, _, w in segments)))] * 2
    rows = max(sum(a.shape[0] for a in lefts) for lefts, _ in groups)
    wide = max(sum(r.shape[1] for r in rights[0]) for _, rights in groups)
    return launch(
        functools.partial(weight_grad, plan, tuple(shapes), len(vectors)),
        info,
        tuple(args),
        [None] * len(args),
        outs,
        [None] * len(outs),
        scratch=[pltpu.VMEM((rows, 1024), BF), pltpu.VMEM((rows, wide), BF)],
        flops=flops,
        grant=40,
    )


def scatter_sum(keep, send):
    value = jnp.concatenate([keep, send])
    value = value.reshape(-1, value.shape[-1])
    return lax.psum_scatter(value, "dp", scatter_dimension=0, tiled=True)


def fold(info, *refs):
    for i in range(3):
        keep, got = refs[2 * i : 2 * i + 2]
        keep_out, send_out = refs[6 + 2 * i : 8 + 2 * i]
        n = keep_out.shape[0]
        keep_out[...] = keep[:n] + got[:n]
        send_out[...] = keep[n:] + got[n:]


def finish_ffn(info, *refs):
    up, down = refs[6:]
    one, two, three = (refs[2 * i][0] + refs[2 * i + 1][0] for i in range(3))
    wide = one.shape[1]
    up[:, :wide] = one
    up[:, wide:] = three[:, : up.shape[1] - wide]
    down[:wide, :] = two.T
    down[wide:, :] = three[:, up.shape[1] - wide :].T


def finish_cross(info, *refs):
    co, cq, ck, cv = refs[6:]
    one, two, three = (refs[2 * i][0] + refs[2 * i + 1][0] for i in range(3))
    co[...] = one[:, :256].T
    cq[...] = two[:, :256]
    ck[:, :128] = one[:, 256:]
    ck[:, 128:] = two[:, 256:]
    cv[...] = three


def finish_self(info, *refs):
    so, sq, sk, sv, vectors = refs[6:]
    one, two = (refs[2 * i][0] + refs[2 * i + 1][0] for i in range(2))
    so[...] = one[:, :256].T
    sq[...] = two[:, :256]
    sv[:, :128] = one[:, 256:]
    sv[:, 128:] = two[:, 256:]
    sk[...] = refs[4][0, :128, :] + refs[5][0, :128, :]
    vectors[...] = refs[4][0, 128:, :128] + refs[5][0, 128:, :128]


FINISH = {
    finish_ffn: [(128, 1024), (1024, 128)],
    finish_cross: [(256, 128), (128, 256), (128, 256), (128, 256)],
    finish_self: [(256, 128), (128, 256), (128, 256), (128, 256), (8, 128)],
}


def exchange(streams, orders, step, first=None, finish=None):
    args = []
    for (keep, send), order in zip(streams, orders):
        got = swap(send, "dp", 8, FLIPS[order[step]])
        args += [keep, got if first is None else after(got, first)]
    if finish is not None:
        outs = [arr(shape) for shape in FINISH[finish]]
        return launch(finish, streams_info(), args, [None] * 6, outs, [None] * len(outs))
    outs = []
    for keep, _ in streams:
        outs += [arr((keep.shape[0] // 2, *keep.shape[1:]))] * 2
    out = launch(fold, streams_info(), args, [None] * 6, outs, [None] * 6)
    return list(zip(out[0::2], out[1::2]))


def streams_info():
    return jnp.zeros((1,), jnp.int32)


def sent(streams):
    return [s for _, s in streams]


def out_second(info, own, got, text_own, text_got, out):
    half = own.shape[0]
    out[:half, :] = own[...] + got[...]
    out[half:, :] = text_own[...] + text_got[...]


def out_sum(info, resid, mine, far, out):
    half = resid.shape[0]
    out[:half, :] = resid[...] + (mine[:half, :] + far[:half, :])
    out[half:, :] = mine[half:, :] + far[half:, :]


def out_place(info, own, sib, out, text_out):
    half = out.shape[0] // 2
    text_half = text_out.shape[0] // 2
    for at, ref in ((CORE, own), (PEER, sib)):
        out[pl.ds(pl.multiple_of(info[at] * half, 16), half), :] = ref[:half, :].astype(BF)
        spot = pl.multiple_of(info[at] * text_half, 8)
        text_out[pl.ds(spot, text_half), :] = ref[half:, :]


def place(info, own, sib, out):
    half = out.shape[0] // 2
    for at, ref in ((CORE, own), (PEER, sib)):
        out[pl.ds(pl.multiple_of(info[at] * half, 16), half), :] = ref[...].astype(BF)


def body(
    hidden,
    text_states,
    text_len,
    ln1_gain,
    ln1_bias,
    self_q,
    self_k,
    self_v,
    self_o,
    ln2_gain,
    ln2_bias,
    cross_q,
    cross_k,
    cross_v,
    cross_o,
    ln3_gain,
    ln3_bias,
    ffn_up,
    ffn_down,
    cotangent,
):
    dp_size = lax.axis_size("dp")
    frames, width = hidden.shape[1:]
    text_rows = text_states.shape[1]
    cols = self_q.shape[1]
    inner = ffn_up.shape[1]
    half = frames // 2
    device = lax.axis_index("dp") * 4 + lax.axis_index("tensor")
    table = jnp.asarray(index_table(dp_size))
    info = lax.dynamic_index_in_dim(table, device, 0, keepdims=False)
    core = lax.axis_index("tensor") & 1
    hid = hidden.reshape(frames, width)
    cot = cotangent.reshape(frames, width)
    text = text_states.reshape(text_rows, width)
    gain1, bias1 = ln1_gain.reshape(1, width), ln1_bias.reshape(1, width)
    gain2, bias2 = ln2_gain.reshape(1, width), ln2_bias.reshape(1, width)
    gain3, bias3 = ln3_gain.reshape(1, width), ln3_bias.reshape(1, width)
    own_rows = pl.BlockSpec((half, width), lambda i, table: (table[CORE], 0))
    sib_rows = pl.BlockSpec((half, width), lambda i, table: (table[PEER], 0))
    half_mm = 2 * half * width
    whole = dp_size == 8
    orders = ("yab", "aby", "bya") if whole else ("bay",) * 3
    order_one, order_two, order_three = orders

    own3, first = launch(
        prepare,
        info,
        (self_o, cross_o, cross_q),
        [None] * 3,
        [arr((3 * cols, width)), arr((cols, width))],
        [None] * 2,
        flops=1 << 20,
    )
    far_one = x_swap(first)
    sib3 = core_swap(own3)

    def weight_at(i):
        return pl.BlockSpec((cols, width), lambda *_: (i, 0))

    step = frames // 4
    a1, q1, k1, v1 = launch(
        norm_project,
        info,
        (after(hid, first), gain1, bias1, self_q, self_k, self_v),
        [pl.BlockSpec((step, width), lambda i, _: (i, 0))] + [None] * 5,
        [arr((frames, width), BF)] + [arr((frames, cols), BF)] * 3,
        [pl.BlockSpec((step, width), lambda i, _: (i, 0))]
        + [pl.BlockSpec((step, cols), lambda i, _: (i, 0))] * 3,
        grid=(4,),
        flops=2 * frames * width * cols * 3,
    )
    heads = cols // HD
    pair_in = pl.BlockSpec((frames, PAIR), lambda h, _: (0, h // 2))
    pair_half = pl.BlockSpec((half, PAIR), lambda h, _: (0, h // 2))
    level = pl.BlockSpec((1, 1, frames), lambda h, _: (h, 0, 0))
    o1_own, o1_sib, total1 = launch(
        self_forward,
        info,
        (q1, k1, v1),
        [pair_in] * 3,
        [arr((half, cols))] * 2 + [arr((heads, 1, frames))],
        [pair_half] * 2 + [level],
        grid=(heads,),
        scratch=[pltpu.VMEM((frames, PAIR), F32)],
        flops=heads * frames * frames * 512,
        exps=heads * frames * frames,
    )
    o1_cross = cross_swap(o1_sib)
    o1_core = core_swap(after(o1_sib, sib3))
    o1_x = x_swap(after(o1_own, far_one))
    far_two = swap(after(far_one, o1_own), "dp", dp_size, FLIPS["y"])
    k2, v2 = launch(
        text_project,
        info,
        (after(text, o1_own), cross_k, cross_v),
        [None] * 3,
        [arr((text_rows, cols), BF)] * 2,
        [None] * 2,
        flops=2 * text_rows * width * cols * 2,
    )

    def mixed(one, two, i):
        return launch(
            mix,
            info,
            (one, two, own3, sib3),
            [None] * 2 + [weight_at(i)] * 2,
            [arr((half, width))],
            [None],
            flops=half_mm * 512,
        )[0]

    pre1 = mixed(after(o1_own, k2), o1_core, 0)
    far_one_core = core_swap(after(far_one, o1_core))
    far_two_core = core_swap(after(far_two, o1_x, o1_cross, pre1))
    far_weights = (far_one, far_two, far_one_core, far_two_core)

    def normed_mix(which, base, spec, pre, one, two, weights, gain, bias, packs=0):
        return launch(
            functools.partial(mix_norm, which),
            info,
            (base, pre, one, two, *weights, gain, bias),
            [spec] + [None] * (5 + len(weights)),
            [arr((half, width))] * 2 + [arr((cols // 2, width))] * packs,
            [None] * (2 + packs),
            scratch=[pltpu.VMEM((2 * cols, width), BF)],
            cost=2,
        )

    h1, a2, pack_co, pack_cq = normed_mix(None, hid, own_rows, pre1, o1_x, o1_cross, far_weights, gain2, bias2, 2)
    a2_sib = core_swap(a2)

    smem = pl.BlockSpec(memory_space=pltpu.SMEM)

    def cross(a):
        return launch(
            cross_forward,
            info,
            (text_len, a, cross_q, k2, v2),
            [smem] + [None] * 4,
            [arr((half, cols), BF), arr((half, cols)), arr((heads, 1, half))],
            [None] * 3,
            flops=half_mm * cols + heads * half * text_rows * 512,
            exps=heads * half * text_rows,
        )

    q2_own, o2_own, total2_own = cross(a2)
    o2_x = x_swap(after(o2_own, o1_x))
    q2_sib, o2_sib, total2_sib = cross(after(a2_sib, q2_own))
    o2_cross = cross_swap(after(o2_sib, o1_cross))
    o2_core = core_swap(o2_sib)
    far_co = swap(pack_co, "dp", dp_size, FLIPS["a"])
    far_cq = swap(pack_cq, "dp", dp_size, FLIPS["b"])
    pre2 = mixed(o2_own, o2_core, 1)
    far_co_core = core_swap(after(far_co, o2_x, o2_cross, far_cq, pre2))
    co_weights = (
        *(far_one, far_two, far_co),
        *(far_one_core, far_two_core, far_co_core),
    )
    h2, a3 = normed_mix(0, h1, None, pre2, o2_x, o2_cross, co_weights, gain3, bias3)
    a3_sib = core_swap(a3)
    far_cq_core = core_swap(after(far_cq, a3))

    unit = 256

    def feed(a, rows):
        return launch(
            feed_forward,
            info,
            (a, cot, ffn_up, ffn_down),
            [
                None,
                rows,
                pl.BlockSpec((width, unit), lambda i, _: (0, i)),
                pl.BlockSpec((unit, width), lambda i, _: (i, 0)),
            ],
            [arr((half, inner), BF)] * 2 + [arr((half, width))],
            [pl.BlockSpec((half, unit), lambda i, _: (0, i))] * 2 + [None],
            grid=(inner // unit,),
            flops=half_mm * inner * 3,
            exps=half * inner * 2,
        )

    g_own, du_own, da3_own = feed(a3, own_rows)
    g_sib, du_sib, da3_sib = feed(after(a3_sib, g_own, far_cq_core), sib_rows)
    da3_sum = da3_own + core_swap(da3_sib)
    da3_far = x_swap(after(da3_sum, o2_x))
    cot_own = lax.dynamic_slice_in_dim(cot, core * half, half)
    cot_sib = lax.dynamic_slice_in_dim(cot, (1 - core) * half, half)
    ffn_plan = (
        (order_one, ((0, 0, 640),)),
        (order_two, ((1, 0, 640),)),
        (order_three, ((0, 640, 384), (1, 640, 384))),
    )
    ffn = weight_grads(
        info,
        [
            ([after(a3, da3_sum), a3_sib], [[du_own], [du_sib]]),
            ([cot_own, cot_sib], [[g_own], [g_sib]]),
        ],
        ffn_plan,
    )
    out_own, out_sib = launch(
        down_project,
        info,
        (after(g_own, *ffn[1::2]), g_sib, ffn_down),
        [None, None, pl.BlockSpec((inner, 512), lambda i, _: (0, i))],
        [arr((half, width))] * 2,
        [pl.BlockSpec((half, 512), lambda i, _: (0, i))] * 2,
        grid=(width // 512,),
        flops=2 * half_mm * inner,
    )
    out_got = core_swap(out_sib)
    e1, grads3 = launch(
        sum_norm_back,
        info,
        (da3_sum, after(da3_far, out_own), gain3, h2, cot),
        [None] * 4 + [own_rows],
        [arr((half, width)), arr((2, width))],
        [None] * 2,
        cost=2,
    )
    e1_sib = core_swap(e1)
    pins = []
    if whole:
        ffn = list(zip(ffn[0::2], ffn[1::2]))
        ffn = exchange(ffn, orders, 0, e1)
        pins = sent(ffn)

    def cross_back(e, q, total, sums):
        last = bool(sums)
        return launch(
            functools.partial(cross_backward, last),
            info,
            (text_len, e, cross_o, q, k2, v2, total, *sums),
            [smem] + [None] * (6 + len(sums)),
            [arr((half, cols))] + [arr((text_rows, cols), BF if last else F32)] * 2,
            [None] * 3,
            cost=0 if last else 5,
        )

    dq2_own, *sums = cross_back(after(e1, out_got, *pins), q2_own, total2_own, ())
    dq2_sib, dk2, dv2 = cross_back(e1_sib, q2_sib, total2_sib, tuple(sums))
    dq2_cross = cross_swap(dq2_sib)
    dq2_core = core_swap(dq2_sib)
    dq2_x = x_swap(after(dq2_own, da3_far))
    pre3 = mixed(dq2_own, dq2_core, 2)
    cq_weights = (
        *(far_one, far_two, far_cq),
        *(far_one_core, far_two_core, far_cq_core),
    )

    text_half = text_rows // 2
    text_own, text_send = launch(
        text_back,
        info,
        (dk2, dv2, cross_k, cross_v),
        [None] * 4,
        [arr((text_half, width))] * 2,
        [None] * 2,
        scratch=[pltpu.VMEM((text_rows, width), F32)],
        flops=2 * text_rows * width * cols * 2,
    )
    cross_plan = (
        (order_one, ((0, 0, 256), (2, 0, 128))),
        (order_two, ((1, 0, 256), (2, 128, 128))),
        (order_three, ((2, 256, 256),)),
    )
    cross = weight_grads(
        info,
        [
            ([e1, e1_sib], [[o2_own], [o2_sib]]),
            ([a2, a2_sib], [[dq2_own], [dq2_sib]]),
            ([text], [[dk2, dv2]]),
        ],
        cross_plan,
    )
    e0, grads2 = launch(
        mix_norm_back,
        info,
        (pre3, dq2_x, dq2_cross, *cq_weights, gain2, h1, e1),
        [None] * (6 + len(cq_weights)),
        [arr((half, width)), arr((2, width))],
        [None] * 2,
        scratch=[pltpu.VMEM((2 * cols, width), BF)],
        cost=0,
    )
    text_got = core_swap(text_send)
    out_two = launch(
        out_second,
        info,
        (out_own, out_got, text_own, after(text_got, e0)),
        [None] * 4,
        [arr((half + text_half, width))],
        [None],
    )[0]
    out_far_two = x_swap(after(out_two, dq2_x))
    e0_sib = core_swap(e0)
    if whole:
        ffn = exchange(ffn, orders, 1, cross[0])
        up_grad, down_grad = exchange(ffn, orders, 2, e0, finish_ffn)
        cross = [(k, after(c, up_grad)) for k, c in zip(cross[0::2], cross[1::2])]

    do1 = launch(
        mixed_back,
        info,
        (e0, e0_sib, self_o),
        [None] * 3,
        [arr((frames, cols), BF)],
        [None],
    )[0]
    dq1, dk1, dv1 = launch(
        self_backward,
        info,
        (q1, k1, v1, do1, total1),
        [pair_in] * 4 + [level],
        [arr((frames, cols), BF)] * 3,
        [pair_in] * 3,
        grid=(heads,),
        scratch=[pltpu.VMEM((frames, PAIR), F32)] * 3,
        flops=heads * frames * frames * 256 * 5,
        exps=heads * frames * frames,
    )
    pins = []
    if whole:
        cross = exchange(cross, orders, 0, dq1)
        pins = sent(cross)
    da1_own, da1_send = launch(
        first_back,
        info,
        (after(dq1, *pins), dk1, dv1, self_q, self_k, self_v),
        [None] * 6,
        [arr((half, width))] * 2,
        [None] * 2,
        flops=2 * half_mm * 3 * cols,
    )
    da1_sum, grads1 = launch(
        sum_first_grads,
        info,
        (da1_own, core_swap(da1_send), hid),
        [None] * 2 + [own_rows],
        [arr((half, width)), arr((2, width))],
        [None] * 2,
        flops=half_mm * 8,
    )
    da1_far = x_swap(after(da1_sum, out_far_two))

    vectors = (grads1, grads2, grads3)
    if not whole:
        stacked = lax.psum(jnp.concatenate(vectors), "tensor")
        stacked = lax.psum_scatter(stacked, "dp", scatter_dimension=1, tiled=True)
        vectors = ()
    self_plan = (
        (order_one, ((0, 0, 256), (1, 512, 128))),
        (order_two, ((1, 0, 256), (1, 640, 128))),
        (order_three, ((1, 256, 256),)),
    )
    own = weight_grads(
        info,
        [
            ([after(e0, da1_sum), e0_sib], [[o1_own], [o1_sib]]),
            ([a1], [[dq1, dk1, dv1]]),
        ],
        self_plan,
        vectors,
    )
    out_final = launch(
        out_sum,
        info,
        (h2, out_two, after(out_far_two, own[0])),
        [None] * 3,
        [arr((half + text_half, width))],
        [None],
    )[0]
    output, text_grad = launch(
        out_place,
        info,
        (out_final, core_swap(out_final)),
        [None] * 2,
        [arr((frames, width), BF), arr((text_rows, width))],
        [None] * 2,
    )
    if whole:
        own = list(zip(own[0::2], own[1::2]))
        cross = exchange(cross, orders, 1, da1_sum)
        co_grad, cq_grad, ck_grad, cv_grad = exchange(cross, orders, 2, None, finish_cross)
        own = exchange([(k, after(c, co_grad)) for k, c in own], orders, 0)
        own = exchange(own, orders, 1)
        so_grad, sq_grad, sk_grad, sv_grad, stacked = exchange(own, orders, 2, None, finish_self)
        pins = [so_grad]
    else:
        ffn, cross, own = (
            [scatter_sum(*p) for p in zip(g[0::2], g[1::2])] for g in (ffn, cross, own)
        )
        up_grad = jnp.concatenate([ffn[0], ffn[2][:, :384]], 1)
        down_grad = jnp.concatenate([ffn[1], ffn[2][:, 384:]], 1).T
        co_grad, cq_grad, cv_grad = cross[0][:, :256].T, cross[1][:, :256], cross[2]
        ck_grad = jnp.concatenate([cross[0][:, 256:], cross[1][:, 256:]], 1)
        so_grad, sq_grad, sk_grad = own[0][:, :256].T, own[1][:, :256], own[2]
        sv_grad = jnp.concatenate([own[0][:, 256:], own[1][:, 256:]], 1)
        pins = []
    last = launch(
        last_norm_back,
        info,
        (da1_sum, after(da1_far, *pins), gain1, hid, e0),
        [None] * 3 + [own_rows, None],
        [arr((half, width))],
        [None],
        flops=half_mm * 8,
    )[0]
    hidden_grad = launch(
        place,
        info,
        (last, core_swap(last)),
        [None] * 2,
        [arr((frames, width), BF)],
        [None],
    )[0]
    if whole:
        stacked = stacked + x_swap(after(stacked, da1_far))
        stacked = stacked + core_swap(stacked)
    return (
        output.reshape(hidden.shape),
        hidden_grad.reshape(hidden.shape),
        text_grad.reshape(text_states.shape),
        stacked[0],
        stacked[1],
        sq_grad,
        sk_grad,
        sv_grad,
        so_grad,
        stacked[2],
        stacked[3],
        cq_grad,
        ck_grad,
        cv_grad,
        co_grad,
        stacked[4],
        stacked[5],
        up_grad,
        down_grad,
    )


def solution(mesh):
    rows = P("dp", None, None)
    column, row = P(None, "tensor"), P("tensor", None)
    in_specs = (
        *(rows, rows, P("dp"), P(), P(), column, column, column, row),
        *(P(), P(), column, column, column, row),
        *(P(), P(), column, row, rows),
    )
    vector, down, across = P("dp"), P("dp", "tensor"), P("tensor", "dp")
    out_specs = (
        *(rows, rows, rows, vector, vector, down, down, down, across),
        *(vector, vector, down, down, down, across),
        *(vector, vector, down, across),
    )
    return jax.shard_map(body, mesh=mesh, in_specs=in_specs, out_specs=out_specs, check_vma=False)
```

```python
import functools

import jax
import jax.numpy as jnp
import numpy as np
from jax import lax
from jax.experimental import pallas as pl
from jax.experimental.pallas import tpu as pltpu
from jax.sharding import PartitionSpec as P

HD = 64
EPS = 1e-05
NEG = -1e30
SCALE = HD ** (-0.5)
BF = jnp.bfloat16
F32 = jnp.float32
PAIR = 2 * HD

FLIPS = WEIGHT = {"y": 1, "a": 2, "m": 4}

CORE, PEER, Y, LABEL, TABLE = 0, 1, 2, 3, 8


def index_table(dp_size):
    rows = []
    for me in range(dp_size):
        for t in range(4):
            row = [t & 1, 1 - (t & 1), me & 1, me & 3, 0, 0, 0, 0]
            row += [(me ^ i) if dp_size == 8 else i for i in range(8)]
            rows.append(row)
    return np.array(rows, np.int32)


def dot(left, right):
    return lax.dot_general(left, right, (((1,), (0,)), ((), ())), preferred_element_type=F32)


def against(left, right):
    return lax.dot_general(left, right, (((1,), (1,)), ((), ())), preferred_element_type=F32)


def over_rows(left, right):
    return lax.dot_general(left, right, (((0,), (0,)), ((), ())), preferred_element_type=F32)


def swap(value, axis, size, flip):
    return lax.ppermute(value, axis, [(i, i ^ flip) for i in range(size)])


def core_swap(value):
    return swap(value, "tensor", 4, 1)


def x_swap(value):
    return swap(value, "tensor", 4, 2)


def cross_swap(value):
    return swap(value, "tensor", 4, 3)


def after(value, *others):
    return lax.optimization_barrier((value, *others))[0]


def full(shape):
    return pl.BlockSpec(shape, lambda *_: (0,) * len(shape))


def launch(body, info, args, in_specs, outs, out_specs, grid=(1,), scratch=(), flops=0, exps=0, grant=20, cost=0):
    specs = [full(a.shape) if s is None else s for a, s in zip(args, in_specs)]
    ospecs = [full(o.shape) if s is None else s for o, s in zip(outs, out_specs)]
    return pl.pallas_call(
        body,
        out_shape=list(outs),
        grid_spec=pltpu.PrefetchScalarGridSpec(
            num_scalar_prefetch=1,
            grid=grid,
            in_specs=specs,
            out_specs=ospecs,
            scratch_shapes=list(scratch),
        ),
        compiler_params=pltpu.CompilerParams(vmem_limit_bytes=grant << 20),
        cost_estimate=pl.CostEstimate(
            flops=1 + cost * 10**9, bytes_accessed=1, transcendentals=0
        ),
        name=body.__name__ if hasattr(body, "__name__") else body.func.__name__,
    )(info, *args)


def arr(shape, dtype=F32):
    return jax.ShapeDtypeStruct(shape, dtype)


def normed(values):
    centred = values - jnp.mean(values, -1, keepdims=True)
    inverse = lax.rsqrt(jnp.mean(centred * centred, -1, keepdims=True) + EPS)
    return centred * inverse, inverse


def norm_back(grad, scaled, inverse, gain):
    weighted = grad * gain
    first = jnp.mean(weighted, -1, keepdims=True)
    second = jnp.mean(weighted * scaled, -1, keepdims=True)
    return inverse * (weighted - first - scaled * second)


def head_lanes(odd, dtype):
    lane = lax.broadcasted_iota(jnp.int32, (1, PAIR), 1)
    return ((lane // HD) == odd).astype(dtype)


def norm_project(info, hid, gain, bias, wq, wk, wv, a1, q, k, v):
    scaled, _ = normed(hid[...].astype(F32))
    low = (scaled * gain[...] + bias[...]).astype(BF)
    a1[...] = low
    q[...] = (dot(low, wq[...]) * SCALE).astype(BF)
    k[...] = dot(low, wk[...]).astype(BF)
    v[...] = dot(low, wv[...]).astype(BF)


def text_project(info, text, wk, wv, k, v):
    k[...] = dot(text[...], wk[...]).astype(BF)
    v[...] = dot(text[...], wv[...]).astype(BF)


def blocks_of(rows, step=256):
    return [(s, min(step, rows - s)) for s in range(0, rows, step)]


def causal(scores):
    key = lax.broadcasted_iota(jnp.int32, scores.shape, 0)
    query = lax.broadcasted_iota(jnp.int32, scores.shape, 1)
    return jnp.where(key <= query, scores, NEG)


def self_forward(info, q, k, v, keep, send, total, mixed):
    rows = q.shape[0]
    half = rows // 2
    odd = lax.rem(pl.program_id(0), 2)
    lanes = head_lanes(odd, BF)
    lanes_on = head_lanes(odd, F32) > 0
    for start, size in blocks_of(rows):
        here = slice(start, start + size)
        query = q[here, :] * lanes
        near = causal(against(k[here, :], query))
        top = jnp.max(near, 0, keepdims=True)
        if start:
            far = against(k[:start, :], query)
            top = jnp.maximum(top, jnp.max(far, 0, keepdims=True))
        near = jnp.exp(near - top)
        count = jnp.sum(near, 0, keepdims=True)
        if start:
            far = jnp.exp(far - top)
            count = count + jnp.sum(far, 0, keepdims=True)
        scale = 1.0 / count
        out = over_rows(v[here, :], (near * scale).astype(BF))
        if start:
            out = out + over_rows(v[:start, :], (far * scale).astype(BF))
        total[0, :, here] = top + jnp.log(count)
        mixed[here, :] = jnp.where(lanes_on, out.T, mixed[here, :])

    @pl.when(odd == 1)
    def _():
        keep[...] = mixed[pl.ds(pl.multiple_of(info[CORE] * half, 8), half), :]
        send[...] = mixed[pl.ds(pl.multiple_of(info[PEER] * half, 8), half), :]


def prepare(info, so, co, cq, own, first):
    own[0:256, :] = so[...].astype(F32)
    own[256:512, :] = co[...].astype(F32)
    own[512:768, :] = cq[...].astype(F32).T
    first[0:128, :] = own[pl.ds(pl.multiple_of(info[Y] * 128, 8), 128), :]
    for i in range(2):
        at = pl.multiple_of(256 + i * 256 + info[LABEL] * 64, 8)
        first[128 + i * 64 : 192 + i * 64, :] = own[pl.ds(at, 64), :]


def mix(info, one, two, w_one, w_two, out):
    out[...] = dot(one[...].astype(BF), w_one[...].astype(BF)) + dot(
        two[...].astype(BF), w_two[...].astype(BF)
    )


def gather_halves(info, far, weights):
    for s in range(2):
        for p in range(2):

            @pl.when(info[Y] == p)
            def _(s=s, p=p):
                weights[s * 256 + p * 128 : s * 256 + p * 128 + 128, :] = far[2 * s][
                    :128, :
                ].astype(BF)

            @pl.when(info[Y] != p)
            def _(s=s, p=p):
                weights[s * 256 + p * 128 : s * 256 + p * 128 + 128, :] = far[2 * s + 1][
                    :128, :
                ].astype(BF)


def gather_quarters(info, far, weights, first):
    for s in range(2):
        over_x, over_y, over_z = far[3 * s : 3 * s + 3]
        pieces = (
            over_x[128 + first : 192 + first, :],
            over_y[128 + first : 192 + first, :],
            over_z[:64, :],
            over_z[64:, :],
        )
        for j, piece in enumerate(pieces):
            at = pl.multiple_of(s * 256 + (info[LABEL] ^ j) * 64, 64)
            weights[pl.ds(at, 64), :] = piece.astype(BF)


def mix_far(info, pre, one, two, far, weights, which):
    if which is None:
        gather_halves(info, far, weights)
    else:
        gather_quarters(info, far, weights, which)
    far_part = dot(one[...].astype(BF), weights[:256, :]) + dot(
        two[...].astype(BF), weights[256:, :]
    )
    return pre[...] + far_part


def mix_norm(which, info, base, pre, one, two, *refs):
    n = 7 if which is None else 5
    far, (gain, bias, resid, low, *packs, weights) = refs[:-n], refs[-n:]
    for i, pack in enumerate(packs):
        for j in range(2):
            pack[j * 64 : j * 64 + 64, :] = far[2 + j][128 + i * 64 : 192 + i * 64, :]
    part = mix_far(info, pre, one, two, far, weights, which)
    total = base[...].astype(F32) + part
    resid[...] = total
    scaled, _ = normed(total)
    low[...] = scaled * gain[...] + bias[...]


def mix_norm_back(info, pre, one, two, *refs):
    far, (gain, resid, e_in, e_out, grads, weights) = refs[:-6], refs[-6:]
    grad = mix_far(info, pre, one, two, far, weights, 64)
    scaled, inverse = normed(resid[...])
    e_out[...] = e_in[...] + norm_back(grad, scaled, inverse, gain[...])
    grads[0:1, :] = jnp.sum(grad * scaled, 0, keepdims=True) * 0.5
    grads[1:2, :] = jnp.sum(grad, 0, keepdims=True) * 0.5


def sum_norm_back(info, mine, far, gain, resid, e_in, e_out, grads):
    grad = mine[...] + far[...]
    scaled, inverse = normed(resid[...])
    e_out[...] = e_in[...].astype(F32) + norm_back(grad, scaled, inverse, gain[...])
    grads[0:1, :] = jnp.sum(grad * scaled, 0, keepdims=True) * 0.5
    grads[1:2, :] = jnp.sum(grad, 0, keepdims=True) * 0.5


def sum_first_grads(info, mine, recv, hid, out, grads):
    grad = mine[...] + recv[...]
    out[...] = grad
    scaled, _ = normed(hid[...].astype(F32))
    grads[0:1, :] = jnp.sum(grad * scaled, 0, keepdims=True)
    grads[1:2, :] = jnp.sum(grad, 0, keepdims=True)


def last_norm_back(info, mine, far, gain, hid, e_in, out):
    grad = mine[...] + far[...]
    scaled, inverse = normed(hid[...].astype(F32))
    out[...] = e_in[...] + norm_back(grad, scaled, inverse, gain[...])


def cross_forward(info, length, a2, wq, k, v, q, mixed, total):
    query_rows = (dot(a2[...].astype(BF), wq[...]) * SCALE).astype(BF)
    q[...] = query_rows
    for pair in range(2):
        cols = slice(pair * PAIR, (pair + 1) * PAIR)
        pair_out = None
        for odd in range(2):
            query = query_rows[:, cols] * head_lanes(odd, BF)
            scores = against(k[:, cols], query)
            slot = lax.broadcasted_iota(jnp.int32, scores.shape, 0)
            scores = jnp.where(slot < length[0], scores, NEG)
            top = jnp.max(scores, 0, keepdims=True)
            scores = jnp.exp(scores - top)
            count = jnp.sum(scores, 0, keepdims=True)
            out = over_rows(v[:, cols], (scores * (1.0 / count)).astype(BF)).T
            total[pair * 2 + odd] = top + jnp.log(count)
            pair_out = out if odd == 0 else jnp.where(head_lanes(1, F32) > 0, out, pair_out)
        mixed[:, cols] = pair_out


def feed_forward(info, a3, cot, up, down, g, du, da3):
    n = pl.program_id(0)
    u = dot(a3[...].astype(BF), up[...])
    cdf = 0.5 + 0.5 * lax.erf(u * (0.5**0.5))
    g[...] = (u * cdf).astype(BF)
    slope = cdf + u * jnp.exp(-0.5 * u * u) * (1.0 / (2.0 * np.pi) ** 0.5)
    dg = against(cot[...], down[...]).astype(BF).astype(F32)
    low = (dg * slope).astype(BF)
    du[...] = low
    part = against(low, up[...])

    @pl.when(n == 0)
    def _():
        da3[...] = part

    @pl.when(n > 0)
    def _():
        da3[...] += part


def down_project(info, own, sib, down, out_own, out_sib):
    out_own[...] = dot(own[...], down[...])
    out_sib[...] = dot(sib[...], down[...])


def cross_backward(second, info, length, e1, wo, q, k, v, total, *rest):
    if second:
        dk_in, dv_in, dq, dk_out, dv_out = rest
    else:
        dq, dk_out, dv_out = rest
    mixed_grad = against(e1[...].astype(BF), wo[...]).astype(BF)
    for pair in range(2):
        cols = slice(pair * PAIR, (pair + 1) * PAIR)
        dk = dk_in[:, cols] if second else None
        dv = dv_in[:, cols] if second else None
        pair_dq = None
        for odd in range(2):
            lanes = head_lanes(odd, BF)
            query = q[:, cols] * lanes
            grad = mixed_grad[:, cols] * lanes
            scores = against(k[:, cols], query)
            slot = lax.broadcasted_iota(jnp.int32, scores.shape, 0)
            scores = jnp.where(slot < length[0], scores, NEG)
            probs = jnp.exp(scores - total[pair * 2 + odd])
            prob_grad = against(v[:, cols], grad)
            part = dot(probs.astype(BF), grad)
            dv = part if dv is None else dv + part
            delta = jnp.sum(probs * prob_grad, 0, keepdims=True)
            low = (probs * (prob_grad - delta)).astype(BF)
            part = dot(low, query)
            dk = part if dk is None else dk + part
            out = over_rows(k[:, cols], low).T
            pair_dq = out if odd == 0 else jnp.where(head_lanes(1, F32) > 0, out, pair_dq)
        dq[:, cols] = pair_dq * SCALE
        dk_out[:, cols] = dk.astype(dk_out.dtype)
        dv_out[:, cols] = dv.astype(dv_out.dtype)


def text_back(info, dk, dv, wk, wv, own, send, scratch):
    half = own.shape[0]
    scratch[...] = against(dk[...], wk[...]) + against(dv[...], wv[...])
    own[...] = scratch[pl.ds(pl.multiple_of(info[CORE] * half, 8), half), :]
    send[...] = scratch[pl.ds(pl.multiple_of(info[PEER] * half, 8), half), :]


def mixed_back(info, own, sib, wo, out):
    half = own.shape[0]
    out[pl.ds(pl.multiple_of(info[CORE] * half, 16), half), :] = against(
        own[...].astype(BF), wo[...]
    ).astype(BF)
    out[pl.ds(pl.multiple_of(info[PEER] * half, 16), half), :] = against(
        sib[...].astype(BF), wo[...]
    ).astype(BF)


def self_backward(info, q, k, v, grad_in, total, dq, dk, dv, dq_sum, dk_sum, dv_sum):
    rows = q.shape[0]
    odd = lax.rem(pl.program_id(0), 2)
    lanes = head_lanes(odd, BF)
    lanes_on = head_lanes(odd, F32) > 0

    @pl.when(odd == 0)
    def _():
        dk_sum[...] = jnp.zeros_like(dk_sum)
        dv_sum[...] = jnp.zeros_like(dv_sum)

    for start, size in blocks_of(rows):
        here = slice(start, start + size)
        query = q[here, :] * lanes
        grad = grad_in[here, :] * lanes
        level = total[0, :, here]
        near = jnp.exp(causal(against(k[here, :], query)) - level)
        near_grad = against(v[here, :], grad)
        delta = jnp.sum(near * near_grad, 0, keepdims=True)
        dv_sum[here, :] += dot(near.astype(BF), grad)
        if start:
            far = jnp.exp(against(k[:start, :], query) - level)
            far_grad = against(v[:start, :], grad)
            delta = delta + jnp.sum(far * far_grad, 0, keepdims=True)
            dv_sum[:start, :] += dot(far.astype(BF), grad)
        near_low = (near * (near_grad - delta)).astype(BF)
        dk_sum[here, :] += dot(near_low, query)
        out = over_rows(k[here, :], near_low)
        if start:
            far_low = (far * (far_grad - delta)).astype(BF)
            dk_sum[:start, :] += dot(far_low, query)
            out = out + over_rows(k[:start, :], far_low)
        dq_sum[here, :] = jnp.where(lanes_on, out.T * SCALE, dq_sum[here, :])

    @pl.when(odd == 1)
    def _():
        dq[...] = dq_sum[...].astype(BF)
        dk[...] = dk_sum[...].astype(BF)
        dv[...] = dv_sum[...].astype(BF)


def first_back(info, dq, dk, dv, wq, wk, wv, own, send):
    half = own.shape[0]
    for at, out in ((PEER, send), (CORE, own)):
        here = pl.ds(pl.multiple_of(info[at] * half, 16), half)
        out[...] = (
            against(dq[here, :], wq[...])
            + against(dk[here, :], wk[...])
            + against(dv[here, :], wv[...])
        )


def weight_grad(plan, shapes, n_v, info, *refs):
    at = 0
    groups = []
    for n_left, n_right in shapes:
        groups.append((refs[at : at + n_left], refs[at + n_left : at + n_left + n_right]))
        at += n_left + n_right
    vectors = refs[at : at + n_v]
    outs = refs[at + n_v : at + n_v + 2 * len(plan)]
    lhs, rhs = refs[-2:]
    for g, (lefts, rights) in enumerate(groups):
        row = 0
        per = len(rights) // len(lefts)
        for i, left in enumerate(lefts):
            rows = left.shape[0]
            for j in range(8):
                block = left[:, pl.ds(pl.multiple_of(info[TABLE + j] * 128, 128), 128)]
                lhs[row : row + rows, j * 128 : (j + 1) * 128] = block.astype(BF)
            col = 0
            for right in rights[i * per : (i + 1) * per]:
                rhs[row : row + rows, col : col + right.shape[1]] = right[...].astype(BF)
                col += right.shape[1]
            row += rows
        for s, (order, segments) in enumerate(plan):
            put = 0
            for group, first, width in segments:
                if group == g:
                    for half in range(2):
                        value = over_rows(
                            lhs[:row, half * 512 : half * 512 + 512],
                            rhs[:row, first : first + width],
                        )
                        for q in range(4):
                            j = half * 4 + q
                            sent, pos = spot(order, j)
                            outs[2 * s + sent][pos, :128, put : put + width] = value[
                                q * 128 : (q + 1) * 128, :
                            ]
                put += width
    if n_v:
        for j in range(8):
            sent, pos = spot(plan[-1][0], j)
            out = outs[2 * len(plan) - 2 + sent]
            out[pos, 128:, :] = jnp.zeros((8, out.shape[2]), F32)
            for i, ref in enumerate(vectors):
                block = ref[:, pl.ds(pl.multiple_of(info[TABLE + j] * 128, 128), 128)]
                out[pos, 128 + 2 * i : 130 + 2 * i, :128] = block


def spot(order, j):
    bits = [(j // WEIGHT[name]) & 1 for name in order]
    return bits[0], bits[1] * 2 + bits[2]


def weight_grads(info, groups, plan, vectors=()):
    args, shapes, flops = [], [], 0
    for lefts, rights in groups:
        flat = [r for group in rights for r in group]
        args += [*lefts, *flat]
        shapes.append((len(lefts), len(flat)))
        flops += 2 * sum(a.shape[0] for a in lefts) * 1024 * sum(r.shape[1] for r in rights[0])
    args += vectors
    outs = []
    for s, (order, segments) in enumerate(plan):
        tall = 136 if vectors and s == len(plan) - 1 else 128
        outs += [arr((4, tall, sum(w for _, _, w in segments)))] * 2
    rows = max(sum(a.shape[0] for a in lefts) for lefts, _ in groups)
    wide = max(sum(r.shape[1] for r in rights[0]) for _, rights in groups)
    return launch(
        functools.partial(weight_grad, plan, tuple(shapes), len(vectors)),
        info,
        tuple(args),
        [None] * len(args),
        outs,
        [None] * len(outs),
        scratch=[pltpu.VMEM((rows, 1024), BF), pltpu.VMEM((rows, wide), BF)],
        flops=flops,
        grant=40,
    )


def scatter_sum(keep, send):
    value = jnp.concatenate([keep, send])
    value = value.reshape(-1, value.shape[-1])
    return lax.psum_scatter(value, "dp", scatter_dimension=0, tiled=True)


def fold(info, *refs):
    for i in range(2):
        keep, got = refs[2 * i : 2 * i + 2]
        keep_out, send_out = refs[4 + 2 * i : 6 + 2 * i]
        n = keep_out.shape[0]
        keep_out[...] = keep[:n] + got[:n]
        send_out[...] = keep[n:] + got[n:]


def fold_last(info, *refs):
    keep_out, send_out = refs[4:]
    col = 0
    for i in range(2):
        keep, got = refs[2 * i : 2 * i + 2]
        rows, wide = keep.shape[1:]
        keep_out[:rows, col : col + wide] = keep[0] + got[0]
        send_out[:rows, col : col + wide] = keep[1] + got[1]
        col += wide


def finish_ffn(info, keep, got, up, down):
    wide = up.shape[1]
    up[...] = keep[:, :wide] + got[:, :wide]
    down[...] = (keep[:, wide:] + got[:, wide:]).T


def finish_cross(info, keep, got, co, ck, cq, cv):
    co[...] = (keep[:, :256] + got[:, :256]).T
    for i, out in enumerate((ck, cq, cv)):
        here = slice(256 * i + 256, 256 * i + 512)
        out[...] = keep[:, here] + got[:, here]


def finish_self(info, keep, got, so, sk, sq, sv, vectors):
    so[...] = (keep[:128, :256] + got[:128, :256]).T
    for i, out in enumerate((sk, sq, sv)):
        here = slice(256 * i + 256, 256 * i + 512)
        out[...] = keep[:128, here] + got[:128, here]
    vectors[...] = keep[128:, 512:640] + got[128:, 512:640]


FINISH = {
    finish_ffn: [(128, 1024), (1024, 128)],
    finish_cross: [(256, 128), (128, 256), (128, 256), (128, 256)],
    finish_self: [(256, 128), (128, 256), (128, 256), (128, 256), (8, 128)],
}


def exchange(streams, orders, step, first=None, cost=10):
    args = []
    for (keep, send), order in zip(streams, orders):
        got = swap(send, "dp", 8, FLIPS[order[step]])
        args += [keep, got if first is None else after(got, first)]
    none = jnp.zeros((1,), jnp.int32)
    if step == 1:
        shape = (max(a.shape[1] for a in args), args[0].shape[2] + args[2].shape[2])
        return launch(
            fold_last, none, args, [None] * 4, [arr(shape)] * 2, [None] * 2, cost=cost
        )
    outs = []
    for keep, _ in streams:
        outs += [arr((keep.shape[0] // 2, *keep.shape[1:]))] * 2
    out = launch(fold, none, args, [None] * 4, outs, [None] * 4, cost=cost)
    return list(zip(out[0::2], out[1::2]))


def finish(pair, body, first=None):
    keep, send = pair
    got = swap(send, "dp", 8, FLIPS["m"])
    got = got if first is None else after(got, first)
    outs = [arr(shape) for shape in FINISH[body]]
    none = jnp.zeros((1,), jnp.int32)
    return launch(body, none, (keep, got), [None] * 2, outs, [None] * len(outs), cost=10)


def sent(streams):
    return [s for _, s in streams]


def out_second(info, own, got, text_own, text_got, out):
    half = own.shape[0]
    out[:half, :] = own[...] + got[...]
    out[half:, :] = text_own[...] + text_got[...]


def out_sum(info, resid, mine, far, out):
    half = resid.shape[0]
    out[:half, :] = resid[...] + (mine[:half, :] + far[:half, :])
    out[half:, :] = mine[half:, :] + far[half:, :]


def out_place(info, own, sib, out, text_out):
    half = out.shape[0] // 2
    text_half = text_out.shape[0] // 2
    for at, ref in ((CORE, own), (PEER, sib)):
        out[pl.ds(pl.multiple_of(info[at] * half, 16), half), :] = ref[:half, :].astype(BF)
        spot = pl.multiple_of(info[at] * text_half, 8)
        text_out[pl.ds(spot, text_half), :] = ref[half:, :]


def place(info, own, sib, out):
    half = out.shape[0] // 2
    for at, ref in ((CORE, own), (PEER, sib)):
        out[pl.ds(pl.multiple_of(info[at] * half, 16), half), :] = ref[...].astype(BF)


def body(
    hidden,
    text_states,
    text_len,
    ln1_gain,
    ln1_bias,
    self_q,
    self_k,
    self_v,
    self_o,
    ln2_gain,
    ln2_bias,
    cross_q,
    cross_k,
    cross_v,
    cross_o,
    ln3_gain,
    ln3_bias,
    ffn_up,
    ffn_down,
    cotangent,
):
    dp_size = lax.axis_size("dp")
    frames, width = hidden.shape[1:]
    text_rows = text_states.shape[1]
    cols = self_q.shape[1]
    inner = ffn_up.shape[1]
    half = frames // 2
    device = lax.axis_index("dp") * 4 + lax.axis_index("tensor")
    table = jnp.asarray(index_table(dp_size))
    info = lax.dynamic_index_in_dim(table, device, 0, keepdims=False)
    core = lax.axis_index("tensor") & 1
    hid = hidden.reshape(frames, width)
    cot = cotangent.reshape(frames, width)
    text = text_states.reshape(text_rows, width)
    gain1, bias1 = ln1_gain.reshape(1, width), ln1_bias.reshape(1, width)
    gain2, bias2 = ln2_gain.reshape(1, width), ln2_bias.reshape(1, width)
    gain3, bias3 = ln3_gain.reshape(1, width), ln3_bias.reshape(1, width)
    own_rows = pl.BlockSpec((half, width), lambda i, table: (table[CORE], 0))
    sib_rows = pl.BlockSpec((half, width), lambda i, table: (table[PEER], 0))
    half_mm = 2 * half * width
    whole = dp_size == 8
    orders = ("yam", "aym") if whole else ("may",) * 2
    order_one, order_two = orders

    own3, first = launch(
        prepare,
        info,
        (self_o, cross_o, cross_q),
        [None] * 3,
        [arr((3 * cols, width)), arr((cols, width))],
        [None] * 2,
        flops=1 << 20,
    )
    far_one = cross_swap(first)
    sib3 = core_swap(own3)

    def weight_at(i):
        return pl.BlockSpec((cols, width), lambda *_: (i, 0))

    step = frames // 4
    a1, q1, k1, v1 = launch(
        norm_project,
        info,
        (after(hid, first), gain1, bias1, self_q, self_k, self_v),
        [pl.BlockSpec((step, width), lambda i, _: (i, 0))] + [None] * 5,
        [arr((frames, width), BF)] + [arr((frames, cols), BF)] * 3,
        [pl.BlockSpec((step, width), lambda i, _: (i, 0))]
        + [pl.BlockSpec((step, cols), lambda i, _: (i, 0))] * 3,
        grid=(4,),
        flops=2 * frames * width * cols * 3,
    )
    heads = cols // HD
    pair_in = pl.BlockSpec((frames, PAIR), lambda h, _: (0, h // 2))
    pair_half = pl.BlockSpec((half, PAIR), lambda h, _: (0, h // 2))
    level = pl.BlockSpec((1, 1, frames), lambda h, _: (h, 0, 0))
    o1_own, o1_sib, total1 = launch(
        self_forward,
        info,
        (q1, k1, v1),
        [pair_in] * 3,
        [arr((half, cols))] * 2 + [arr((heads, 1, frames))],
        [pair_half] * 2 + [level],
        grid=(heads,),
        scratch=[pltpu.VMEM((frames, PAIR), F32)],
        flops=heads * frames * frames * 512,
        exps=heads * frames * frames,
    )
    o1_cross = cross_swap(after(o1_sib, far_one))
    o1_core = core_swap(after(o1_sib, sib3))
    o1_x = x_swap(o1_own)
    far_two = swap(after(far_one, o1_own), "dp", dp_size, FLIPS["y"])
    k2, v2 = launch(
        text_project,
        info,
        (after(text, o1_own), cross_k, cross_v),
        [None] * 3,
        [arr((text_rows, cols), BF)] * 2,
        [None] * 2,
        flops=2 * text_rows * width * cols * 2,
    )

    def mixed(one, two, i):
        return launch(
            mix,
            info,
            (one, two, own3, sib3),
            [None] * 2 + [weight_at(i)] * 2,
            [arr((half, width))],
            [None],
            flops=half_mm * 512,
        )[0]

    pre1 = mixed(after(o1_own, k2), o1_core, 0)
    far_one_core = core_swap(after(far_one, o1_core))
    far_two_core = core_swap(after(far_two, o1_x, o1_cross, pre1))
    far_weights = (far_one_core, far_two_core, far_one, far_two)

    def normed_mix(which, base, spec, pre, one, two, weights, gain, bias, packs=0):
        return launch(
            functools.partial(mix_norm, which),
            info,
            (base, pre, one, two, *weights, gain, bias),
            [spec] + [None] * (5 + len(weights)),
            [arr((half, width))] * 2 + [arr((cols // 2, width))] * packs,
            [None] * (2 + packs),
            scratch=[pltpu.VMEM((2 * cols, width), BF)],
            cost=2,
        )

    h1, a2, pack_co, pack_cq = normed_mix(None, hid, own_rows, pre1, o1_x, o1_cross, far_weights, gain2, bias2, 2)
    a2_sib = core_swap(a2)

    smem = pl.BlockSpec(memory_space=pltpu.SMEM)

    def cross(a):
        return launch(
            cross_forward,
            info,
            (text_len, a, cross_q, k2, v2),
            [smem] + [None] * 4,
            [arr((half, cols), BF), arr((half, cols)), arr((heads, 1, half))],
            [None] * 3,
            flops=half_mm * cols + heads * half * text_rows * 512,
            exps=heads * half * text_rows,
        )

    q2_own, o2_own, total2_own = cross(a2)
    o2_x = x_swap(after(o2_own, o1_x))
    q2_sib, o2_sib, total2_sib = cross(after(a2_sib, q2_own))
    o2_cross = cross_swap(after(o2_sib, o1_cross))
    o2_core = core_swap(o2_sib)
    far_co = swap(pack_co, "dp", dp_size, FLIPS["a"])
    far_cq = swap(pack_cq, "dp", dp_size, FLIPS["a"])
    pre2 = mixed(o2_own, o2_core, 1)
    far_co_core = core_swap(after(far_co, o2_x, o2_cross, far_cq, pre2))
    co_weights = (
        *(far_one_core, far_two_core, far_co_core),
        *(far_one, far_two, far_co),
    )
    h2, a3 = normed_mix(0, h1, None, pre2, o2_x, o2_cross, co_weights, gain3, bias3)
    a3_sib = core_swap(a3)
    far_cq_core = core_swap(after(far_cq, a3))

    unit = 256

    def feed(a, rows):
        return launch(
            feed_forward,
            info,
            (a, cot, ffn_up, ffn_down),
            [
                None,
                rows,
                pl.BlockSpec((width, unit), lambda i, _: (0, i)),
                pl.BlockSpec((unit, width), lambda i, _: (i, 0)),
            ],
            [arr((half, inner), BF)] * 2 + [arr((half, width))],
            [pl.BlockSpec((half, unit), lambda i, _: (0, i))] * 2 + [None],
            grid=(inner // unit,),
            flops=half_mm * inner * 3,
            exps=half * inner * 2,
        )

    g_own, du_own, da3_own = feed(a3, own_rows)
    g_sib, du_sib, da3_sib = feed(after(a3_sib, g_own, far_cq_core), sib_rows)
    da3_sum = da3_own + core_swap(da3_sib)
    da3_far = x_swap(after(da3_sum, o2_x))
    cot_own = lax.dynamic_slice_in_dim(cot, core * half, half)
    cot_sib = lax.dynamic_slice_in_dim(cot, (1 - core) * half, half)
    ffn_plan = (
        (order_one, ((0, 0, 1024),)),
        (order_two, ((1, 0, 1024),)),
    )
    ffn = weight_grads(
        info,
        [
            ([after(a3, da3_sum), a3_sib], [[du_own], [du_sib]]),
            ([cot_own, cot_sib], [[g_own], [g_sib]]),
        ],
        ffn_plan,
    )
    out_own, out_sib = launch(
        down_project,
        info,
        (after(g_own, *ffn[1::2]), g_sib, ffn_down),
        [None, None, pl.BlockSpec((inner, 512), lambda i, _: (0, i))],
        [arr((half, width))] * 2,
        [pl.BlockSpec((half, 512), lambda i, _: (0, i))] * 2,
        grid=(width // 512,),
        flops=2 * half_mm * inner,
    )
    out_got = core_swap(out_sib)
    e1, grads3 = launch(
        sum_norm_back,
        info,
        (da3_sum, after(da3_far, out_own), gain3, h2, cot),
        [None] * 4 + [own_rows],
        [arr((half, width)), arr((2, width))],
        [None] * 2,
    )
    e1_sib = core_swap(e1)
    def cross_back(e, q, total, sums):
        last = bool(sums)
        return launch(
            functools.partial(cross_backward, last),
            info,
            (text_len, e, cross_o, q, k2, v2, total, *sums),
            [smem] + [None] * (6 + len(sums)),
            [arr((half, cols))] + [arr((text_rows, cols), BF if last else F32)] * 2,
            [None] * 3,
        )

    dq2_own, *sums = cross_back(after(e1, out_got), q2_own, total2_own, ())
    dq2_sib, dk2, dv2 = cross_back(e1_sib, q2_sib, total2_sib, tuple(sums))
    dq2_cross = cross_swap(dq2_sib)
    dq2_core = core_swap(dq2_sib)
    dq2_x = x_swap(after(dq2_own, da3_far))
    pre3 = mixed(dq2_own, dq2_core, 2)
    cq_weights = (
        *(far_one_core, far_two_core, far_cq_core),
        *(far_one, far_two, far_cq),
    )

    text_half = text_rows // 2
    text_own, text_send = launch(
        text_back,
        info,
        (dk2, dv2, cross_k, cross_v),
        [None] * 4,
        [arr((text_half, width))] * 2,
        [None] * 2,
        scratch=[pltpu.VMEM((text_rows, width), F32)],
        flops=2 * text_rows * width * cols * 2,
    )
    cross_plan = (
        (order_one, ((0, 0, 256), (2, 0, 256))),
        (order_two, ((1, 0, 256), (2, 256, 256))),
    )
    cross = weight_grads(
        info,
        [
            ([e1, e1_sib], [[o2_own], [o2_sib]]),
            ([a2, a2_sib], [[dq2_own], [dq2_sib]]),
            ([text], [[dk2, dv2]]),
        ],
        cross_plan,
    )
    pins = []
    if whole:
        ffn = exchange(list(zip(ffn[0::2], ffn[1::2])), orders, 0, cross[0], 12)
        pins = sent(ffn)
    e0, grads2 = launch(
        mix_norm_back,
        info,
        (after(pre3, *pins), dq2_x, dq2_cross, *cq_weights, gain2, h1, e1),
        [None] * (6 + len(cq_weights)),
        [arr((half, width)), arr((2, width))],
        [None] * 2,
        scratch=[pltpu.VMEM((2 * cols, width), BF)],
        cost=0,
    )
    text_got = core_swap(text_send)
    out_two = launch(
        out_second,
        info,
        (out_own, out_got, text_own, after(text_got, e0)),
        [None] * 4,
        [arr((half + text_half, width))],
        [None],
    )[0]
    out_far_two = x_swap(after(out_two, dq2_x))
    e0_sib = core_swap(e0)
    do1 = launch(
        mixed_back,
        info,
        (e0, e0_sib, self_o),
        [None] * 3,
        [arr((frames, cols), BF)],
        [None],
    )[0]
    dq1, dk1, dv1 = launch(
        self_backward,
        info,
        (q1, k1, v1, do1, total1),
        [pair_in] * 4 + [level],
        [arr((frames, cols), BF)] * 3,
        [pair_in] * 3,
        grid=(heads,),
        scratch=[pltpu.VMEM((frames, PAIR), F32)] * 3,
        flops=heads * frames * frames * 256 * 5,
        exps=heads * frames * frames,
    )
    da1_own, da1_send = launch(
        first_back,
        info,
        (dq1, dk1, dv1, self_q, self_k, self_v),
        [None] * 6,
        [arr((half, width))] * 2,
        [None] * 2,
        flops=2 * half_mm * 3 * cols,
    )
    pins = [out_far_two]
    if whole:
        ffn = exchange(ffn, orders, 1, da1_own, 10)
        pins += [ffn[1]]
    da1_sum, grads1 = launch(
        sum_first_grads,
        info,
        (da1_own, after(core_swap(da1_send), *pins), hid),
        [None] * 2 + [own_rows],
        [arr((half, width)), arr((2, width))],
        [None] * 2,
        cost=10,
    )
    da1_far = x_swap(da1_sum)

    vectors = (grads1, grads2, grads3)
    if not whole:
        stacked = lax.psum(jnp.concatenate(vectors), "tensor")
        stacked = lax.psum_scatter(stacked, "dp", scatter_dimension=1, tiled=True)
        vectors = ()
    self_plan = (
        (order_one, ((0, 0, 256), (1, 256, 256))),
        (order_two, ((1, 0, 256), (1, 512, 256))),
    )
    own = weight_grads(
        info,
        [
            ([after(e0, da1_sum), e0_sib], [[o1_own], [o1_sib]]),
            ([a1], [[dq1, dk1, dv1]]),
        ],
        self_plan,
        vectors,
    )
    out_final = launch(
        out_sum,
        info,
        (h2, out_two, after(out_far_two, own[0])),
        [None] * 3,
        [arr((half + text_half, width))],
        [None],
    )[0]
    output, text_grad = launch(
        out_place,
        info,
        (out_final, core_swap(out_final)),
        [None] * 2,
        [arr((frames, width), BF), arr((text_rows, width))],
        [None] * 2,
    )
    if whole:
        own = list(zip(own[0::2], own[1::2]))
        cross = [(k, after(c, ffn[1])) for k, c in zip(cross[0::2], cross[1::2])]
        cross = exchange(cross, orders, 0, own[0][0])
        own = [(k, after(c, *sent(cross))) for k, c in own]
        pins = sent(cross)
    else:
        ffn, cross, own = (
            [scatter_sum(*p) for p in zip(g[0::2], g[1::2])] for g in (ffn, cross, own)
        )
        up_grad, down_grad = ffn[0], ffn[1].T
        co_grad, ck_grad = cross[0][:, :256].T, cross[0][:, 256:]
        cq_grad, cv_grad = cross[1][:, :256], cross[1][:, 256:]
        so_grad, sk_grad = own[0][:, :256].T, own[0][:, 256:]
        sq_grad, sv_grad = own[1][:, :256], own[1][:, 256:]
        pins = []
    last = launch(
        last_norm_back,
        info,
        (da1_sum, after(da1_far, *pins), gain1, hid, e0),
        [None] * 3 + [own_rows, None],
        [arr((half, width))],
        [None],
        flops=half_mm * 8,
    )[0]
    if whole:
        cross = exchange(cross, orders, 1, last)
        own = exchange(own, orders, 0, cross[1])
        up_grad, down_grad = finish(ffn, finish_ffn, last)
        cross = (cross[0], after(cross[1], up_grad))
        co_grad, ck_grad, cq_grad, cv_grad = finish(cross, finish_cross)
        own = exchange(own, orders, 1)
        own = (own[0], after(own[1], co_grad))
        so_grad, sk_grad, sq_grad, sv_grad, stacked = finish(own, finish_self)
    hidden_grad = launch(
        place,
        info,
        (last, core_swap(last)),
        [None] * 2,
        [arr((frames, width), BF)],
        [None],
    )[0]
    if whole:
        stacked = stacked + x_swap(after(stacked, da1_far))
        stacked = stacked + core_swap(stacked)
    return (
        output.reshape(hidden.shape),
        hidden_grad.reshape(hidden.shape),
        text_grad.reshape(text_states.shape),
        stacked[0],
        stacked[1],
        sq_grad,
        sk_grad,
        sv_grad,
        so_grad,
        stacked[2],
        stacked[3],
        cq_grad,
        ck_grad,
        cv_grad,
        co_grad,
        stacked[4],
        stacked[5],
        up_grad,
        down_grad,
    )


def solution(mesh):
    rows = P("dp", None, None)
    column, row = P(None, "tensor"), P("tensor", None)
    in_specs = (
        *(rows, rows, P("dp"), P(), P(), column, column, column, row),
        *(P(), P(), column, column, column, row),
        *(P(), P(), column, row, rows),
    )
    vector, down, across = P("dp"), P("dp", "tensor"), P("tensor", "dp")
    out_specs = (
        *(rows, rows, rows, vector, vector, down, down, down, across),
        *(vector, vector, down, down, down, across),
        *(vector, vector, down, across),
    )
    return jax.shard_map(body, mesh=mesh, in_specs=in_specs, out_specs=out_specs, check_vma=False)
```

```python
import functools

import jax
import jax.numpy as jnp
import numpy as np
from jax import lax
from jax.experimental import pallas as pl
from jax.experimental.pallas import tpu as pltpu
from jax.sharding import PartitionSpec as P

HD = 64
EPS = 1e-05
NEG = -1e30
SCALE = HD ** (-0.5)
BF = jnp.bfloat16
F32 = jnp.float32
PAIR = 2 * HD

FLIPS = WEIGHT = {"y": 1, "a": 2, "m": 4}

CORE, PEER, Y, LABEL, TABLE = 0, 1, 2, 3, 8


def index_table(dp_size):
    rows = []
    for me in range(dp_size):
        for t in range(4):
            row = [t & 1, 1 - (t & 1), me & 1, me & 3, 0, 0, 0, 0]
            row += [(me ^ i) if dp_size == 8 else i for i in range(8)]
            rows.append(row)
    return np.array(rows, np.int32)


def dot(left, right):
    return lax.dot_general(left, right, (((1,), (0,)), ((), ())), preferred_element_type=F32)


def against(left, right):
    return lax.dot_general(left, right, (((1,), (1,)), ((), ())), preferred_element_type=F32)


def over_rows(left, right):
    return lax.dot_general(left, right, (((0,), (0,)), ((), ())), preferred_element_type=F32)


def swap(value, axis, size, flip):
    return lax.ppermute(value, axis, [(i, i ^ flip) for i in range(size)])


def core_swap(value):
    return swap(value, "tensor", 4, 1)


def x_swap(value):
    return swap(value, "tensor", 4, 2)


def cross_swap(value):
    return swap(value, "tensor", 4, 3)


def after(value, *others):
    return lax.optimization_barrier((value, *others))[0]


def full(shape):
    return pl.BlockSpec(shape, lambda *_: (0,) * len(shape))


def launch(body, info, args, in_specs, outs, out_specs, grid=(1,), scratch=(), flops=0, exps=0, grant=20, cost=0):
    specs = [full(a.shape) if s is None else s for a, s in zip(args, in_specs)]
    ospecs = [full(o.shape) if s is None else s for o, s in zip(outs, out_specs)]
    return pl.pallas_call(
        body,
        out_shape=list(outs),
        grid_spec=pltpu.PrefetchScalarGridSpec(
            num_scalar_prefetch=1,
            grid=grid,
            in_specs=specs,
            out_specs=ospecs,
            scratch_shapes=list(scratch),
        ),
        compiler_params=pltpu.CompilerParams(vmem_limit_bytes=grant << 20),
        cost_estimate=pl.CostEstimate(
            flops=1 + cost * 10**9, bytes_accessed=1, transcendentals=0
        ),
        name=body.__name__ if hasattr(body, "__name__") else body.func.__name__,
    )(info, *args)


def arr(shape, dtype=F32):
    return jax.ShapeDtypeStruct(shape, dtype)


def normed(values):
    centred = values - jnp.mean(values, -1, keepdims=True)
    inverse = lax.rsqrt(jnp.mean(centred * centred, -1, keepdims=True) + EPS)
    return centred * inverse, inverse


def norm_back(grad, scaled, inverse, gain):
    weighted = grad * gain
    first = jnp.mean(weighted, -1, keepdims=True)
    second = jnp.mean(weighted * scaled, -1, keepdims=True)
    return inverse * (weighted - first - scaled * second)


def head_lanes(odd, dtype):
    lane = lax.broadcasted_iota(jnp.int32, (1, PAIR), 1)
    return ((lane // HD) == odd).astype(dtype)


def norm_project(info, hid, gain, bias, wq, wk, wv, a1, q, k, v):
    scaled, _ = normed(hid[...].astype(F32))
    low = (scaled * gain[...] + bias[...]).astype(BF)
    a1[...] = low
    q[...] = (dot(low, wq[...]) * SCALE).astype(BF)
    k[...] = dot(low, wk[...]).astype(BF)
    v[...] = dot(low, wv[...]).astype(BF)


def text_project(info, text, wk, wv, k, v):
    k[...] = dot(text[...], wk[...]).astype(BF)
    v[...] = dot(text[...], wv[...]).astype(BF)


def blocks_of(rows, step=256):
    return [(s, min(step, rows - s)) for s in range(0, rows, step)]


def causal(scores):
    key = lax.broadcasted_iota(jnp.int32, scores.shape, 0)
    query = lax.broadcasted_iota(jnp.int32, scores.shape, 1)
    return jnp.where(key <= query, scores, NEG)


def self_forward(info, q, k, v, keep, send, total, mixed):
    rows = q.shape[0]
    half = rows // 2
    odd = lax.rem(pl.program_id(0), 2)
    lanes = head_lanes(odd, BF)
    lanes_on = head_lanes(odd, F32) > 0
    for start, size in blocks_of(rows):
        here = slice(start, start + size)
        query = q[here, :] * lanes
        near = causal(against(k[here, :], query))
        top = jnp.max(near, 0, keepdims=True)
        if start:
            far = against(k[:start, :], query)
            top = jnp.maximum(top, jnp.max(far, 0, keepdims=True))
        near = jnp.exp(near - top)
        count = jnp.sum(near, 0, keepdims=True)
        if start:
            far = jnp.exp(far - top)
            count = count + jnp.sum(far, 0, keepdims=True)
        scale = 1.0 / count
        out = over_rows(v[here, :], (near * scale).astype(BF))
        if start:
            out = out + over_rows(v[:start, :], (far * scale).astype(BF))
        total[0, :, here] = top + jnp.log(count)
        mixed[here, :] = jnp.where(lanes_on, out.T, mixed[here, :])

    @pl.when(odd == 1)
    def _():
        keep[...] = mixed[pl.ds(pl.multiple_of(info[CORE] * half, 8), half), :]
        send[...] = mixed[pl.ds(pl.multiple_of(info[PEER] * half, 8), half), :]


def prepare(info, so, co, cq, own, first):
    own[0:256, :] = so[...].astype(F32)
    own[256:512, :] = co[...].astype(F32)
    own[512:768, :] = cq[...].astype(F32).T
    first[0:128, :] = own[pl.ds(pl.multiple_of(info[Y] * 128, 8), 128), :]
    for i in range(2):
        at = pl.multiple_of(256 + i * 256 + info[LABEL] * 64, 8)
        first[128 + i * 64 : 192 + i * 64, :] = own[pl.ds(at, 64), :]


def mix(info, one, two, w_one, w_two, out):
    out[...] = dot(one[...].astype(BF), w_one[...].astype(BF)) + dot(
        two[...].astype(BF), w_two[...].astype(BF)
    )


def gather_halves(info, far, weights):
    for s in range(2):
        for p in range(2):

            @pl.when(info[Y] == p)
            def _(s=s, p=p):
                weights[s * 256 + p * 128 : s * 256 + p * 128 + 128, :] = far[2 * s][
                    :128, :
                ].astype(BF)

            @pl.when(info[Y] != p)
            def _(s=s, p=p):
                weights[s * 256 + p * 128 : s * 256 + p * 128 + 128, :] = far[2 * s + 1][
                    :128, :
                ].astype(BF)


def gather_quarters(info, far, weights, first):
    for s in range(2):
        over_x, over_y, over_z = far[3 * s : 3 * s + 3]
        pieces = (
            over_x[128 + first : 192 + first, :],
            over_y[128 + first : 192 + first, :],
            over_z[:64, :],
            over_z[64:, :],
        )
        for j, piece in enumerate(pieces):
            at = pl.multiple_of(s * 256 + (info[LABEL] ^ j) * 64, 64)
            weights[pl.ds(at, 64), :] = piece.astype(BF)


def mix_far(info, pre, one, two, far, weights, which):
    if which is None:
        gather_halves(info, far, weights)
    else:
        gather_quarters(info, far, weights, which)
    far_part = dot(one[...].astype(BF), weights[:256, :]) + dot(
        two[...].astype(BF), weights[256:, :]
    )
    return pre[...] + far_part


def mix_norm(which, info, base, pre, one, two, *refs):
    n = 7 if which is None else 5
    far, (gain, bias, resid, low, *packs, weights) = refs[:-n], refs[-n:]
    for i, pack in enumerate(packs):
        for j in range(2):
            pack[j * 64 : j * 64 + 64, :] = far[2 + j][128 + i * 64 : 192 + i * 64, :]
    part = mix_far(info, pre, one, two, far, weights, which)
    total = base[...].astype(F32) + part
    resid[...] = total
    scaled, _ = normed(total)
    low[...] = scaled * gain[...] + bias[...]


def mix_norm_back(info, pre, one, two, *refs):
    far, (gain, resid, e_in, e_out, grads, weights) = refs[:-6], refs[-6:]
    grad = mix_far(info, pre, one, two, far, weights, 64)
    scaled, inverse = normed(resid[...])
    e_out[...] = e_in[...] + norm_back(grad, scaled, inverse, gain[...])
    grads[0:1, :] = jnp.sum(grad * scaled, 0, keepdims=True) * 0.5
    grads[1:2, :] = jnp.sum(grad, 0, keepdims=True) * 0.5


def sum_norm_back(info, mine, far, gain, resid, e_in, e_out, grads):
    grad = mine[...] + far[...]
    scaled, inverse = normed(resid[...])
    e_out[...] = e_in[...].astype(F32) + norm_back(grad, scaled, inverse, gain[...])
    grads[0:1, :] = jnp.sum(grad * scaled, 0, keepdims=True) * 0.5
    grads[1:2, :] = jnp.sum(grad, 0, keepdims=True) * 0.5


def sum_first_grads(info, mine, recv, hid, out, grads):
    grad = mine[...] + recv[...]
    out[...] = grad
    scaled, _ = normed(hid[...].astype(F32))
    grads[0:1, :] = jnp.sum(grad * scaled, 0, keepdims=True)
    grads[1:2, :] = jnp.sum(grad, 0, keepdims=True)


def last_norm_back(info, mine, far, gain, hid, e_in, out):
    grad = mine[...] + far[...]
    scaled, inverse = normed(hid[...].astype(F32))
    out[...] = e_in[...] + norm_back(grad, scaled, inverse, gain[...])


def cross_forward(info, length, a2, wq, k, v, q, mixed, total):
    query_rows = (dot(a2[...].astype(BF), wq[...]) * SCALE).astype(BF)
    q[...] = query_rows
    for pair in range(2):
        cols = slice(pair * PAIR, (pair + 1) * PAIR)
        pair_out = None
        for odd in range(2):
            query = query_rows[:, cols] * head_lanes(odd, BF)
            scores = against(k[:, cols], query)
            slot = lax.broadcasted_iota(jnp.int32, scores.shape, 0)
            scores = jnp.where(slot < length[0], scores, NEG)
            top = jnp.max(scores, 0, keepdims=True)
            scores = jnp.exp(scores - top)
            count = jnp.sum(scores, 0, keepdims=True)
            out = over_rows(v[:, cols], (scores * (1.0 / count)).astype(BF)).T
            total[pair * 2 + odd] = top + jnp.log(count)
            pair_out = out if odd == 0 else jnp.where(head_lanes(1, F32) > 0, out, pair_out)
        mixed[:, cols] = pair_out


def feed_forward(info, a3, cot, up, down, g, du, da3):
    n = pl.program_id(0)
    u = dot(a3[...].astype(BF), up[...])
    cdf = 0.5 + 0.5 * lax.erf(u * (0.5**0.5))
    g[...] = (u * cdf).astype(BF)
    slope = cdf + u * jnp.exp(-0.5 * u * u) * (1.0 / (2.0 * np.pi) ** 0.5)
    dg = against(cot[...], down[...]).astype(BF).astype(F32)
    low = (dg * slope).astype(BF)
    du[...] = low
    part = against(low, up[...])

    @pl.when(n == 0)
    def _():
        da3[...] = part

    @pl.when(n > 0)
    def _():
        da3[...] += part


def down_project(info, own, sib, down, out_own, out_sib):
    out_own[...] = dot(own[...], down[...])
    out_sib[...] = dot(sib[...], down[...])


def cross_backward(second, info, length, e1, wo, q, k, v, total, *rest):
    if second:
        dk_in, dv_in, dq, dk_out, dv_out = rest
    else:
        dq, dk_out, dv_out = rest
    mixed_grad = against(e1[...].astype(BF), wo[...]).astype(BF)
    for pair in range(2):
        cols = slice(pair * PAIR, (pair + 1) * PAIR)
        dk = dk_in[:, cols] if second else None
        dv = dv_in[:, cols] if second else None
        pair_dq = None
        for odd in range(2):
            lanes = head_lanes(odd, BF)
            query = q[:, cols] * lanes
            grad = mixed_grad[:, cols] * lanes
            scores = against(k[:, cols], query)
            slot = lax.broadcasted_iota(jnp.int32, scores.shape, 0)
            scores = jnp.where(slot < length[0], scores, NEG)
            probs = jnp.exp(scores - total[pair * 2 + odd])
            prob_grad = against(v[:, cols], grad)
            part = dot(probs.astype(BF), grad)
            dv = part if dv is None else dv + part
            delta = jnp.sum(probs * prob_grad, 0, keepdims=True)
            low = (probs * (prob_grad - delta)).astype(BF)
            part = dot(low, query)
            dk = part if dk is None else dk + part
            out = over_rows(k[:, cols], low).T
            pair_dq = out if odd == 0 else jnp.where(head_lanes(1, F32) > 0, out, pair_dq)
        dq[:, cols] = pair_dq * SCALE
        dk_out[:, cols] = dk.astype(dk_out.dtype)
        dv_out[:, cols] = dv.astype(dv_out.dtype)


def text_back(info, dk, dv, wk, wv, own, send, scratch):
    half = own.shape[0]
    scratch[...] = against(dk[...], wk[...]) + against(dv[...], wv[...])
    own[...] = scratch[pl.ds(pl.multiple_of(info[CORE] * half, 8), half), :]
    send[...] = scratch[pl.ds(pl.multiple_of(info[PEER] * half, 8), half), :]


def mixed_back(info, own, sib, wo, out):
    half = own.shape[0]
    out[pl.ds(pl.multiple_of(info[CORE] * half, 16), half), :] = against(
        own[...].astype(BF), wo[...]
    ).astype(BF)
    out[pl.ds(pl.multiple_of(info[PEER] * half, 16), half), :] = against(
        sib[...].astype(BF), wo[...]
    ).astype(BF)


def self_backward(info, q, k, v, grad_in, total, dq, dk, dv, dq_sum, dk_sum, dv_sum):
    rows = q.shape[0]
    odd = lax.rem(pl.program_id(0), 2)
    lanes = head_lanes(odd, BF)
    lanes_on = head_lanes(odd, F32) > 0

    @pl.when(odd == 0)
    def _():
        dk_sum[...] = jnp.zeros_like(dk_sum)
        dv_sum[...] = jnp.zeros_like(dv_sum)

    for start, size in blocks_of(rows):
        here = slice(start, start + size)
        query = q[here, :] * lanes
        grad = grad_in[here, :] * lanes
        level = total[0, :, here]
        near = jnp.exp(causal(against(k[here, :], query)) - level)
        near_grad = against(v[here, :], grad)
        delta = jnp.sum(near * near_grad, 0, keepdims=True)
        dv_sum[here, :] += dot(near.astype(BF), grad)
        if start:
            far = jnp.exp(against(k[:start, :], query) - level)
            far_grad = against(v[:start, :], grad)
            delta = delta + jnp.sum(far * far_grad, 0, keepdims=True)
            dv_sum[:start, :] += dot(far.astype(BF), grad)
        near_low = (near * (near_grad - delta)).astype(BF)
        dk_sum[here, :] += dot(near_low, query)
        out = over_rows(k[here, :], near_low)
        if start:
            far_low = (far * (far_grad - delta)).astype(BF)
            dk_sum[:start, :] += dot(far_low, query)
            out = out + over_rows(k[:start, :], far_low)
        dq_sum[here, :] = jnp.where(lanes_on, out.T * SCALE, dq_sum[here, :])

    @pl.when(odd == 1)
    def _():
        dq[...] = dq_sum[...].astype(BF)
        dk[...] = dk_sum[...].astype(BF)
        dv[...] = dv_sum[...].astype(BF)


def first_back(info, dq, dk, dv, wq, wk, wv, own, send):
    half = own.shape[0]
    for at, out in ((PEER, send), (CORE, own)):
        here = pl.ds(pl.multiple_of(info[at] * half, 16), half)
        out[...] = (
            against(dq[here, :], wq[...])
            + against(dk[here, :], wk[...])
            + against(dv[here, :], wv[...])
        )


def weight_grad(plan, shapes, n_v, info, *refs):
    at = 0
    groups = []
    for n_left, n_right in shapes:
        groups.append((refs[at : at + n_left], refs[at + n_left : at + n_left + n_right]))
        at += n_left + n_right
    vectors = refs[at : at + n_v]
    outs = refs[at + n_v : at + n_v + 2 * len(plan)]
    lhs, rhs = refs[-2:]
    for g, (lefts, rights) in enumerate(groups):
        row = 0
        per = len(rights) // len(lefts)
        for i, left in enumerate(lefts):
            rows = left.shape[0]
            for j in range(8):
                block = left[:, pl.ds(pl.multiple_of(info[TABLE + j] * 128, 128), 128)]
                lhs[row : row + rows, j * 128 : (j + 1) * 128] = block.astype(BF)
            col = 0
            for right in rights[i * per : (i + 1) * per]:
                rhs[row : row + rows, col : col + right.shape[1]] = right[...].astype(BF)
                col += right.shape[1]
            row += rows
        for s, (order, segments) in enumerate(plan):
            put = 0
            for group, first, width in segments:
                if group == g:
                    for half in range(2):
                        value = over_rows(
                            lhs[:row, half * 512 : half * 512 + 512],
                            rhs[:row, first : first + width],
                        )
                        for q in range(4):
                            j = half * 4 + q
                            sent, pos = spot(order, j)
                            outs[2 * s + sent][pos, :128, put : put + width] = value[
                                q * 128 : (q + 1) * 128, :
                            ]
                put += width
    if n_v:
        for j in range(8):
            sent, pos = spot(plan[-1][0], j)
            out = outs[2 * len(plan) - 2 + sent]
            out[pos, 128:, :] = jnp.zeros((8, out.shape[2]), F32)
            for i, ref in enumerate(vectors):
                block = ref[:, pl.ds(pl.multiple_of(info[TABLE + j] * 128, 128), 128)]
                out[pos, 128 + 2 * i : 130 + 2 * i, :128] = block


def spot(order, j):
    bits = [(j // WEIGHT[name]) & 1 for name in order]
    return bits[0], bits[1] * 2 + bits[2]


def weight_grads(info, groups, plan, vectors=()):
    args, shapes, flops = [], [], 0
    for lefts, rights in groups:
        flat = [r for group in rights for r in group]
        args += [*lefts, *flat]
        shapes.append((len(lefts), len(flat)))
        flops += 2 * sum(a.shape[0] for a in lefts) * 1024 * sum(r.shape[1] for r in rights[0])
    args += vectors
    outs = []
    for s, (order, segments) in enumerate(plan):
        tall = 136 if vectors and s == len(plan) - 1 else 128
        outs += [arr((4, tall, sum(w for _, _, w in segments)))] * 2
    rows = max(sum(a.shape[0] for a in lefts) for lefts, _ in groups)
    wide = max(sum(r.shape[1] for r in rights[0]) for _, rights in groups)
    return launch(
        functools.partial(weight_grad, plan, tuple(shapes), len(vectors)),
        info,
        tuple(args),
        [None] * len(args),
        outs,
        [None] * len(outs),
        scratch=[pltpu.VMEM((rows, 1024), BF), pltpu.VMEM((rows, wide), BF)],
        flops=flops,
        grant=40,
    )


def scatter_sum(keep, send):
    value = jnp.concatenate([keep, send])
    value = value.reshape(-1, value.shape[-1])
    return lax.psum_scatter(value, "dp", scatter_dimension=0, tiled=True)


def fold(info, *refs):
    for i in range(2):
        keep, got = refs[2 * i : 2 * i + 2]
        keep_out, send_out = refs[4 + 2 * i : 6 + 2 * i]
        n = keep_out.shape[0]
        keep_out[...] = keep[:n] + got[:n]
        send_out[...] = keep[n:] + got[n:]


def fold_one(info, keep, got, keep_out, send_out):
    keep_out[...] = keep[0] + got[0]
    send_out[...] = keep[1] + got[1]


def fold_last(info, *refs):
    keep_out, send_out = refs[4:]
    col = 0
    for i in range(2):
        keep, got = refs[2 * i : 2 * i + 2]
        rows, wide = keep.shape[1:]
        keep_out[:rows, col : col + wide] = keep[0] + got[0]
        send_out[:rows, col : col + wide] = keep[1] + got[1]
        col += wide


def finish_ffn(info, keep_up, got_up, keep_down, got_down, up, down):
    up[...] = keep_up[...] + got_up[...]
    down[...] = (keep_down[...] + got_down[...]).T


def finish_cross(info, keep, got, co, ck, cq, cv):
    co[...] = (keep[:, :256] + got[:, :256]).T
    for i, out in enumerate((ck, cq, cv)):
        here = slice(256 * i + 256, 256 * i + 512)
        out[...] = keep[:, here] + got[:, here]


def finish_self(info, keep, got, so, sk, sq, sv, vectors):
    so[...] = (keep[:128, :256] + got[:128, :256]).T
    for i, out in enumerate((sk, sq, sv)):
        here = slice(256 * i + 256, 256 * i + 512)
        out[...] = keep[:128, here] + got[:128, here]
    vectors[...] = keep[128:, 512:640] + got[128:, 512:640]


FINISH = {
    finish_ffn: [(128, 1024), (1024, 128)],
    finish_cross: [(256, 128), (128, 256), (128, 256), (128, 256)],
    finish_self: [(256, 128), (128, 256), (128, 256), (128, 256), (8, 128)],
}


def exchange(streams, orders, step, first=None, cost=10):
    args = []
    for (keep, send), order in zip(streams, orders):
        got = swap(send, "dp", 8, FLIPS[order[step]])
        args += [keep, got if first is None else after(got, first)]
    none = jnp.zeros((1,), jnp.int32)
    if step == 1:
        shape = (max(a.shape[1] for a in args), args[0].shape[2] + args[2].shape[2])
        return launch(
            fold_last, none, args, [None] * 4, [arr(shape)] * 2, [None] * 2, cost=cost
        )
    outs = []
    for keep, _ in streams:
        outs += [arr((keep.shape[0] // 2, *keep.shape[1:]))] * 2
    out = launch(fold, none, args, [None] * 4, outs, [None] * 4, cost=cost)
    return list(zip(out[0::2], out[1::2]))


def fold_stream(pair, name, first, cost=0):
    keep, send = pair
    got = after(swap(send, "dp", 8, FLIPS[name]), first)
    none = jnp.zeros((1,), jnp.int32)
    outs = [arr(keep.shape[1:])] * 2
    return launch(fold_one, none, (keep, got), [None] * 2, outs, [None] * 2, cost=cost)


def finish(pair, body, first=None):
    keep, send = pair
    got = swap(send, "dp", 8, FLIPS["m"])
    got = got if first is None else after(got, first)
    outs = [arr(shape) for shape in FINISH[body]]
    none = jnp.zeros((1,), jnp.int32)
    return launch(body, none, (keep, got), [None] * 2, outs, [None] * len(outs), cost=10)


def sent(streams):
    return [s for _, s in streams]


def out_second(info, own, got, text_own, text_got, out):
    half = own.shape[0]
    out[:half, :] = own[...] + got[...]
    out[half:, :] = text_own[...] + text_got[...]


def out_sum(info, resid, mine, far, out):
    half = resid.shape[0]
    out[:half, :] = resid[...] + (mine[:half, :] + far[:half, :])
    out[half:, :] = mine[half:, :] + far[half:, :]


def out_place(info, own, sib, out, text_out):
    half = out.shape[0] // 2
    text_half = text_out.shape[0] // 2
    for at, ref in ((CORE, own), (PEER, sib)):
        out[pl.ds(pl.multiple_of(info[at] * half, 16), half), :] = ref[:half, :].astype(BF)
        spot = pl.multiple_of(info[at] * text_half, 8)
        text_out[pl.ds(spot, text_half), :] = ref[half:, :]


def place(info, own, sib, out):
    half = out.shape[0] // 2
    for at, ref in ((CORE, own), (PEER, sib)):
        out[pl.ds(pl.multiple_of(info[at] * half, 16), half), :] = ref[...].astype(BF)


def body(
    hidden,
    text_states,
    text_len,
    ln1_gain,
    ln1_bias,
    self_q,
    self_k,
    self_v,
    self_o,
    ln2_gain,
    ln2_bias,
    cross_q,
    cross_k,
    cross_v,
    cross_o,
    ln3_gain,
    ln3_bias,
    ffn_up,
    ffn_down,
    cotangent,
):
    dp_size = lax.axis_size("dp")
    frames, width = hidden.shape[1:]
    text_rows = text_states.shape[1]
    cols = self_q.shape[1]
    inner = ffn_up.shape[1]
    half = frames // 2
    device = lax.axis_index("dp") * 4 + lax.axis_index("tensor")
    table = jnp.asarray(index_table(dp_size))
    info = lax.dynamic_index_in_dim(table, device, 0, keepdims=False)
    core = lax.axis_index("tensor") & 1
    hid = hidden.reshape(frames, width)
    cot = cotangent.reshape(frames, width)
    text = text_states.reshape(text_rows, width)
    gain1, bias1 = ln1_gain.reshape(1, width), ln1_bias.reshape(1, width)
    gain2, bias2 = ln2_gain.reshape(1, width), ln2_bias.reshape(1, width)
    gain3, bias3 = ln3_gain.reshape(1, width), ln3_bias.reshape(1, width)
    own_rows = pl.BlockSpec((half, width), lambda i, table: (table[CORE], 0))
    sib_rows = pl.BlockSpec((half, width), lambda i, table: (table[PEER], 0))
    half_mm = 2 * half * width
    whole = dp_size == 8
    orders = ("yam", "aym") if whole else ("may",) * 2
    order_one, order_two = orders

    own3, first = launch(
        prepare,
        info,
        (self_o, cross_o, cross_q),
        [None] * 3,
        [arr((3 * cols, width)), arr((cols, width))],
        [None] * 2,
        flops=1 << 20,
    )
    far_one = cross_swap(first)
    sib3 = core_swap(own3)

    def weight_at(i):
        return pl.BlockSpec((cols, width), lambda *_: (i, 0))

    step = frames // 4
    a1, q1, k1, v1 = launch(
        norm_project,
        info,
        (after(hid, first), gain1, bias1, self_q, self_k, self_v),
        [pl.BlockSpec((step, width), lambda i, _: (i, 0))] + [None] * 5,
        [arr((frames, width), BF)] + [arr((frames, cols), BF)] * 3,
        [pl.BlockSpec((step, width), lambda i, _: (i, 0))]
        + [pl.BlockSpec((step, cols), lambda i, _: (i, 0))] * 3,
        grid=(4,),
        flops=2 * frames * width * cols * 3,
    )
    heads = cols // HD
    pair_in = pl.BlockSpec((frames, PAIR), lambda h, _: (0, h // 2))
    pair_half = pl.BlockSpec((half, PAIR), lambda h, _: (0, h // 2))
    level = pl.BlockSpec((1, 1, frames), lambda h, _: (h, 0, 0))
    o1_own, o1_sib, total1 = launch(
        self_forward,
        info,
        (q1, k1, v1),
        [pair_in] * 3,
        [arr((half, cols))] * 2 + [arr((heads, 1, frames))],
        [pair_half] * 2 + [level],
        grid=(heads,),
        scratch=[pltpu.VMEM((frames, PAIR), F32)],
        flops=heads * frames * frames * 512,
        exps=heads * frames * frames,
    )
    o1_cross = cross_swap(after(o1_sib, far_one))
    o1_core = core_swap(after(o1_sib, sib3))
    o1_x = x_swap(o1_own)
    far_two = swap(after(far_one, o1_own), "dp", dp_size, FLIPS["y"])
    k2, v2 = launch(
        text_project,
        info,
        (after(text, o1_own), cross_k, cross_v),
        [None] * 3,
        [arr((text_rows, cols), BF)] * 2,
        [None] * 2,
        flops=2 * text_rows * width * cols * 2,
    )

    def mixed(one, two, i):
        return launch(
            mix,
            info,
            (one, two, own3, sib3),
            [None] * 2 + [weight_at(i)] * 2,
            [arr((half, width))],
            [None],
            flops=half_mm * 512,
        )[0]

    pre1 = mixed(after(o1_own, k2), o1_core, 0)
    far_one_core = core_swap(after(far_one, o1_core))
    far_two_core = core_swap(after(far_two, o1_x, o1_cross, pre1))
    far_weights = (far_one_core, far_two_core, far_one, far_two)

    def normed_mix(which, base, spec, pre, one, two, weights, gain, bias, packs=0):
        return launch(
            functools.partial(mix_norm, which),
            info,
            (base, pre, one, two, *weights, gain, bias),
            [spec] + [None] * (5 + len(weights)),
            [arr((half, width))] * 2 + [arr((cols // 2, width))] * packs,
            [None] * (2 + packs),
            scratch=[pltpu.VMEM((2 * cols, width), BF)],
            cost=2,
        )

    h1, a2, pack_co, pack_cq = normed_mix(None, hid, own_rows, pre1, o1_x, o1_cross, far_weights, gain2, bias2, 2)
    a2_sib = core_swap(a2)

    smem = pl.BlockSpec(memory_space=pltpu.SMEM)

    def cross(a):
        return launch(
            cross_forward,
            info,
            (text_len, a, cross_q, k2, v2),
            [smem] + [None] * 4,
            [arr((half, cols), BF), arr((half, cols)), arr((heads, 1, half))],
            [None] * 3,
            flops=half_mm * cols + heads * half * text_rows * 512,
            exps=heads * half * text_rows,
        )

    q2_own, o2_own, total2_own = cross(a2)
    o2_x = x_swap(after(o2_own, o1_x))
    q2_sib, o2_sib, total2_sib = cross(after(a2_sib, q2_own))
    o2_cross = cross_swap(after(o2_sib, o1_cross))
    o2_core = core_swap(o2_sib)
    far_co = swap(pack_co, "dp", dp_size, FLIPS["a"])
    far_cq = swap(pack_cq, "dp", dp_size, FLIPS["a"])
    pre2 = mixed(o2_own, o2_core, 1)
    far_co_core = core_swap(after(far_co, o2_x, o2_cross, far_cq, pre2))
    co_weights = (
        *(far_one_core, far_two_core, far_co_core),
        *(far_one, far_two, far_co),
    )
    h2, a3 = normed_mix(0, h1, None, pre2, o2_x, o2_cross, co_weights, gain3, bias3)
    a3_sib = core_swap(a3)
    far_cq_core = core_swap(after(far_cq, a3))

    unit = 256

    def feed(a, rows):
        return launch(
            feed_forward,
            info,
            (a, cot, ffn_up, ffn_down),
            [
                None,
                rows,
                pl.BlockSpec((width, unit), lambda i, _: (0, i)),
                pl.BlockSpec((unit, width), lambda i, _: (i, 0)),
            ],
            [arr((half, inner), BF)] * 2 + [arr((half, width))],
            [pl.BlockSpec((half, unit), lambda i, _: (0, i))] * 2 + [None],
            grid=(inner // unit,),
            flops=half_mm * inner * 3,
            exps=half * inner * 2,
        )

    g_own, du_own, da3_own = feed(a3, own_rows)
    g_sib, du_sib, da3_sib = feed(after(a3_sib, g_own, far_cq_core), sib_rows)
    da3_sum = da3_own + core_swap(da3_sib)
    da3_far = x_swap(after(da3_sum, o2_x))
    cot_own = lax.dynamic_slice_in_dim(cot, core * half, half)
    cot_sib = lax.dynamic_slice_in_dim(cot, (1 - core) * half, half)
    ffn_plan = (
        (order_one, ((0, 0, 1024),)),
        ("amy" if whole else order_two, ((1, 0, 1024),)),
    )
    ffn = weight_grads(
        info,
        [
            ([after(a3, da3_sum), a3_sib], [[du_own], [du_sib]]),
            ([cot_own, cot_sib], [[g_own], [g_sib]]),
        ],
        ffn_plan,
    )
    out_own, out_sib = launch(
        down_project,
        info,
        (after(g_own, *ffn[1::2]), g_sib, ffn_down),
        [None, None, pl.BlockSpec((inner, 512), lambda i, _: (0, i))],
        [arr((half, width))] * 2,
        [pl.BlockSpec((half, 512), lambda i, _: (0, i))] * 2,
        grid=(width // 512,),
        flops=2 * half_mm * inner,
    )
    out_got = core_swap(out_sib)
    e1, grads3 = launch(
        sum_norm_back,
        info,
        (da3_sum, after(da3_far, out_own), gain3, h2, cot),
        [None] * 4 + [own_rows],
        [arr((half, width)), arr((2, width))],
        [None] * 2,
    )
    e1_sib = core_swap(e1)
    def cross_back(e, q, total, sums):
        last = bool(sums)
        return launch(
            functools.partial(cross_backward, last),
            info,
            (text_len, e, cross_o, q, k2, v2, total, *sums),
            [smem] + [None] * (6 + len(sums)),
            [arr((half, cols))] + [arr((text_rows, cols), BF if last else F32)] * 2,
            [None] * 3,
        )

    dq2_own, *sums = cross_back(after(e1, out_got), q2_own, total2_own, ())
    dq2_sib, dk2, dv2 = cross_back(e1_sib, q2_sib, total2_sib, tuple(sums))
    dq2_cross = cross_swap(dq2_sib)
    dq2_core = core_swap(dq2_sib)
    dq2_x = x_swap(after(dq2_own, da3_far))
    pre3 = mixed(dq2_own, dq2_core, 2)
    cq_weights = (
        *(far_one_core, far_two_core, far_cq_core),
        *(far_one, far_two, far_cq),
    )

    text_half = text_rows // 2
    text_own, text_send = launch(
        text_back,
        info,
        (dk2, dv2, cross_k, cross_v),
        [None] * 4,
        [arr((text_half, width))] * 2,
        [None] * 2,
        scratch=[pltpu.VMEM((text_rows, width), F32)],
        flops=2 * text_rows * width * cols * 2,
    )
    text_got = core_swap(text_send)
    out_two = launch(
        out_second,
        info,
        (out_own, out_got, text_own, text_got),
        [None] * 4,
        [arr((half + text_half, width))],
        [None],
    )[0]
    cross_plan = (
        (order_one, ((0, 0, 256), (2, 0, 256))),
        (order_two, ((1, 0, 256), (2, 256, 256))),
    )
    cross = weight_grads(
        info,
        [
            ([e1, e1_sib], [[o2_own], [o2_sib]]),
            ([a2, a2_sib], [[dq2_own], [dq2_sib]]),
            ([text], [[dk2, dv2]]),
        ],
        cross_plan,
    )
    pins = [out_two]
    if whole:
        ffn = exchange(list(zip(ffn[0::2], ffn[1::2])), orders, 0, cross[0], 12)
        pins += sent(ffn)
    e0, grads2 = launch(
        mix_norm_back,
        info,
        (after(pre3, *pins), dq2_x, dq2_cross, *cq_weights, gain2, h1, e1),
        [None] * (6 + len(cq_weights)),
        [arr((half, width)), arr((2, width))],
        [None] * 2,
        scratch=[pltpu.VMEM((2 * cols, width), BF)],
        cost=0,
    )
    out_far_two = x_swap(after(out_two, dq2_x))
    e0_sib = core_swap(e0)
    do1 = launch(
        mixed_back,
        info,
        (e0, e0_sib, self_o),
        [None] * 3,
        [arr((frames, cols), BF)],
        [None],
    )[0]
    dq1, dk1, dv1 = launch(
        self_backward,
        info,
        (q1, k1, v1, do1, total1),
        [pair_in] * 4 + [level],
        [arr((frames, cols), BF)] * 3,
        [pair_in] * 3,
        grid=(heads,),
        scratch=[pltpu.VMEM((frames, PAIR), F32)] * 3,
        flops=heads * frames * frames * 256 * 5,
        exps=heads * frames * frames,
    )
    pins = []
    if whole:
        up_keep, up_send = fold_stream(ffn[0], "a", dq1)
        pins = [up_send]
        cross = [(k, after(c, up_send)) for k, c in zip(cross[0::2], cross[1::2])]
    da1_own, da1_send = launch(
        first_back,
        info,
        (after(dq1, *pins), dk1, dv1, self_q, self_k, self_v),
        [None] * 6,
        [arr((half, width))] * 2,
        [None] * 2,
        flops=2 * half_mm * 3 * cols,
    )
    pins = []
    if whole:
        down_keep, down_send = fold_stream(ffn[1], "m", da1_own, 10)
        pins = [down_send]
    da1_sum, grads1 = launch(
        sum_first_grads,
        info,
        (da1_own, after(core_swap(da1_send), *pins), hid),
        [None] * 2 + [own_rows],
        [arr((half, width)), arr((2, width))],
        [None] * 2,
    )

    vectors = (grads1, grads2, grads3)
    if not whole:
        stacked = lax.psum(jnp.concatenate(vectors), "tensor")
        stacked = lax.psum_scatter(stacked, "dp", scatter_dimension=1, tiled=True)
        vectors = ()
    self_plan = (
        (order_one, ((0, 0, 256), (1, 256, 256))),
        (order_two, ((1, 0, 256), (1, 512, 256))),
    )
    own = weight_grads(
        info,
        [
            ([after(e0, da1_sum), e0_sib], [[o1_own], [o1_sib]]),
            ([a1], [[dq1, dk1, dv1]]),
        ],
        self_plan,
        vectors,
    )
    pins = [own[0]]
    if whole:
        own = list(zip(own[0::2], own[1::2]))
        cross = exchange(cross, orders, 0, own[0][0], 0)
        own = [(k, after(c, *sent(cross))) for k, c in own]
        pins = sent(cross)
    out_final = launch(
        out_sum,
        info,
        (h2, out_two, after(out_far_two, *pins)),
        [None] * 3,
        [arr((half + text_half, width))],
        [None],
        cost=10,
    )[0]
    da1_far = x_swap(after(da1_sum, out_final))
    output, text_grad = launch(
        out_place,
        info,
        (out_final, core_swap(out_final)),
        [None] * 2,
        [arr((frames, width), BF), arr((text_rows, width))],
        [None] * 2,
    )
    pins = []
    if not whole:
        ffn, cross, own = (
            [scatter_sum(*p) for p in zip(g[0::2], g[1::2])] for g in (ffn, cross, own)
        )
        up_grad, down_grad = ffn[0], ffn[1].T
        co_grad, ck_grad = cross[0][:, :256].T, cross[0][:, 256:]
        cq_grad, cv_grad = cross[1][:, :256], cross[1][:, 256:]
        so_grad, sk_grad = own[0][:, :256].T, own[0][:, 256:]
        sq_grad, sv_grad = own[1][:, :256], own[1][:, 256:]
    last = launch(
        last_norm_back,
        info,
        (da1_sum, after(da1_far, *pins), gain1, hid, e0),
        [None] * 3 + [own_rows, None],
        [arr((half, width))],
        [None],
        flops=half_mm * 8,
    )[0]
    if whole:
        cross = exchange(cross, orders, 1, last)
        own = exchange(own, orders, 0, cross[1])
        up_got = after(swap(after(up_send, down_send), "dp", 8, FLIPS["m"]), last)
        down_got = after(swap(after(down_send, cross[1]), "dp", 8, FLIPS["y"]), last)
        up_grad, down_grad = launch(
            finish_ffn,
            info,
            (up_keep, up_got, down_keep, down_got),
            [None] * 4,
            [arr(shape) for shape in FINISH[finish_ffn]],
            [None] * 2,
            cost=30,
        )
        cross = (cross[0], after(cross[1], up_grad))
        co_grad, ck_grad, cq_grad, cv_grad = finish(cross, finish_cross)
        own = exchange(own, orders, 1)
        own = (own[0], after(own[1], co_grad))
        so_grad, sk_grad, sq_grad, sv_grad, stacked = finish(own, finish_self)
    hidden_grad = launch(
        place,
        info,
        (last, core_swap(last)),
        [None] * 2,
        [arr((frames, width), BF)],
        [None],
    )[0]
    if whole:
        stacked = stacked + x_swap(after(stacked, da1_far))
        stacked = stacked + core_swap(stacked)
    return (
        output.reshape(hidden.shape),
        hidden_grad.reshape(hidden.shape),
        text_grad.reshape(text_states.shape),
        stacked[0],
        stacked[1],
        sq_grad,
        sk_grad,
        sv_grad,
        so_grad,
        stacked[2],
        stacked[3],
        cq_grad,
        ck_grad,
        cv_grad,
        co_grad,
        stacked[4],
        stacked[5],
        up_grad,
        down_grad,
    )


def solution(mesh):
    rows = P("dp", None, None)
    column, row = P(None, "tensor"), P("tensor", None)
    in_specs = (
        *(rows, rows, P("dp"), P(), P(), column, column, column, row),
        *(P(), P(), column, column, column, row),
        *(P(), P(), column, row, rows),
    )
    vector, down, across = P("dp"), P("dp", "tensor"), P("tensor", "dp")
    out_specs = (
        *(rows, rows, rows, vector, vector, down, down, down, across),
        *(vector, vector, down, down, down, across),
        *(vector, vector, down, across),
    )
    return jax.shard_map(body, mesh=mesh, in_specs=in_specs, out_specs=out_specs, check_vma=False)
```

```python
import functools

import jax
import jax.numpy as jnp
import numpy as np
from jax import lax
from jax.experimental import pallas as pl
from jax.experimental.pallas import tpu as pltpu
from jax.sharding import PartitionSpec as P

HD = 64
EPS = 1e-05
NEG = -1e30
SCALE = HD ** (-0.5)
BF = jnp.bfloat16
F32 = jnp.float32
PAIR = 2 * HD

FLIPS = WEIGHT = {"y": 1, "a": 2, "m": 4}

CORE, PEER, Y, LABEL, TABLE = 0, 1, 2, 3, 8


def index_table(dp_size):
    rows = []
    for me in range(dp_size):
        for t in range(4):
            row = [t & 1, 1 - (t & 1), me & 1, me & 3, 0, 0, 0, 0]
            row += [(me ^ i) if dp_size == 8 else i for i in range(8)]
            rows.append(row)
    return np.array(rows, np.int32)


def dot(left, right):
    return lax.dot_general(left, right, (((1,), (0,)), ((), ())), preferred_element_type=F32)


def against(left, right):
    return lax.dot_general(left, right, (((1,), (1,)), ((), ())), preferred_element_type=F32)


def over_rows(left, right):
    return lax.dot_general(left, right, (((0,), (0,)), ((), ())), preferred_element_type=F32)


def swap(value, axis, size, flip):
    return lax.ppermute(value, axis, [(i, i ^ flip) for i in range(size)])


def core_swap(value):
    return swap(value, "tensor", 4, 1)


def x_swap(value):
    return swap(value, "tensor", 4, 2)


def cross_swap(value):
    return swap(value, "tensor", 4, 3)


def after(value, *others):
    return lax.optimization_barrier((value, *others))[0]


def full(shape):
    return pl.BlockSpec(shape, lambda *_: (0,) * len(shape))


def launch(body, info, args, in_specs, outs, out_specs, grid=(1,), scratch=(), flops=0, exps=0, grant=20, cost=0):
    specs = [full(a.shape) if s is None else s for a, s in zip(args, in_specs)]
    ospecs = [full(o.shape) if s is None else s for o, s in zip(outs, out_specs)]
    return pl.pallas_call(
        body,
        out_shape=list(outs),
        grid_spec=pltpu.PrefetchScalarGridSpec(
            num_scalar_prefetch=1,
            grid=grid,
            in_specs=specs,
            out_specs=ospecs,
            scratch_shapes=list(scratch),
        ),
        compiler_params=pltpu.CompilerParams(vmem_limit_bytes=grant << 20),
        cost_estimate=pl.CostEstimate(
            flops=1 + cost * 10**9, bytes_accessed=1, transcendentals=0
        ),
        name=body.__name__ if hasattr(body, "__name__") else body.func.__name__,
    )(info, *args)


def arr(shape, dtype=F32):
    return jax.ShapeDtypeStruct(shape, dtype)


def normed(values):
    centred = values - jnp.mean(values, -1, keepdims=True)
    inverse = lax.rsqrt(jnp.mean(centred * centred, -1, keepdims=True) + EPS)
    return centred * inverse, inverse


def norm_back(grad, scaled, inverse, gain):
    weighted = grad * gain
    first = jnp.mean(weighted, -1, keepdims=True)
    second = jnp.mean(weighted * scaled, -1, keepdims=True)
    return inverse * (weighted - first - scaled * second)


def head_lanes(odd, dtype):
    lane = lax.broadcasted_iota(jnp.int32, (1, PAIR), 1)
    return ((lane // HD) == odd).astype(dtype)


def norm_project(info, hid, gain, bias, wq, wk, wv, a1, q, k, v):
    scaled, _ = normed(hid[...].astype(F32))
    low = (scaled * gain[...] + bias[...]).astype(BF)
    a1[...] = low
    q[...] = (dot(low, wq[...]) * SCALE).astype(BF)
    k[...] = dot(low, wk[...]).astype(BF)
    v[...] = dot(low, wv[...]).astype(BF)


def text_project(info, text, wk, wv, k, v):
    k[...] = dot(text[...], wk[...]).astype(BF)
    v[...] = dot(text[...], wv[...]).astype(BF)


def blocks_of(rows, step=256):
    return [(s, min(step, rows - s)) for s in range(0, rows, step)]


def causal(scores):
    key = lax.broadcasted_iota(jnp.int32, scores.shape, 0)
    query = lax.broadcasted_iota(jnp.int32, scores.shape, 1)
    return jnp.where(key <= query, scores, NEG)


def self_forward(info, q, k, v, keep, send, total, mixed):
    rows = q.shape[0]
    half = rows // 2
    odd = lax.rem(pl.program_id(0), 2)
    lanes = head_lanes(odd, BF)
    lanes_on = head_lanes(odd, F32) > 0
    for start, size in blocks_of(rows):
        here = slice(start, start + size)
        query = q[here, :] * lanes
        near = causal(against(k[here, :], query))
        top = jnp.max(near, 0, keepdims=True)
        if start:
            far = against(k[:start, :], query)
            top = jnp.maximum(top, jnp.max(far, 0, keepdims=True))
        near = jnp.exp(near - top)
        count = jnp.sum(near, 0, keepdims=True)
        if start:
            far = jnp.exp(far - top)
            count = count + jnp.sum(far, 0, keepdims=True)
        scale = 1.0 / count
        out = over_rows(v[here, :], (near * scale).astype(BF))
        if start:
            out = out + over_rows(v[:start, :], (far * scale).astype(BF))
        total[0, :, here] = top + jnp.log(count)
        mixed[here, :] = jnp.where(lanes_on, out.T, mixed[here, :])

    @pl.when(odd == 1)
    def _():
        keep[...] = mixed[pl.ds(pl.multiple_of(info[CORE] * half, 8), half), :]
        send[...] = mixed[pl.ds(pl.multiple_of(info[PEER] * half, 8), half), :]


def prepare(info, so, co, cq, own, first):
    own[0:256, :] = so[...].astype(F32)
    own[256:512, :] = co[...].astype(F32)
    own[512:768, :] = cq[...].astype(F32).T
    first[0:128, :] = own[pl.ds(pl.multiple_of(info[Y] * 128, 8), 128), :]
    for i in range(2):
        at = pl.multiple_of(256 + i * 256 + info[LABEL] * 64, 8)
        first[128 + i * 64 : 192 + i * 64, :] = own[pl.ds(at, 64), :]


def mix(info, one, two, w_one, w_two, out):
    out[...] = dot(one[...].astype(BF), w_one[...].astype(BF)) + dot(
        two[...].astype(BF), w_two[...].astype(BF)
    )


def gather_halves(info, far, weights):
    for s in range(2):
        for p in range(2):

            @pl.when(info[Y] == p)
            def _(s=s, p=p):
                weights[s * 256 + p * 128 : s * 256 + p * 128 + 128, :] = far[2 * s][
                    :128, :
                ].astype(BF)

            @pl.when(info[Y] != p)
            def _(s=s, p=p):
                weights[s * 256 + p * 128 : s * 256 + p * 128 + 128, :] = far[2 * s + 1][
                    :128, :
                ].astype(BF)


def gather_quarters(info, far, weights, first):
    for s in range(2):
        over_x, over_y, over_z = far[3 * s : 3 * s + 3]
        pieces = (
            over_x[128 + first : 192 + first, :],
            over_y[128 + first : 192 + first, :],
            over_z[:64, :],
            over_z[64:, :],
        )
        for j, piece in enumerate(pieces):
            at = pl.multiple_of(s * 256 + (info[LABEL] ^ j) * 64, 64)
            weights[pl.ds(at, 64), :] = piece.astype(BF)


def mix_far(info, pre, one, two, far, weights, which):
    if which is None:
        gather_halves(info, far, weights)
    else:
        gather_quarters(info, far, weights, which)
    far_part = dot(one[...].astype(BF), weights[:256, :]) + dot(
        two[...].astype(BF), weights[256:, :]
    )
    return pre[...] + far_part


def mix_norm(which, info, base, pre, one, two, *refs):
    n = 7 if which is None else 5
    far, (gain, bias, resid, low, *packs, weights) = refs[:-n], refs[-n:]
    for i, pack in enumerate(packs):
        for j in range(2):
            pack[j * 64 : j * 64 + 64, :] = far[2 + j][128 + i * 64 : 192 + i * 64, :]
    part = mix_far(info, pre, one, two, far, weights, which)
    total = base[...].astype(F32) + part
    resid[...] = total
    scaled, _ = normed(total)
    low[...] = scaled * gain[...] + bias[...]


def mix_norm_back(info, pre, one, two, *refs):
    far, (gain, resid, e_in, e_out, grads, weights) = refs[:-6], refs[-6:]
    grad = mix_far(info, pre, one, two, far, weights, 64)
    scaled, inverse = normed(resid[...])
    e_out[...] = e_in[...] + norm_back(grad, scaled, inverse, gain[...])
    grads[0:1, :] = jnp.sum(grad * scaled, 0, keepdims=True) * 0.5
    grads[1:2, :] = jnp.sum(grad, 0, keepdims=True) * 0.5


def sum_norm_back(info, mine, far, gain, resid, e_in, e_out, grads):
    grad = mine[...] + far[...]
    scaled, inverse = normed(resid[...])
    e_out[...] = e_in[...].astype(F32) + norm_back(grad, scaled, inverse, gain[...])
    grads[0:1, :] = jnp.sum(grad * scaled, 0, keepdims=True) * 0.5
    grads[1:2, :] = jnp.sum(grad, 0, keepdims=True) * 0.5


def sum_first_grads(info, mine, recv, hid, out, grads):
    grad = mine[...] + recv[...]
    out[...] = grad
    scaled, _ = normed(hid[...].astype(F32))
    grads[0:1, :] = jnp.sum(grad * scaled, 0, keepdims=True)
    grads[1:2, :] = jnp.sum(grad, 0, keepdims=True)


def last_norm_back(info, mine, far, gain, hid, e_in, out):
    grad = mine[...] + far[...]
    scaled, inverse = normed(hid[...].astype(F32))
    out[...] = e_in[...] + norm_back(grad, scaled, inverse, gain[...])


def cross_forward(info, length, a2, wq, k, v, q, mixed, total):
    query_rows = (dot(a2[...].astype(BF), wq[...]) * SCALE).astype(BF)
    q[...] = query_rows
    for pair in range(2):
        cols = slice(pair * PAIR, (pair + 1) * PAIR)
        pair_out = None
        for odd in range(2):
            query = query_rows[:, cols] * head_lanes(odd, BF)
            scores = against(k[:, cols], query)
            slot = lax.broadcasted_iota(jnp.int32, scores.shape, 0)
            scores = jnp.where(slot < length[0], scores, NEG)
            top = jnp.max(scores, 0, keepdims=True)
            scores = jnp.exp(scores - top)
            count = jnp.sum(scores, 0, keepdims=True)
            out = over_rows(v[:, cols], (scores * (1.0 / count)).astype(BF)).T
            total[pair * 2 + odd] = top + jnp.log(count)
            pair_out = out if odd == 0 else jnp.where(head_lanes(1, F32) > 0, out, pair_out)
        mixed[:, cols] = pair_out


def feed_forward(info, a3, cot, up, down, g, du, da3):
    n = pl.program_id(0)
    u = dot(a3[...].astype(BF), up[...])
    cdf = 0.5 + 0.5 * lax.erf(u * (0.5**0.5))
    g[...] = (u * cdf).astype(BF)
    slope = cdf + u * jnp.exp(-0.5 * u * u) * (1.0 / (2.0 * np.pi) ** 0.5)
    dg = against(cot[...], down[...]).astype(BF).astype(F32)
    low = (dg * slope).astype(BF)
    du[...] = low
    part = against(low, up[...])

    @pl.when(n == 0)
    def _():
        da3[...] = part

    @pl.when(n > 0)
    def _():
        da3[...] += part


def down_project(info, own, sib, down, out_own, out_sib):
    out_own[...] = dot(own[...], down[...])
    out_sib[...] = dot(sib[...], down[...])


def cross_backward(second, info, length, e1, wo, q, k, v, total, *rest):
    if second:
        dk_in, dv_in, dq, dk_out, dv_out = rest
    else:
        dq, dk_out, dv_out = rest
    mixed_grad = against(e1[...].astype(BF), wo[...]).astype(BF)
    for pair in range(2):
        cols = slice(pair * PAIR, (pair + 1) * PAIR)
        dk = dk_in[:, cols] if second else None
        dv = dv_in[:, cols] if second else None
        pair_dq = None
        for odd in range(2):
            lanes = head_lanes(odd, BF)
            query = q[:, cols] * lanes
            grad = mixed_grad[:, cols] * lanes
            scores = against(k[:, cols], query)
            slot = lax.broadcasted_iota(jnp.int32, scores.shape, 0)
            scores = jnp.where(slot < length[0], scores, NEG)
            probs = jnp.exp(scores - total[pair * 2 + odd])
            prob_grad = against(v[:, cols], grad)
            part = dot(probs.astype(BF), grad)
            dv = part if dv is None else dv + part
            delta = jnp.sum(probs * prob_grad, 0, keepdims=True)
            low = (probs * (prob_grad - delta)).astype(BF)
            part = dot(low, query)
            dk = part if dk is None else dk + part
            out = over_rows(k[:, cols], low).T
            pair_dq = out if odd == 0 else jnp.where(head_lanes(1, F32) > 0, out, pair_dq)
        dq[:, cols] = pair_dq * SCALE
        dk_out[:, cols] = dk.astype(dk_out.dtype)
        dv_out[:, cols] = dv.astype(dv_out.dtype)


def text_back(info, dk, dv, wk, wv, own, send, scratch):
    half = own.shape[0]
    scratch[...] = against(dk[...], wk[...]) + against(dv[...], wv[...])
    own[...] = scratch[pl.ds(pl.multiple_of(info[CORE] * half, 8), half), :]
    send[...] = scratch[pl.ds(pl.multiple_of(info[PEER] * half, 8), half), :]


def mixed_back(info, own, sib, wo, out):
    half = own.shape[0]
    out[pl.ds(pl.multiple_of(info[CORE] * half, 16), half), :] = against(
        own[...].astype(BF), wo[...]
    ).astype(BF)
    out[pl.ds(pl.multiple_of(info[PEER] * half, 16), half), :] = against(
        sib[...].astype(BF), wo[...]
    ).astype(BF)


def self_backward(info, q, k, v, grad_in, total, dq, dk, dv, dq_sum, dk_sum, dv_sum):
    rows = q.shape[0]
    odd = lax.rem(pl.program_id(0), 2)
    lanes = head_lanes(odd, BF)
    lanes_on = head_lanes(odd, F32) > 0

    @pl.when(odd == 0)
    def _():
        dk_sum[...] = jnp.zeros_like(dk_sum)
        dv_sum[...] = jnp.zeros_like(dv_sum)

    for start, size in blocks_of(rows):
        here = slice(start, start + size)
        query = q[here, :] * lanes
        grad = grad_in[here, :] * lanes
        level = total[0, :, here]
        near = jnp.exp(causal(against(k[here, :], query)) - level)
        near_grad = against(v[here, :], grad)
        delta = jnp.sum(near * near_grad, 0, keepdims=True)
        dv_sum[here, :] += dot(near.astype(BF), grad)
        if start:
            far = jnp.exp(against(k[:start, :], query) - level)
            far_grad = against(v[:start, :], grad)
            delta = delta + jnp.sum(far * far_grad, 0, keepdims=True)
            dv_sum[:start, :] += dot(far.astype(BF), grad)
        near_low = (near * (near_grad - delta)).astype(BF)
        dk_sum[here, :] += dot(near_low, query)
        out = over_rows(k[here, :], near_low)
        if start:
            far_low = (far * (far_grad - delta)).astype(BF)
            dk_sum[:start, :] += dot(far_low, query)
            out = out + over_rows(k[:start, :], far_low)
        dq_sum[here, :] = jnp.where(lanes_on, out.T * SCALE, dq_sum[here, :])

    @pl.when(odd == 1)
    def _():
        dq[...] = dq_sum[...].astype(BF)
        dk[...] = dk_sum[...].astype(BF)
        dv[...] = dv_sum[...].astype(BF)


def first_back(info, dq, dk, dv, wq, wk, wv, own, send):
    half = own.shape[0]
    for at, out in ((PEER, send), (CORE, own)):
        here = pl.ds(pl.multiple_of(info[at] * half, 16), half)
        out[...] = (
            against(dq[here, :], wq[...])
            + against(dk[here, :], wk[...])
            + against(dv[here, :], wv[...])
        )


def weight_grad(plan, shapes, n_v, info, *refs):
    at = 0
    groups = []
    for n_left, n_right in shapes:
        groups.append((refs[at : at + n_left], refs[at + n_left : at + n_left + n_right]))
        at += n_left + n_right
    vectors = refs[at : at + n_v]
    outs = refs[at + n_v : at + n_v + 2 * len(plan)]
    lhs, rhs = refs[-2:]
    for g, (lefts, rights) in enumerate(groups):
        row = 0
        per = len(rights) // len(lefts)
        for i, left in enumerate(lefts):
            rows = left.shape[0]
            for j in range(8):
                block = left[:, pl.ds(pl.multiple_of(info[TABLE + j] * 128, 128), 128)]
                lhs[row : row + rows, j * 128 : (j + 1) * 128] = block.astype(BF)
            col = 0
            for right in rights[i * per : (i + 1) * per]:
                rhs[row : row + rows, col : col + right.shape[1]] = right[...].astype(BF)
                col += right.shape[1]
            row += rows
        for s, (order, segments) in enumerate(plan):
            put = 0
            for group, first, width in segments:
                if group == g:
                    for half in range(2):
                        value = over_rows(
                            lhs[:row, half * 512 : half * 512 + 512],
                            rhs[:row, first : first + width],
                        )
                        for q in range(4):
                            j = half * 4 + q
                            sent, pos = spot(order, j)
                            outs[2 * s + sent][pos, :128, put : put + width] = value[
                                q * 128 : (q + 1) * 128, :
                            ]
                put += width
    if n_v:
        for j in range(8):
            sent, pos = spot(plan[-1][0], j)
            out = outs[2 * len(plan) - 2 + sent]
            out[pos, 128:, :] = jnp.zeros((8, out.shape[2]), F32)
            for i, ref in enumerate(vectors):
                block = ref[:, pl.ds(pl.multiple_of(info[TABLE + j] * 128, 128), 128)]
                out[pos, 128 + 2 * i : 130 + 2 * i, :128] = block


def spot(order, j):
    bits = [(j // WEIGHT[name]) & 1 for name in order]
    return bits[0], bits[1] * 2 + bits[2]


def weight_grads(info, groups, plan, vectors=()):
    args, shapes, flops = [], [], 0
    for lefts, rights in groups:
        flat = [r for group in rights for r in group]
        args += [*lefts, *flat]
        shapes.append((len(lefts), len(flat)))
        flops += 2 * sum(a.shape[0] for a in lefts) * 1024 * sum(r.shape[1] for r in rights[0])
    args += vectors
    outs = []
    for s, (order, segments) in enumerate(plan):
        tall = 136 if vectors and s == len(plan) - 1 else 128
        outs += [arr((4, tall, sum(w for _, _, w in segments)))] * 2
    rows = max(sum(a.shape[0] for a in lefts) for lefts, _ in groups)
    wide = max(sum(r.shape[1] for r in rights[0]) for _, rights in groups)
    return launch(
        functools.partial(weight_grad, plan, tuple(shapes), len(vectors)),
        info,
        tuple(args),
        [None] * len(args),
        outs,
        [None] * len(outs),
        scratch=[pltpu.VMEM((rows, 1024), BF), pltpu.VMEM((rows, wide), BF)],
        flops=flops,
        grant=40,
    )


def scatter_sum(keep, send):
    value = jnp.concatenate([keep, send])
    value = value.reshape(-1, value.shape[-1])
    return lax.psum_scatter(value, "dp", scatter_dimension=0, tiled=True)


def fold(info, *refs):
    for i in range(2):
        keep, got = refs[2 * i : 2 * i + 2]
        keep_out, send_out = refs[4 + 2 * i : 6 + 2 * i]
        n = keep_out.shape[0]
        keep_out[...] = keep[:n] + got[:n]
        send_out[...] = keep[n:] + got[n:]


def fold_one(info, keep, got, keep_out, send_out):
    keep_out[...] = keep[0] + got[0]
    send_out[...] = keep[1] + got[1]


def fold_last(info, *refs):
    keep_out, send_out = refs[4:]
    col = 0
    for i in range(2):
        keep, got = refs[2 * i : 2 * i + 2]
        rows, wide = keep.shape[1:]
        keep_out[:rows, col : col + wide] = keep[0] + got[0]
        send_out[:rows, col : col + wide] = keep[1] + got[1]
        col += wide


def finish_ffn(info, keep, got, up, down):
    wide = up.shape[1]
    up[...] = keep[:, :wide] + got[:, :wide]
    down[...] = (keep[:, wide:] + got[:, wide:]).T


def finish_cross(info, keep, got, co, ck, cq, cv):
    co[...] = (keep[:, :256] + got[:, :256]).T
    for i, out in enumerate((ck, cq, cv)):
        here = slice(256 * i + 256, 256 * i + 512)
        out[...] = keep[:, here] + got[:, here]


def finish_self(info, keep, got, so, sk, sq, sv, vectors):
    so[...] = (keep[:128, :256] + got[:128, :256]).T
    for i, out in enumerate((sk, sq, sv)):
        here = slice(256 * i + 256, 256 * i + 512)
        out[...] = keep[:128, here] + got[:128, here]
    vectors[...] = keep[128:, 512:640] + got[128:, 512:640]


FINISH = {
    finish_ffn: [(128, 1024), (1024, 128)],
    finish_cross: [(256, 128), (128, 256), (128, 256), (128, 256)],
    finish_self: [(256, 128), (128, 256), (128, 256), (128, 256), (8, 128)],
}


def exchange(streams, orders, step, first=None, cost=10):
    args = []
    for (keep, send), order in zip(streams, orders):
        got = swap(send, "dp", 8, FLIPS[order[step]])
        args += [keep, got if first is None else after(got, first)]
    none = jnp.zeros((1,), jnp.int32)
    if step == 1:
        shape = (max(a.shape[1] for a in args), args[0].shape[2] + args[2].shape[2])
        return launch(
            fold_last, none, args, [None] * 4, [arr(shape)] * 2, [None] * 2, cost=cost
        )
    outs = []
    for keep, _ in streams:
        outs += [arr((keep.shape[0] // 2, *keep.shape[1:]))] * 2
    out = launch(fold, none, args, [None] * 4, outs, [None] * 4, cost=cost)
    return list(zip(out[0::2], out[1::2]))


def fold_stream(pair, name, first, cost=0):
    keep, send = pair
    got = after(swap(send, "dp", 8, FLIPS[name]), first)
    none = jnp.zeros((1,), jnp.int32)
    outs = [arr(keep.shape[1:])] * 2
    return launch(fold_one, none, (keep, got), [None] * 2, outs, [None] * 2, cost=cost)


def finish(pair, body, first=None, cost=10):
    keep, send = pair
    got = swap(send, "dp", 8, FLIPS["m"])
    got = got if first is None else after(got, first)
    outs = [arr(shape) for shape in FINISH[body]]
    none = jnp.zeros((1,), jnp.int32)
    return launch(body, none, (keep, got), [None] * 2, outs, [None] * len(outs), cost=cost)


def sent(streams):
    return [s for _, s in streams]


def out_second(info, own, got, text_own, text_got, out):
    half = own.shape[0]
    out[:half, :] = own[...] + got[...]
    out[half:, :] = text_own[...] + text_got[...]


def out_sum(info, resid, mine, far, out):
    half = resid.shape[0]
    out[:half, :] = resid[...] + (mine[:half, :] + far[:half, :])
    out[half:, :] = mine[half:, :] + far[half:, :]


def out_place(info, own, sib, out, text_out):
    half = out.shape[0] // 2
    text_half = text_out.shape[0] // 2
    for at, ref in ((CORE, own), (PEER, sib)):
        out[pl.ds(pl.multiple_of(info[at] * half, 16), half), :] = ref[:half, :].astype(BF)
        spot = pl.multiple_of(info[at] * text_half, 8)
        text_out[pl.ds(spot, text_half), :] = ref[half:, :]


def place(info, own, sib, out):
    half = out.shape[0] // 2
    for at, ref in ((CORE, own), (PEER, sib)):
        out[pl.ds(pl.multiple_of(info[at] * half, 16), half), :] = ref[...].astype(BF)


def body(
    hidden,
    text_states,
    text_len,
    ln1_gain,
    ln1_bias,
    self_q,
    self_k,
    self_v,
    self_o,
    ln2_gain,
    ln2_bias,
    cross_q,
    cross_k,
    cross_v,
    cross_o,
    ln3_gain,
    ln3_bias,
    ffn_up,
    ffn_down,
    cotangent,
):
    dp_size = lax.axis_size("dp")
    frames, width = hidden.shape[1:]
    text_rows = text_states.shape[1]
    cols = self_q.shape[1]
    inner = ffn_up.shape[1]
    half = frames // 2
    device = lax.axis_index("dp") * 4 + lax.axis_index("tensor")
    table = jnp.asarray(index_table(dp_size))
    info = lax.dynamic_index_in_dim(table, device, 0, keepdims=False)
    core = lax.axis_index("tensor") & 1
    hid = hidden.reshape(frames, width)
    cot = cotangent.reshape(frames, width)
    text = text_states.reshape(text_rows, width)
    gain1, bias1 = ln1_gain.reshape(1, width), ln1_bias.reshape(1, width)
    gain2, bias2 = ln2_gain.reshape(1, width), ln2_bias.reshape(1, width)
    gain3, bias3 = ln3_gain.reshape(1, width), ln3_bias.reshape(1, width)
    own_rows = pl.BlockSpec((half, width), lambda i, table: (table[CORE], 0))
    sib_rows = pl.BlockSpec((half, width), lambda i, table: (table[PEER], 0))
    half_mm = 2 * half * width
    whole = dp_size == 8
    orders = ("yam", "aym") if whole else ("may",) * 2
    order_one, order_two = orders

    own3, first = launch(
        prepare,
        info,
        (self_o, cross_o, cross_q),
        [None] * 3,
        [arr((3 * cols, width)), arr((cols, width))],
        [None] * 2,
        flops=1 << 20,
    )
    far_one = cross_swap(first)
    sib3 = core_swap(own3)

    def weight_at(i):
        return pl.BlockSpec((cols, width), lambda *_: (i, 0))

    step = frames // 4
    a1, q1, k1, v1 = launch(
        norm_project,
        info,
        (after(hid, first), gain1, bias1, self_q, self_k, self_v),
        [pl.BlockSpec((step, width), lambda i, _: (i, 0))] + [None] * 5,
        [arr((frames, width), BF)] + [arr((frames, cols), BF)] * 3,
        [pl.BlockSpec((step, width), lambda i, _: (i, 0))]
        + [pl.BlockSpec((step, cols), lambda i, _: (i, 0))] * 3,
        grid=(4,),
        flops=2 * frames * width * cols * 3,
    )
    heads = cols // HD
    pair_in = pl.BlockSpec((frames, PAIR), lambda h, _: (0, h // 2))
    pair_half = pl.BlockSpec((half, PAIR), lambda h, _: (0, h // 2))
    level = pl.BlockSpec((1, 1, frames), lambda h, _: (h, 0, 0))
    o1_own, o1_sib, total1 = launch(
        self_forward,
        info,
        (q1, k1, v1),
        [pair_in] * 3,
        [arr((half, cols))] * 2 + [arr((heads, 1, frames))],
        [pair_half] * 2 + [level],
        grid=(heads,),
        scratch=[pltpu.VMEM((frames, PAIR), F32)],
        flops=heads * frames * frames * 512,
        exps=heads * frames * frames,
    )
    o1_cross = cross_swap(after(o1_sib, far_one))
    o1_core = core_swap(after(o1_sib, sib3))
    o1_x = x_swap(o1_own)
    far_two = swap(after(far_one, o1_own), "dp", dp_size, FLIPS["y"])
    k2, v2 = launch(
        text_project,
        info,
        (after(text, o1_own), cross_k, cross_v),
        [None] * 3,
        [arr((text_rows, cols), BF)] * 2,
        [None] * 2,
        flops=2 * text_rows * width * cols * 2,
    )

    def mixed(one, two, i):
        return launch(
            mix,
            info,
            (one, two, own3, sib3),
            [None] * 2 + [weight_at(i)] * 2,
            [arr((half, width))],
            [None],
            flops=half_mm * 512,
        )[0]

    pre1 = mixed(after(o1_own, k2), o1_core, 0)
    far_one_core = core_swap(after(far_one, o1_core))
    far_two_core = core_swap(after(far_two, o1_x, o1_cross, pre1))
    far_weights = (far_one_core, far_two_core, far_one, far_two)

    def normed_mix(which, base, spec, pre, one, two, weights, gain, bias, packs=0):
        return launch(
            functools.partial(mix_norm, which),
            info,
            (base, pre, one, two, *weights, gain, bias),
            [spec] + [None] * (5 + len(weights)),
            [arr((half, width))] * 2 + [arr((cols // 2, width))] * packs,
            [None] * (2 + packs),
            scratch=[pltpu.VMEM((2 * cols, width), BF)],
            cost=2,
        )

    h1, a2, pack_co, pack_cq = normed_mix(None, hid, own_rows, pre1, o1_x, o1_cross, far_weights, gain2, bias2, 2)
    a2_sib = core_swap(a2)

    smem = pl.BlockSpec(memory_space=pltpu.SMEM)

    def cross(a):
        return launch(
            cross_forward,
            info,
            (text_len, a, cross_q, k2, v2),
            [smem] + [None] * 4,
            [arr((half, cols), BF), arr((half, cols)), arr((heads, 1, half))],
            [None] * 3,
            flops=half_mm * cols + heads * half * text_rows * 512,
            exps=heads * half * text_rows,
        )

    q2_own, o2_own, total2_own = cross(a2)
    o2_x = x_swap(after(o2_own, o1_x))
    q2_sib, o2_sib, total2_sib = cross(after(a2_sib, q2_own))
    o2_cross = cross_swap(after(o2_sib, o1_cross))
    o2_core = core_swap(o2_sib)
    far_co = swap(pack_co, "dp", dp_size, FLIPS["a"])
    far_cq = swap(pack_cq, "dp", dp_size, FLIPS["a"])
    pre2 = mixed(o2_own, o2_core, 1)
    far_co_core = core_swap(after(far_co, o2_x, o2_cross, far_cq, pre2))
    co_weights = (
        *(far_one_core, far_two_core, far_co_core),
        *(far_one, far_two, far_co),
    )
    h2, a3 = normed_mix(0, h1, None, pre2, o2_x, o2_cross, co_weights, gain3, bias3)
    a3_sib = core_swap(a3)
    far_cq_core = core_swap(after(far_cq, a3))

    unit = 256

    def feed(a, rows):
        return launch(
            feed_forward,
            info,
            (a, cot, ffn_up, ffn_down),
            [
                None,
                rows,
                pl.BlockSpec((width, unit), lambda i, _: (0, i)),
                pl.BlockSpec((unit, width), lambda i, _: (i, 0)),
            ],
            [arr((half, inner), BF)] * 2 + [arr((half, width))],
            [pl.BlockSpec((half, unit), lambda i, _: (0, i))] * 2 + [None],
            grid=(inner // unit,),
            flops=half_mm * inner * 3,
            exps=half * inner * 2,
        )

    g_own, du_own, da3_own = feed(a3, own_rows)
    g_sib, du_sib, da3_sib = feed(after(a3_sib, g_own, far_cq_core), sib_rows)
    da3_sum = da3_own + core_swap(da3_sib)
    da3_far = x_swap(after(da3_sum, o2_x))
    cot_own = lax.dynamic_slice_in_dim(cot, core * half, half)
    cot_sib = lax.dynamic_slice_in_dim(cot, (1 - core) * half, half)
    ffn_plan = (
        (order_one, ((0, 0, 1024),)),
        (order_two, ((1, 0, 1024),)),
    )
    ffn = weight_grads(
        info,
        [
            ([after(a3, da3_sum), a3_sib], [[du_own], [du_sib]]),
            ([cot_own, cot_sib], [[g_own], [g_sib]]),
        ],
        ffn_plan,
    )
    out_own, out_sib = launch(
        down_project,
        info,
        (after(g_own, *ffn[1::2]), g_sib, ffn_down),
        [None, None, pl.BlockSpec((inner, 512), lambda i, _: (0, i))],
        [arr((half, width))] * 2,
        [pl.BlockSpec((half, 512), lambda i, _: (0, i))] * 2,
        grid=(width // 512,),
        flops=2 * half_mm * inner,
    )
    out_got = core_swap(out_sib)
    e1, grads3 = launch(
        sum_norm_back,
        info,
        (da3_sum, after(da3_far, out_own), gain3, h2, cot),
        [None] * 4 + [own_rows],
        [arr((half, width)), arr((2, width))],
        [None] * 2,
    )
    e1_sib = core_swap(e1)
    def cross_back(e, q, total, sums):
        last = bool(sums)
        return launch(
            functools.partial(cross_backward, last),
            info,
            (text_len, e, cross_o, q, k2, v2, total, *sums),
            [smem] + [None] * (6 + len(sums)),
            [arr((half, cols))] + [arr((text_rows, cols), BF if last else F32)] * 2,
            [None] * 3,
        )

    dq2_own, *sums = cross_back(after(e1, out_got), q2_own, total2_own, ())
    dq2_sib, dk2, dv2 = cross_back(e1_sib, q2_sib, total2_sib, tuple(sums))
    dq2_cross = cross_swap(dq2_sib)
    dq2_core = core_swap(dq2_sib)
    dq2_x = x_swap(after(dq2_own, da3_far))
    pre3 = mixed(dq2_own, dq2_core, 2)
    cq_weights = (
        *(far_one_core, far_two_core, far_cq_core),
        *(far_one, far_two, far_cq),
    )

    text_half = text_rows // 2
    text_own, text_send = launch(
        text_back,
        info,
        (dk2, dv2, cross_k, cross_v),
        [None] * 4,
        [arr((text_half, width))] * 2,
        [None] * 2,
        scratch=[pltpu.VMEM((text_rows, width), F32)],
        flops=2 * text_rows * width * cols * 2,
    )
    text_got = core_swap(text_send)
    out_two = launch(
        out_second,
        info,
        (out_own, out_got, text_own, text_got),
        [None] * 4,
        [arr((half + text_half, width))],
        [None],
    )[0]
    cross_plan = (
        (order_one, ((0, 0, 256), (2, 0, 256))),
        (order_two, ((1, 0, 256), (2, 256, 256))),
    )
    cross = weight_grads(
        info,
        [
            ([e1, e1_sib], [[o2_own], [o2_sib]]),
            ([a2, a2_sib], [[dq2_own], [dq2_sib]]),
            ([text], [[dk2, dv2]]),
        ],
        cross_plan,
    )
    pins = [out_two]
    if whole:
        ffn = exchange(list(zip(ffn[0::2], ffn[1::2])), orders, 0, cross[0], 12)
        pins += sent(ffn)
    e0, grads2 = launch(
        mix_norm_back,
        info,
        (after(pre3, *pins), dq2_x, dq2_cross, *cq_weights, gain2, h1, e1),
        [None] * (6 + len(cq_weights)),
        [arr((half, width)), arr((2, width))],
        [None] * 2,
        scratch=[pltpu.VMEM((2 * cols, width), BF)],
        cost=0,
    )
    out_far_two = x_swap(after(out_two, dq2_x))
    e0_sib = core_swap(e0)
    do1 = launch(
        mixed_back,
        info,
        (e0, e0_sib, self_o),
        [None] * 3,
        [arr((frames, cols), BF)],
        [None],
    )[0]
    dq1, dk1, dv1 = launch(
        self_backward,
        info,
        (q1, k1, v1, do1, total1),
        [pair_in] * 4 + [level],
        [arr((frames, cols), BF)] * 3,
        [pair_in] * 3,
        grid=(heads,),
        scratch=[pltpu.VMEM((frames, PAIR), F32)] * 3,
        flops=heads * frames * frames * 256 * 5,
        exps=heads * frames * frames,
    )
    da1_own, da1_send = launch(
        first_back,
        info,
        (dq1, dk1, dv1, self_q, self_k, self_v),
        [None] * 6,
        [arr((half, width))] * 2,
        [None] * 2,
        flops=2 * half_mm * 3 * cols,
    )
    pins = []
    if whole:
        ffn = exchange(ffn, orders, 1, da1_own, 4)
        pins = [ffn[1]]
        cross = [(k, after(c, ffn[1])) for k, c in zip(cross[0::2], cross[1::2])]
    da1_sum, grads1 = launch(
        sum_first_grads,
        info,
        (da1_own, after(core_swap(da1_send), *pins), hid),
        [None] * 2 + [own_rows],
        [arr((half, width)), arr((2, width))],
        [None] * 2,
    )

    vectors = (grads1, grads2, grads3)
    if not whole:
        stacked = lax.psum(jnp.concatenate(vectors), "tensor")
        stacked = lax.psum_scatter(stacked, "dp", scatter_dimension=1, tiled=True)
        vectors = ()
    self_plan = (
        (order_one, ((0, 0, 256), (1, 256, 256))),
        (order_two, ((1, 0, 256), (1, 512, 256))),
    )
    own = weight_grads(
        info,
        [
            ([after(e0, da1_sum), e0_sib], [[o1_own], [o1_sib]]),
            ([a1], [[dq1, dk1, dv1]]),
        ],
        self_plan,
        vectors,
    )
    pins = [own[0]]
    if whole:
        own = list(zip(own[0::2], own[1::2]))
    out_final = launch(
        out_sum,
        info,
        (h2, out_two, after(out_far_two, *pins)),
        [None] * 3,
        [arr((half + text_half, width))],
        [None],
    )[0]
    da1_far = x_swap(after(da1_sum, out_final))
    output, text_grad = launch(
        out_place,
        info,
        (out_final, core_swap(out_final)),
        [None] * 2,
        [arr((frames, width), BF), arr((text_rows, width))],
        [None] * 2,
    )
    pins = []
    if not whole:
        ffn, cross, own = (
            [scatter_sum(*p) for p in zip(g[0::2], g[1::2])] for g in (ffn, cross, own)
        )
        up_grad, down_grad = ffn[0], ffn[1].T
        co_grad, ck_grad = cross[0][:, :256].T, cross[0][:, 256:]
        cq_grad, cv_grad = cross[1][:, :256], cross[1][:, 256:]
        so_grad, sk_grad = own[0][:, :256].T, own[0][:, 256:]
        sq_grad, sv_grad = own[1][:, :256], own[1][:, 256:]
    if whole:
        cross = exchange(cross, orders, 0, own[0][0], 0)
        own[0] = (own[0][0], after(own[0][1], cross[0][1]))
        up_grad, down_grad = finish(ffn, finish_ffn, cross[0][0], 1)
        cross = exchange(cross, orders, 1, up_grad, 8)
        own[1] = (own[1][0], after(own[1][1], up_grad))
        pins = [cross[1]]
    last = launch(
        last_norm_back,
        info,
        (da1_sum, after(da1_far, *pins), gain1, hid, e0),
        [None] * 3 + [own_rows, None],
        [arr((half, width))],
        [None],
        flops=half_mm * 8,
    )[0]
    if whole:
        own = exchange(own, orders, 0, last)
        cross = (cross[0], after(cross[1], up_grad))
        co_grad, ck_grad, cq_grad, cv_grad = finish(cross, finish_cross, last)
        own = exchange(own, orders, 1)
        so_grad, sk_grad, sq_grad, sv_grad, stacked = finish(own, finish_self)
    hidden_grad = launch(
        place,
        info,
        (last, core_swap(last)),
        [None] * 2,
        [arr((frames, width), BF)],
        [None],
    )[0]
    if whole:
        stacked = stacked + x_swap(after(stacked, da1_far))
        stacked = stacked + core_swap(stacked)
    return (
        output.reshape(hidden.shape),
        hidden_grad.reshape(hidden.shape),
        text_grad.reshape(text_states.shape),
        stacked[0],
        stacked[1],
        sq_grad,
        sk_grad,
        sv_grad,
        so_grad,
        stacked[2],
        stacked[3],
        cq_grad,
        ck_grad,
        cv_grad,
        co_grad,
        stacked[4],
        stacked[5],
        up_grad,
        down_grad,
    )


def solution(mesh):
    rows = P("dp", None, None)
    column, row = P(None, "tensor"), P("tensor", None)
    in_specs = (
        *(rows, rows, P("dp"), P(), P(), column, column, column, row),
        *(P(), P(), column, column, column, row),
        *(P(), P(), column, row, rows),
    )
    vector, down, across = P("dp"), P("dp", "tensor"), P("tensor", "dp")
    out_specs = (
        *(rows, rows, rows, vector, vector, down, down, down, across),
        *(vector, vector, down, down, down, across),
        *(vector, vector, down, across),
    )
    return jax.shard_map(body, mesh=mesh, in_specs=in_specs, out_specs=out_specs, check_vma=False)
```

```python
import functools

import jax
import jax.numpy as jnp
import numpy as np
from jax import lax
from jax.experimental import pallas as pl
from jax.experimental.pallas import tpu as pltpu
from jax.sharding import PartitionSpec as P

HD = 64
EPS = 1e-05
NEG = -1e30
SCALE = HD ** (-0.5)
BF = jnp.bfloat16
F32 = jnp.float32
PAIR = 2 * HD

FLIPS = WEIGHT = {"y": 1, "a": 2, "m": 4}

CORE, PEER, Y, LABEL, TABLE = 0, 1, 2, 3, 8


def index_table(dp_size):
    rows = []
    for me in range(dp_size):
        for t in range(4):
            row = [t & 1, 1 - (t & 1), me & 1, me & 3, 0, 0, 0, 0]
            row += [(me ^ i) if dp_size == 8 else i for i in range(8)]
            rows.append(row)
    return np.array(rows, np.int32)


def dot(left, right):
    return lax.dot_general(left, right, (((1,), (0,)), ((), ())), preferred_element_type=F32)


def against(left, right):
    return lax.dot_general(left, right, (((1,), (1,)), ((), ())), preferred_element_type=F32)


def over_rows(left, right):
    return lax.dot_general(left, right, (((0,), (0,)), ((), ())), preferred_element_type=F32)


def swap(value, axis, size, flip):
    return lax.ppermute(value, axis, [(i, i ^ flip) for i in range(size)])


def core_swap(value):
    return swap(value, "tensor", 4, 1)


def x_swap(value):
    return swap(value, "tensor", 4, 2)


def cross_swap(value):
    return swap(value, "tensor", 4, 3)


def after(value, *others):
    return lax.optimization_barrier((value, *others))[0]


def full(shape):
    return pl.BlockSpec(shape, lambda *_: (0,) * len(shape))


def launch(body, info, args, in_specs, outs, out_specs, grid=(1,), scratch=(), flops=0, exps=0, grant=20, cost=0):
    specs = [full(a.shape) if s is None else s for a, s in zip(args, in_specs)]
    ospecs = [full(o.shape) if s is None else s for o, s in zip(outs, out_specs)]
    return pl.pallas_call(
        body,
        out_shape=list(outs),
        grid_spec=pltpu.PrefetchScalarGridSpec(
            num_scalar_prefetch=1,
            grid=grid,
            in_specs=specs,
            out_specs=ospecs,
            scratch_shapes=list(scratch),
        ),
        compiler_params=pltpu.CompilerParams(vmem_limit_bytes=min(grant, 12) << 20),
        cost_estimate=pl.CostEstimate(
            flops=1 + cost * 10**9, bytes_accessed=1, transcendentals=0
        ),
        name=body.__name__ if hasattr(body, "__name__") else body.func.__name__,
    )(info, *args)


def arr(shape, dtype=F32):
    return jax.ShapeDtypeStruct(shape, dtype)


def normed(values):
    centred = values - jnp.mean(values, -1, keepdims=True)
    inverse = lax.rsqrt(jnp.mean(centred * centred, -1, keepdims=True) + EPS)
    return centred * inverse, inverse


def norm_back(grad, scaled, inverse, gain):
    weighted = grad * gain
    first = jnp.mean(weighted, -1, keepdims=True)
    second = jnp.mean(weighted * scaled, -1, keepdims=True)
    return inverse * (weighted - first - scaled * second)


def head_lanes(odd, dtype):
    lane = lax.broadcasted_iota(jnp.int32, (1, PAIR), 1)
    return ((lane // HD) == odd).astype(dtype)


def norm_project(info, hid, gain, bias, wq, wk, wv, a1, q, k, v):
    scaled, _ = normed(hid[...].astype(F32))
    low = (scaled * gain[...] + bias[...]).astype(BF)
    a1[...] = low
    q[...] = (dot(low, wq[...]) * SCALE).astype(BF)
    k[...] = dot(low, wk[...]).astype(BF)
    v[...] = dot(low, wv[...]).astype(BF)


def text_project(info, text, wk, wv, k, v):
    k[...] = dot(text[...], wk[...]).astype(BF)
    v[...] = dot(text[...], wv[...]).astype(BF)


def blocks_of(rows, step=256):
    return [(s, min(step, rows - s)) for s in range(0, rows, step)]


def causal(scores):
    key = lax.broadcasted_iota(jnp.int32, scores.shape, 0)
    query = lax.broadcasted_iota(jnp.int32, scores.shape, 1)
    return jnp.where(key <= query, scores, NEG)


def self_forward(info, q, k, v, keep, send, total, mixed):
    rows = q.shape[0]
    half = rows // 2
    odd = lax.rem(pl.program_id(0), 2)
    lanes = head_lanes(odd, BF)
    lanes_on = head_lanes(odd, F32) > 0
    for start, size in blocks_of(rows):
        here = slice(start, start + size)
        query = q[here, :] * lanes
        near = causal(against(k[here, :], query))
        top = jnp.max(near, 0, keepdims=True)
        if start:
            far = against(k[:start, :], query)
            top = jnp.maximum(top, jnp.max(far, 0, keepdims=True))
        near = jnp.exp(near - top)
        count = jnp.sum(near, 0, keepdims=True)
        if start:
            far = jnp.exp(far - top)
            count = count + jnp.sum(far, 0, keepdims=True)
        scale = 1.0 / count
        out = over_rows(v[here, :], (near * scale).astype(BF))
        if start:
            out = out + over_rows(v[:start, :], (far * scale).astype(BF))
        total[0, :, here] = top + jnp.log(count)
        mixed[here, :] = jnp.where(lanes_on, out.T, mixed[here, :])

    @pl.when(odd == 1)
    def _():
        keep[...] = mixed[pl.ds(pl.multiple_of(info[CORE] * half, 8), half), :]
        send[...] = mixed[pl.ds(pl.multiple_of(info[PEER] * half, 8), half), :]


def prepare(info, so, co, cq, own, first):
    own[0:256, :] = so[...].astype(F32)
    own[256:512, :] = co[...].astype(F32)
    own[512:768, :] = cq[...].astype(F32).T
    first[0:128, :] = own[pl.ds(pl.multiple_of(info[Y] * 128, 8), 128), :]
    for i in range(2):
        at = pl.multiple_of(256 + i * 256 + info[LABEL] * 64, 8)
        first[128 + i * 64 : 192 + i * 64, :] = own[pl.ds(at, 64), :]


def mix(info, one, two, w_one, w_two, out):
    out[...] = dot(one[...].astype(BF), w_one[...].astype(BF)) + dot(
        two[...].astype(BF), w_two[...].astype(BF)
    )


def gather_halves(info, far, weights):
    for s in range(2):
        for p in range(2):

            @pl.when(info[Y] == p)
            def _(s=s, p=p):
                weights[s * 256 + p * 128 : s * 256 + p * 128 + 128, :] = far[2 * s][
                    :128, :
                ].astype(BF)

            @pl.when(info[Y] != p)
            def _(s=s, p=p):
                weights[s * 256 + p * 128 : s * 256 + p * 128 + 128, :] = far[2 * s + 1][
                    :128, :
                ].astype(BF)


def gather_quarters(info, far, weights, first):
    for s in range(2):
        over_x, over_y, over_z = far[3 * s : 3 * s + 3]
        pieces = (
            over_x[128 + first : 192 + first, :],
            over_y[128 + first : 192 + first, :],
            over_z[:64, :],
            over_z[64:, :],
        )
        for j, piece in enumerate(pieces):
            at = pl.multiple_of(s * 256 + (info[LABEL] ^ j) * 64, 64)
            weights[pl.ds(at, 64), :] = piece.astype(BF)


def mix_far(info, pre, one, two, far, weights, which):
    if which is None:
        gather_halves(info, far, weights)
    else:
        gather_quarters(info, far, weights, which)
    far_part = dot(one[...].astype(BF), weights[:256, :]) + dot(
        two[...].astype(BF), weights[256:, :]
    )
    return pre[...] + far_part


def mix_norm(which, info, base, pre, one, two, *refs):
    n = 7 if which is None else 5
    far, (gain, bias, resid, low, *packs, weights) = refs[:-n], refs[-n:]
    for i, pack in enumerate(packs):
        for j in range(2):
            pack[j * 64 : j * 64 + 64, :] = far[2 + j][128 + i * 64 : 192 + i * 64, :]
    part = mix_far(info, pre, one, two, far, weights, which)
    total = base[...].astype(F32) + part
    resid[...] = total
    scaled, _ = normed(total)
    low[...] = scaled * gain[...] + bias[...]


def mix_norm_back(info, pre, one, two, *refs):
    far, (gain, resid, e_in, e_out, grads, weights) = refs[:-6], refs[-6:]
    grad = mix_far(info, pre, one, two, far, weights, 64)
    scaled, inverse = normed(resid[...])
    e_out[...] = e_in[...] + norm_back(grad, scaled, inverse, gain[...])
    grads[0:1, :] = jnp.sum(grad * scaled, 0, keepdims=True) * 0.5
    grads[1:2, :] = jnp.sum(grad, 0, keepdims=True) * 0.5


def sum_norm_back(info, mine, far, gain, resid, e_in, e_out, grads):
    grad = mine[...] + far[...]
    scaled, inverse = normed(resid[...])
    e_out[...] = e_in[...].astype(F32) + norm_back(grad, scaled, inverse, gain[...])
    grads[0:1, :] = jnp.sum(grad * scaled, 0, keepdims=True) * 0.5
    grads[1:2, :] = jnp.sum(grad, 0, keepdims=True) * 0.5


def sum_first_grads(info, mine, recv, hid, out, grads):
    grad = mine[...] + recv[...]
    out[...] = grad
    scaled, _ = normed(hid[...].astype(F32))
    grads[0:1, :] = jnp.sum(grad * scaled, 0, keepdims=True)
    grads[1:2, :] = jnp.sum(grad, 0, keepdims=True)


def last_norm_back(info, mine, far, gain, hid, e_in, out):
    grad = mine[...] + far[...]
    scaled, inverse = normed(hid[...].astype(F32))
    out[...] = e_in[...] + norm_back(grad, scaled, inverse, gain[...])


def cross_forward(info, length, a2, wq, k, v, q, mixed, total):
    query_rows = (dot(a2[...].astype(BF), wq[...]) * SCALE).astype(BF)
    q[...] = query_rows
    for pair in range(2):
        cols = slice(pair * PAIR, (pair + 1) * PAIR)
        pair_out = None
        for odd in range(2):
            query = query_rows[:, cols] * head_lanes(odd, BF)
            scores = against(k[:, cols], query)
            slot = lax.broadcasted_iota(jnp.int32, scores.shape, 0)
            scores = jnp.where(slot < length[0], scores, NEG)
            top = jnp.max(scores, 0, keepdims=True)
            scores = jnp.exp(scores - top)
            count = jnp.sum(scores, 0, keepdims=True)
            out = over_rows(v[:, cols], (scores * (1.0 / count)).astype(BF)).T
            total[pair * 2 + odd] = top + jnp.log(count)
            pair_out = out if odd == 0 else jnp.where(head_lanes(1, F32) > 0, out, pair_out)
        mixed[:, cols] = pair_out


def feed_forward(info, a3, cot, up, down, g, du, da3):
    n = pl.program_id(0)
    u = dot(a3[...].astype(BF), up[...])
    cdf = 0.5 + 0.5 * lax.erf(u * (0.5**0.5))
    g[...] = (u * cdf).astype(BF)
    slope = cdf + u * jnp.exp(-0.5 * u * u) * (1.0 / (2.0 * np.pi) ** 0.5)
    dg = against(cot[...], down[...]).astype(BF).astype(F32)
    low = (dg * slope).astype(BF)
    du[...] = low
    part = against(low, up[...])

    @pl.when(n == 0)
    def _():
        da3[...] = part

    @pl.when(n > 0)
    def _():
        da3[...] += part


def add_two(info, one, two, out):
    out[...] = one[...] + two[...]


def down_project(info, own, sib, down, out_own, out_sib):
    out_own[...] = dot(own[...], down[...])
    out_sib[...] = dot(sib[...], down[...])


def cross_backward(second, info, length, e1, wo, q, k, v, total, *rest):
    if second:
        dk_in, dv_in, dq, dk_out, dv_out = rest
    else:
        dq, dk_out, dv_out = rest
    mixed_grad = against(e1[...].astype(BF), wo[...]).astype(BF)
    for pair in range(2):
        cols = slice(pair * PAIR, (pair + 1) * PAIR)
        dk = dk_in[:, cols] if second else None
        dv = dv_in[:, cols] if second else None
        pair_dq = None
        for odd in range(2):
            lanes = head_lanes(odd, BF)
            query = q[:, cols] * lanes
            grad = mixed_grad[:, cols] * lanes
            scores = against(k[:, cols], query)
            slot = lax.broadcasted_iota(jnp.int32, scores.shape, 0)
            scores = jnp.where(slot < length[0], scores, NEG)
            probs = jnp.exp(scores - total[pair * 2 + odd])
            prob_grad = against(v[:, cols], grad)
            part = dot(probs.astype(BF), grad)
            dv = part if dv is None else dv + part
            delta = jnp.sum(probs * prob_grad, 0, keepdims=True)
            low = (probs * (prob_grad - delta)).astype(BF)
            part = dot(low, query)
            dk = part if dk is None else dk + part
            out = over_rows(k[:, cols], low).T
            pair_dq = out if odd == 0 else jnp.where(head_lanes(1, F32) > 0, out, pair_dq)
        dq[:, cols] = pair_dq * SCALE
        dk_out[:, cols] = dk.astype(dk_out.dtype)
        dv_out[:, cols] = dv.astype(dv_out.dtype)


def text_back(info, dk, dv, wk, wv, own, send, scratch):
    half = own.shape[0]
    scratch[...] = against(dk[...], wk[...]) + against(dv[...], wv[...])
    own[...] = scratch[pl.ds(pl.multiple_of(info[CORE] * half, 8), half), :]
    send[...] = scratch[pl.ds(pl.multiple_of(info[PEER] * half, 8), half), :]


def mixed_back(info, own, sib, wo, out):
    half = own.shape[0]
    out[pl.ds(pl.multiple_of(info[CORE] * half, 16), half), :] = against(
        own[...].astype(BF), wo[...]
    ).astype(BF)
    out[pl.ds(pl.multiple_of(info[PEER] * half, 16), half), :] = against(
        sib[...].astype(BF), wo[...]
    ).astype(BF)


def self_backward(info, q, k, v, grad_in, total, dq, dk, dv, dq_sum, dk_sum, dv_sum):
    rows = q.shape[0]
    odd = lax.rem(pl.program_id(0), 2)
    lanes = head_lanes(odd, BF)
    lanes_on = head_lanes(odd, F32) > 0

    @pl.when(odd == 0)
    def _():
        dk_sum[...] = jnp.zeros_like(dk_sum)
        dv_sum[...] = jnp.zeros_like(dv_sum)

    for start, size in blocks_of(rows):
        here = slice(start, start + size)
        query = q[here, :] * lanes
        grad = grad_in[here, :] * lanes
        level = total[0, :, here]
        near = jnp.exp(causal(against(k[here, :], query)) - level)
        near_grad = against(v[here, :], grad)
        delta = jnp.sum(near * near_grad, 0, keepdims=True)
        dv_sum[here, :] += dot(near.astype(BF), grad)
        if start:
            far = jnp.exp(against(k[:start, :], query) - level)
            far_grad = against(v[:start, :], grad)
            delta = delta + jnp.sum(far * far_grad, 0, keepdims=True)
            dv_sum[:start, :] += dot(far.astype(BF), grad)
        near_low = (near * (near_grad - delta)).astype(BF)
        dk_sum[here, :] += dot(near_low, query)
        out = over_rows(k[here, :], near_low)
        if start:
            far_low = (far * (far_grad - delta)).astype(BF)
            dk_sum[:start, :] += dot(far_low, query)
            out = out + over_rows(k[:start, :], far_low)
        dq_sum[here, :] = jnp.where(lanes_on, out.T * SCALE, dq_sum[here, :])

    @pl.when(odd == 1)
    def _():
        dq[...] = dq_sum[...].astype(BF)
        dk[...] = dk_sum[...].astype(BF)
        dv[...] = dv_sum[...].astype(BF)


def first_back(info, dq, dk, dv, wq, wk, wv, own, send):
    half = own.shape[0]
    for at, out in ((PEER, send), (CORE, own)):
        here = pl.ds(pl.multiple_of(info[at] * half, 16), half)
        out[...] = (
            against(dq[here, :], wq[...])
            + against(dk[here, :], wk[...])
            + against(dv[here, :], wv[...])
        )


def weight_grad(plan, shapes, n_v, info, *refs):
    at = 0
    groups = []
    for n_left, n_right in shapes:
        groups.append((refs[at : at + n_left], refs[at + n_left : at + n_left + n_right]))
        at += n_left + n_right
    vectors = refs[at : at + n_v]
    outs = refs[at + n_v : at + n_v + 2 * len(plan)]
    lhs, rhs = refs[-2:]
    for g, (lefts, rights) in enumerate(groups):
        row = 0
        per = len(rights) // len(lefts)
        for i, left in enumerate(lefts):
            rows = left.shape[0]
            for j in range(8):
                block = left[:, pl.ds(pl.multiple_of(info[TABLE + j] * 128, 128), 128)]
                lhs[row : row + rows, j * 128 : (j + 1) * 128] = block.astype(BF)
            col = 0
            for right in rights[i * per : (i + 1) * per]:
                rhs[row : row + rows, col : col + right.shape[1]] = right[...].astype(BF)
                col += right.shape[1]
            row += rows
        for s, (order, segments) in enumerate(plan):
            put = 0
            for group, first, width in segments:
                if group == g:
                    for half in range(2):
                        value = over_rows(
                            lhs[:row, half * 512 : half * 512 + 512],
                            rhs[:row, first : first + width],
                        )
                        for q in range(4):
                            j = half * 4 + q
                            sent, pos = spot(order, j)
                            outs[2 * s + sent][pos, :128, put : put + width] = value[
                                q * 128 : (q + 1) * 128, :
                            ]
                put += width
    if n_v:
        for j in range(8):
            sent, pos = spot(plan[-1][0], j)
            out = outs[2 * len(plan) - 2 + sent]
            out[pos, 128:, :] = jnp.zeros((8, out.shape[2]), F32)
            for i, ref in enumerate(vectors):
                block = ref[:, pl.ds(pl.multiple_of(info[TABLE + j] * 128, 128), 128)]
                out[pos, 128 + 2 * i : 130 + 2 * i, :128] = block


def spot(order, j):
    bits = [(j // WEIGHT[name]) & 1 for name in order]
    return bits[0], bits[1] * 2 + bits[2]


def weight_grads(info, groups, plan, vectors=()):
    args, specs, shapes = [], [], []
    for lefts, rights in groups:
        flat = [r for group in rights for r in group]
        for left in lefts:
            array, spec = left if isinstance(left, tuple) else (left, None)
            args.append(array)
            specs.append(spec)
        args += flat
        specs += [None] * len(flat)
        shapes.append((len(lefts), len(flat)))
    args += vectors
    specs += [None] * len(vectors)
    outs = []
    for s, (order, segments) in enumerate(plan):
        tall = 136 if vectors and s == len(plan) - 1 else 128
        outs += [arr((4, tall, sum(w for _, _, w in segments)))] * 2
    rows = max(sum(group[0].shape[0] for group in rights) for _, rights in groups)
    wide = max(sum(r.shape[1] for r in rights[0]) for _, rights in groups)
    return launch(
        functools.partial(weight_grad, plan, tuple(shapes), len(vectors)),
        info,
        tuple(args),
        specs,
        outs,
        [None] * len(outs),
        scratch=[pltpu.VMEM((rows, 1024), BF), pltpu.VMEM((rows, wide), BF)],
        grant=40,
    )


def scatter_sum(keep, send):
    value = jnp.concatenate([keep, send])
    value = value.reshape(-1, value.shape[-1])
    return lax.psum_scatter(value, "dp", scatter_dimension=0, tiled=True)


def fold(info, *refs):
    for i in range(2):
        keep, got = refs[2 * i : 2 * i + 2]
        keep_out, send_out = refs[4 + 2 * i : 6 + 2 * i]
        n = keep_out.shape[0]
        keep_out[...] = keep[:n] + got[:n]
        send_out[...] = keep[n:] + got[n:]


def fold_one(info, keep, got, keep_out, send_out):
    keep_out[...] = keep[0] + got[0]
    send_out[...] = keep[1] + got[1]


def fold_last(info, *refs):
    keep_out, send_out = refs[4:]
    col = 0
    for i in range(2):
        keep, got = refs[2 * i : 2 * i + 2]
        rows, wide = keep.shape[1:]
        keep_out[:rows, col : col + wide] = keep[0] + got[0]
        send_out[:rows, col : col + wide] = keep[1] + got[1]
        col += wide


def finish_ffn(info, keep, got, up, down):
    wide = up.shape[1]
    up[...] = keep[:, :wide] + got[:, :wide]
    down[...] = (keep[:, wide:] + got[:, wide:]).T


def finish_cross(info, keep, got, co, ck, cq, cv):
    co[...] = (keep[:, :256] + got[:, :256]).T
    for i, out in enumerate((ck, cq, cv)):
        here = slice(256 * i + 256, 256 * i + 512)
        out[...] = keep[:, here] + got[:, here]


def finish_self(info, keep, got, so, sk, sq, sv, vectors):
    so[...] = (keep[:128, :256] + got[:128, :256]).T
    for i, out in enumerate((sk, sq, sv)):
        here = slice(256 * i + 256, 256 * i + 512)
        out[...] = keep[:128, here] + got[:128, here]
    vectors[...] = keep[128:, 512:640] + got[128:, 512:640]


FINISH = {
    finish_ffn: [(128, 1024), (1024, 128)],
    finish_cross: [(256, 128), (128, 256), (128, 256), (128, 256)],
    finish_self: [(256, 128), (128, 256), (128, 256), (128, 256), (8, 128)],
}


def exchange(streams, orders, step, first=None, cost=10):
    args = []
    for (keep, send), order in zip(streams, orders):
        got = swap(send, "dp", 8, FLIPS[order[step]])
        args += [keep, got if first is None else after(got, first)]
    none = jnp.zeros((1,), jnp.int32)
    if step == 1:
        shape = (max(a.shape[1] for a in args), args[0].shape[2] + args[2].shape[2])
        return launch(
            fold_last, none, args, [None] * 4, [arr(shape)] * 2, [None] * 2, cost=cost
        )
    outs = []
    for keep, _ in streams:
        outs += [arr((keep.shape[0] // 2, *keep.shape[1:]))] * 2
    out = launch(fold, none, args, [None] * 4, outs, [None] * 4, cost=cost)
    return list(zip(out[0::2], out[1::2]))


def fold_stream(pair, name, first, cost=0):
    keep, send = pair
    got = after(swap(send, "dp", 8, FLIPS[name]), first)
    none = jnp.zeros((1,), jnp.int32)
    outs = [arr(keep.shape[1:])] * 2
    return launch(fold_one, none, (keep, got), [None] * 2, outs, [None] * 2, cost=cost)


def finish(pair, body, first=None, cost=10):
    keep, send = pair
    got = swap(send, "dp", 8, FLIPS["m"])
    got = got if first is None else after(got, first)
    outs = [arr(shape) for shape in FINISH[body]]
    none = jnp.zeros((1,), jnp.int32)
    return launch(body, none, (keep, got), [None] * 2, outs, [None] * len(outs), cost=cost)


def sent(streams):
    return [s for _, s in streams]


def out_second(info, own, got, text_own, text_got, out):
    half = own.shape[0]
    out[:half, :] = own[...] + got[...]
    out[half:, :] = text_own[...] + text_got[...]


def out_sum(info, resid, mine, far, out):
    half = resid.shape[0]
    out[:half, :] = resid[...] + (mine[:half, :] + far[:half, :])
    out[half:, :] = mine[half:, :] + far[half:, :]


def out_place(info, own, sib, out, text_out):
    half = out.shape[0] // 2
    text_half = text_out.shape[0] // 2
    for at, ref in ((CORE, own), (PEER, sib)):
        out[pl.ds(pl.multiple_of(info[at] * half, 16), half), :] = ref[:half, :].astype(BF)
        spot = pl.multiple_of(info[at] * text_half, 8)
        text_out[pl.ds(spot, text_half), :] = ref[half:, :]


def place(info, own, sib, out):
    half = out.shape[0] // 2
    for at, ref in ((CORE, own), (PEER, sib)):
        out[pl.ds(pl.multiple_of(info[at] * half, 16), half), :] = ref[...].astype(BF)


def body(
    hidden,
    text_states,
    text_len,
    ln1_gain,
    ln1_bias,
    self_q,
    self_k,
    self_v,
    self_o,
    ln2_gain,
    ln2_bias,
    cross_q,
    cross_k,
    cross_v,
    cross_o,
    ln3_gain,
    ln3_bias,
    ffn_up,
    ffn_down,
    cotangent,
):
    dp_size = lax.axis_size("dp")
    frames, width = hidden.shape[1:]
    text_rows = text_states.shape[1]
    cols = self_q.shape[1]
    inner = ffn_up.shape[1]
    half = frames // 2
    device = lax.axis_index("dp") * 4 + lax.axis_index("tensor")
    table = jnp.asarray(index_table(dp_size))
    info = lax.dynamic_index_in_dim(table, device, 0, keepdims=False)
    hid = hidden.reshape(frames, width)
    cot = cotangent.reshape(frames, width)
    text = text_states.reshape(text_rows, width)
    gain1, bias1 = ln1_gain.reshape(1, width), ln1_bias.reshape(1, width)
    gain2, bias2 = ln2_gain.reshape(1, width), ln2_bias.reshape(1, width)
    gain3, bias3 = ln3_gain.reshape(1, width), ln3_bias.reshape(1, width)
    own_rows = pl.BlockSpec((half, width), lambda i, table: (table[CORE], 0))
    sib_rows = pl.BlockSpec((half, width), lambda i, table: (table[PEER], 0))
    half_mm = 2 * half * width
    whole = dp_size == 8
    orders = ("yam", "aym") if whole else ("may",) * 2
    order_one, order_two = orders

    own3, first = launch(
        prepare,
        info,
        (self_o, cross_o, cross_q),
        [None] * 3,
        [arr((3 * cols, width)), arr((cols, width))],
        [None] * 2,
        flops=1 << 20,
    )
    far_one = cross_swap(first)
    sib3 = core_swap(own3)

    def weight_at(i):
        return pl.BlockSpec((cols, width), lambda *_: (i, 0))

    step = frames // 4
    a1, q1, k1, v1 = launch(
        norm_project,
        info,
        (after(hid, first), gain1, bias1, self_q, self_k, self_v),
        [pl.BlockSpec((step, width), lambda i, _: (i, 0))] + [None] * 5,
        [arr((frames, width), BF)] + [arr((frames, cols), BF)] * 3,
        [pl.BlockSpec((step, width), lambda i, _: (i, 0))]
        + [pl.BlockSpec((step, cols), lambda i, _: (i, 0))] * 3,
        grid=(4,),
        flops=2 * frames * width * cols * 3,
    )
    heads = cols // HD
    pair_in = pl.BlockSpec((frames, PAIR), lambda h, _: (0, h // 2))
    pair_half = pl.BlockSpec((half, PAIR), lambda h, _: (0, h // 2))
    level = pl.BlockSpec((1, 1, frames), lambda h, _: (h, 0, 0))
    o1_own, o1_sib, total1 = launch(
        self_forward,
        info,
        (q1, k1, v1),
        [pair_in] * 3,
        [arr((half, cols))] * 2 + [arr((heads, 1, frames))],
        [pair_half] * 2 + [level],
        grid=(heads,),
        scratch=[pltpu.VMEM((frames, PAIR), F32)],
        flops=heads * frames * frames * 512,
        exps=heads * frames * frames,
    )
    o1_cross = cross_swap(after(o1_sib, far_one))
    o1_core = core_swap(after(o1_sib, sib3))
    o1_x = x_swap(o1_own)
    far_two = swap(after(far_one, o1_own), "dp", dp_size, FLIPS["y"])
    k2, v2 = launch(
        text_project,
        info,
        (after(text, o1_own), cross_k, cross_v),
        [None] * 3,
        [arr((text_rows, cols), BF)] * 2,
        [None] * 2,
        flops=2 * text_rows * width * cols * 2,
    )

    def mixed(one, two, i):
        return launch(
            mix,
            info,
            (one, two, own3, sib3),
            [None] * 2 + [weight_at(i)] * 2,
            [arr((half, width))],
            [None],
            flops=half_mm * 512,
        )[0]

    pre1 = mixed(after(o1_own, k2), o1_core, 0)
    far_one_core = core_swap(after(far_one, o1_core))
    far_two_core = core_swap(after(far_two, o1_x, o1_cross, pre1))
    far_weights = (far_one_core, far_two_core, far_one, far_two)

    def normed_mix(which, base, spec, pre, one, two, weights, gain, bias, packs=0):
        return launch(
            functools.partial(mix_norm, which),
            info,
            (base, pre, one, two, *weights, gain, bias),
            [spec] + [None] * (5 + len(weights)),
            [arr((half, width))] * 2 + [arr((cols // 2, width))] * packs,
            [None] * (2 + packs),
            scratch=[pltpu.VMEM((2 * cols, width), BF)],
            cost=2,
        )

    h1, a2, pack_co, pack_cq = normed_mix(None, hid, own_rows, pre1, o1_x, o1_cross, far_weights, gain2, bias2, 2)
    a2_sib = core_swap(a2)

    smem = pl.BlockSpec(memory_space=pltpu.SMEM)

    def cross(a):
        return launch(
            cross_forward,
            info,
            (text_len, a, cross_q, k2, v2),
            [smem] + [None] * 4,
            [arr((half, cols), BF), arr((half, cols)), arr((heads, 1, half))],
            [None] * 3,
            flops=half_mm * cols + heads * half * text_rows * 512,
            exps=heads * half * text_rows,
        )

    q2_own, o2_own, total2_own = cross(a2)
    o2_x = x_swap(after(o2_own, o1_x))
    q2_sib, o2_sib, total2_sib = cross(after(a2_sib, q2_own))
    o2_cross = cross_swap(after(o2_sib, o1_cross))
    o2_core = core_swap(o2_sib)
    far_co = swap(pack_co, "dp", dp_size, FLIPS["a"])
    far_cq = swap(pack_cq, "dp", dp_size, FLIPS["a"])
    pre2 = mixed(o2_own, o2_core, 1)
    far_co_core = core_swap(after(far_co, o2_x, o2_cross, far_cq, pre2))
    co_weights = (
        *(far_one_core, far_two_core, far_co_core),
        *(far_one, far_two, far_co),
    )
    h2, a3 = normed_mix(0, h1, None, pre2, o2_x, o2_cross, co_weights, gain3, bias3)
    a3_sib = core_swap(a3)
    far_cq_core = core_swap(after(far_cq, a3))

    unit = 256

    def feed(a, rows):
        return launch(
            feed_forward,
            info,
            (a, cot, ffn_up, ffn_down),
            [
                None,
                rows,
                pl.BlockSpec((width, unit), lambda i, _: (0, i)),
                pl.BlockSpec((unit, width), lambda i, _: (i, 0)),
            ],
            [arr((half, inner), BF)] * 2 + [arr((half, width))],
            [pl.BlockSpec((half, unit), lambda i, _: (0, i))] * 2 + [None],
            grid=(inner // unit,),
            flops=half_mm * inner * 3,
            exps=half * inner * 2,
        )

    g_own, du_own, da3_own = feed(a3, own_rows)
    g_sib, du_sib, da3_sib = feed(after(a3_sib, g_own, far_cq_core), sib_rows)
    da3_sum = launch(
        add_two,
        info,
        (da3_own, core_swap(da3_sib)),
        [None] * 2,
        [arr((half, width))],
        [None],
    )[0]
    da3_far = x_swap(after(da3_sum, o2_x))
    ffn_plan = (
        (order_one, ((0, 0, 1024),)),
        (order_two, ((1, 0, 1024),)),
    )
    ffn = weight_grads(
        info,
        [
            ([after(a3, da3_sum), a3_sib], [[du_own], [du_sib]]),
            ([(cot, own_rows), (cot, sib_rows)], [[g_own], [g_sib]]),
        ],
        ffn_plan,
    )
    out_own, out_sib = launch(
        down_project,
        info,
        (after(g_own, *ffn[1::2]), g_sib, ffn_down),
        [None, None, pl.BlockSpec((inner, 512), lambda i, _: (0, i))],
        [arr((half, width))] * 2,
        [pl.BlockSpec((half, 512), lambda i, _: (0, i))] * 2,
        grid=(width // 512,),
        flops=2 * half_mm * inner,
    )
    out_got = core_swap(out_sib)
    e1, grads3 = launch(
        sum_norm_back,
        info,
        (da3_sum, after(da3_far, out_own), gain3, h2, cot),
        [None] * 4 + [own_rows],
        [arr((half, width)), arr((2, width))],
        [None] * 2,
    )
    e1_sib = core_swap(e1)
    def cross_back(e, q, total, sums):
        last = bool(sums)
        return launch(
            functools.partial(cross_backward, last),
            info,
            (text_len, e, cross_o, q, k2, v2, total, *sums),
            [smem] + [None] * (6 + len(sums)),
            [arr((half, cols))] + [arr((text_rows, cols), BF if last else F32)] * 2,
            [None] * 3,
        )

    dq2_own, *sums = cross_back(after(e1, out_got), q2_own, total2_own, ())
    dq2_sib, dk2, dv2 = cross_back(e1_sib, q2_sib, total2_sib, tuple(sums))
    dq2_cross = cross_swap(dq2_sib)
    dq2_core = core_swap(dq2_sib)
    dq2_x = x_swap(after(dq2_own, da3_far))
    pre3 = mixed(dq2_own, dq2_core, 2)
    cq_weights = (
        *(far_one_core, far_two_core, far_cq_core),
        *(far_one, far_two, far_cq),
    )

    text_half = text_rows // 2
    text_own, text_send = launch(
        text_back,
        info,
        (dk2, dv2, cross_k, cross_v),
        [None] * 4,
        [arr((text_half, width))] * 2,
        [None] * 2,
        scratch=[pltpu.VMEM((text_rows, width), F32)],
        flops=2 * text_rows * width * cols * 2,
    )
    text_got = core_swap(text_send)
    out_two = launch(
        out_second,
        info,
        (out_own, out_got, text_own, text_got),
        [None] * 4,
        [arr((half + text_half, width))],
        [None],
    )[0]
    cross_plan = (
        (order_one, ((0, 0, 256), (2, 0, 256))),
        (order_two, ((1, 0, 256), (2, 256, 256))),
    )
    cross = weight_grads(
        info,
        [
            ([e1, e1_sib], [[o2_own], [o2_sib]]),
            ([a2, a2_sib], [[dq2_own], [dq2_sib]]),
            ([text], [[dk2, dv2]]),
        ],
        cross_plan,
    )
    pins = [out_two]
    if whole:
        ffn = exchange(list(zip(ffn[0::2], ffn[1::2])), orders, 0, cross[0], 12)
        pins += sent(ffn)
    e0, grads2 = launch(
        mix_norm_back,
        info,
        (after(pre3, *pins), dq2_x, dq2_cross, *cq_weights, gain2, h1, e1),
        [None] * (6 + len(cq_weights)),
        [arr((half, width)), arr((2, width))],
        [None] * 2,
        scratch=[pltpu.VMEM((2 * cols, width), BF)],
        cost=0,
    )
    out_far_two = x_swap(after(out_two, dq2_x))
    e0_sib = core_swap(e0)
    do1 = launch(
        mixed_back,
        info,
        (e0, e0_sib, self_o),
        [None] * 3,
        [arr((frames, cols), BF)],
        [None],
    )[0]
    dq1, dk1, dv1 = launch(
        self_backward,
        info,
        (q1, k1, v1, do1, total1),
        [pair_in] * 4 + [level],
        [arr((frames, cols), BF)] * 3,
        [pair_in] * 3,
        grid=(heads,),
        scratch=[pltpu.VMEM((frames, PAIR), F32)] * 3,
        flops=heads * frames * frames * 256 * 5,
        exps=heads * frames * frames,
    )
    da1_own, da1_send = launch(
        first_back,
        info,
        (dq1, dk1, dv1, self_q, self_k, self_v),
        [None] * 6,
        [arr((half, width))] * 2,
        [None] * 2,
        flops=2 * half_mm * 3 * cols,
    )
    pins = []
    if whole:
        ffn = exchange(ffn, orders, 1, da1_own, 4)
        pins = [ffn[1]]
        cross = [(k, after(c, ffn[1])) for k, c in zip(cross[0::2], cross[1::2])]
    da1_sum, grads1 = launch(
        sum_first_grads,
        info,
        (da1_own, after(core_swap(da1_send), *pins), hid),
        [None] * 2 + [own_rows],
        [arr((half, width)), arr((2, width))],
        [None] * 2,
    )

    vectors = (grads1, grads2, grads3)
    if not whole:
        stacked = lax.psum(jnp.concatenate(vectors), "tensor")
        stacked = lax.psum_scatter(stacked, "dp", scatter_dimension=1, tiled=True)
        vectors = ()
    self_plan = (
        (order_one, ((0, 0, 256), (1, 256, 256))),
        (order_two, ((1, 0, 256), (1, 512, 256))),
    )
    own = weight_grads(
        info,
        [
            ([after(e0, da1_sum), e0_sib], [[o1_own], [o1_sib]]),
            ([a1], [[dq1, dk1, dv1]]),
        ],
        self_plan,
        vectors,
    )
    pins = [own[0]]
    if whole:
        own = list(zip(own[0::2], own[1::2]))
    out_final = launch(
        out_sum,
        info,
        (h2, out_two, after(out_far_two, *pins)),
        [None] * 3,
        [arr((half + text_half, width))],
        [None],
    )[0]
    da1_far = x_swap(after(da1_sum, out_final))
    output, text_grad = launch(
        out_place,
        info,
        (out_final, core_swap(out_final)),
        [None] * 2,
        [arr((frames, width), BF), arr((text_rows, width))],
        [None] * 2,
    )
    pins = []
    if not whole:
        ffn, cross, own = (
            [scatter_sum(*p) for p in zip(g[0::2], g[1::2])] for g in (ffn, cross, own)
        )
        up_grad, down_grad = ffn[0], ffn[1].T
        co_grad, ck_grad = cross[0][:, :256].T, cross[0][:, 256:]
        cq_grad, cv_grad = cross[1][:, :256], cross[1][:, 256:]
        so_grad, sk_grad = own[0][:, :256].T, own[0][:, 256:]
        sq_grad, sv_grad = own[1][:, :256], own[1][:, 256:]
    if whole:
        cross = exchange(cross, orders, 0, own[0][0], 0)
        own[0] = (own[0][0], after(own[0][1], cross[0][1]))
        up_grad, down_grad = finish(ffn, finish_ffn, cross[0][0], 1)
        cross = exchange(cross, orders, 1, up_grad, 8)
        own[1] = (own[1][0], after(own[1][1], up_grad))
        pins = [cross[1]]
    last = launch(
        last_norm_back,
        info,
        (da1_sum, after(da1_far, *pins), gain1, hid, e0),
        [None] * 3 + [own_rows, None],
        [arr((half, width))],
        [None],
        flops=half_mm * 8,
    )[0]
    if whole:
        own = exchange(own, orders, 0, last)
        cross = (cross[0], after(cross[1], up_grad))
        co_grad, ck_grad, cq_grad, cv_grad = finish(cross, finish_cross, last)
        own = exchange(own, orders, 1)
        so_grad, sk_grad, sq_grad, sv_grad, stacked = finish(own, finish_self)
    hidden_grad = launch(
        place,
        info,
        (last, core_swap(last)),
        [None] * 2,
        [arr((frames, width), BF)],
        [None],
    )[0]
    if whole:
        stacked = stacked + x_swap(after(stacked, da1_far))
        stacked = stacked + core_swap(stacked)
    return (
        output.reshape(hidden.shape),
        hidden_grad.reshape(hidden.shape),
        text_grad.reshape(text_states.shape),
        stacked[0],
        stacked[1],
        sq_grad,
        sk_grad,
        sv_grad,
        so_grad,
        stacked[2],
        stacked[3],
        cq_grad,
        ck_grad,
        cv_grad,
        co_grad,
        stacked[4],
        stacked[5],
        up_grad,
        down_grad,
    )


def solution(mesh):
    rows = P("dp", None, None)
    column, row = P(None, "tensor"), P("tensor", None)
    in_specs = (
        *(rows, rows, P("dp"), P(), P(), column, column, column, row),
        *(P(), P(), column, column, column, row),
        *(P(), P(), column, row, rows),
    )
    vector, down, across = P("dp"), P("dp", "tensor"), P("tensor", "dp")
    out_specs = (
        *(rows, rows, rows, vector, vector, down, down, down, across),
        *(vector, vector, down, down, down, across),
        *(vector, vector, down, across),
    )
    return jax.shard_map(body, mesh=mesh, in_specs=in_specs, out_specs=out_specs, check_vma=False)
```

```python
import functools

import jax
import jax.numpy as jnp
import numpy as np
from jax import lax
from jax.experimental import pallas as pl
from jax.experimental.pallas import tpu as pltpu
from jax.sharding import PartitionSpec as P

HD = 64
EPS = 1e-05
NEG = -1e30
SCALE = HD ** (-0.5)
BF = jnp.bfloat16
F32 = jnp.float32
PAIR = 2 * HD

FLIPS = WEIGHT = {"y": 1, "a": 2, "m": 4}

CORE, PEER, Y, LABEL, TABLE = 0, 1, 2, 3, 8


def index_table(dp_size):
    rows = []
    for me in range(dp_size):
        for t in range(4):
            row = [t & 1, 1 - (t & 1), me & 1, me & 3, 0, 0, 0, 0]
            row += [(me ^ i) if dp_size == 8 else i for i in range(8)]
            rows.append(row)
    return np.array(rows, np.int32)


def dot(left, right):
    return lax.dot_general(left, right, (((1,), (0,)), ((), ())), preferred_element_type=F32)


def against(left, right):
    return lax.dot_general(left, right, (((1,), (1,)), ((), ())), preferred_element_type=F32)


def over_rows(left, right):
    return lax.dot_general(left, right, (((0,), (0,)), ((), ())), preferred_element_type=F32)


def swap(value, axis, size, flip):
    return lax.ppermute(value, axis, [(i, i ^ flip) for i in range(size)])


def core_swap(value):
    return swap(value, "tensor", 4, 1)


def x_swap(value):
    return swap(value, "tensor", 4, 2)


def cross_swap(value):
    return swap(value, "tensor", 4, 3)


def after(value, *others):
    return lax.optimization_barrier((value, *others))[0]


def full(shape):
    return pl.BlockSpec(shape, lambda *_: (0,) * len(shape))


def launch(body, info, args, in_specs, outs, out_specs, grid=(1,), scratch=(), flops=0, exps=0, grant=20, cost=0):
    specs = [full(a.shape) if s is None else s for a, s in zip(args, in_specs)]
    ospecs = [full(o.shape) if s is None else s for o, s in zip(outs, out_specs)]
    return pl.pallas_call(
        body,
        out_shape=list(outs),
        grid_spec=pltpu.PrefetchScalarGridSpec(
            num_scalar_prefetch=1,
            grid=grid,
            in_specs=specs,
            out_specs=ospecs,
            scratch_shapes=list(scratch),
        ),
        compiler_params=pltpu.CompilerParams(vmem_limit_bytes=min(grant, 12) << 20),
        cost_estimate=pl.CostEstimate(
            flops=1 + cost * 10**9, bytes_accessed=1, transcendentals=0
        ),
        name=body.__name__ if hasattr(body, "__name__") else body.func.__name__,
    )(info, *args)


def arr(shape, dtype=F32):
    return jax.ShapeDtypeStruct(shape, dtype)


def normed(values):
    centred = values - jnp.mean(values, -1, keepdims=True)
    inverse = lax.rsqrt(jnp.mean(centred * centred, -1, keepdims=True) + EPS)
    return centred * inverse, inverse


def norm_back(grad, scaled, inverse, gain):
    weighted = grad * gain
    first = jnp.mean(weighted, -1, keepdims=True)
    second = jnp.mean(weighted * scaled, -1, keepdims=True)
    return inverse * (weighted - first - scaled * second)


def head_lanes(odd, dtype):
    lane = lax.broadcasted_iota(jnp.int32, (1, PAIR), 1)
    return ((lane // HD) == odd).astype(dtype)


def norm_project(info, hid, gain, bias, wq, wk, wv, a1, q, k, v):
    scaled, _ = normed(hid[...].astype(F32))
    low = (scaled * gain[...] + bias[...]).astype(BF)
    a1[...] = low
    q[...] = (dot(low, wq[...]) * SCALE).astype(BF)
    k[...] = dot(low, wk[...]).astype(BF)
    v[...] = dot(low, wv[...]).astype(BF)


def text_project(info, text, wk, wv, k, v):
    k[...] = dot(text[...], wk[...]).astype(BF)
    v[...] = dot(text[...], wv[...]).astype(BF)


def blocks_of(rows, step=256):
    return [(s, min(step, rows - s)) for s in range(0, rows, step)]


def causal(scores):
    key = lax.broadcasted_iota(jnp.int32, scores.shape, 0)
    query = lax.broadcasted_iota(jnp.int32, scores.shape, 1)
    return jnp.where(key <= query, scores, NEG)


def self_forward(info, q, k, v, keep, send, total, mixed):
    rows = q.shape[0]
    half = rows // 2
    odd = lax.rem(pl.program_id(0), 2)
    lanes = head_lanes(odd, BF)
    lanes_on = head_lanes(odd, F32) > 0
    for start, size in blocks_of(rows):
        here = slice(start, start + size)
        query = q[here, :] * lanes
        near = causal(against(k[here, :], query))
        top = jnp.max(near, 0, keepdims=True)
        if start:
            far = against(k[:start, :], query)
            top = jnp.maximum(top, jnp.max(far, 0, keepdims=True))
        near = jnp.exp(near - top)
        count = jnp.sum(near, 0, keepdims=True)
        if start:
            far = jnp.exp(far - top)
            count = count + jnp.sum(far, 0, keepdims=True)
        scale = 1.0 / count
        out = over_rows(v[here, :], (near * scale).astype(BF))
        if start:
            out = out + over_rows(v[:start, :], (far * scale).astype(BF))
        total[0, :, here] = top + jnp.log(count)
        mixed[here, :] = jnp.where(lanes_on, out.T, mixed[here, :])

    @pl.when(odd == 1)
    def _():
        keep[...] = mixed[pl.ds(pl.multiple_of(info[CORE] * half, 8), half), :]
        send[...] = mixed[pl.ds(pl.multiple_of(info[PEER] * half, 8), half), :]


def prepare(info, so, co, cq, own, first):
    own[0:256, :] = so[...].astype(F32)
    own[256:512, :] = co[...].astype(F32)
    own[512:768, :] = cq[...].astype(F32).T
    first[0:128, :] = own[pl.ds(pl.multiple_of(info[Y] * 128, 8), 128), :]
    for i in range(2):
        at = pl.multiple_of(256 + i * 256 + info[LABEL] * 64, 8)
        first[128 + i * 64 : 192 + i * 64, :] = own[pl.ds(at, 64), :]


def mix(info, one, two, w_one, w_two, out):
    out[...] = dot(one[...].astype(BF), w_one[...].astype(BF)) + dot(
        two[...].astype(BF), w_two[...].astype(BF)
    )


def gather_halves(info, far, weights):
    for s in range(2):
        for p in range(2):

            @pl.when(info[Y] == p)
            def _(s=s, p=p):
                weights[s * 256 + p * 128 : s * 256 + p * 128 + 128, :] = far[2 * s][
                    :128, :
                ].astype(BF)

            @pl.when(info[Y] != p)
            def _(s=s, p=p):
                weights[s * 256 + p * 128 : s * 256 + p * 128 + 128, :] = far[2 * s + 1][
                    :128, :
                ].astype(BF)


def gather_quarters(info, far, weights, first):
    for s in range(2):
        over_x, over_y, over_z = far[3 * s : 3 * s + 3]
        pieces = (
            over_x[128 + first : 192 + first, :],
            over_y[128 + first : 192 + first, :],
            over_z[:64, :],
            over_z[64:, :],
        )
        for j, piece in enumerate(pieces):
            at = pl.multiple_of(s * 256 + (info[LABEL] ^ j) * 64, 64)
            weights[pl.ds(at, 64), :] = piece.astype(BF)


def mix_far(info, pre, one, two, far, weights, which):
    if which is None:
        gather_halves(info, far, weights)
    else:
        gather_quarters(info, far, weights, which)
    far_part = dot(one[...].astype(BF), weights[:256, :]) + dot(
        two[...].astype(BF), weights[256:, :]
    )
    return pre[...] + far_part


def mix_norm(which, info, base, pre, one, two, *refs):
    n = 7 if which is None else 5
    far, (gain, bias, resid, low, *packs, weights) = refs[:-n], refs[-n:]
    for i, pack in enumerate(packs):
        for j in range(2):
            pack[j * 64 : j * 64 + 64, :] = far[2 + j][128 + i * 64 : 192 + i * 64, :]
    part = mix_far(info, pre, one, two, far, weights, which)
    total = base[...].astype(F32) + part
    resid[...] = total
    scaled, _ = normed(total)
    low[...] = scaled * gain[...] + bias[...]


def mix_norm_back(info, pre, one, two, *refs):
    far, (gain, resid, e_in, e_out, grads, weights) = refs[:-6], refs[-6:]
    grad = mix_far(info, pre, one, two, far, weights, 64)
    scaled, inverse = normed(resid[...])
    e_out[...] = e_in[...] + norm_back(grad, scaled, inverse, gain[...])
    grads[0:1, :] = jnp.sum(grad * scaled, 0, keepdims=True) * 0.5
    grads[1:2, :] = jnp.sum(grad, 0, keepdims=True) * 0.5


def sum_norm_back(info, mine, far, gain, resid, e_in, e_out, grads):
    grad = mine[...] + far[...]
    scaled, inverse = normed(resid[...])
    e_out[...] = e_in[...].astype(F32) + norm_back(grad, scaled, inverse, gain[...])
    grads[0:1, :] = jnp.sum(grad * scaled, 0, keepdims=True) * 0.5
    grads[1:2, :] = jnp.sum(grad, 0, keepdims=True) * 0.5


def sum_first_grads(info, mine, recv, hid, out, grads):
    grad = mine[...] + recv[...]
    out[...] = grad
    scaled, _ = normed(hid[...].astype(F32))
    grads[0:1, :] = jnp.sum(grad * scaled, 0, keepdims=True)
    grads[1:2, :] = jnp.sum(grad, 0, keepdims=True)


def last_norm_back(info, mine, far, gain, hid, e_in, out):
    grad = mine[...] + far[...]
    scaled, inverse = normed(hid[...].astype(F32))
    out[...] = e_in[...] + norm_back(grad, scaled, inverse, gain[...])


def cross_forward(info, length, a2, wq, k, v, q, mixed, total):
    query_rows = (dot(a2[...].astype(BF), wq[...]) * SCALE).astype(BF)
    q[...] = query_rows
    for pair in range(2):
        cols = slice(pair * PAIR, (pair + 1) * PAIR)
        pair_out = None
        for odd in range(2):
            query = query_rows[:, cols] * head_lanes(odd, BF)
            scores = against(k[:, cols], query)
            slot = lax.broadcasted_iota(jnp.int32, scores.shape, 0)
            scores = jnp.where(slot < length[0], scores, NEG)
            top = jnp.max(scores, 0, keepdims=True)
            scores = jnp.exp(scores - top)
            count = jnp.sum(scores, 0, keepdims=True)
            out = over_rows(v[:, cols], (scores * (1.0 / count)).astype(BF)).T
            total[pair * 2 + odd] = top + jnp.log(count)
            pair_out = out if odd == 0 else jnp.where(head_lanes(1, F32) > 0, out, pair_out)
        mixed[:, cols] = pair_out


def feed_forward(info, a3, cot, up, down, g, du, da3):
    n = pl.program_id(0)
    u = dot(a3[...].astype(BF), up[...])
    cdf = 0.5 + 0.5 * lax.erf(u * (0.5**0.5))
    g[...] = (u * cdf).astype(BF)
    slope = cdf + u * jnp.exp(-0.5 * u * u) * (1.0 / (2.0 * np.pi) ** 0.5)
    dg = against(cot[...], down[...]).astype(BF).astype(F32)
    low = (dg * slope).astype(BF)
    du[...] = low
    part = against(low, up[...])

    @pl.when(n == 0)
    def _():
        da3[...] = part

    @pl.when(n > 0)
    def _():
        da3[...] += part


def add_two(info, one, two, out):
    out[...] = one[...] + two[...]


def down_project(info, own, sib, down, out_own, out_sib):
    out_own[...] = dot(own[...], down[...])
    out_sib[...] = dot(sib[...], down[...])


def cross_backward(second, info, length, e1, wo, q, k, v, total, *rest):
    if second:
        dk_in, dv_in, dq, dk_out, dv_out = rest
    else:
        dq, dk_out, dv_out = rest
    mixed_grad = against(e1[...].astype(BF), wo[...]).astype(BF)
    for pair in range(2):
        cols = slice(pair * PAIR, (pair + 1) * PAIR)
        dk = dk_in[:, cols] if second else None
        dv = dv_in[:, cols] if second else None
        pair_dq = None
        for odd in range(2):
            lanes = head_lanes(odd, BF)
            query = q[:, cols] * lanes
            grad = mixed_grad[:, cols] * lanes
            scores = against(k[:, cols], query)
            slot = lax.broadcasted_iota(jnp.int32, scores.shape, 0)
            scores = jnp.where(slot < length[0], scores, NEG)
            probs = jnp.exp(scores - total[pair * 2 + odd])
            prob_grad = against(v[:, cols], grad)
            part = dot(probs.astype(BF), grad)
            dv = part if dv is None else dv + part
            delta = jnp.sum(probs * prob_grad, 0, keepdims=True)
            low = (probs * (prob_grad - delta)).astype(BF)
            part = dot(low, query)
            dk = part if dk is None else dk + part
            out = over_rows(k[:, cols], low).T
            pair_dq = out if odd == 0 else jnp.where(head_lanes(1, F32) > 0, out, pair_dq)
        dq[:, cols] = pair_dq * SCALE
        dk_out[:, cols] = dk.astype(dk_out.dtype)
        dv_out[:, cols] = dv.astype(dv_out.dtype)


def text_back(info, dk, dv, wk, wv, own, send, scratch):
    half = own.shape[0]
    scratch[...] = against(dk[...], wk[...]) + against(dv[...], wv[...])
    own[...] = scratch[pl.ds(pl.multiple_of(info[CORE] * half, 8), half), :]
    send[...] = scratch[pl.ds(pl.multiple_of(info[PEER] * half, 8), half), :]


def mixed_back(info, own, sib, wo, out):
    half = own.shape[0]
    out[pl.ds(pl.multiple_of(info[CORE] * half, 16), half), :] = against(
        own[...].astype(BF), wo[...]
    ).astype(BF)
    out[pl.ds(pl.multiple_of(info[PEER] * half, 16), half), :] = against(
        sib[...].astype(BF), wo[...]
    ).astype(BF)


def self_backward(info, q, k, v, grad_in, total, dq, dk, dv, dq_sum, dk_sum, dv_sum):
    rows = q.shape[0]
    odd = lax.rem(pl.program_id(0), 2)
    lanes = head_lanes(odd, BF)
    lanes_on = head_lanes(odd, F32) > 0

    @pl.when(odd == 0)
    def _():
        dk_sum[...] = jnp.zeros_like(dk_sum)
        dv_sum[...] = jnp.zeros_like(dv_sum)

    for start, size in blocks_of(rows):
        here = slice(start, start + size)
        query = q[here, :] * lanes
        grad = grad_in[here, :] * lanes
        level = total[0, :, here]
        near = jnp.exp(causal(against(k[here, :], query)) - level)
        near_grad = against(v[here, :], grad)
        delta = jnp.sum(near * near_grad, 0, keepdims=True)
        dv_sum[here, :] += dot(near.astype(BF), grad)
        if start:
            far = jnp.exp(against(k[:start, :], query) - level)
            far_grad = against(v[:start, :], grad)
            delta = delta + jnp.sum(far * far_grad, 0, keepdims=True)
            dv_sum[:start, :] += dot(far.astype(BF), grad)
        near_low = (near * (near_grad - delta)).astype(BF)
        dk_sum[here, :] += dot(near_low, query)
        out = over_rows(k[here, :], near_low)
        if start:
            far_low = (far * (far_grad - delta)).astype(BF)
            dk_sum[:start, :] += dot(far_low, query)
            out = out + over_rows(k[:start, :], far_low)
        dq_sum[here, :] = jnp.where(lanes_on, out.T * SCALE, dq_sum[here, :])

    @pl.when(odd == 1)
    def _():
        dq[...] = dq_sum[...].astype(BF)
        dk[...] = dk_sum[...].astype(BF)
        dv[...] = dv_sum[...].astype(BF)


def first_back(info, dq, dk, dv, wq, wk, wv, own, send):
    half = own.shape[0]
    for at, out in ((PEER, send), (CORE, own)):
        here = pl.ds(pl.multiple_of(info[at] * half, 16), half)
        out[...] = (
            against(dq[here, :], wq[...])
            + against(dk[here, :], wk[...])
            + against(dv[here, :], wv[...])
        )


def weight_grad(plan, shapes, n_v, info, *refs):
    at = 0
    groups = []
    for n_left, n_right in shapes:
        groups.append((refs[at : at + n_left], refs[at + n_left : at + n_left + n_right]))
        at += n_left + n_right
    vectors = refs[at : at + n_v]
    outs = refs[at + n_v : at + n_v + 2 * len(plan)]
    lhs, rhs = refs[-2:]
    for g, (lefts, rights) in enumerate(groups):
        row = 0
        per = len(rights) // len(lefts)
        for i, left in enumerate(lefts):
            rows = left.shape[0]
            for j in range(8):
                block = left[:, pl.ds(pl.multiple_of(info[TABLE + j] * 128, 128), 128)]
                lhs[row : row + rows, j * 128 : (j + 1) * 128] = block.astype(BF)
            col = 0
            for right in rights[i * per : (i + 1) * per]:
                rhs[row : row + rows, col : col + right.shape[1]] = right[...].astype(BF)
                col += right.shape[1]
            row += rows
        for s, (order, segments) in enumerate(plan):
            put = 0
            for group, first, width in segments:
                if group == g:
                    for half in range(2):
                        value = over_rows(
                            lhs[:row, half * 512 : half * 512 + 512],
                            rhs[:row, first : first + width],
                        )
                        for q in range(4):
                            j = half * 4 + q
                            sent, pos = spot(order, j)
                            outs[2 * s + sent][pos, :128, put : put + width] = value[
                                q * 128 : (q + 1) * 128, :
                            ]
                put += width
    if n_v:
        for j in range(8):
            sent, pos = spot(plan[-1][0], j)
            out = outs[2 * len(plan) - 2 + sent]
            out[pos, 128:, :] = jnp.zeros((8, out.shape[2]), F32)
            for i, ref in enumerate(vectors):
                block = ref[:, pl.ds(pl.multiple_of(info[TABLE + j] * 128, 128), 128)]
                out[pos, 128 + 2 * i : 130 + 2 * i, :128] = block


def spot(order, j):
    bits = [(j // WEIGHT[name]) & 1 for name in order]
    return bits[0], bits[1] * 2 + bits[2]


def weight_grads(info, groups, plan, vectors=()):
    args, specs, shapes = [], [], []
    for lefts, rights in groups:
        flat = [r for group in rights for r in group]
        for left in lefts:
            array, spec = left if isinstance(left, tuple) else (left, None)
            args.append(array)
            specs.append(spec)
        args += flat
        specs += [None] * len(flat)
        shapes.append((len(lefts), len(flat)))
    args += vectors
    specs += [None] * len(vectors)
    outs = []
    for s, (order, segments) in enumerate(plan):
        tall = 136 if vectors and s == len(plan) - 1 else 128
        outs += [arr((4, tall, sum(w for _, _, w in segments)))] * 2
    rows = max(sum(group[0].shape[0] for group in rights) for _, rights in groups)
    wide = max(sum(r.shape[1] for r in rights[0]) for _, rights in groups)
    return launch(
        functools.partial(weight_grad, plan, tuple(shapes), len(vectors)),
        info,
        tuple(args),
        specs,
        outs,
        [None] * len(outs),
        scratch=[pltpu.VMEM((rows, 1024), BF), pltpu.VMEM((rows, wide), BF)],
        grant=40,
    )


def scatter_sum(keep, send):
    value = jnp.concatenate([keep, send])
    value = value.reshape(-1, value.shape[-1])
    return lax.psum_scatter(value, "dp", scatter_dimension=0, tiled=True)


def fold(info, *refs):
    for i in range(2):
        keep, got = refs[2 * i : 2 * i + 2]
        keep_out, send_out = refs[4 + 2 * i : 6 + 2 * i]
        n = keep_out.shape[0]
        keep_out[...] = keep[:n] + got[:n]
        send_out[...] = keep[n:] + got[n:]


def fold_one(info, keep, got, keep_out, send_out):
    keep_out[...] = keep[0] + got[0]
    send_out[...] = keep[1] + got[1]


def fold_last(info, *refs):
    keep_out, send_out = refs[4:]
    col = 0
    for i in range(2):
        keep, got = refs[2 * i : 2 * i + 2]
        rows, wide = keep.shape[1:]
        keep_out[:rows, col : col + wide] = keep[0] + got[0]
        send_out[:rows, col : col + wide] = keep[1] + got[1]
        col += wide


def finish_ffn(info, keep, got, up, down):
    wide = up.shape[1]
    up[...] = keep[:, :wide] + got[:, :wide]
    down[...] = (keep[:, wide:] + got[:, wide:]).T


def finish_cross(info, keep, got, co, ck, cv, cq):
    co[...] = (keep[:, :256] + got[:, :256]).T
    for i, out in enumerate((ck, cv, cq)):
        here = slice(256 * i + 256, 256 * i + 512)
        out[...] = keep[:, here] + got[:, here]


def finish_self(info, keep, got, so, sk, sq, sv, vectors):
    so[...] = (keep[:128, :256] + got[:128, :256]).T
    for i, out in enumerate((sk, sq, sv)):
        here = slice(256 * i + 256, 256 * i + 512)
        out[...] = keep[:128, here] + got[:128, here]
    vectors[...] = keep[128:, 512:640] + got[128:, 512:640]


FINISH = {
    finish_ffn: [(128, 1024), (1024, 128)],
    finish_cross: [(256, 128), (128, 256), (128, 256), (128, 256)],
    finish_self: [(256, 128), (128, 256), (128, 256), (128, 256), (8, 128)],
}


def exchange(streams, orders, step, first=None, cost=10):
    args = []
    for (keep, send), order in zip(streams, orders):
        got = swap(send, "dp", 8, FLIPS[order[step]])
        args += [keep, got if first is None else after(got, first)]
    none = jnp.zeros((1,), jnp.int32)
    if step == 1:
        shape = (max(a.shape[1] for a in args), args[0].shape[2] + args[2].shape[2])
        return launch(
            fold_last, none, args, [None] * 4, [arr(shape)] * 2, [None] * 2, cost=cost
        )
    outs = []
    for keep, _ in streams:
        outs += [arr((keep.shape[0] // 2, *keep.shape[1:]))] * 2
    out = launch(fold, none, args, [None] * 4, outs, [None] * 4, cost=cost)
    return list(zip(out[0::2], out[1::2]))


def fold_stream(pair, name, first, cost=0):
    keep, send = pair
    got = after(swap(send, "dp", 8, FLIPS[name]), first)
    none = jnp.zeros((1,), jnp.int32)
    outs = [arr(keep.shape[1:])] * 2
    return launch(fold_one, none, (keep, got), [None] * 2, outs, [None] * 2, cost=cost)


def finish(pair, body, first=None, cost=10):
    keep, send = pair
    got = swap(send, "dp", 8, FLIPS["m"])
    got = got if first is None else after(got, first)
    outs = [arr(shape) for shape in FINISH[body]]
    none = jnp.zeros((1,), jnp.int32)
    return launch(body, none, (keep, got), [None] * 2, outs, [None] * len(outs), cost=cost)


def sent(streams):
    return [s for _, s in streams]


def out_second(info, own, got, text_own, text_got, out):
    half = own.shape[0]
    out[:half, :] = own[...] + got[...]
    out[half:, :] = text_own[...] + text_got[...]


def out_sum(info, resid, mine, far, out):
    half = resid.shape[0]
    out[:half, :] = resid[...] + (mine[:half, :] + far[:half, :])
    out[half:, :] = mine[half:, :] + far[half:, :]


def out_place(info, own, sib, out, text_out):
    half = out.shape[0] // 2
    text_half = text_out.shape[0] // 2
    for at, ref in ((CORE, own), (PEER, sib)):
        out[pl.ds(pl.multiple_of(info[at] * half, 16), half), :] = ref[:half, :].astype(BF)
        spot = pl.multiple_of(info[at] * text_half, 8)
        text_out[pl.ds(spot, text_half), :] = ref[half:, :]


def place(info, own, sib, out):
    half = out.shape[0] // 2
    for at, ref in ((CORE, own), (PEER, sib)):
        out[pl.ds(pl.multiple_of(info[at] * half, 16), half), :] = ref[...].astype(BF)


def body(
    hidden,
    text_states,
    text_len,
    ln1_gain,
    ln1_bias,
    self_q,
    self_k,
    self_v,
    self_o,
    ln2_gain,
    ln2_bias,
    cross_q,
    cross_k,
    cross_v,
    cross_o,
    ln3_gain,
    ln3_bias,
    ffn_up,
    ffn_down,
    cotangent,
):
    dp_size = lax.axis_size("dp")
    frames, width = hidden.shape[1:]
    text_rows = text_states.shape[1]
    cols = self_q.shape[1]
    inner = ffn_up.shape[1]
    half = frames // 2
    device = lax.axis_index("dp") * 4 + lax.axis_index("tensor")
    table = jnp.asarray(index_table(dp_size))
    info = lax.dynamic_index_in_dim(table, device, 0, keepdims=False)
    hid = hidden.reshape(frames, width)
    cot = cotangent.reshape(frames, width)
    text = text_states.reshape(text_rows, width)
    gain1, bias1 = ln1_gain.reshape(1, width), ln1_bias.reshape(1, width)
    gain2, bias2 = ln2_gain.reshape(1, width), ln2_bias.reshape(1, width)
    gain3, bias3 = ln3_gain.reshape(1, width), ln3_bias.reshape(1, width)
    own_rows = pl.BlockSpec((half, width), lambda i, table: (table[CORE], 0))
    sib_rows = pl.BlockSpec((half, width), lambda i, table: (table[PEER], 0))
    half_mm = 2 * half * width
    whole = dp_size == 8
    orders = ("yam", "aym") if whole else ("may",) * 2
    order_one, order_two = orders

    own3, first = launch(
        prepare,
        info,
        (self_o, cross_o, cross_q),
        [None] * 3,
        [arr((3 * cols, width)), arr((cols, width))],
        [None] * 2,
        flops=1 << 20,
    )
    far_one = cross_swap(first)
    sib3 = core_swap(own3)

    def weight_at(i):
        return pl.BlockSpec((cols, width), lambda *_: (i, 0))

    step = frames // 4
    a1, q1, k1, v1 = launch(
        norm_project,
        info,
        (after(hid, first), gain1, bias1, self_q, self_k, self_v),
        [pl.BlockSpec((step, width), lambda i, _: (i, 0))] + [None] * 5,
        [arr((frames, width), BF)] + [arr((frames, cols), BF)] * 3,
        [pl.BlockSpec((step, width), lambda i, _: (i, 0))]
        + [pl.BlockSpec((step, cols), lambda i, _: (i, 0))] * 3,
        grid=(4,),
        flops=2 * frames * width * cols * 3,
    )
    heads = cols // HD
    pair_in = pl.BlockSpec((frames, PAIR), lambda h, _: (0, h // 2))
    pair_half = pl.BlockSpec((half, PAIR), lambda h, _: (0, h // 2))
    level = pl.BlockSpec((1, 1, frames), lambda h, _: (h, 0, 0))
    o1_own, o1_sib, total1 = launch(
        self_forward,
        info,
        (q1, k1, v1),
        [pair_in] * 3,
        [arr((half, cols))] * 2 + [arr((heads, 1, frames))],
        [pair_half] * 2 + [level],
        grid=(heads,),
        scratch=[pltpu.VMEM((frames, PAIR), F32)],
        flops=heads * frames * frames * 512,
        exps=heads * frames * frames,
    )
    o1_cross = cross_swap(after(o1_sib, far_one))
    o1_core = core_swap(after(o1_sib, sib3))
    o1_x = x_swap(o1_own)
    far_two = swap(after(far_one, o1_own), "dp", dp_size, FLIPS["y"])
    k2, v2 = launch(
        text_project,
        info,
        (after(text, o1_own), cross_k, cross_v),
        [None] * 3,
        [arr((text_rows, cols), BF)] * 2,
        [None] * 2,
        flops=2 * text_rows * width * cols * 2,
    )

    def mixed(one, two, i):
        return launch(
            mix,
            info,
            (one, two, own3, sib3),
            [None] * 2 + [weight_at(i)] * 2,
            [arr((half, width))],
            [None],
            flops=half_mm * 512,
        )[0]

    pre1 = mixed(after(o1_own, k2), o1_core, 0)
    far_one_core = core_swap(after(far_one, o1_core))
    far_two_core = core_swap(after(far_two, o1_x, o1_cross, pre1))
    far_weights = (far_one_core, far_two_core, far_one, far_two)

    def normed_mix(which, base, spec, pre, one, two, weights, gain, bias, packs=0):
        return launch(
            functools.partial(mix_norm, which),
            info,
            (base, pre, one, two, *weights, gain, bias),
            [spec] + [None] * (5 + len(weights)),
            [arr((half, width))] * 2 + [arr((cols // 2, width))] * packs,
            [None] * (2 + packs),
            scratch=[pltpu.VMEM((2 * cols, width), BF)],
            cost=2,
        )

    h1, a2, pack_co, pack_cq = normed_mix(None, hid, own_rows, pre1, o1_x, o1_cross, far_weights, gain2, bias2, 2)
    a2_sib = core_swap(a2)

    smem = pl.BlockSpec(memory_space=pltpu.SMEM)

    def cross(a):
        return launch(
            cross_forward,
            info,
            (text_len, a, cross_q, k2, v2),
            [smem] + [None] * 4,
            [arr((half, cols), BF), arr((half, cols)), arr((heads, 1, half))],
            [None] * 3,
            flops=half_mm * cols + heads * half * text_rows * 512,
            exps=heads * half * text_rows,
        )

    q2_own, o2_own, total2_own = cross(a2)
    o2_x = x_swap(after(o2_own, o1_x))
    q2_sib, o2_sib, total2_sib = cross(after(a2_sib, q2_own))
    o2_cross = cross_swap(after(o2_sib, o1_cross))
    o2_core = core_swap(o2_sib)
    far_co = swap(pack_co, "dp", dp_size, FLIPS["a"])
    far_cq = swap(pack_cq, "dp", dp_size, FLIPS["a"])
    pre2 = mixed(o2_own, o2_core, 1)
    far_co_core = core_swap(after(far_co, o2_x, o2_cross, far_cq, pre2))
    co_weights = (
        *(far_one_core, far_two_core, far_co_core),
        *(far_one, far_two, far_co),
    )
    h2, a3 = normed_mix(0, h1, None, pre2, o2_x, o2_cross, co_weights, gain3, bias3)
    a3_sib = core_swap(a3)
    far_cq_core = core_swap(after(far_cq, a3))

    unit = 256

    def feed(a, rows):
        return launch(
            feed_forward,
            info,
            (a, cot, ffn_up, ffn_down),
            [
                None,
                rows,
                pl.BlockSpec((width, unit), lambda i, _: (0, i)),
                pl.BlockSpec((unit, width), lambda i, _: (i, 0)),
            ],
            [arr((half, inner), BF)] * 2 + [arr((half, width))],
            [pl.BlockSpec((half, unit), lambda i, _: (0, i))] * 2 + [None],
            grid=(inner // unit,),
            flops=half_mm * inner * 3,
            exps=half * inner * 2,
        )

    g_own, du_own, da3_own = feed(a3, own_rows)
    g_sib, du_sib, da3_sib = feed(after(a3_sib, g_own, far_cq_core), sib_rows)
    da3_sum = launch(
        add_two,
        info,
        (da3_own, core_swap(da3_sib)),
        [None] * 2,
        [arr((half, width))],
        [None],
    )[0]
    da3_far = x_swap(after(da3_sum, o2_x))
    ffn_plan = (
        (order_one, ((0, 0, 1024),)),
        (order_two, ((1, 0, 1024),)),
    )
    ffn = weight_grads(
        info,
        [
            ([after(a3, da3_sum), a3_sib], [[du_own], [du_sib]]),
            ([(cot, own_rows), (cot, sib_rows)], [[g_own], [g_sib]]),
        ],
        ffn_plan,
    )
    out_own, out_sib = launch(
        down_project,
        info,
        (after(g_own, *ffn[1::2]), g_sib, ffn_down),
        [None, None, pl.BlockSpec((inner, 512), lambda i, _: (0, i))],
        [arr((half, width))] * 2,
        [pl.BlockSpec((half, 512), lambda i, _: (0, i))] * 2,
        grid=(width // 512,),
        flops=2 * half_mm * inner,
    )
    out_got = core_swap(out_sib)
    e1, grads3 = launch(
        sum_norm_back,
        info,
        (da3_sum, after(da3_far, out_own), gain3, h2, cot),
        [None] * 4 + [own_rows],
        [arr((half, width)), arr((2, width))],
        [None] * 2,
    )
    e1_sib = core_swap(e1)
    def cross_back(e, q, total, sums):
        last = bool(sums)
        return launch(
            functools.partial(cross_backward, last),
            info,
            (text_len, e, cross_o, q, k2, v2, total, *sums),
            [smem] + [None] * (6 + len(sums)),
            [arr((half, cols))] + [arr((text_rows, cols), BF if last else F32)] * 2,
            [None] * 3,
        )

    dq2_own, *sums = cross_back(after(e1, out_got), q2_own, total2_own, ())
    dq2_sib, dk2, dv2 = cross_back(e1_sib, q2_sib, total2_sib, tuple(sums))
    dq2_cross = cross_swap(dq2_sib)
    dq2_core = core_swap(dq2_sib)
    dq2_x = x_swap(after(dq2_own, da3_far))
    pre3 = mixed(dq2_own, dq2_core, 2)
    cq_weights = (
        *(far_one_core, far_two_core, far_cq_core),
        *(far_one, far_two, far_cq),
    )

    text_half = text_rows // 2
    text_own, text_send = launch(
        text_back,
        info,
        (dk2, dv2, cross_k, cross_v),
        [None] * 4,
        [arr((text_half, width))] * 2,
        [None] * 2,
        scratch=[pltpu.VMEM((text_rows, width), F32)],
        flops=2 * text_rows * width * cols * 2,
    )
    text_got = core_swap(text_send)
    out_two = launch(
        out_second,
        info,
        (out_own, out_got, text_own, text_got),
        [None] * 4,
        [arr((half + text_half, width))],
        [None],
    )[0]
    cross_plan = (
        (order_one, ((0, 0, 256), (2, 0, 512))),
        (order_two, ((1, 0, 256),)),
    )
    cross = weight_grads(
        info,
        [
            ([e1, e1_sib], [[o2_own], [o2_sib]]),
            ([a2, a2_sib], [[dq2_own], [dq2_sib]]),
            ([text], [[dk2, dv2]]),
        ],
        cross_plan,
    )
    pins = [out_two]
    if whole:
        ffn = exchange(list(zip(ffn[0::2], ffn[1::2])), orders, 0, cross[0], 12)
        pins += sent(ffn)
    e0, grads2 = launch(
        mix_norm_back,
        info,
        (after(pre3, *pins), dq2_x, dq2_cross, *cq_weights, gain2, h1, e1),
        [None] * (6 + len(cq_weights)),
        [arr((half, width)), arr((2, width))],
        [None] * 2,
        scratch=[pltpu.VMEM((2 * cols, width), BF)],
        cost=0,
    )
    out_far_two = x_swap(after(out_two, dq2_x))
    e0_sib = core_swap(e0)
    do1 = launch(
        mixed_back,
        info,
        (e0, e0_sib, self_o),
        [None] * 3,
        [arr((frames, cols), BF)],
        [None],
    )[0]
    dq1, dk1, dv1 = launch(
        self_backward,
        info,
        (q1, k1, v1, do1, total1),
        [pair_in] * 4 + [level],
        [arr((frames, cols), BF)] * 3,
        [pair_in] * 3,
        grid=(heads,),
        scratch=[pltpu.VMEM((frames, PAIR), F32)] * 3,
        flops=heads * frames * frames * 256 * 5,
        exps=heads * frames * frames,
    )
    da1_own, da1_send = launch(
        first_back,
        info,
        (dq1, dk1, dv1, self_q, self_k, self_v),
        [None] * 6,
        [arr((half, width))] * 2,
        [None] * 2,
        flops=2 * half_mm * 3 * cols,
    )
    pins = []
    if whole:
        ffn = exchange(ffn, orders, 1, da1_own, 4)
        pins = [ffn[1]]
        cross = [(k, after(c, ffn[1])) for k, c in zip(cross[0::2], cross[1::2])]
    da1_sum, grads1 = launch(
        sum_first_grads,
        info,
        (da1_own, after(core_swap(da1_send), *pins), hid),
        [None] * 2 + [own_rows],
        [arr((half, width)), arr((2, width))],
        [None] * 2,
    )

    vectors = (grads1, grads2, grads3)
    if not whole:
        stacked = lax.psum(jnp.concatenate(vectors), "tensor")
        stacked = lax.psum_scatter(stacked, "dp", scatter_dimension=1, tiled=True)
        vectors = ()
    self_plan = (
        (order_one, ((0, 0, 256), (1, 256, 256))),
        (order_two, ((1, 0, 256), (1, 512, 256))),
    )
    own = weight_grads(
        info,
        [
            ([after(e0, da1_sum), e0_sib], [[o1_own], [o1_sib]]),
            ([a1], [[dq1, dk1, dv1]]),
        ],
        self_plan,
        vectors,
    )
    pins = [own[0]]
    if whole:
        own = list(zip(own[0::2], own[1::2]))
    out_final = launch(
        out_sum,
        info,
        (h2, out_two, after(out_far_two, *pins)),
        [None] * 3,
        [arr((half + text_half, width))],
        [None],
        cost=0,
    )[0]
    da1_far = x_swap(after(da1_sum, out_final))
    output, text_grad = launch(
        out_place,
        info,
        (out_final, core_swap(out_final)),
        [None] * 2,
        [arr((frames, width), BF), arr((text_rows, width))],
        [None] * 2,
    )
    pins = []
    if not whole:
        ffn, cross, own = (
            [scatter_sum(*p) for p in zip(g[0::2], g[1::2])] for g in (ffn, cross, own)
        )
        up_grad, down_grad = ffn[0], ffn[1].T
        co_grad, cq_grad = cross[0][:, :256].T, cross[1]
        ck_grad, cv_grad = cross[0][:, 256:512], cross[0][:, 512:]
        so_grad, sk_grad = own[0][:, :256].T, own[0][:, 256:]
        sq_grad, sv_grad = own[1][:, :256], own[1][:, 256:]
    if whole:
        cross = exchange(cross, orders, 0, own[0][0], 0)
        own = [(k, after(c, cross[0][1])) for k, c in own]
        up_grad, down_grad = finish(ffn, finish_ffn, cross[0][0], 1)
        cross = exchange(cross, orders, 1, up_grad, 8)
        pins = [cross[1]]
    last = launch(
        last_norm_back,
        info,
        (da1_sum, after(da1_far, *pins), gain1, hid, e0),
        [None] * 3 + [own_rows, None],
        [arr((half, width))],
        [None],
        flops=half_mm * 8,
    )[0]
    if whole:
        own = exchange(own, orders, 0, last)
        cross = (cross[0], after(cross[1], up_grad))
        co_grad, ck_grad, cv_grad, cq_grad = finish(cross, finish_cross, last)
        own = exchange(own, orders, 1, co_grad)
        so_grad, sk_grad, sq_grad, sv_grad, stacked = finish(own, finish_self)
    hidden_grad = launch(
        place,
        info,
        (last, core_swap(last)),
        [None] * 2,
        [arr((frames, width), BF)],
        [None],
    )[0]
    if whole:
        stacked = stacked + x_swap(after(stacked, da1_far))
        stacked = stacked + core_swap(stacked)
    return (
        output.reshape(hidden.shape),
        hidden_grad.reshape(hidden.shape),
        text_grad.reshape(text_states.shape),
        stacked[0],
        stacked[1],
        sq_grad,
        sk_grad,
        sv_grad,
        so_grad,
        stacked[2],
        stacked[3],
        cq_grad,
        ck_grad,
        cv_grad,
        co_grad,
        stacked[4],
        stacked[5],
        up_grad,
        down_grad,
    )


def solution(mesh):
    rows = P("dp", None, None)
    column, row = P(None, "tensor"), P("tensor", None)
    in_specs = (
        *(rows, rows, P("dp"), P(), P(), column, column, column, row),
        *(P(), P(), column, column, column, row),
        *(P(), P(), column, row, rows),
    )
    vector, down, across = P("dp"), P("dp", "tensor"), P("tensor", "dp")
    out_specs = (
        *(rows, rows, rows, vector, vector, down, down, down, across),
        *(vector, vector, down, down, down, across),
        *(vector, vector, down, across),
    )
    return jax.shard_map(body, mesh=mesh, in_specs=in_specs, out_specs=out_specs, check_vma=False)
```

```python
import functools

import jax
import jax.numpy as jnp
import numpy as np
from jax import lax
from jax.experimental import pallas as pl
from jax.experimental.pallas import tpu as pltpu
from jax.sharding import PartitionSpec as P

HD = 64
EPS = 1e-05
NEG = -1e30
SCALE = HD ** (-0.5)
BF = jnp.bfloat16
F32 = jnp.float32
PAIR = 2 * HD

FLIPS = WEIGHT = {"y": 1, "a": 2, "m": 4}

CORE, PEER, Y, LABEL, TABLE = 0, 1, 2, 3, 8


def index_table(dp_size):
    rows = []
    for me in range(dp_size):
        for t in range(4):
            row = [t & 1, 1 - (t & 1), me & 1, me & 3, 0, 0, 0, 0]
            row += [(me ^ i) if dp_size == 8 else i for i in range(8)]
            rows.append(row)
    return np.array(rows, np.int32)


def dot(left, right):
    return lax.dot_general(left, right, (((1,), (0,)), ((), ())), preferred_element_type=F32)


def against(left, right):
    return lax.dot_general(left, right, (((1,), (1,)), ((), ())), preferred_element_type=F32)


def over_rows(left, right):
    return lax.dot_general(left, right, (((0,), (0,)), ((), ())), preferred_element_type=F32)


def swap(value, axis, size, flip):
    return lax.ppermute(value, axis, [(i, i ^ flip) for i in range(size)])


def core_swap(value):
    return swap(value, "tensor", 4, 1)


def x_swap(value):
    return swap(value, "tensor", 4, 2)


def cross_swap(value):
    return swap(value, "tensor", 4, 3)


def after(value, *others):
    return lax.optimization_barrier((value, *others))[0]


def full(shape):
    return pl.BlockSpec(shape, lambda *_: (0,) * len(shape))


def launch(body, info, args, in_specs, outs, out_specs, grid=(1,), scratch=(), flops=0, exps=0, grant=20, cost=0):
    specs = [full(a.shape) if s is None else s for a, s in zip(args, in_specs)]
    ospecs = [full(o.shape) if s is None else s for o, s in zip(outs, out_specs)]
    return pl.pallas_call(
        body,
        out_shape=list(outs),
        grid_spec=pltpu.PrefetchScalarGridSpec(
            num_scalar_prefetch=1,
            grid=grid,
            in_specs=specs,
            out_specs=ospecs,
            scratch_shapes=list(scratch),
        ),
        compiler_params=pltpu.CompilerParams(vmem_limit_bytes=min(grant, 12) << 20),
        cost_estimate=pl.CostEstimate(
            flops=1 + cost * 10**9, bytes_accessed=1, transcendentals=0
        ),
        name=body.__name__ if hasattr(body, "__name__") else body.func.__name__,
    )(info, *args)


def arr(shape, dtype=F32):
    return jax.ShapeDtypeStruct(shape, dtype)


def normed(values):
    centred = values - jnp.mean(values, -1, keepdims=True)
    inverse = lax.rsqrt(jnp.mean(centred * centred, -1, keepdims=True) + EPS)
    return centred * inverse, inverse


def norm_back(grad, scaled, inverse, gain):
    weighted = grad * gain
    first = jnp.mean(weighted, -1, keepdims=True)
    second = jnp.mean(weighted * scaled, -1, keepdims=True)
    return inverse * (weighted - first - scaled * second)


def head_lanes(odd, dtype):
    lane = lax.broadcasted_iota(jnp.int32, (1, PAIR), 1)
    return ((lane // HD) == odd).astype(dtype)


def norm_project(info, hid, gain, bias, wq, wk, wv, a1, q, k, v):
    scaled, _ = normed(hid[...].astype(F32))
    low = (scaled * gain[...] + bias[...]).astype(BF)
    a1[...] = low
    q[...] = (dot(low, wq[...]) * SCALE).astype(BF)
    k[...] = dot(low, wk[...]).astype(BF)
    v[...] = dot(low, wv[...]).astype(BF)


def text_project(info, text, wk, wv, k, v):
    k[...] = dot(text[...], wk[...]).astype(BF)
    v[...] = dot(text[...], wv[...]).astype(BF)


def blocks_of(rows, step=256):
    return [(s, min(step, rows - s)) for s in range(0, rows, step)]


def causal(scores):
    key = lax.broadcasted_iota(jnp.int32, scores.shape, 0)
    query = lax.broadcasted_iota(jnp.int32, scores.shape, 1)
    return jnp.where(key <= query, scores, NEG)


def self_forward(info, q, k, v, keep, send, total, mixed):
    rows = q.shape[0]
    half = rows // 2
    odd = lax.rem(pl.program_id(0), 2)
    lanes = head_lanes(odd, BF)
    lanes_on = head_lanes(odd, F32) > 0
    for start, size in blocks_of(rows):
        here = slice(start, start + size)
        query = q[here, :] * lanes
        near = causal(against(k[here, :], query))
        top = jnp.max(near, 0, keepdims=True)
        if start:
            far = against(k[:start, :], query)
            top = jnp.maximum(top, jnp.max(far, 0, keepdims=True))
        near = jnp.exp(near - top)
        count = jnp.sum(near, 0, keepdims=True)
        if start:
            far = jnp.exp(far - top)
            count = count + jnp.sum(far, 0, keepdims=True)
        scale = 1.0 / count
        out = over_rows(v[here, :], (near * scale).astype(BF))
        if start:
            out = out + over_rows(v[:start, :], (far * scale).astype(BF))
        total[0, :, here] = top + jnp.log(count)
        mixed[here, :] = jnp.where(lanes_on, out.T, mixed[here, :])

    @pl.when(odd == 1)
    def _():
        keep[...] = mixed[pl.ds(pl.multiple_of(info[CORE] * half, 8), half), :]
        send[...] = mixed[pl.ds(pl.multiple_of(info[PEER] * half, 8), half), :]


def prepare(info, so, co, cq, own, first):
    own[0:256, :] = so[...].astype(F32)
    own[256:512, :] = co[...].astype(F32)
    own[512:768, :] = cq[...].astype(F32).T
    first[0:128, :] = own[pl.ds(pl.multiple_of(info[Y] * 128, 8), 128), :]
    for i in range(2):
        at = pl.multiple_of(256 + i * 256 + info[LABEL] * 64, 8)
        first[128 + i * 64 : 192 + i * 64, :] = own[pl.ds(at, 64), :]


def mix(info, one, two, w_one, w_two, out):
    out[...] = dot(one[...].astype(BF), w_one[...].astype(BF)) + dot(
        two[...].astype(BF), w_two[...].astype(BF)
    )


def gather_halves(info, far, weights):
    for s in range(2):
        for p in range(2):

            @pl.when(info[Y] == p)
            def _(s=s, p=p):
                weights[s * 256 + p * 128 : s * 256 + p * 128 + 128, :] = far[2 * s][
                    :128, :
                ].astype(BF)

            @pl.when(info[Y] != p)
            def _(s=s, p=p):
                weights[s * 256 + p * 128 : s * 256 + p * 128 + 128, :] = far[2 * s + 1][
                    :128, :
                ].astype(BF)


def gather_quarters(info, far, weights, first):
    for s in range(2):
        over_x, over_y, over_z = far[3 * s : 3 * s + 3]
        pieces = (
            over_x[128 + first : 192 + first, :],
            over_y[128 + first : 192 + first, :],
            over_z[:64, :],
            over_z[64:, :],
        )
        for j, piece in enumerate(pieces):
            at = pl.multiple_of(s * 256 + (info[LABEL] ^ j) * 64, 64)
            weights[pl.ds(at, 64), :] = piece.astype(BF)


def mix_far(info, pre, one, two, far, weights, which):
    if which is None:
        gather_halves(info, far, weights)
    else:
        gather_quarters(info, far, weights, which)
    far_part = dot(one[...].astype(BF), weights[:256, :]) + dot(
        two[...].astype(BF), weights[256:, :]
    )
    return pre[...] + far_part


def mix_norm(which, info, base, pre, one, two, *refs):
    n = 7 if which is None else 5
    far, (gain, bias, resid, low, *packs, weights) = refs[:-n], refs[-n:]
    for i, pack in enumerate(packs):
        for j in range(2):
            pack[j * 64 : j * 64 + 64, :] = far[2 + j][128 + i * 64 : 192 + i * 64, :]
    part = mix_far(info, pre, one, two, far, weights, which)
    total = base[...].astype(F32) + part
    resid[...] = total
    scaled, _ = normed(total)
    low[...] = scaled * gain[...] + bias[...]


def mix_norm_back(info, pre, one, two, *refs):
    far, (gain, resid, e_in, e_out, grads, weights) = refs[:-6], refs[-6:]
    grad = mix_far(info, pre, one, two, far, weights, 64)
    scaled, inverse = normed(resid[...])
    e_out[...] = e_in[...] + norm_back(grad, scaled, inverse, gain[...])
    grads[0:1, :] = jnp.sum(grad * scaled, 0, keepdims=True) * 0.5
    grads[1:2, :] = jnp.sum(grad, 0, keepdims=True) * 0.5


def sum_norm_back(info, mine, far, gain, resid, e_in, e_out, grads):
    grad = mine[...] + far[...]
    scaled, inverse = normed(resid[...])
    e_out[...] = e_in[...].astype(F32) + norm_back(grad, scaled, inverse, gain[...])
    grads[0:1, :] = jnp.sum(grad * scaled, 0, keepdims=True) * 0.5
    grads[1:2, :] = jnp.sum(grad, 0, keepdims=True) * 0.5


def sum_first_grads(info, mine, recv, hid, out, grads):
    grad = mine[...] + recv[...]
    out[...] = grad
    scaled, _ = normed(hid[...].astype(F32))
    grads[0:1, :] = jnp.sum(grad * scaled, 0, keepdims=True)
    grads[1:2, :] = jnp.sum(grad, 0, keepdims=True)


def last_norm_back(info, mine, far, gain, hid, e_in, out):
    grad = mine[...] + far[...]
    scaled, inverse = normed(hid[...].astype(F32))
    out[...] = e_in[...] + norm_back(grad, scaled, inverse, gain[...])


def cross_forward(info, length, a2, wq, k, v, q, mixed, total):
    query_rows = (dot(a2[...].astype(BF), wq[...]) * SCALE).astype(BF)
    q[...] = query_rows
    for pair in range(2):
        cols = slice(pair * PAIR, (pair + 1) * PAIR)
        pair_out = None
        for odd in range(2):
            query = query_rows[:, cols] * head_lanes(odd, BF)
            scores = against(k[:, cols], query)
            slot = lax.broadcasted_iota(jnp.int32, scores.shape, 0)
            scores = jnp.where(slot < length[0], scores, NEG)
            top = jnp.max(scores, 0, keepdims=True)
            scores = jnp.exp(scores - top)
            count = jnp.sum(scores, 0, keepdims=True)
            out = over_rows(v[:, cols], (scores * (1.0 / count)).astype(BF)).T
            total[pair * 2 + odd] = top + jnp.log(count)
            pair_out = out if odd == 0 else jnp.where(head_lanes(1, F32) > 0, out, pair_out)
        mixed[:, cols] = pair_out


def feed_forward(info, a3, cot, up, down, g, du, da3):
    n = pl.program_id(0)
    u = dot(a3[...].astype(BF), up[...])
    cdf = 0.5 + 0.5 * lax.erf(u * (0.5**0.5))
    g[...] = (u * cdf).astype(BF)
    slope = cdf + u * jnp.exp(-0.5 * u * u) * (1.0 / (2.0 * np.pi) ** 0.5)
    dg = against(cot[...], down[...]).astype(BF).astype(F32)
    low = (dg * slope).astype(BF)
    du[...] = low
    part = against(low, up[...])

    @pl.when(n == 0)
    def _():
        da3[...] = part

    @pl.when(n > 0)
    def _():
        da3[...] += part


def add_two(info, one, two, out):
    out[...] = one[...] + two[...]


def down_project(info, own, sib, down, out_own, out_sib):
    out_own[...] = dot(own[...], down[...])
    out_sib[...] = dot(sib[...], down[...])


def cross_backward(second, info, length, e1, wo, q, k, v, total, *rest):
    if second:
        dk_in, dv_in, dq, dk_out, dv_out = rest
    else:
        dq, dk_out, dv_out = rest
    mixed_grad = against(e1[...].astype(BF), wo[...]).astype(BF)
    for pair in range(2):
        cols = slice(pair * PAIR, (pair + 1) * PAIR)
        dk = dk_in[:, cols] if second else None
        dv = dv_in[:, cols] if second else None
        pair_dq = None
        for odd in range(2):
            lanes = head_lanes(odd, BF)
            query = q[:, cols] * lanes
            grad = mixed_grad[:, cols] * lanes
            scores = against(k[:, cols], query)
            slot = lax.broadcasted_iota(jnp.int32, scores.shape, 0)
            scores = jnp.where(slot < length[0], scores, NEG)
            probs = jnp.exp(scores - total[pair * 2 + odd])
            prob_grad = against(v[:, cols], grad)
            part = dot(probs.astype(BF), grad)
            dv = part if dv is None else dv + part
            delta = jnp.sum(probs * prob_grad, 0, keepdims=True)
            low = (probs * (prob_grad - delta)).astype(BF)
            part = dot(low, query)
            dk = part if dk is None else dk + part
            out = over_rows(k[:, cols], low).T
            pair_dq = out if odd == 0 else jnp.where(head_lanes(1, F32) > 0, out, pair_dq)
        dq[:, cols] = pair_dq * SCALE
        dk_out[:, cols] = dk.astype(dk_out.dtype)
        dv_out[:, cols] = dv.astype(dv_out.dtype)


def text_back(info, dk, dv, wk, wv, own, send, scratch):
    half = own.shape[0]
    scratch[...] = against(dk[...], wk[...]) + against(dv[...], wv[...])
    own[...] = scratch[pl.ds(pl.multiple_of(info[CORE] * half, 8), half), :]
    send[...] = scratch[pl.ds(pl.multiple_of(info[PEER] * half, 8), half), :]


def mixed_back(info, own, sib, wo, out):
    half = own.shape[0]
    out[pl.ds(pl.multiple_of(info[CORE] * half, 16), half), :] = against(
        own[...].astype(BF), wo[...]
    ).astype(BF)
    out[pl.ds(pl.multiple_of(info[PEER] * half, 16), half), :] = against(
        sib[...].astype(BF), wo[...]
    ).astype(BF)


def self_backward(info, q, k, v, grad_in, total, dq, dk, dv, dq_sum, dk_sum, dv_sum):
    rows = q.shape[0]
    odd = lax.rem(pl.program_id(0), 2)
    lanes = head_lanes(odd, BF)
    lanes_on = head_lanes(odd, F32) > 0

    @pl.when(odd == 0)
    def _():
        dk_sum[...] = jnp.zeros_like(dk_sum)
        dv_sum[...] = jnp.zeros_like(dv_sum)

    for start, size in blocks_of(rows):
        here = slice(start, start + size)
        query = q[here, :] * lanes
        grad = grad_in[here, :] * lanes
        level = total[0, :, here]
        near = jnp.exp(causal(against(k[here, :], query)) - level)
        near_grad = against(v[here, :], grad)
        delta = jnp.sum(near * near_grad, 0, keepdims=True)
        dv_sum[here, :] += dot(near.astype(BF), grad)
        if start:
            far = jnp.exp(against(k[:start, :], query) - level)
            far_grad = against(v[:start, :], grad)
            delta = delta + jnp.sum(far * far_grad, 0, keepdims=True)
            dv_sum[:start, :] += dot(far.astype(BF), grad)
        near_low = (near * (near_grad - delta)).astype(BF)
        dk_sum[here, :] += dot(near_low, query)
        out = over_rows(k[here, :], near_low)
        if start:
            far_low = (far * (far_grad - delta)).astype(BF)
            dk_sum[:start, :] += dot(far_low, query)
            out = out + over_rows(k[:start, :], far_low)
        dq_sum[here, :] = jnp.where(lanes_on, out.T * SCALE, dq_sum[here, :])

    @pl.when(odd == 1)
    def _():
        dq[...] = dq_sum[...].astype(BF)
        dk[...] = dk_sum[...].astype(BF)
        dv[...] = dv_sum[...].astype(BF)


def first_back(info, dq, dk, dv, wq, wk, wv, own, send):
    half = own.shape[0]
    for at, out in ((PEER, send), (CORE, own)):
        here = pl.ds(pl.multiple_of(info[at] * half, 16), half)
        out[...] = (
            against(dq[here, :], wq[...])
            + against(dk[here, :], wk[...])
            + against(dv[here, :], wv[...])
        )


def weight_grad(plan, shapes, n_v, info, *refs):
    at = 0
    groups = []
    for n_left, n_right in shapes:
        groups.append((refs[at : at + n_left], refs[at + n_left : at + n_left + n_right]))
        at += n_left + n_right
    vectors = refs[at : at + n_v]
    outs = refs[at + n_v : at + n_v + 2 * len(plan)]
    lhs, rhs = refs[-2:]
    for g, (lefts, rights) in enumerate(groups):
        row = 0
        per = len(rights) // len(lefts)
        for i, left in enumerate(lefts):
            rows = left.shape[0]
            for j in range(8):
                block = left[:, pl.ds(pl.multiple_of(info[TABLE + j] * 128, 128), 128)]
                lhs[row : row + rows, j * 128 : (j + 1) * 128] = block.astype(BF)
            col = 0
            for right in rights[i * per : (i + 1) * per]:
                rhs[row : row + rows, col : col + right.shape[1]] = right[...].astype(BF)
                col += right.shape[1]
            row += rows
        for s, (order, segments) in enumerate(plan):
            put = 0
            for group, first, width in segments:
                if group == g:
                    for half in range(2):
                        value = over_rows(
                            lhs[:row, half * 512 : half * 512 + 512],
                            rhs[:row, first : first + width],
                        )
                        for q in range(4):
                            j = half * 4 + q
                            sent, pos = spot(order, j)
                            outs[2 * s + sent][pos, :128, put : put + width] = value[
                                q * 128 : (q + 1) * 128, :
                            ]
                put += width
    if n_v:
        for j in range(8):
            sent, pos = spot(plan[-1][0], j)
            out = outs[2 * len(plan) - 2 + sent]
            out[pos, 128:, :] = jnp.zeros((8, out.shape[2]), F32)
            for i, ref in enumerate(vectors):
                block = ref[:, pl.ds(pl.multiple_of(info[TABLE + j] * 128, 128), 128)]
                out[pos, 128 + 2 * i : 130 + 2 * i, :128] = block


def spot(order, j):
    bits = [(j // WEIGHT[name]) & 1 for name in order]
    return bits[0], bits[1] * 2 + bits[2]


def weight_grads(info, groups, plan, vectors=()):
    args, specs, shapes = [], [], []
    for lefts, rights in groups:
        flat = [r for group in rights for r in group]
        for left in lefts:
            array, spec = left if isinstance(left, tuple) else (left, None)
            args.append(array)
            specs.append(spec)
        args += flat
        specs += [None] * len(flat)
        shapes.append((len(lefts), len(flat)))
    args += vectors
    specs += [None] * len(vectors)
    outs = []
    for s, (order, segments) in enumerate(plan):
        tall = 136 if vectors and s == len(plan) - 1 else 128
        outs += [arr((4, tall, sum(w for _, _, w in segments)))] * 2
    rows = max(sum(group[0].shape[0] for group in rights) for _, rights in groups)
    wide = max(sum(r.shape[1] for r in rights[0]) for _, rights in groups)
    return launch(
        functools.partial(weight_grad, plan, tuple(shapes), len(vectors)),
        info,
        tuple(args),
        specs,
        outs,
        [None] * len(outs),
        scratch=[pltpu.VMEM((rows, 1024), BF), pltpu.VMEM((rows, wide), BF)],
        grant=40,
    )


def scatter_sum(keep, send):
    value = jnp.concatenate([keep, send])
    value = value.reshape(-1, value.shape[-1])
    return lax.psum_scatter(value, "dp", scatter_dimension=0, tiled=True)


def fold(info, *refs):
    for i in range(2):
        keep, got = refs[2 * i : 2 * i + 2]
        keep_out, send_out = refs[4 + 2 * i : 6 + 2 * i]
        n = keep_out.shape[0]
        keep_out[...] = keep[:n] + got[:n]
        send_out[...] = keep[n:] + got[n:]


def fold_one(info, keep, got, keep_out, send_out):
    keep_out[...] = keep[0] + got[0]
    send_out[...] = keep[1] + got[1]


def fold_last(info, *refs):
    keep_out, send_out = refs[4:]
    col = 0
    for i in range(2):
        keep, got = refs[2 * i : 2 * i + 2]
        rows, wide = keep.shape[1:]
        keep_out[:rows, col : col + wide] = keep[0] + got[0]
        send_out[:rows, col : col + wide] = keep[1] + got[1]
        col += wide


def finish_ffn(info, keep, got, up, down):
    wide = up.shape[1]
    up[...] = keep[:, :wide] + got[:, :wide]
    down[...] = (keep[:, wide:] + got[:, wide:]).T


def finish_cross(info, keep, got, co, ck, cv, cq):
    co[...] = (keep[:, :256] + got[:, :256]).T
    for i, out in enumerate((ck, cv, cq)):
        here = slice(256 * i + 256, 256 * i + 512)
        out[...] = keep[:, here] + got[:, here]


def finish_self(info, keep, got, so, sk, sv, sq, vectors):
    so[...] = (keep[:128, :256] + got[:128, :256]).T
    for i, out in enumerate((sk, sv, sq)):
        here = slice(256 * i + 256, 256 * i + 512)
        out[...] = keep[:128, here] + got[:128, here]
    vectors[...] = keep[128:, 768:896] + got[128:, 768:896]


FINISH = {
    finish_ffn: [(128, 1024), (1024, 128)],
    finish_cross: [(256, 128), (128, 256), (128, 256), (128, 256)],
    finish_self: [(256, 128), (128, 256), (128, 256), (128, 256), (8, 128)],
}


def exchange(streams, orders, step, first=None, cost=10):
    args = []
    for (keep, send), order in zip(streams, orders):
        got = swap(send, "dp", 8, FLIPS[order[step]])
        args += [keep, got if first is None else after(got, first)]
    none = jnp.zeros((1,), jnp.int32)
    if step == 1:
        shape = (max(a.shape[1] for a in args), args[0].shape[2] + args[2].shape[2])
        return launch(
            fold_last, none, args, [None] * 4, [arr(shape)] * 2, [None] * 2, cost=cost
        )
    outs = []
    for keep, _ in streams:
        outs += [arr((keep.shape[0] // 2, *keep.shape[1:]))] * 2
    out = launch(fold, none, args, [None] * 4, outs, [None] * 4, cost=cost)
    return list(zip(out[0::2], out[1::2]))


def fold_stream(pair, name, first, cost=0):
    keep, send = pair
    got = after(swap(send, "dp", 8, FLIPS[name]), first)
    none = jnp.zeros((1,), jnp.int32)
    outs = [arr(keep.shape[1:])] * 2
    return launch(fold_one, none, (keep, got), [None] * 2, outs, [None] * 2, cost=cost)


def finish(pair, body, first=None, cost=10):
    keep, send = pair
    got = swap(send, "dp", 8, FLIPS["m"])
    got = got if first is None else after(got, first)
    outs = [arr(shape) for shape in FINISH[body]]
    none = jnp.zeros((1,), jnp.int32)
    return launch(body, none, (keep, got), [None] * 2, outs, [None] * len(outs), cost=cost)


def sent(streams):
    return [s for _, s in streams]


def out_second(info, own, got, text_own, text_got, out):
    half = own.shape[0]
    out[:half, :] = own[...] + got[...]
    out[half:, :] = text_own[...] + text_got[...]


def out_sum(info, resid, mine, far, out):
    half = resid.shape[0]
    out[:half, :] = resid[...] + (mine[:half, :] + far[:half, :])
    out[half:, :] = mine[half:, :] + far[half:, :]


def out_place(info, own, sib, out, text_out):
    half = out.shape[0] // 2
    text_half = text_out.shape[0] // 2
    for at, ref in ((CORE, own), (PEER, sib)):
        out[pl.ds(pl.multiple_of(info[at] * half, 16), half), :] = ref[:half, :].astype(BF)
        spot = pl.multiple_of(info[at] * text_half, 8)
        text_out[pl.ds(spot, text_half), :] = ref[half:, :]


def place(info, own, sib, out):
    half = out.shape[0] // 2
    for at, ref in ((CORE, own), (PEER, sib)):
        out[pl.ds(pl.multiple_of(info[at] * half, 16), half), :] = ref[...].astype(BF)


def body(
    hidden,
    text_states,
    text_len,
    ln1_gain,
    ln1_bias,
    self_q,
    self_k,
    self_v,
    self_o,
    ln2_gain,
    ln2_bias,
    cross_q,
    cross_k,
    cross_v,
    cross_o,
    ln3_gain,
    ln3_bias,
    ffn_up,
    ffn_down,
    cotangent,
):
    dp_size = lax.axis_size("dp")
    frames, width = hidden.shape[1:]
    text_rows = text_states.shape[1]
    cols = self_q.shape[1]
    inner = ffn_up.shape[1]
    half = frames // 2
    device = lax.axis_index("dp") * 4 + lax.axis_index("tensor")
    table = jnp.asarray(index_table(dp_size))
    info = lax.dynamic_index_in_dim(table, device, 0, keepdims=False)
    hid = hidden.reshape(frames, width)
    cot = cotangent.reshape(frames, width)
    text = text_states.reshape(text_rows, width)
    gain1, bias1 = ln1_gain.reshape(1, width), ln1_bias.reshape(1, width)
    gain2, bias2 = ln2_gain.reshape(1, width), ln2_bias.reshape(1, width)
    gain3, bias3 = ln3_gain.reshape(1, width), ln3_bias.reshape(1, width)
    own_rows = pl.BlockSpec((half, width), lambda i, table: (table[CORE], 0))
    sib_rows = pl.BlockSpec((half, width), lambda i, table: (table[PEER], 0))
    half_mm = 2 * half * width
    whole = dp_size == 8
    orders = ("yam", "aym") if whole else ("may",) * 2
    order_one, order_two = orders

    own3, first = launch(
        prepare,
        info,
        (self_o, cross_o, cross_q),
        [None] * 3,
        [arr((3 * cols, width)), arr((cols, width))],
        [None] * 2,
        flops=1 << 20,
    )
    far_one = cross_swap(first)
    sib3 = core_swap(own3)

    def weight_at(i):
        return pl.BlockSpec((cols, width), lambda *_: (i, 0))

    step = frames // 4
    a1, q1, k1, v1 = launch(
        norm_project,
        info,
        (after(hid, first), gain1, bias1, self_q, self_k, self_v),
        [pl.BlockSpec((step, width), lambda i, _: (i, 0))] + [None] * 5,
        [arr((frames, width), BF)] + [arr((frames, cols), BF)] * 3,
        [pl.BlockSpec((step, width), lambda i, _: (i, 0))]
        + [pl.BlockSpec((step, cols), lambda i, _: (i, 0))] * 3,
        grid=(4,),
        flops=2 * frames * width * cols * 3,
    )
    heads = cols // HD
    pair_in = pl.BlockSpec((frames, PAIR), lambda h, _: (0, h // 2))
    pair_half = pl.BlockSpec((half, PAIR), lambda h, _: (0, h // 2))
    level = pl.BlockSpec((1, 1, frames), lambda h, _: (h, 0, 0))
    o1_own, o1_sib, total1 = launch(
        self_forward,
        info,
        (q1, k1, v1),
        [pair_in] * 3,
        [arr((half, cols))] * 2 + [arr((heads, 1, frames))],
        [pair_half] * 2 + [level],
        grid=(heads,),
        scratch=[pltpu.VMEM((frames, PAIR), F32)],
        flops=heads * frames * frames * 512,
        exps=heads * frames * frames,
    )
    o1_cross = cross_swap(after(o1_sib, far_one))
    o1_core = core_swap(after(o1_sib, sib3))
    o1_x = x_swap(o1_own)
    far_two = swap(after(far_one, o1_own), "dp", dp_size, FLIPS["y"])
    k2, v2 = launch(
        text_project,
        info,
        (after(text, o1_own), cross_k, cross_v),
        [None] * 3,
        [arr((text_rows, cols), BF)] * 2,
        [None] * 2,
        flops=2 * text_rows * width * cols * 2,
    )

    def mixed(one, two, i):
        return launch(
            mix,
            info,
            (one, two, own3, sib3),
            [None] * 2 + [weight_at(i)] * 2,
            [arr((half, width))],
            [None],
            flops=half_mm * 512,
        )[0]

    pre1 = mixed(after(o1_own, k2), o1_core, 0)
    far_one_core = core_swap(after(far_one, o1_core))
    far_two_core = core_swap(after(far_two, o1_x, o1_cross, pre1))
    far_weights = (far_one_core, far_two_core, far_one, far_two)

    def normed_mix(which, base, spec, pre, one, two, weights, gain, bias, packs=0):
        return launch(
            functools.partial(mix_norm, which),
            info,
            (base, pre, one, two, *weights, gain, bias),
            [spec] + [None] * (5 + len(weights)),
            [arr((half, width))] * 2 + [arr((cols // 2, width))] * packs,
            [None] * (2 + packs),
            scratch=[pltpu.VMEM((2 * cols, width), BF)],
            cost=2,
        )

    h1, a2, pack_co, pack_cq = normed_mix(None, hid, own_rows, pre1, o1_x, o1_cross, far_weights, gain2, bias2, 2)
    a2_sib = core_swap(a2)

    smem = pl.BlockSpec(memory_space=pltpu.SMEM)

    def cross(a):
        return launch(
            cross_forward,
            info,
            (text_len, a, cross_q, k2, v2),
            [smem] + [None] * 4,
            [arr((half, cols), BF), arr((half, cols)), arr((heads, 1, half))],
            [None] * 3,
            flops=half_mm * cols + heads * half * text_rows * 512,
            exps=heads * half * text_rows,
        )

    q2_own, o2_own, total2_own = cross(a2)
    o2_x = x_swap(after(o2_own, o1_x))
    q2_sib, o2_sib, total2_sib = cross(after(a2_sib, q2_own))
    o2_cross = cross_swap(after(o2_sib, o1_cross))
    o2_core = core_swap(o2_sib)
    far_co = swap(pack_co, "dp", dp_size, FLIPS["a"])
    far_cq = swap(pack_cq, "dp", dp_size, FLIPS["a"])
    pre2 = mixed(o2_own, o2_core, 1)
    far_co_core = core_swap(after(far_co, o2_x, o2_cross, far_cq, pre2))
    co_weights = (
        *(far_one_core, far_two_core, far_co_core),
        *(far_one, far_two, far_co),
    )
    h2, a3 = normed_mix(0, h1, None, pre2, o2_x, o2_cross, co_weights, gain3, bias3)
    a3_sib = core_swap(a3)
    far_cq_core = core_swap(after(far_cq, a3))

    unit = 256

    def feed(a, rows):
        return launch(
            feed_forward,
            info,
            (a, cot, ffn_up, ffn_down),
            [
                None,
                rows,
                pl.BlockSpec((width, unit), lambda i, _: (0, i)),
                pl.BlockSpec((unit, width), lambda i, _: (i, 0)),
            ],
            [arr((half, inner), BF)] * 2 + [arr((half, width))],
            [pl.BlockSpec((half, unit), lambda i, _: (0, i))] * 2 + [None],
            grid=(inner // unit,),
            flops=half_mm * inner * 3,
            exps=half * inner * 2,
        )

    g_own, du_own, da3_own = feed(a3, own_rows)
    g_sib, du_sib, da3_sib = feed(after(a3_sib, g_own, far_cq_core), sib_rows)
    da3_sum = launch(
        add_two,
        info,
        (da3_own, core_swap(da3_sib)),
        [None] * 2,
        [arr((half, width))],
        [None],
    )[0]
    da3_far = x_swap(after(da3_sum, o2_x))
    ffn_plan = (
        (order_one, ((0, 0, 1024),)),
        (order_two, ((1, 0, 1024),)),
    )
    ffn = weight_grads(
        info,
        [
            ([after(a3, da3_sum), a3_sib], [[du_own], [du_sib]]),
            ([(cot, own_rows), (cot, sib_rows)], [[g_own], [g_sib]]),
        ],
        ffn_plan,
    )
    out_own, out_sib = launch(
        down_project,
        info,
        (after(g_own, *ffn[1::2]), g_sib, ffn_down),
        [None, None, pl.BlockSpec((inner, 512), lambda i, _: (0, i))],
        [arr((half, width))] * 2,
        [pl.BlockSpec((half, 512), lambda i, _: (0, i))] * 2,
        grid=(width // 512,),
        flops=2 * half_mm * inner,
    )
    out_got = core_swap(out_sib)
    e1, grads3 = launch(
        sum_norm_back,
        info,
        (da3_sum, after(da3_far, out_own), gain3, h2, cot),
        [None] * 4 + [own_rows],
        [arr((half, width)), arr((2, width))],
        [None] * 2,
    )
    e1_sib = core_swap(e1)
    def cross_back(e, q, total, sums):
        last = bool(sums)
        return launch(
            functools.partial(cross_backward, last),
            info,
            (text_len, e, cross_o, q, k2, v2, total, *sums),
            [smem] + [None] * (6 + len(sums)),
            [arr((half, cols))] + [arr((text_rows, cols), BF if last else F32)] * 2,
            [None] * 3,
        )

    dq2_own, *sums = cross_back(after(e1, out_got), q2_own, total2_own, ())
    dq2_sib, dk2, dv2 = cross_back(e1_sib, q2_sib, total2_sib, tuple(sums))
    dq2_cross = cross_swap(dq2_sib)
    dq2_core = core_swap(dq2_sib)
    dq2_x = x_swap(after(dq2_own, da3_far))
    pre3 = mixed(dq2_own, dq2_core, 2)
    cq_weights = (
        *(far_one_core, far_two_core, far_cq_core),
        *(far_one, far_two, far_cq),
    )

    text_half = text_rows // 2
    text_own, text_send = launch(
        text_back,
        info,
        (dk2, dv2, cross_k, cross_v),
        [None] * 4,
        [arr((text_half, width))] * 2,
        [None] * 2,
        scratch=[pltpu.VMEM((text_rows, width), F32)],
        flops=2 * text_rows * width * cols * 2,
    )
    text_got = core_swap(text_send)
    out_two = launch(
        out_second,
        info,
        (out_own, out_got, text_own, text_got),
        [None] * 4,
        [arr((half + text_half, width))],
        [None],
    )[0]
    cross_plan = (
        (order_one, ((0, 0, 256), (2, 0, 512))),
        (order_two, ((1, 0, 256),)),
    )
    cross = weight_grads(
        info,
        [
            ([e1, e1_sib], [[o2_own], [o2_sib]]),
            ([a2, a2_sib], [[dq2_own], [dq2_sib]]),
            ([text], [[dk2, dv2]]),
        ],
        cross_plan,
    )
    pins = [out_two]
    if whole:
        ffn = exchange(list(zip(ffn[0::2], ffn[1::2])), orders, 0, cross[0], 12)
        pins += sent(ffn)
    e0, grads2 = launch(
        mix_norm_back,
        info,
        (after(pre3, *pins), dq2_x, dq2_cross, *cq_weights, gain2, h1, e1),
        [None] * (6 + len(cq_weights)),
        [arr((half, width)), arr((2, width))],
        [None] * 2,
        scratch=[pltpu.VMEM((2 * cols, width), BF)],
        cost=0,
    )
    out_far_two = x_swap(after(out_two, dq2_x))
    e0_sib = core_swap(e0)
    do1 = launch(
        mixed_back,
        info,
        (e0, e0_sib, self_o),
        [None] * 3,
        [arr((frames, cols), BF)],
        [None],
    )[0]
    dq1, dk1, dv1 = launch(
        self_backward,
        info,
        (q1, k1, v1, do1, total1),
        [pair_in] * 4 + [level],
        [arr((frames, cols), BF)] * 3,
        [pair_in] * 3,
        grid=(heads,),
        scratch=[pltpu.VMEM((frames, PAIR), F32)] * 3,
        flops=heads * frames * frames * 256 * 5,
        exps=heads * frames * frames,
    )
    da1_own, da1_send = launch(
        first_back,
        info,
        (dq1, dk1, dv1, self_q, self_k, self_v),
        [None] * 6,
        [arr((half, width))] * 2,
        [None] * 2,
        flops=2 * half_mm * 3 * cols,
    )
    pins = []
    if whole:
        ffn = exchange(ffn, orders, 1, da1_own, 4)
        pins = [ffn[1]]
        cross = [(k, after(c, ffn[1])) for k, c in zip(cross[0::2], cross[1::2])]
    da1_sum, grads1 = launch(
        sum_first_grads,
        info,
        (da1_own, after(core_swap(da1_send), *pins), hid),
        [None] * 2 + [own_rows],
        [arr((half, width)), arr((2, width))],
        [None] * 2,
    )

    vectors = (grads1, grads2, grads3)
    if not whole:
        stacked = lax.psum(jnp.concatenate(vectors), "tensor")
        stacked = lax.psum_scatter(stacked, "dp", scatter_dimension=1, tiled=True)
        vectors = ()
    self_plan = (
        (order_one, ((0, 0, 256), (1, 256, 512))),
        (order_two, ((1, 0, 256),)),
    )
    own = weight_grads(
        info,
        [
            ([after(e0, da1_sum), e0_sib], [[o1_own], [o1_sib]]),
            ([a1], [[dq1, dk1, dv1]]),
        ],
        self_plan,
        vectors,
    )
    pins = [own[0]]
    if whole:
        own = list(zip(own[0::2], own[1::2]))
    out_final = launch(
        out_sum,
        info,
        (h2, out_two, after(out_far_two, *pins)),
        [None] * 3,
        [arr((half + text_half, width))],
        [None],
        cost=0,
    )[0]
    da1_far = x_swap(after(da1_sum, out_final))
    output, text_grad = launch(
        out_place,
        info,
        (out_final, core_swap(out_final)),
        [None] * 2,
        [arr((frames, width), BF), arr((text_rows, width))],
        [None] * 2,
    )
    pins = []
    if not whole:
        ffn, cross, own = (
            [scatter_sum(*p) for p in zip(g[0::2], g[1::2])] for g in (ffn, cross, own)
        )
        up_grad, down_grad = ffn[0], ffn[1].T
        co_grad, cq_grad = cross[0][:, :256].T, cross[1]
        ck_grad, cv_grad = cross[0][:, 256:512], cross[0][:, 512:]
        so_grad, sq_grad = own[0][:, :256].T, own[1]
        sk_grad, sv_grad = own[0][:, 256:512], own[0][:, 512:]
    if whole:
        cross = exchange(cross, orders, 0, own[0][0], 0)
        own = [(k, after(c, cross[0][1])) for k, c in own]
        up_grad, down_grad = finish(ffn, finish_ffn, cross[0][0], 1)
        cross = exchange(cross, orders, 1, up_grad, 8)
        pins = [cross[1]]
    last = launch(
        last_norm_back,
        info,
        (da1_sum, after(da1_far, *pins), gain1, hid, e0),
        [None] * 3 + [own_rows, None],
        [arr((half, width))],
        [None],
        flops=half_mm * 8,
    )[0]
    if whole:
        own = exchange(own, orders, 0, last)
        cross = (cross[0], after(cross[1], up_grad))
        co_grad, ck_grad, cv_grad, cq_grad = finish(cross, finish_cross, last)
        own = exchange(own, orders, 1, co_grad)
        so_grad, sk_grad, sv_grad, sq_grad, stacked = finish(own, finish_self)
    hidden_grad = launch(
        place,
        info,
        (last, core_swap(last)),
        [None] * 2,
        [arr((frames, width), BF)],
        [None],
    )[0]
    if whole:
        stacked = stacked + x_swap(after(stacked, da1_far))
        stacked = stacked + core_swap(stacked)
    return (
        output.reshape(hidden.shape),
        hidden_grad.reshape(hidden.shape),
        text_grad.reshape(text_states.shape),
        stacked[0],
        stacked[1],
        sq_grad,
        sk_grad,
        sv_grad,
        so_grad,
        stacked[2],
        stacked[3],
        cq_grad,
        ck_grad,
        cv_grad,
        co_grad,
        stacked[4],
        stacked[5],
        up_grad,
        down_grad,
    )


def solution(mesh):
    rows = P("dp", None, None)
    column, row = P(None, "tensor"), P("tensor", None)
    in_specs = (
        *(rows, rows, P("dp"), P(), P(), column, column, column, row),
        *(P(), P(), column, column, column, row),
        *(P(), P(), column, row, rows),
    )
    vector, down, across = P("dp"), P("dp", "tensor"), P("tensor", "dp")
    out_specs = (
        *(rows, rows, rows, vector, vector, down, down, down, across),
        *(vector, vector, down, down, down, across),
        *(vector, vector, down, across),
    )
    return jax.shard_map(body, mesh=mesh, in_specs=in_specs, out_specs=out_specs, check_vma=False)
```

```python
import functools

import jax
import jax.numpy as jnp
import numpy as np
from jax import lax
from jax.experimental import pallas as pl
from jax.experimental.pallas import tpu as pltpu
from jax.sharding import PartitionSpec as P

HD = 64
EPS = 1e-05
NEG = -1e30
SCALE = HD ** (-0.5)
BF = jnp.bfloat16
F32 = jnp.float32
PAIR = 2 * HD

FLIPS = WEIGHT = {"y": 1, "a": 2, "m": 4}

CORE, PEER, Y, LABEL, TABLE = 0, 1, 2, 3, 8


def index_table(dp_size):
    rows = []
    for me in range(dp_size):
        for t in range(4):
            row = [t & 1, 1 - (t & 1), me & 1, me & 3, 0, 0, 0, 0]
            row += [(me ^ i) if dp_size == 8 else i for i in range(8)]
            rows.append(row)
    return np.array(rows, np.int32)


def dot(left, right):
    return lax.dot_general(left, right, (((1,), (0,)), ((), ())), preferred_element_type=F32)


def against(left, right):
    return lax.dot_general(left, right, (((1,), (1,)), ((), ())), preferred_element_type=F32)


def over_rows(left, right):
    return lax.dot_general(left, right, (((0,), (0,)), ((), ())), preferred_element_type=F32)


def swap(value, axis, size, flip):
    return lax.ppermute(value, axis, [(i, i ^ flip) for i in range(size)])


def core_swap(value):
    return swap(value, "tensor", 4, 1)


def x_swap(value):
    return swap(value, "tensor", 4, 2)


def cross_swap(value):
    return swap(value, "tensor", 4, 3)


def after(value, *others):
    return lax.optimization_barrier((value, *others))[0]


def full(shape):
    return pl.BlockSpec(shape, lambda *_: (0,) * len(shape))


def launch(body, info, args, in_specs, outs, out_specs, grid=(1,), scratch=(), flops=0, exps=0, grant=20, cost=0):
    specs = [full(a.shape) if s is None else s for a, s in zip(args, in_specs)]
    ospecs = [full(o.shape) if s is None else s for o, s in zip(outs, out_specs)]
    return pl.pallas_call(
        body,
        out_shape=list(outs),
        grid_spec=pltpu.PrefetchScalarGridSpec(
            num_scalar_prefetch=1,
            grid=grid,
            in_specs=specs,
            out_specs=ospecs,
            scratch_shapes=list(scratch),
        ),
        compiler_params=pltpu.CompilerParams(vmem_limit_bytes=min(grant, 12) << 20),
        cost_estimate=pl.CostEstimate(
            flops=1 + cost * 10**9, bytes_accessed=1, transcendentals=0
        ),
        name=body.__name__ if hasattr(body, "__name__") else body.func.__name__,
    )(info, *args)


def arr(shape, dtype=F32):
    return jax.ShapeDtypeStruct(shape, dtype)


def normed(values):
    centred = values - jnp.mean(values, -1, keepdims=True)
    inverse = lax.rsqrt(jnp.mean(centred * centred, -1, keepdims=True) + EPS)
    return centred * inverse, inverse


def norm_back(grad, scaled, inverse, gain):
    weighted = grad * gain
    first = jnp.mean(weighted, -1, keepdims=True)
    second = jnp.mean(weighted * scaled, -1, keepdims=True)
    return inverse * (weighted - first - scaled * second)


def head_lanes(odd, dtype):
    lane = lax.broadcasted_iota(jnp.int32, (1, PAIR), 1)
    return ((lane // HD) == odd).astype(dtype)


def norm_project(info, hid, gain, bias, wq, wk, wv, a1, q, k, v):
    scaled, _ = normed(hid[...].astype(F32))
    low = (scaled * gain[...] + bias[...]).astype(BF)
    a1[...] = low
    q[...] = (dot(low, wq[...]) * SCALE).astype(BF)
    k[...] = dot(low, wk[...]).astype(BF)
    v[...] = dot(low, wv[...]).astype(BF)


def text_project(info, text, wk, wv, k, v):
    k[...] = dot(text[...], wk[...]).astype(BF)
    v[...] = dot(text[...], wv[...]).astype(BF)


def blocks_of(rows, step=256):
    return [(s, min(step, rows - s)) for s in range(0, rows, step)]


def causal(scores):
    key = lax.broadcasted_iota(jnp.int32, scores.shape, 0)
    query = lax.broadcasted_iota(jnp.int32, scores.shape, 1)
    return jnp.where(key <= query, scores, NEG)


def self_forward(info, q, k, v, keep, send, total, mixed):
    rows = q.shape[0]
    half = rows // 2
    odd = lax.rem(pl.program_id(0), 2)
    lanes = head_lanes(odd, BF)
    lanes_on = head_lanes(odd, F32) > 0
    for start, size in blocks_of(rows):
        here = slice(start, start + size)
        query = q[here, :] * lanes
        near = causal(against(k[here, :], query))
        top = jnp.max(near, 0, keepdims=True)
        if start:
            far = against(k[:start, :], query)
            top = jnp.maximum(top, jnp.max(far, 0, keepdims=True))
        near = jnp.exp(near - top)
        count = jnp.sum(near, 0, keepdims=True)
        if start:
            far = jnp.exp(far - top)
            count = count + jnp.sum(far, 0, keepdims=True)
        scale = 1.0 / count
        out = over_rows(v[here, :], (near * scale).astype(BF))
        if start:
            out = out + over_rows(v[:start, :], (far * scale).astype(BF))
        total[0, :, here] = top + jnp.log(count)
        mixed[here, :] = jnp.where(lanes_on, out.T, mixed[here, :])

    @pl.when(odd == 1)
    def _():
        keep[...] = mixed[pl.ds(pl.multiple_of(info[CORE] * half, 8), half), :]
        send[...] = mixed[pl.ds(pl.multiple_of(info[PEER] * half, 8), half), :]


def prepare(info, so, co, cq, own, first):
    own[0:256, :] = so[...].astype(F32)
    own[256:512, :] = co[...].astype(F32)
    own[512:768, :] = cq[...].astype(F32).T
    first[0:128, :] = own[pl.ds(pl.multiple_of(info[Y] * 128, 8), 128), :]
    for i in range(2):
        at = pl.multiple_of(256 + i * 256 + info[LABEL] * 64, 8)
        first[128 + i * 64 : 192 + i * 64, :] = own[pl.ds(at, 64), :]


def mix(info, one, two, w_one, w_two, out):
    out[...] = dot(one[...].astype(BF), w_one[...].astype(BF)) + dot(
        two[...].astype(BF), w_two[...].astype(BF)
    )


def gather_halves(info, far, weights):
    for s in range(2):
        for p in range(2):

            @pl.when(info[Y] == p)
            def _(s=s, p=p):
                weights[s * 256 + p * 128 : s * 256 + p * 128 + 128, :] = far[2 * s][
                    :128, :
                ].astype(BF)

            @pl.when(info[Y] != p)
            def _(s=s, p=p):
                weights[s * 256 + p * 128 : s * 256 + p * 128 + 128, :] = far[2 * s + 1][
                    :128, :
                ].astype(BF)


def gather_quarters(info, far, weights, first):
    for s in range(2):
        over_x, over_y, over_z = far[3 * s : 3 * s + 3]
        pieces = (
            over_x[128 + first : 192 + first, :],
            over_y[128 + first : 192 + first, :],
            over_z[:64, :],
            over_z[64:, :],
        )
        for j, piece in enumerate(pieces):
            at = pl.multiple_of(s * 256 + (info[LABEL] ^ j) * 64, 64)
            weights[pl.ds(at, 64), :] = piece.astype(BF)


def mix_far(info, pre, one, two, far, weights, which):
    if which is None:
        gather_halves(info, far, weights)
    else:
        gather_quarters(info, far, weights, which)
    far_part = dot(one[...].astype(BF), weights[:256, :]) + dot(
        two[...].astype(BF), weights[256:, :]
    )
    return pre[...] + far_part


def mix_norm(which, info, base, pre, one, two, *refs):
    n = 7 if which is None else 5
    far, (gain, bias, resid, low, *packs, weights) = refs[:-n], refs[-n:]
    for i, pack in enumerate(packs):
        for j in range(2):
            pack[j * 64 : j * 64 + 64, :] = far[2 + j][128 + i * 64 : 192 + i * 64, :]
    part = mix_far(info, pre, one, two, far, weights, which)
    total = base[...].astype(F32) + part
    resid[...] = total
    scaled, _ = normed(total)
    low[...] = scaled * gain[...] + bias[...]


def mix_norm_back(info, pre, one, two, *refs):
    far, (gain, resid, e_in, e_out, grads, weights) = refs[:-6], refs[-6:]
    grad = mix_far(info, pre, one, two, far, weights, 64)
    scaled, inverse = normed(resid[...])
    e_out[...] = e_in[...] + norm_back(grad, scaled, inverse, gain[...])
    grads[0:1, :] = jnp.sum(grad * scaled, 0, keepdims=True) * 0.5
    grads[1:2, :] = jnp.sum(grad, 0, keepdims=True) * 0.5


def sum_norm_back(info, mine, far, gain, resid, e_in, e_out, grads):
    grad = mine[...] + far[...]
    scaled, inverse = normed(resid[...])
    e_out[...] = e_in[...].astype(F32) + norm_back(grad, scaled, inverse, gain[...])
    grads[0:1, :] = jnp.sum(grad * scaled, 0, keepdims=True) * 0.5
    grads[1:2, :] = jnp.sum(grad, 0, keepdims=True) * 0.5


def sum_first_grads(info, mine, recv, hid, out, grads):
    grad = mine[...] + recv[...]
    out[...] = grad
    scaled, _ = normed(hid[...].astype(F32))
    grads[0:1, :] = jnp.sum(grad * scaled, 0, keepdims=True)
    grads[1:2, :] = jnp.sum(grad, 0, keepdims=True)


def last_norm_back(info, mine, far, gain, hid, e_in, out):
    grad = mine[...] + far[...]
    scaled, inverse = normed(hid[...].astype(F32))
    out[...] = e_in[...] + norm_back(grad, scaled, inverse, gain[...])


def cross_forward(info, length, a2, wq, k, v, q, mixed, total):
    query_rows = (dot(a2[...].astype(BF), wq[...]) * SCALE).astype(BF)
    q[...] = query_rows
    for pair in range(2):
        cols = slice(pair * PAIR, (pair + 1) * PAIR)
        pair_out = None
        for odd in range(2):
            query = query_rows[:, cols] * head_lanes(odd, BF)
            scores = against(k[:, cols], query)
            slot = lax.broadcasted_iota(jnp.int32, scores.shape, 0)
            scores = jnp.where(slot < length[0], scores, NEG)
            top = jnp.max(scores, 0, keepdims=True)
            scores = jnp.exp(scores - top)
            count = jnp.sum(scores, 0, keepdims=True)
            out = over_rows(v[:, cols], (scores * (1.0 / count)).astype(BF)).T
            total[pair * 2 + odd] = top + jnp.log(count)
            pair_out = out if odd == 0 else jnp.where(head_lanes(1, F32) > 0, out, pair_out)
        mixed[:, cols] = pair_out


def feed_forward(info, a3, cot, up, down, g, du, da3):
    n = pl.program_id(0)
    u = dot(a3[...].astype(BF), up[...])
    cdf = 0.5 + 0.5 * lax.erf(u * (0.5**0.5))
    g[...] = (u * cdf).astype(BF)
    slope = cdf + u * jnp.exp(-0.5 * u * u) * (1.0 / (2.0 * np.pi) ** 0.5)
    dg = against(cot[...], down[...]).astype(BF).astype(F32)
    low = (dg * slope).astype(BF)
    du[...] = low
    part = against(low, up[...])

    @pl.when(n == 0)
    def _():
        da3[...] = part

    @pl.when(n > 0)
    def _():
        da3[...] += part


def add_two(info, one, two, out):
    out[...] = one[...] + two[...]


def down_project(info, own, sib, down, out_own, out_sib):
    out_own[...] = dot(own[...], down[...])
    out_sib[...] = dot(sib[...], down[...])


def cross_backward(second, info, length, e1, wo, q, k, v, total, *rest):
    if second:
        dk_in, dv_in, dq, dk_out, dv_out = rest
    else:
        dq, dk_out, dv_out = rest
    mixed_grad = against(e1[...].astype(BF), wo[...]).astype(BF)
    for pair in range(2):
        cols = slice(pair * PAIR, (pair + 1) * PAIR)
        dk = dk_in[:, cols] if second else None
        dv = dv_in[:, cols] if second else None
        pair_dq = None
        for odd in range(2):
            lanes = head_lanes(odd, BF)
            query = q[:, cols] * lanes
            grad = mixed_grad[:, cols] * lanes
            scores = against(k[:, cols], query)
            slot = lax.broadcasted_iota(jnp.int32, scores.shape, 0)
            scores = jnp.where(slot < length[0], scores, NEG)
            probs = jnp.exp(scores - total[pair * 2 + odd])
            prob_grad = against(v[:, cols], grad)
            part = dot(probs.astype(BF), grad)
            dv = part if dv is None else dv + part
            delta = jnp.sum(probs * prob_grad, 0, keepdims=True)
            low = (probs * (prob_grad - delta)).astype(BF)
            part = dot(low, query)
            dk = part if dk is None else dk + part
            out = over_rows(k[:, cols], low).T
            pair_dq = out if odd == 0 else jnp.where(head_lanes(1, F32) > 0, out, pair_dq)
        dq[:, cols] = pair_dq * SCALE
        dk_out[:, cols] = dk.astype(dk_out.dtype)
        dv_out[:, cols] = dv.astype(dv_out.dtype)


def text_back(info, dk, dv, wk, wv, own, send, scratch):
    half = own.shape[0]
    scratch[...] = against(dk[...], wk[...]) + against(dv[...], wv[...])
    own[...] = scratch[pl.ds(pl.multiple_of(info[CORE] * half, 8), half), :]
    send[...] = scratch[pl.ds(pl.multiple_of(info[PEER] * half, 8), half), :]


def mixed_back(info, own, sib, wo, out):
    half = own.shape[0]
    out[pl.ds(pl.multiple_of(info[CORE] * half, 16), half), :] = against(
        own[...].astype(BF), wo[...]
    ).astype(BF)
    out[pl.ds(pl.multiple_of(info[PEER] * half, 16), half), :] = against(
        sib[...].astype(BF), wo[...]
    ).astype(BF)


def self_backward(info, q, k, v, grad_in, total, dq, dk, dv, dq_sum, dk_sum, dv_sum):
    rows = q.shape[0]
    odd = lax.rem(pl.program_id(0), 2)
    lanes = head_lanes(odd, BF)
    lanes_on = head_lanes(odd, F32) > 0

    @pl.when(odd == 0)
    def _():
        dk_sum[...] = jnp.zeros_like(dk_sum)
        dv_sum[...] = jnp.zeros_like(dv_sum)

    for start, size in blocks_of(rows):
        here = slice(start, start + size)
        query = q[here, :] * lanes
        grad = grad_in[here, :] * lanes
        level = total[0, :, here]
        near = jnp.exp(causal(against(k[here, :], query)) - level)
        near_grad = against(v[here, :], grad)
        delta = jnp.sum(near * near_grad, 0, keepdims=True)
        dv_sum[here, :] += dot(near.astype(BF), grad)
        if start:
            far = jnp.exp(against(k[:start, :], query) - level)
            far_grad = against(v[:start, :], grad)
            delta = delta + jnp.sum(far * far_grad, 0, keepdims=True)
            dv_sum[:start, :] += dot(far.astype(BF), grad)
        near_low = (near * (near_grad - delta)).astype(BF)
        dk_sum[here, :] += dot(near_low, query)
        out = over_rows(k[here, :], near_low)
        if start:
            far_low = (far * (far_grad - delta)).astype(BF)
            dk_sum[:start, :] += dot(far_low, query)
            out = out + over_rows(k[:start, :], far_low)
        dq_sum[here, :] = jnp.where(lanes_on, out.T * SCALE, dq_sum[here, :])

    @pl.when(odd == 1)
    def _():
        dq[...] = dq_sum[...].astype(BF)
        dk[...] = dk_sum[...].astype(BF)
        dv[...] = dv_sum[...].astype(BF)


def first_back(info, dq, dk, dv, wq, wk, wv, own, send):
    half = own.shape[0]
    for at, out in ((PEER, send), (CORE, own)):
        here = pl.ds(pl.multiple_of(info[at] * half, 16), half)
        out[...] = (
            against(dq[here, :], wq[...])
            + against(dk[here, :], wk[...])
            + against(dv[here, :], wv[...])
        )


def weight_grad(plan, shapes, n_v, info, *refs):
    at = 0
    groups = []
    for n_left, n_right in shapes:
        groups.append((refs[at : at + n_left], refs[at + n_left : at + n_left + n_right]))
        at += n_left + n_right
    vectors = refs[at : at + n_v]
    outs = refs[at + n_v : at + n_v + 2 * len(plan)]
    lhs, rhs = refs[-2:]
    for g, (lefts, rights) in enumerate(groups):
        row = 0
        per = len(rights) // len(lefts)
        for i, left in enumerate(lefts):
            rows = left.shape[0]
            for j in range(8):
                block = left[:, pl.ds(pl.multiple_of(info[TABLE + j] * 128, 128), 128)]
                lhs[row : row + rows, j * 128 : (j + 1) * 128] = block.astype(BF)
            col = 0
            for right in rights[i * per : (i + 1) * per]:
                rhs[row : row + rows, col : col + right.shape[1]] = right[...].astype(BF)
                col += right.shape[1]
            row += rows
        for s, (order, segments) in enumerate(plan):
            put = 0
            for group, first, width in segments:
                if group == g:
                    for half in range(2):
                        value = over_rows(
                            lhs[:row, half * 512 : half * 512 + 512],
                            rhs[:row, first : first + width],
                        )
                        for q in range(4):
                            j = half * 4 + q
                            sent, pos = spot(order, j)
                            outs[2 * s + sent][pos, :128, put : put + width] = value[
                                q * 128 : (q + 1) * 128, :
                            ]
                put += width
    if n_v:
        for j in range(8):
            sent, pos = spot(plan[-1][0], j)
            out = outs[2 * len(plan) - 2 + sent]
            out[pos, 128:, :] = jnp.zeros((8, out.shape[2]), F32)
            for i, ref in enumerate(vectors):
                block = ref[:, pl.ds(pl.multiple_of(info[TABLE + j] * 128, 128), 128)]
                out[pos, 128 + 2 * i : 130 + 2 * i, :128] = block


def spot(order, j):
    bits = [(j // WEIGHT[name]) & 1 for name in order]
    return bits[0], bits[1] * 2 + bits[2]


def weight_grads(info, groups, plan, vectors=()):
    args, specs, shapes = [], [], []
    for lefts, rights in groups:
        flat = [r for group in rights for r in group]
        for left in lefts:
            array, spec = left if isinstance(left, tuple) else (left, None)
            args.append(array)
            specs.append(spec)
        args += flat
        specs += [None] * len(flat)
        shapes.append((len(lefts), len(flat)))
    args += vectors
    specs += [None] * len(vectors)
    outs = []
    for s, (order, segments) in enumerate(plan):
        tall = 136 if vectors and s == len(plan) - 1 else 128
        outs += [arr((4, tall, sum(w for _, _, w in segments)))] * 2
    rows = max(sum(group[0].shape[0] for group in rights) for _, rights in groups)
    wide = max(sum(r.shape[1] for r in rights[0]) for _, rights in groups)
    return launch(
        functools.partial(weight_grad, plan, tuple(shapes), len(vectors)),
        info,
        tuple(args),
        specs,
        outs,
        [None] * len(outs),
        scratch=[pltpu.VMEM((rows, 1024), BF), pltpu.VMEM((rows, wide), BF)],
        grant=40,
    )


def scatter_sum(keep, send):
    value = jnp.concatenate([keep, send])
    value = value.reshape(-1, value.shape[-1])
    return lax.psum_scatter(value, "dp", scatter_dimension=0, tiled=True)


def fold(info, *refs):
    for i in range(2):
        keep, got = refs[2 * i : 2 * i + 2]
        keep_out, send_out = refs[4 + 2 * i : 6 + 2 * i]
        n = keep_out.shape[0]
        keep_out[...] = keep[:n] + got[:n]
        send_out[...] = keep[n:] + got[n:]


def fold_one(info, keep, got, keep_out, send_out):
    keep_out[...] = keep[0] + got[0]
    send_out[...] = keep[1] + got[1]


def fold_last(info, *refs):
    keep_out, send_out = refs[4:]
    col = 0
    for i in range(2):
        keep, got = refs[2 * i : 2 * i + 2]
        rows, wide = keep.shape[1:]
        keep_out[:rows, col : col + wide] = keep[0] + got[0]
        send_out[:rows, col : col + wide] = keep[1] + got[1]
        col += wide


def finish_ffn(info, keep, got, up, down):
    wide = up.shape[1]
    up[...] = keep[:, :wide] + got[:, :wide]
    down[...] = (keep[:, wide:] + got[:, wide:]).T


def finish_cross(info, keep, got, co, ck, cv, cq):
    co[...] = (keep[:, :256] + got[:, :256]).T
    for i, out in enumerate((ck, cv, cq)):
        here = slice(256 * i + 256, 256 * i + 512)
        out[...] = keep[:, here] + got[:, here]


def finish_self(info, keep, got, so, sk, sv, sq, vectors):
    so[...] = (keep[:128, :256] + got[:128, :256]).T
    for i, out in enumerate((sk, sv, sq)):
        here = slice(256 * i + 256, 256 * i + 512)
        out[...] = keep[:128, here] + got[:128, here]
    vectors[...] = keep[128:, 768:896] + got[128:, 768:896]


FINISH = {
    finish_ffn: [(128, 1024), (1024, 128)],
    finish_cross: [(256, 128), (128, 256), (128, 256), (128, 256)],
    finish_self: [(256, 128), (128, 256), (128, 256), (128, 256), (8, 128)],
}


def exchange(streams, orders, step, first=None, cost=10, ready=()):
    args = []
    for i, ((keep, send), order) in enumerate(zip(streams, orders)):
        got = ready[i] if ready else swap(send, "dp", 8, FLIPS[order[step]])
        args += [keep, got if first is None else after(got, first)]
    none = jnp.zeros((1,), jnp.int32)
    if step == 1:
        shape = (max(a.shape[1] for a in args), args[0].shape[2] + args[2].shape[2])
        return launch(
            fold_last, none, args, [None] * 4, [arr(shape)] * 2, [None] * 2, cost=cost
        )
    outs = []
    for keep, _ in streams:
        outs += [arr((keep.shape[0] // 2, *keep.shape[1:]))] * 2
    out = launch(fold, none, args, [None] * 4, outs, [None] * 4, cost=cost)
    return list(zip(out[0::2], out[1::2]))


def fold_stream(pair, name, first, cost=0):
    keep, send = pair
    got = after(swap(send, "dp", 8, FLIPS[name]), first)
    none = jnp.zeros((1,), jnp.int32)
    outs = [arr(keep.shape[1:])] * 2
    return launch(fold_one, none, (keep, got), [None] * 2, outs, [None] * 2, cost=cost)


def finish(pair, body, first=None, cost=10):
    keep, send = pair
    got = swap(send, "dp", 8, FLIPS["m"])
    got = got if first is None else after(got, first)
    outs = [arr(shape) for shape in FINISH[body]]
    none = jnp.zeros((1,), jnp.int32)
    return launch(body, none, (keep, got), [None] * 2, outs, [None] * len(outs), cost=cost)


def sent(streams):
    return [s for _, s in streams]


def out_second(info, own, got, text_own, text_got, out):
    half = own.shape[0]
    out[:half, :] = own[...] + got[...]
    out[half:, :] = text_own[...] + text_got[...]


def out_sum(info, resid, mine, far, out):
    half = resid.shape[0]
    out[:half, :] = resid[...] + (mine[:half, :] + far[:half, :])
    out[half:, :] = mine[half:, :] + far[half:, :]


def out_place(info, own, sib, out, text_out):
    half = out.shape[0] // 2
    text_half = text_out.shape[0] // 2
    for at, ref in ((CORE, own), (PEER, sib)):
        out[pl.ds(pl.multiple_of(info[at] * half, 16), half), :] = ref[:half, :].astype(BF)
        spot = pl.multiple_of(info[at] * text_half, 8)
        text_out[pl.ds(spot, text_half), :] = ref[half:, :]


def place(info, own, sib, out):
    half = out.shape[0] // 2
    for at, ref in ((CORE, own), (PEER, sib)):
        out[pl.ds(pl.multiple_of(info[at] * half, 16), half), :] = ref[...].astype(BF)


def body(
    hidden,
    text_states,
    text_len,
    ln1_gain,
    ln1_bias,
    self_q,
    self_k,
    self_v,
    self_o,
    ln2_gain,
    ln2_bias,
    cross_q,
    cross_k,
    cross_v,
    cross_o,
    ln3_gain,
    ln3_bias,
    ffn_up,
    ffn_down,
    cotangent,
):
    dp_size = lax.axis_size("dp")
    frames, width = hidden.shape[1:]
    text_rows = text_states.shape[1]
    cols = self_q.shape[1]
    inner = ffn_up.shape[1]
    half = frames // 2
    device = lax.axis_index("dp") * 4 + lax.axis_index("tensor")
    table = jnp.asarray(index_table(dp_size))
    info = lax.dynamic_index_in_dim(table, device, 0, keepdims=False)
    hid = hidden.reshape(frames, width)
    cot = cotangent.reshape(frames, width)
    text = text_states.reshape(text_rows, width)
    gain1, bias1 = ln1_gain.reshape(1, width), ln1_bias.reshape(1, width)
    gain2, bias2 = ln2_gain.reshape(1, width), ln2_bias.reshape(1, width)
    gain3, bias3 = ln3_gain.reshape(1, width), ln3_bias.reshape(1, width)
    own_rows = pl.BlockSpec((half, width), lambda i, table: (table[CORE], 0))
    sib_rows = pl.BlockSpec((half, width), lambda i, table: (table[PEER], 0))
    half_mm = 2 * half * width
    whole = dp_size == 8
    orders = ("yam", "aym") if whole else ("may",) * 2
    order_one, order_two = orders

    own3, first = launch(
        prepare,
        info,
        (self_o, cross_o, cross_q),
        [None] * 3,
        [arr((3 * cols, width)), arr((cols, width))],
        [None] * 2,
        flops=1 << 20,
    )
    far_one = cross_swap(first)
    sib3 = core_swap(own3)

    def weight_at(i):
        return pl.BlockSpec((cols, width), lambda *_: (i, 0))

    step = frames // 4
    a1, q1, k1, v1 = launch(
        norm_project,
        info,
        (after(hid, first), gain1, bias1, self_q, self_k, self_v),
        [pl.BlockSpec((step, width), lambda i, _: (i, 0))] + [None] * 5,
        [arr((frames, width), BF)] + [arr((frames, cols), BF)] * 3,
        [pl.BlockSpec((step, width), lambda i, _: (i, 0))]
        + [pl.BlockSpec((step, cols), lambda i, _: (i, 0))] * 3,
        grid=(4,),
        flops=2 * frames * width * cols * 3,
    )
    heads = cols // HD
    pair_in = pl.BlockSpec((frames, PAIR), lambda h, _: (0, h // 2))
    pair_half = pl.BlockSpec((half, PAIR), lambda h, _: (0, h // 2))
    level = pl.BlockSpec((1, 1, frames), lambda h, _: (h, 0, 0))
    o1_own, o1_sib, total1 = launch(
        self_forward,
        info,
        (q1, k1, v1),
        [pair_in] * 3,
        [arr((half, cols))] * 2 + [arr((heads, 1, frames))],
        [pair_half] * 2 + [level],
        grid=(heads,),
        scratch=[pltpu.VMEM((frames, PAIR), F32)],
        flops=heads * frames * frames * 512,
        exps=heads * frames * frames,
    )
    o1_cross = cross_swap(after(o1_sib, far_one))
    o1_core = core_swap(after(o1_sib, sib3))
    o1_x = x_swap(o1_own)
    far_two = swap(after(far_one, o1_own), "dp", dp_size, FLIPS["y"])
    k2, v2 = launch(
        text_project,
        info,
        (after(text, o1_own), cross_k, cross_v),
        [None] * 3,
        [arr((text_rows, cols), BF)] * 2,
        [None] * 2,
        flops=2 * text_rows * width * cols * 2,
    )

    def mixed(one, two, i):
        return launch(
            mix,
            info,
            (one, two, own3, sib3),
            [None] * 2 + [weight_at(i)] * 2,
            [arr((half, width))],
            [None],
            flops=half_mm * 512,
        )[0]

    pre1 = mixed(after(o1_own, k2), o1_core, 0)
    far_one_core = core_swap(after(far_one, o1_core))
    far_two_core = core_swap(after(far_two, o1_x, o1_cross, pre1))
    far_weights = (far_one_core, far_two_core, far_one, far_two)

    def normed_mix(which, base, spec, pre, one, two, weights, gain, bias, packs=0):
        return launch(
            functools.partial(mix_norm, which),
            info,
            (base, pre, one, two, *weights, gain, bias),
            [spec] + [None] * (5 + len(weights)),
            [arr((half, width))] * 2 + [arr((cols // 2, width))] * packs,
            [None] * (2 + packs),
            scratch=[pltpu.VMEM((2 * cols, width), BF)],
            cost=2,
        )

    h1, a2, pack_co, pack_cq = normed_mix(None, hid, own_rows, pre1, o1_x, o1_cross, far_weights, gain2, bias2, 2)
    a2_sib = core_swap(a2)

    smem = pl.BlockSpec(memory_space=pltpu.SMEM)

    def cross(a):
        return launch(
            cross_forward,
            info,
            (text_len, a, cross_q, k2, v2),
            [smem] + [None] * 4,
            [arr((half, cols), BF), arr((half, cols)), arr((heads, 1, half))],
            [None] * 3,
            flops=half_mm * cols + heads * half * text_rows * 512,
            exps=heads * half * text_rows,
        )

    q2_own, o2_own, total2_own = cross(a2)
    o2_x = x_swap(after(o2_own, o1_x))
    q2_sib, o2_sib, total2_sib = cross(after(a2_sib, q2_own))
    o2_cross = cross_swap(after(o2_sib, o1_cross))
    o2_core = core_swap(o2_sib)
    far_co = swap(pack_co, "dp", dp_size, FLIPS["a"])
    far_cq = swap(pack_cq, "dp", dp_size, FLIPS["a"])
    pre2 = mixed(o2_own, o2_core, 1)
    far_co_core = core_swap(after(far_co, o2_x, o2_cross, far_cq, pre2))
    co_weights = (
        *(far_one_core, far_two_core, far_co_core),
        *(far_one, far_two, far_co),
    )
    h2, a3 = normed_mix(0, h1, None, pre2, o2_x, o2_cross, co_weights, gain3, bias3)
    a3_sib = core_swap(a3)
    far_cq_core = core_swap(after(far_cq, a3))

    unit = 256

    def feed(a, rows):
        return launch(
            feed_forward,
            info,
            (a, cot, ffn_up, ffn_down),
            [
                None,
                rows,
                pl.BlockSpec((width, unit), lambda i, _: (0, i)),
                pl.BlockSpec((unit, width), lambda i, _: (i, 0)),
            ],
            [arr((half, inner), BF)] * 2 + [arr((half, width))],
            [pl.BlockSpec((half, unit), lambda i, _: (0, i))] * 2 + [None],
            grid=(inner // unit,),
            flops=half_mm * inner * 3,
            exps=half * inner * 2,
        )

    g_own, du_own, da3_own = feed(a3, own_rows)
    g_sib, du_sib, da3_sib = feed(after(a3_sib, g_own, far_cq_core), sib_rows)
    da3_sum = launch(
        add_two,
        info,
        (da3_own, core_swap(da3_sib)),
        [None] * 2,
        [arr((half, width))],
        [None],
    )[0]
    da3_far = x_swap(after(da3_sum, o2_x))
    ffn_plan = (
        (order_one, ((0, 0, 1024),)),
        (order_two, ((1, 0, 1024),)),
    )
    ffn = weight_grads(
        info,
        [
            ([after(a3, da3_sum), a3_sib], [[du_own], [du_sib]]),
            ([(cot, own_rows), (cot, sib_rows)], [[g_own], [g_sib]]),
        ],
        ffn_plan,
    )
    out_own, out_sib = launch(
        down_project,
        info,
        (after(g_own, *ffn[1::2]), g_sib, ffn_down),
        [None, None, pl.BlockSpec((inner, 512), lambda i, _: (0, i))],
        [arr((half, width))] * 2,
        [pl.BlockSpec((half, 512), lambda i, _: (0, i))] * 2,
        grid=(width // 512,),
        flops=2 * half_mm * inner,
    )
    out_got = core_swap(out_sib)
    e1, grads3 = launch(
        sum_norm_back,
        info,
        (da3_sum, after(da3_far, out_own), gain3, h2, cot),
        [None] * 4 + [own_rows],
        [arr((half, width)), arr((2, width))],
        [None] * 2,
    )
    e1_sib = core_swap(e1)
    def cross_back(e, q, total, sums):
        last = bool(sums)
        return launch(
            functools.partial(cross_backward, last),
            info,
            (text_len, e, cross_o, q, k2, v2, total, *sums),
            [smem] + [None] * (6 + len(sums)),
            [arr((half, cols))] + [arr((text_rows, cols), BF if last else F32)] * 2,
            [None] * 3,
        )

    dq2_own, *sums = cross_back(after(e1, out_got), q2_own, total2_own, ())
    dq2_sib, dk2, dv2 = cross_back(e1_sib, q2_sib, total2_sib, tuple(sums))
    dq2_cross = cross_swap(dq2_sib)
    dq2_core = core_swap(dq2_sib)
    dq2_x = x_swap(after(dq2_own, da3_far))
    pre3 = mixed(dq2_own, dq2_core, 2)
    cq_weights = (
        *(far_one_core, far_two_core, far_cq_core),
        *(far_one, far_two, far_cq),
    )

    text_half = text_rows // 2
    text_own, text_send = launch(
        text_back,
        info,
        (dk2, dv2, cross_k, cross_v),
        [None] * 4,
        [arr((text_half, width))] * 2,
        [None] * 2,
        scratch=[pltpu.VMEM((text_rows, width), F32)],
        flops=2 * text_rows * width * cols * 2,
    )
    text_got = core_swap(text_send)
    out_two = launch(
        out_second,
        info,
        (out_own, out_got, text_own, text_got),
        [None] * 4,
        [arr((half + text_half, width))],
        [None],
    )[0]
    cross_plan = (
        (order_one, ((0, 0, 256), (2, 0, 512))),
        (order_two, ((1, 0, 256),)),
    )
    cross = weight_grads(
        info,
        [
            ([e1, e1_sib], [[o2_own], [o2_sib]]),
            ([a2, a2_sib], [[dq2_own], [dq2_sib]]),
            ([text], [[dk2, dv2]]),
        ],
        cross_plan,
    )
    pins = [out_two]
    if whole:
        ffn = exchange(list(zip(ffn[0::2], ffn[1::2])), orders, 0, cross[0], 12)
        pins += sent(ffn)
    e0, grads2 = launch(
        mix_norm_back,
        info,
        (after(pre3, *pins), dq2_x, dq2_cross, *cq_weights, gain2, h1, e1),
        [None] * (6 + len(cq_weights)),
        [arr((half, width)), arr((2, width))],
        [None] * 2,
        scratch=[pltpu.VMEM((2 * cols, width), BF)],
        cost=0,
    )
    out_far_two = x_swap(after(out_two, dq2_x))
    e0_sib = core_swap(e0)
    do1 = launch(
        mixed_back,
        info,
        (e0, e0_sib, self_o),
        [None] * 3,
        [arr((frames, cols), BF)],
        [None],
    )[0]
    dq1, dk1, dv1 = launch(
        self_backward,
        info,
        (q1, k1, v1, do1, total1),
        [pair_in] * 4 + [level],
        [arr((frames, cols), BF)] * 3,
        [pair_in] * 3,
        grid=(heads,),
        scratch=[pltpu.VMEM((frames, PAIR), F32)] * 3,
        flops=heads * frames * frames * 256 * 5,
        exps=heads * frames * frames,
    )
    da1_own, da1_send = launch(
        first_back,
        info,
        (dq1, dk1, dv1, self_q, self_k, self_v),
        [None] * 6,
        [arr((half, width))] * 2,
        [None] * 2,
        flops=2 * half_mm * 3 * cols,
    )
    pins = []
    if whole:
        ffn = exchange(ffn, orders, 1, da1_own, 4)
        pins = [ffn[1]]
        cross = [(k, after(c, ffn[1])) for k, c in zip(cross[0::2], cross[1::2])]
    da1_sum, grads1 = launch(
        sum_first_grads,
        info,
        (da1_own, after(core_swap(da1_send), *pins), hid),
        [None] * 2 + [own_rows],
        [arr((half, width)), arr((2, width))],
        [None] * 2,
    )

    vectors = (grads1, grads2, grads3)
    if not whole:
        stacked = lax.psum(jnp.concatenate(vectors), "tensor")
        stacked = lax.psum_scatter(stacked, "dp", scatter_dimension=1, tiled=True)
        vectors = ()
    self_plan = (
        (order_one, ((0, 0, 256), (1, 256, 512))),
        (order_two, ((1, 0, 256),)),
    )
    own = weight_grads(
        info,
        [
            ([after(e0, da1_sum), e0_sib], [[o1_own], [o1_sib]]),
            ([a1], [[dq1, dk1, dv1]]),
        ],
        self_plan,
        vectors,
    )
    pins = [own[0]]
    if whole:
        own = list(zip(own[0::2], own[1::2]))
    out_final = launch(
        out_sum,
        info,
        (h2, out_two, after(out_far_two, *pins)),
        [None] * 3,
        [arr((half + text_half, width))],
        [None],
        cost=0,
    )[0]
    da1_far = x_swap(after(da1_sum, out_final))
    output, text_grad = launch(
        out_place,
        info,
        (out_final, core_swap(out_final)),
        [None] * 2,
        [arr((frames, width), BF), arr((text_rows, width))],
        [None] * 2,
    )
    pins = []
    if not whole:
        ffn, cross, own = (
            [scatter_sum(*p) for p in zip(g[0::2], g[1::2])] for g in (ffn, cross, own)
        )
        up_grad, down_grad = ffn[0], ffn[1].T
        co_grad, cq_grad = cross[0][:, :256].T, cross[1]
        ck_grad, cv_grad = cross[0][:, 256:512], cross[0][:, 512:]
        so_grad, sq_grad = own[0][:, :256].T, own[1]
        sk_grad, sv_grad = own[0][:, 256:512], own[0][:, 512:]
    if whole:
        cross = exchange(cross, orders, 0, own[0][0], 0)
        ready = (
            swap(cross[0][1], "dp", 8, FLIPS["a"]),
            swap(cross[1][1], "dp", 8, FLIPS["y"]),
        )
        own = [(own[0][0], after(own[0][1], ready[1])), (own[1][0], after(own[1][1], cross[0][1]))]
        up_grad, down_grad = finish(ffn, finish_ffn, cross[0][0], 1)
        cross = exchange(cross, orders, 1, up_grad, 8, ready)
        pins = [cross[1]]
    last = launch(
        last_norm_back,
        info,
        (da1_sum, after(da1_far, *pins), gain1, hid, e0),
        [None] * 3 + [own_rows, None],
        [arr((half, width))],
        [None],
        flops=half_mm * 8,
    )[0]
    if whole:
        own = exchange(own, orders, 0, last)
        cross = (cross[0], after(cross[1], up_grad))
        co_grad, ck_grad, cv_grad, cq_grad = finish(cross, finish_cross, last)
        own = exchange(own, orders, 1, co_grad)
    hidden_grad = launch(
        place,
        info,
        (last, core_swap(last)),
        [None] * 2,
        [arr((frames, width), BF)],
        [None],
    )[0]
    if whole:
        so_grad, sk_grad, sv_grad, sq_grad, stacked = finish(
            own, finish_self, (hidden_grad, output)
        )
        stacked = stacked + x_swap(after(stacked, da1_far))
        stacked = stacked + core_swap(stacked)
    return (
        output.reshape(hidden.shape),
        hidden_grad.reshape(hidden.shape),
        text_grad.reshape(text_states.shape),
        stacked[0],
        stacked[1],
        sq_grad,
        sk_grad,
        sv_grad,
        so_grad,
        stacked[2],
        stacked[3],
        cq_grad,
        ck_grad,
        cv_grad,
        co_grad,
        stacked[4],
        stacked[5],
        up_grad,
        down_grad,
    )


def solution(mesh):
    rows = P("dp", None, None)
    column, row = P(None, "tensor"), P("tensor", None)
    in_specs = (
        *(rows, rows, P("dp"), P(), P(), column, column, column, row),
        *(P(), P(), column, column, column, row),
        *(P(), P(), column, row, rows),
    )
    vector, down, across = P("dp"), P("dp", "tensor"), P("tensor", "dp")
    out_specs = (
        *(rows, rows, rows, vector, vector, down, down, down, across),
        *(vector, vector, down, down, down, across),
        *(vector, vector, down, across),
    )
    return jax.shard_map(body, mesh=mesh, in_specs=in_specs, out_specs=out_specs, check_vma=False)
```

```python
import functools

import jax
import jax.numpy as jnp
import numpy as np
from jax import lax
from jax.experimental import pallas as pl
from jax.experimental.pallas import tpu as pltpu
from jax.sharding import PartitionSpec as P

HD = 64
EPS = 1e-05
NEG = -1e30
SCALE = HD ** (-0.5)
BF = jnp.bfloat16
F32 = jnp.float32
PAIR = 2 * HD

FLIPS = WEIGHT = {"y": 1, "a": 2, "m": 4}

CORE, PEER, Y, LABEL, TABLE = 0, 1, 2, 3, 8


def index_table(dp_size):
    rows = []
    for me in range(dp_size):
        for t in range(4):
            row = [t & 1, 1 - (t & 1), me & 1, me & 3, 0, 0, 0, 0]
            row += [(me ^ i) if dp_size == 8 else i for i in range(8)]
            rows.append(row)
    return np.array(rows, np.int32)


def dot(left, right):
    return lax.dot_general(left, right, (((1,), (0,)), ((), ())), preferred_element_type=F32)


def against(left, right):
    return lax.dot_general(left, right, (((1,), (1,)), ((), ())), preferred_element_type=F32)


def over_rows(left, right):
    return lax.dot_general(left, right, (((0,), (0,)), ((), ())), preferred_element_type=F32)


def swap(value, axis, size, flip):
    return lax.ppermute(value, axis, [(i, i ^ flip) for i in range(size)])


def core_swap(value):
    return swap(value, "tensor", 4, 1)


def x_swap(value):
    return swap(value, "tensor", 4, 2)


def cross_swap(value):
    return swap(value, "tensor", 4, 3)


def after(value, *others):
    return lax.optimization_barrier((value, *others))[0]


def full(shape):
    return pl.BlockSpec(shape, lambda *_: (0,) * len(shape))


def launch(body, info, args, in_specs, outs, out_specs, grid=(1,), scratch=(), flops=0, exps=0, grant=20, cost=0):
    specs = [full(a.shape) if s is None else s for a, s in zip(args, in_specs)]
    ospecs = [full(o.shape) if s is None else s for o, s in zip(outs, out_specs)]
    return pl.pallas_call(
        body,
        out_shape=list(outs),
        grid_spec=pltpu.PrefetchScalarGridSpec(
            num_scalar_prefetch=1,
            grid=grid,
            in_specs=specs,
            out_specs=ospecs,
            scratch_shapes=list(scratch),
        ),
        compiler_params=pltpu.CompilerParams(vmem_limit_bytes=min(grant, 12) << 20),
        cost_estimate=pl.CostEstimate(
            flops=1 + cost * 10**9, bytes_accessed=1, transcendentals=0
        ),
        name=body.__name__ if hasattr(body, "__name__") else body.func.__name__,
    )(info, *args)


def arr(shape, dtype=F32):
    return jax.ShapeDtypeStruct(shape, dtype)


def normed(values):
    centred = values - jnp.mean(values, -1, keepdims=True)
    inverse = lax.rsqrt(jnp.mean(centred * centred, -1, keepdims=True) + EPS)
    return centred * inverse, inverse


def norm_back(grad, scaled, inverse, gain):
    weighted = grad * gain
    first = jnp.mean(weighted, -1, keepdims=True)
    second = jnp.mean(weighted * scaled, -1, keepdims=True)
    return inverse * (weighted - first - scaled * second)


def head_lanes(odd, dtype):
    lane = lax.broadcasted_iota(jnp.int32, (1, PAIR), 1)
    return ((lane // HD) == odd).astype(dtype)


def norm_project(info, hid, gain, bias, wq, wk, wv, a1, q, k, v):
    scaled, _ = normed(hid[...].astype(F32))
    low = (scaled * gain[...] + bias[...]).astype(BF)
    a1[...] = low
    q[...] = (dot(low, wq[...]) * SCALE).astype(BF)
    k[...] = dot(low, wk[...]).astype(BF)
    v[...] = dot(low, wv[...]).astype(BF)


def text_project(info, text, wk, wv, k, v):
    k[...] = dot(text[...], wk[...]).astype(BF)
    v[...] = dot(text[...], wv[...]).astype(BF)


def blocks_of(rows, step=256):
    return [(s, min(step, rows - s)) for s in range(0, rows, step)]


def causal(scores):
    key = lax.broadcasted_iota(jnp.int32, scores.shape, 0)
    query = lax.broadcasted_iota(jnp.int32, scores.shape, 1)
    return jnp.where(key <= query, scores, NEG)


def self_forward(info, q, k, v, keep, send, total, mixed):
    rows = q.shape[0]
    half = rows // 2
    odd = lax.rem(pl.program_id(0), 2)
    lanes = head_lanes(odd, BF)
    lanes_on = head_lanes(odd, F32) > 0
    for start, size in blocks_of(rows):
        here = slice(start, start + size)
        query = q[here, :] * lanes
        near = causal(against(k[here, :], query))
        top = jnp.max(near, 0, keepdims=True)
        if start:
            far = against(k[:start, :], query)
            top = jnp.maximum(top, jnp.max(far, 0, keepdims=True))
        near = jnp.exp(near - top)
        count = jnp.sum(near, 0, keepdims=True)
        if start:
            far = jnp.exp(far - top)
            count = count + jnp.sum(far, 0, keepdims=True)
        scale = 1.0 / count
        out = over_rows(v[here, :], (near * scale).astype(BF))
        if start:
            out = out + over_rows(v[:start, :], (far * scale).astype(BF))
        total[0, :, here] = top + jnp.log(count)
        mixed[here, :] = jnp.where(lanes_on, out.T, mixed[here, :])

    @pl.when(odd == 1)
    def _():
        keep[...] = mixed[pl.ds(pl.multiple_of(info[CORE] * half, 8), half), :]
        send[...] = mixed[pl.ds(pl.multiple_of(info[PEER] * half, 8), half), :]


def prepare(info, so, co, cq, own, first):
    own[0:256, :] = so[...].astype(F32)
    own[256:512, :] = co[...].astype(F32)
    own[512:768, :] = cq[...].astype(F32).T
    first[0:128, :] = own[pl.ds(pl.multiple_of(info[Y] * 128, 8), 128), :]
    for i in range(2):
        at = pl.multiple_of(256 + i * 256 + info[LABEL] * 64, 8)
        first[128 + i * 64 : 192 + i * 64, :] = own[pl.ds(at, 64), :]


def mix(info, one, two, w_one, w_two, out):
    out[...] = dot(one[...].astype(BF), w_one[...].astype(BF)) + dot(
        two[...].astype(BF), w_two[...].astype(BF)
    )


def gather_halves(info, far, weights):
    for s in range(2):
        for p in range(2):

            @pl.when(info[Y] == p)
            def _(s=s, p=p):
                weights[s * 256 + p * 128 : s * 256 + p * 128 + 128, :] = far[2 * s][
                    :128, :
                ].astype(BF)

            @pl.when(info[Y] != p)
            def _(s=s, p=p):
                weights[s * 256 + p * 128 : s * 256 + p * 128 + 128, :] = far[2 * s + 1][
                    :128, :
                ].astype(BF)


def gather_quarters(info, far, weights, first):
    for s in range(2):
        over_x, over_y, over_z = far[3 * s : 3 * s + 3]
        pieces = (
            over_x[128 + first : 192 + first, :],
            over_y[128 + first : 192 + first, :],
            over_z[:64, :],
            over_z[64:, :],
        )
        for j, piece in enumerate(pieces):
            at = pl.multiple_of(s * 256 + (info[LABEL] ^ j) * 64, 64)
            weights[pl.ds(at, 64), :] = piece.astype(BF)


def mix_far(info, pre, one, two, far, weights, which):
    if which is None:
        gather_halves(info, far, weights)
    else:
        gather_quarters(info, far, weights, which)
    far_part = dot(one[...].astype(BF), weights[:256, :]) + dot(
        two[...].astype(BF), weights[256:, :]
    )
    return pre[...] + far_part


def mix_norm(which, info, base, pre, one, two, *refs):
    n = 7 if which is None else 5
    far, (gain, bias, resid, low, *packs, weights) = refs[:-n], refs[-n:]
    for i, pack in enumerate(packs):
        for j in range(2):
            pack[j * 64 : j * 64 + 64, :] = far[2 + j][128 + i * 64 : 192 + i * 64, :]
    part = mix_far(info, pre, one, two, far, weights, which)
    total = base[...].astype(F32) + part
    resid[...] = total
    scaled, _ = normed(total)
    low[...] = scaled * gain[...] + bias[...]


def mix_norm_back(info, pre, one, two, *refs):
    far, (gain, resid, e_in, e_out, grads, weights) = refs[:-6], refs[-6:]
    grad = mix_far(info, pre, one, two, far, weights, 64)
    scaled, inverse = normed(resid[...])
    e_out[...] = e_in[...] + norm_back(grad, scaled, inverse, gain[...])
    grads[0:1, :] = jnp.sum(grad * scaled, 0, keepdims=True) * 0.5
    grads[1:2, :] = jnp.sum(grad, 0, keepdims=True) * 0.5


def sum_norm_back(info, mine, far, gain, resid, e_in, e_out, grads):
    grad = mine[...] + far[...]
    scaled, inverse = normed(resid[...])
    e_out[...] = e_in[...].astype(F32) + norm_back(grad, scaled, inverse, gain[...])
    grads[0:1, :] = jnp.sum(grad * scaled, 0, keepdims=True) * 0.5
    grads[1:2, :] = jnp.sum(grad, 0, keepdims=True) * 0.5


def sum_first_grads(info, mine, recv, hid, out, grads):
    grad = mine[...] + recv[...]
    out[...] = grad
    scaled, _ = normed(hid[...].astype(F32))
    grads[0:1, :] = jnp.sum(grad * scaled, 0, keepdims=True)
    grads[1:2, :] = jnp.sum(grad, 0, keepdims=True)


def last_norm_back(info, mine, far, gain, hid, e_in, out):
    grad = mine[...] + far[...]
    scaled, inverse = normed(hid[...].astype(F32))
    out[...] = e_in[...] + norm_back(grad, scaled, inverse, gain[...])


def cross_forward(info, length, a2, wq, k, v, q, mixed, total):
    query_rows = (dot(a2[...].astype(BF), wq[...]) * SCALE).astype(BF)
    q[...] = query_rows
    for pair in range(2):
        cols = slice(pair * PAIR, (pair + 1) * PAIR)
        pair_out = None
        for odd in range(2):
            query = query_rows[:, cols] * head_lanes(odd, BF)
            scores = against(k[:, cols], query)
            slot = lax.broadcasted_iota(jnp.int32, scores.shape, 0)
            scores = jnp.where(slot < length[0], scores, NEG)
            top = jnp.max(scores, 0, keepdims=True)
            scores = jnp.exp(scores - top)
            count = jnp.sum(scores, 0, keepdims=True)
            out = over_rows(v[:, cols], (scores * (1.0 / count)).astype(BF)).T
            total[pair * 2 + odd] = top + jnp.log(count)
            pair_out = out if odd == 0 else jnp.where(head_lanes(1, F32) > 0, out, pair_out)
        mixed[:, cols] = pair_out


def feed_forward(info, a3, cot, up, down, g, du, da3):
    n = pl.program_id(0)
    u = dot(a3[...].astype(BF), up[...])
    cdf = 0.5 + 0.5 * lax.erf(u * (0.5**0.5))
    g[...] = (u * cdf).astype(BF)
    slope = cdf + u * jnp.exp(-0.5 * u * u) * (1.0 / (2.0 * np.pi) ** 0.5)
    dg = against(cot[...], down[...]).astype(BF).astype(F32)
    low = (dg * slope).astype(BF)
    du[...] = low
    part = against(low, up[...])

    @pl.when(n == 0)
    def _():
        da3[...] = part

    @pl.when(n > 0)
    def _():
        da3[...] += part


def stack_rows(info, one, two, three, out):
    for i, ref in enumerate((one, two, three)):
        out[2 * i : 2 * i + 2, :] = ref[...]
    out[6:, :] = jnp.zeros((2, out.shape[1]), F32)


def add_two(info, one, two, out):
    out[...] = one[...] + two[...]


def down_project(info, own, sib, down, out_own, out_sib):
    out_own[...] = dot(own[...], down[...])
    out_sib[...] = dot(sib[...], down[...])


def cross_backward(second, info, length, e1, wo, q, k, v, total, *rest):
    if second:
        dk_in, dv_in, dq, dk_out, dv_out = rest
    else:
        dq, dk_out, dv_out = rest
    mixed_grad = against(e1[...].astype(BF), wo[...]).astype(BF)
    for pair in range(2):
        cols = slice(pair * PAIR, (pair + 1) * PAIR)
        dk = dk_in[:, cols] if second else None
        dv = dv_in[:, cols] if second else None
        pair_dq = None
        for odd in range(2):
            lanes = head_lanes(odd, BF)
            query = q[:, cols] * lanes
            grad = mixed_grad[:, cols] * lanes
            scores = against(k[:, cols], query)
            slot = lax.broadcasted_iota(jnp.int32, scores.shape, 0)
            scores = jnp.where(slot < length[0], scores, NEG)
            probs = jnp.exp(scores - total[pair * 2 + odd])
            prob_grad = against(v[:, cols], grad)
            part = dot(probs.astype(BF), grad)
            dv = part if dv is None else dv + part
            delta = jnp.sum(probs * prob_grad, 0, keepdims=True)
            low = (probs * (prob_grad - delta)).astype(BF)
            part = dot(low, query)
            dk = part if dk is None else dk + part
            out = over_rows(k[:, cols], low).T
            pair_dq = out if odd == 0 else jnp.where(head_lanes(1, F32) > 0, out, pair_dq)
        dq[:, cols] = pair_dq * SCALE
        dk_out[:, cols] = dk.astype(dk_out.dtype)
        dv_out[:, cols] = dv.astype(dv_out.dtype)


def text_back(info, dk, dv, wk, wv, own, send, scratch):
    half = own.shape[0]
    scratch[...] = against(dk[...], wk[...]) + against(dv[...], wv[...])
    own[...] = scratch[pl.ds(pl.multiple_of(info[CORE] * half, 8), half), :]
    send[...] = scratch[pl.ds(pl.multiple_of(info[PEER] * half, 8), half), :]


def mixed_back(info, own, sib, wo, out):
    half = own.shape[0]
    out[pl.ds(pl.multiple_of(info[CORE] * half, 16), half), :] = against(
        own[...].astype(BF), wo[...]
    ).astype(BF)
    out[pl.ds(pl.multiple_of(info[PEER] * half, 16), half), :] = against(
        sib[...].astype(BF), wo[...]
    ).astype(BF)


def self_backward(info, q, k, v, grad_in, total, dq, dk, dv, dq_sum, dk_sum, dv_sum):
    rows = q.shape[0]
    odd = lax.rem(pl.program_id(0), 2)
    lanes = head_lanes(odd, BF)
    lanes_on = head_lanes(odd, F32) > 0

    @pl.when(odd == 0)
    def _():
        dk_sum[...] = jnp.zeros_like(dk_sum)
        dv_sum[...] = jnp.zeros_like(dv_sum)

    for start, size in blocks_of(rows):
        here = slice(start, start + size)
        query = q[here, :] * lanes
        grad = grad_in[here, :] * lanes
        level = total[0, :, here]
        near = jnp.exp(causal(against(k[here, :], query)) - level)
        near_grad = against(v[here, :], grad)
        delta = jnp.sum(near * near_grad, 0, keepdims=True)
        dv_sum[here, :] += dot(near.astype(BF), grad)
        if start:
            far = jnp.exp(against(k[:start, :], query) - level)
            far_grad = against(v[:start, :], grad)
            delta = delta + jnp.sum(far * far_grad, 0, keepdims=True)
            dv_sum[:start, :] += dot(far.astype(BF), grad)
        near_low = (near * (near_grad - delta)).astype(BF)
        dk_sum[here, :] += dot(near_low, query)
        out = over_rows(k[here, :], near_low)
        if start:
            far_low = (far * (far_grad - delta)).astype(BF)
            dk_sum[:start, :] += dot(far_low, query)
            out = out + over_rows(k[:start, :], far_low)
        dq_sum[here, :] = jnp.where(lanes_on, out.T * SCALE, dq_sum[here, :])

    @pl.when(odd == 1)
    def _():
        dq[...] = dq_sum[...].astype(BF)
        dk[...] = dk_sum[...].astype(BF)
        dv[...] = dv_sum[...].astype(BF)


def first_back(info, dq, dk, dv, wq, wk, wv, own, send):
    half = own.shape[0]
    for at, out in ((PEER, send), (CORE, own)):
        here = pl.ds(pl.multiple_of(info[at] * half, 16), half)
        out[...] = (
            against(dq[here, :], wq[...])
            + against(dk[here, :], wk[...])
            + against(dv[here, :], wv[...])
        )


def weight_grad(plan, shapes, n_v, info, *refs):
    at = 0
    groups = []
    for n_left, n_right in shapes:
        groups.append((refs[at : at + n_left], refs[at + n_left : at + n_left + n_right]))
        at += n_left + n_right
    vectors = refs[at : at + n_v]
    outs = refs[at + n_v : at + n_v + 2 * len(plan)]
    lhs, rhs = refs[-2:]
    for g, (lefts, rights) in enumerate(groups):
        row = 0
        per = len(rights) // len(lefts)
        for i, left in enumerate(lefts):
            rows = left.shape[0]
            for j in range(8):
                block = left[:, pl.ds(pl.multiple_of(info[TABLE + j] * 128, 128), 128)]
                lhs[row : row + rows, j * 128 : (j + 1) * 128] = block.astype(BF)
            col = 0
            for right in rights[i * per : (i + 1) * per]:
                rhs[row : row + rows, col : col + right.shape[1]] = right[...].astype(BF)
                col += right.shape[1]
            row += rows
        for s, (order, segments) in enumerate(plan):
            put = 0
            for group, first, width in segments:
                if group == g:
                    for half in range(2):
                        value = over_rows(
                            lhs[:row, half * 512 : half * 512 + 512],
                            rhs[:row, first : first + width],
                        )
                        for q in range(4):
                            j = half * 4 + q
                            sent, pos = spot(order, j)
                            outs[2 * s + sent][pos, :128, put : put + width] = value[
                                q * 128 : (q + 1) * 128, :
                            ]
                put += width
    if n_v:
        for j in range(8):
            sent, pos = spot(plan[-1][0], j)
            out = outs[2 * len(plan) - 2 + sent]
            out[pos, 128:, :] = jnp.zeros((8, out.shape[2]), F32)
            block = vectors[0][:, pl.ds(pl.multiple_of(info[TABLE + j] * 128, 128), 128)]
            out[pos, 128:, :128] = block


def spot(order, j):
    bits = [(j // WEIGHT[name]) & 1 for name in order]
    return bits[0], bits[1] * 2 + bits[2]


def weight_grads(info, groups, plan, vectors=()):
    args, specs, shapes = [], [], []
    for lefts, rights in groups:
        flat = [r for group in rights for r in group]
        for left in lefts:
            array, spec = left if isinstance(left, tuple) else (left, None)
            args.append(array)
            specs.append(spec)
        args += flat
        specs += [None] * len(flat)
        shapes.append((len(lefts), len(flat)))
    args += vectors
    specs += [None] * len(vectors)
    outs = []
    for s, (order, segments) in enumerate(plan):
        tall = 136 if vectors and s == len(plan) - 1 else 128
        outs += [arr((4, tall, sum(w for _, _, w in segments)))] * 2
    rows = max(sum(group[0].shape[0] for group in rights) for _, rights in groups)
    wide = max(sum(r.shape[1] for r in rights[0]) for _, rights in groups)
    return launch(
        functools.partial(weight_grad, plan, tuple(shapes), len(vectors)),
        info,
        tuple(args),
        specs,
        outs,
        [None] * len(outs),
        scratch=[pltpu.VMEM((rows, 1024), BF), pltpu.VMEM((rows, wide), BF)],
        grant=40,
    )


def scatter_sum(keep, send):
    value = jnp.concatenate([keep, send])
    value = value.reshape(-1, value.shape[-1])
    return lax.psum_scatter(value, "dp", scatter_dimension=0, tiled=True)


def fold(info, *refs):
    for i in range(2):
        keep, got = refs[2 * i : 2 * i + 2]
        keep_out, send_out = refs[4 + 2 * i : 6 + 2 * i]
        n = keep_out.shape[0]
        keep_out[...] = keep[:n] + got[:n]
        send_out[...] = keep[n:] + got[n:]


def fold_one(info, keep, got, keep_out, send_out):
    keep_out[...] = keep[0] + got[0]
    send_out[...] = keep[1] + got[1]


def fold_last(info, *refs):
    keep_out, send_out = refs[4:]
    col = 0
    for i in range(2):
        keep, got = refs[2 * i : 2 * i + 2]
        rows, wide = keep.shape[1:]
        keep_out[:rows, col : col + wide] = keep[0] + got[0]
        send_out[:rows, col : col + wide] = keep[1] + got[1]
        col += wide


def finish_ffn(info, keep, got, up, down):
    wide = up.shape[1]
    up[...] = keep[:, :wide] + got[:, :wide]
    down[...] = (keep[:, wide:] + got[:, wide:]).T


def finish_cross(info, keep, got, co, ck, cv, cq):
    co[...] = (keep[:, :256] + got[:, :256]).T
    for i, out in enumerate((ck, cv, cq)):
        here = slice(256 * i + 256, 256 * i + 512)
        out[...] = keep[:, here] + got[:, here]


def finish_self(info, keep, got, so, sk, sv, sq, vectors):
    so[...] = (keep[:128, :256] + got[:128, :256]).T
    for i, out in enumerate((sk, sv, sq)):
        here = slice(256 * i + 256, 256 * i + 512)
        out[...] = keep[:128, here] + got[:128, here]
    vectors[...] = keep[128:, 768:896] + got[128:, 768:896]


FINISH = {
    finish_ffn: [(128, 1024), (1024, 128)],
    finish_cross: [(256, 128), (128, 256), (128, 256), (128, 256)],
    finish_self: [(256, 128), (128, 256), (128, 256), (128, 256), (8, 128)],
}


def exchange(streams, orders, step, first=None, cost=10, ready=()):
    args = []
    for i, ((keep, send), order) in enumerate(zip(streams, orders)):
        got = ready[i] if ready else swap(send, "dp", 8, FLIPS[order[step]])
        args += [keep, got if first is None else after(got, first)]
    none = jnp.zeros((1,), jnp.int32)
    if step == 1:
        shape = (max(a.shape[1] for a in args), args[0].shape[2] + args[2].shape[2])
        return launch(
            fold_last, none, args, [None] * 4, [arr(shape)] * 2, [None] * 2, cost=cost
        )
    outs = []
    for keep, _ in streams:
        outs += [arr((keep.shape[0] // 2, *keep.shape[1:]))] * 2
    out = launch(fold, none, args, [None] * 4, outs, [None] * 4, cost=cost)
    return list(zip(out[0::2], out[1::2]))


def fold_stream(pair, name, first, cost=0):
    keep, send = pair
    got = after(swap(send, "dp", 8, FLIPS[name]), first)
    none = jnp.zeros((1,), jnp.int32)
    outs = [arr(keep.shape[1:])] * 2
    return launch(fold_one, none, (keep, got), [None] * 2, outs, [None] * 2, cost=cost)


def finish(pair, body, first=None, cost=10):
    keep, send = pair
    got = swap(send, "dp", 8, FLIPS["m"])
    got = got if first is None else after(got, first)
    outs = [arr(shape) for shape in FINISH[body]]
    none = jnp.zeros((1,), jnp.int32)
    return launch(body, none, (keep, got), [None] * 2, outs, [None] * len(outs), cost=cost)


def sent(streams):
    return [s for _, s in streams]


def out_second(info, own, got, text_own, text_got, out):
    half = own.shape[0]
    out[:half, :] = own[...] + got[...]
    out[half:, :] = text_own[...] + text_got[...]


def out_sum(info, resid, mine, far, out):
    half = resid.shape[0]
    out[:half, :] = resid[...] + (mine[:half, :] + far[:half, :])
    out[half:, :] = mine[half:, :] + far[half:, :]


def out_place(info, own, sib, out, text_out):
    half = out.shape[0] // 2
    text_half = text_out.shape[0] // 2
    for at, ref in ((CORE, own), (PEER, sib)):
        out[pl.ds(pl.multiple_of(info[at] * half, 16), half), :] = ref[:half, :].astype(BF)
        spot = pl.multiple_of(info[at] * text_half, 8)
        text_out[pl.ds(spot, text_half), :] = ref[half:, :]


def place(info, own, sib, out):
    half = out.shape[0] // 2
    for at, ref in ((CORE, own), (PEER, sib)):
        out[pl.ds(pl.multiple_of(info[at] * half, 16), half), :] = ref[...].astype(BF)


def body(
    hidden,
    text_states,
    text_len,
    ln1_gain,
    ln1_bias,
    self_q,
    self_k,
    self_v,
    self_o,
    ln2_gain,
    ln2_bias,
    cross_q,
    cross_k,
    cross_v,
    cross_o,
    ln3_gain,
    ln3_bias,
    ffn_up,
    ffn_down,
    cotangent,
):
    dp_size = lax.axis_size("dp")
    frames, width = hidden.shape[1:]
    text_rows = text_states.shape[1]
    cols = self_q.shape[1]
    inner = ffn_up.shape[1]
    half = frames // 2
    device = lax.axis_index("dp") * 4 + lax.axis_index("tensor")
    table = jnp.asarray(index_table(dp_size))
    info = lax.dynamic_index_in_dim(table, device, 0, keepdims=False)
    hid = hidden.reshape(frames, width)
    cot = cotangent.reshape(frames, width)
    text = text_states.reshape(text_rows, width)
    gain1, bias1 = ln1_gain.reshape(1, width), ln1_bias.reshape(1, width)
    gain2, bias2 = ln2_gain.reshape(1, width), ln2_bias.reshape(1, width)
    gain3, bias3 = ln3_gain.reshape(1, width), ln3_bias.reshape(1, width)
    own_rows = pl.BlockSpec((half, width), lambda i, table: (table[CORE], 0))
    sib_rows = pl.BlockSpec((half, width), lambda i, table: (table[PEER], 0))
    half_mm = 2 * half * width
    whole = dp_size == 8
    orders = ("yam", "aym") if whole else ("may",) * 2
    order_one, order_two = orders

    own3, first = launch(
        prepare,
        info,
        (self_o, cross_o, cross_q),
        [None] * 3,
        [arr((3 * cols, width)), arr((cols, width))],
        [None] * 2,
        flops=1 << 20,
    )
    far_one = cross_swap(first)
    sib3 = core_swap(own3)

    def weight_at(i):
        return pl.BlockSpec((cols, width), lambda *_: (i, 0))

    step = frames // 4
    a1, q1, k1, v1 = launch(
        norm_project,
        info,
        (after(hid, first), gain1, bias1, self_q, self_k, self_v),
        [pl.BlockSpec((step, width), lambda i, _: (i, 0))] + [None] * 5,
        [arr((frames, width), BF)] + [arr((frames, cols), BF)] * 3,
        [pl.BlockSpec((step, width), lambda i, _: (i, 0))]
        + [pl.BlockSpec((step, cols), lambda i, _: (i, 0))] * 3,
        grid=(4,),
        flops=2 * frames * width * cols * 3,
    )
    heads = cols // HD
    pair_in = pl.BlockSpec((frames, PAIR), lambda h, _: (0, h // 2))
    pair_half = pl.BlockSpec((half, PAIR), lambda h, _: (0, h // 2))
    level = pl.BlockSpec((1, 1, frames), lambda h, _: (h, 0, 0))
    o1_own, o1_sib, total1 = launch(
        self_forward,
        info,
        (q1, k1, v1),
        [pair_in] * 3,
        [arr((half, cols))] * 2 + [arr((heads, 1, frames))],
        [pair_half] * 2 + [level],
        grid=(heads,),
        scratch=[pltpu.VMEM((frames, PAIR), F32)],
        flops=heads * frames * frames * 512,
        exps=heads * frames * frames,
    )
    o1_cross = cross_swap(after(o1_sib, far_one))
    o1_core = core_swap(after(o1_sib, sib3))
    o1_x = x_swap(o1_own)
    far_two = swap(after(far_one, o1_own), "dp", dp_size, FLIPS["y"])
    k2, v2 = launch(
        text_project,
        info,
        (after(text, o1_own), cross_k, cross_v),
        [None] * 3,
        [arr((text_rows, cols), BF)] * 2,
        [None] * 2,
        flops=2 * text_rows * width * cols * 2,
    )

    def mixed(one, two, i):
        return launch(
            mix,
            info,
            (one, two, own3, sib3),
            [None] * 2 + [weight_at(i)] * 2,
            [arr((half, width))],
            [None],
            flops=half_mm * 512,
        )[0]

    pre1 = mixed(after(o1_own, k2), o1_core, 0)
    far_one_core = core_swap(after(far_one, o1_core))
    far_two_core = core_swap(after(far_two, o1_x, o1_cross, pre1))
    far_weights = (far_one_core, far_two_core, far_one, far_two)

    def normed_mix(which, base, spec, pre, one, two, weights, gain, bias, packs=0):
        return launch(
            functools.partial(mix_norm, which),
            info,
            (base, pre, one, two, *weights, gain, bias),
            [spec] + [None] * (5 + len(weights)),
            [arr((half, width))] * 2 + [arr((cols // 2, width))] * packs,
            [None] * (2 + packs),
            scratch=[pltpu.VMEM((2 * cols, width), BF)],
            cost=2,
        )

    h1, a2, pack_co, pack_cq = normed_mix(None, hid, own_rows, pre1, o1_x, o1_cross, far_weights, gain2, bias2, 2)
    a2_sib = core_swap(a2)

    smem = pl.BlockSpec(memory_space=pltpu.SMEM)

    def cross(a):
        return launch(
            cross_forward,
            info,
            (text_len, a, cross_q, k2, v2),
            [smem] + [None] * 4,
            [arr((half, cols), BF), arr((half, cols)), arr((heads, 1, half))],
            [None] * 3,
            flops=half_mm * cols + heads * half * text_rows * 512,
            exps=heads * half * text_rows,
        )

    q2_own, o2_own, total2_own = cross(a2)
    o2_x = x_swap(after(o2_own, o1_x))
    q2_sib, o2_sib, total2_sib = cross(after(a2_sib, q2_own))
    o2_cross = cross_swap(after(o2_sib, o1_cross))
    o2_core = core_swap(o2_sib)
    far_co = swap(pack_co, "dp", dp_size, FLIPS["a"])
    far_cq = swap(pack_cq, "dp", dp_size, FLIPS["a"])
    pre2 = mixed(o2_own, o2_core, 1)
    far_co_core = core_swap(after(far_co, o2_x, o2_cross, far_cq, pre2))
    co_weights = (
        *(far_one_core, far_two_core, far_co_core),
        *(far_one, far_two, far_co),
    )
    h2, a3 = normed_mix(0, h1, None, pre2, o2_x, o2_cross, co_weights, gain3, bias3)
    a3_sib = core_swap(a3)
    far_cq_core = core_swap(after(far_cq, a3))

    unit = 256

    def feed(a, rows):
        return launch(
            feed_forward,
            info,
            (a, cot, ffn_up, ffn_down),
            [
                None,
                rows,
                pl.BlockSpec((width, unit), lambda i, _: (0, i)),
                pl.BlockSpec((unit, width), lambda i, _: (i, 0)),
            ],
            [arr((half, inner), BF)] * 2 + [arr((half, width))],
            [pl.BlockSpec((half, unit), lambda i, _: (0, i))] * 2 + [None],
            grid=(inner // unit,),
            flops=half_mm * inner * 3,
            exps=half * inner * 2,
        )

    g_own, du_own, da3_own = feed(a3, own_rows)
    g_sib, du_sib, da3_sib = feed(after(a3_sib, g_own, far_cq_core), sib_rows)
    da3_sum = launch(
        add_two,
        info,
        (da3_own, core_swap(da3_sib)),
        [None] * 2,
        [arr((half, width))],
        [None],
    )[0]
    da3_far = x_swap(after(da3_sum, o2_x))
    ffn_plan = (
        (order_one, ((0, 0, 1024),)),
        (order_two, ((1, 0, 1024),)),
    )
    ffn = weight_grads(
        info,
        [
            ([after(a3, da3_sum), a3_sib], [[du_own], [du_sib]]),
            ([(cot, own_rows), (cot, sib_rows)], [[g_own], [g_sib]]),
        ],
        ffn_plan,
    )
    out_own, out_sib = launch(
        down_project,
        info,
        (after(g_own, *ffn[1::2]), g_sib, ffn_down),
        [None, None, pl.BlockSpec((inner, 512), lambda i, _: (0, i))],
        [arr((half, width))] * 2,
        [pl.BlockSpec((half, 512), lambda i, _: (0, i))] * 2,
        grid=(width // 512,),
        flops=2 * half_mm * inner,
    )
    out_got = core_swap(out_sib)
    e1, grads3 = launch(
        sum_norm_back,
        info,
        (da3_sum, after(da3_far, out_own), gain3, h2, cot),
        [None] * 4 + [own_rows],
        [arr((half, width)), arr((2, width))],
        [None] * 2,
    )
    e1_sib = core_swap(e1)
    def cross_back(e, q, total, sums):
        last = bool(sums)
        return launch(
            functools.partial(cross_backward, last),
            info,
            (text_len, e, cross_o, q, k2, v2, total, *sums),
            [smem] + [None] * (6 + len(sums)),
            [arr((half, cols))] + [arr((text_rows, cols), BF if last else F32)] * 2,
            [None] * 3,
        )

    dq2_own, *sums = cross_back(after(e1, out_got), q2_own, total2_own, ())
    dq2_sib, dk2, dv2 = cross_back(e1_sib, q2_sib, total2_sib, tuple(sums))
    dq2_cross = cross_swap(dq2_sib)
    dq2_core = core_swap(dq2_sib)
    dq2_x = x_swap(after(dq2_own, da3_far))
    pre3 = mixed(dq2_own, dq2_core, 2)
    cq_weights = (
        *(far_one_core, far_two_core, far_cq_core),
        *(far_one, far_two, far_cq),
    )

    text_half = text_rows // 2
    text_own, text_send = launch(
        text_back,
        info,
        (dk2, dv2, cross_k, cross_v),
        [None] * 4,
        [arr((text_half, width))] * 2,
        [None] * 2,
        scratch=[pltpu.VMEM((text_rows, width), F32)],
        flops=2 * text_rows * width * cols * 2,
    )
    text_got = core_swap(text_send)
    out_two = launch(
        out_second,
        info,
        (out_own, out_got, text_own, text_got),
        [None] * 4,
        [arr((half + text_half, width))],
        [None],
    )[0]
    cross_plan = (
        (order_one, ((0, 0, 256), (2, 0, 512))),
        (order_two, ((1, 0, 256),)),
    )
    cross = weight_grads(
        info,
        [
            ([e1, e1_sib], [[o2_own], [o2_sib]]),
            ([a2, a2_sib], [[dq2_own], [dq2_sib]]),
            ([text], [[dk2, dv2]]),
        ],
        cross_plan,
    )
    pins = [out_two]
    if whole:
        ffn = exchange(list(zip(ffn[0::2], ffn[1::2])), orders, 0, cross[0], 12)
        pins += sent(ffn)
    e0, grads2 = launch(
        mix_norm_back,
        info,
        (after(pre3, *pins), dq2_x, dq2_cross, *cq_weights, gain2, h1, e1),
        [None] * (6 + len(cq_weights)),
        [arr((half, width)), arr((2, width))],
        [None] * 2,
        scratch=[pltpu.VMEM((2 * cols, width), BF)],
        cost=0,
    )
    out_far_two = x_swap(after(out_two, dq2_x))
    e0_sib = core_swap(e0)
    do1 = launch(
        mixed_back,
        info,
        (e0, e0_sib, self_o),
        [None] * 3,
        [arr((frames, cols), BF)],
        [None],
    )[0]
    dq1, dk1, dv1 = launch(
        self_backward,
        info,
        (q1, k1, v1, do1, total1),
        [pair_in] * 4 + [level],
        [arr((frames, cols), BF)] * 3,
        [pair_in] * 3,
        grid=(heads,),
        scratch=[pltpu.VMEM((frames, PAIR), F32)] * 3,
        flops=heads * frames * frames * 256 * 5,
        exps=heads * frames * frames,
    )
    da1_own, da1_send = launch(
        first_back,
        info,
        (dq1, dk1, dv1, self_q, self_k, self_v),
        [None] * 6,
        [arr((half, width))] * 2,
        [None] * 2,
        flops=2 * half_mm * 3 * cols,
    )
    pins = []
    if whole:
        ffn = exchange(ffn, orders, 1, da1_own, 4)
        pins = [ffn[1]]
        cross = [(k, after(c, ffn[1])) for k, c in zip(cross[0::2], cross[1::2])]
    da1_sum, grads1 = launch(
        sum_first_grads,
        info,
        (da1_own, after(core_swap(da1_send), *pins), hid),
        [None] * 2 + [own_rows],
        [arr((half, width)), arr((2, width))],
        [None] * 2,
    )

    vectors = (grads1, grads2, grads3)
    if whole:
        stacked = launch(stack_rows, info, vectors, [None] * 3, [arr((8, width))], [None])[0]
        for flip in (1, 3):
            stacked = launch(
                add_two,
                info,
                (stacked, swap(stacked, "tensor", 4, flip)),
                [None] * 2,
                [arr((8, width))],
                [None],
            )[0]
        vectors = (stacked,)
    if not whole:
        stacked = lax.psum(jnp.concatenate(vectors), "tensor")
        stacked = lax.psum_scatter(stacked, "dp", scatter_dimension=1, tiled=True)
        vectors = ()
    self_plan = (
        (order_one, ((0, 0, 256), (1, 256, 512))),
        (order_two, ((1, 0, 256),)),
    )
    own = weight_grads(
        info,
        [
            ([after(e0, da1_sum), e0_sib], [[o1_own], [o1_sib]]),
            ([a1], [[dq1, dk1, dv1]]),
        ],
        self_plan,
        vectors,
    )
    pins = [own[0]]
    if whole:
        own = list(zip(own[0::2], own[1::2]))
    out_final = launch(
        out_sum,
        info,
        (h2, out_two, after(out_far_two, *pins)),
        [None] * 3,
        [arr((half + text_half, width))],
        [None],
        cost=0,
    )[0]
    da1_far = x_swap(after(da1_sum, out_final))
    output, text_grad = launch(
        out_place,
        info,
        (out_final, core_swap(out_final)),
        [None] * 2,
        [arr((frames, width), BF), arr((text_rows, width))],
        [None] * 2,
    )
    pins = []
    if not whole:
        ffn, cross, own = (
            [scatter_sum(*p) for p in zip(g[0::2], g[1::2])] for g in (ffn, cross, own)
        )
        up_grad, down_grad = ffn[0], ffn[1].T
        co_grad, cq_grad = cross[0][:, :256].T, cross[1]
        ck_grad, cv_grad = cross[0][:, 256:512], cross[0][:, 512:]
        so_grad, sq_grad = own[0][:, :256].T, own[1]
        sk_grad, sv_grad = own[0][:, 256:512], own[0][:, 512:]
    if whole:
        cross = exchange(cross, orders, 0, own[0][0], 0)
        ready = (
            swap(cross[0][1], "dp", 8, FLIPS["a"]),
            swap(cross[1][1], "dp", 8, FLIPS["y"]),
        )
        own = [(own[0][0], after(own[0][1], ready[1])), (own[1][0], after(own[1][1], cross[0][1]))]
        up_grad, down_grad = finish(ffn, finish_ffn, cross[0][0], 1)
        cross = exchange(cross, orders, 1, up_grad, 10, ready)
        pins = [cross[1]]
    last = launch(
        last_norm_back,
        info,
        (da1_sum, after(da1_far, *pins), gain1, hid, e0),
        [None] * 3 + [own_rows, None],
        [arr((half, width))],
        [None],
        flops=half_mm * 8,
    )[0]
    if whole:
        own = exchange(own, orders, 0, last)
        cross = (cross[0], after(cross[1], up_grad))
        co_grad, ck_grad, cv_grad, cq_grad = finish(cross, finish_cross, own[0][1])
        own = exchange(own, orders, 1, co_grad)
    hidden_grad = launch(
        place,
        info,
        (last, core_swap(last)),
        [None] * 2,
        [arr((frames, width), BF)],
        [None],
    )[0]
    if whole:
        so_grad, sk_grad, sv_grad, sq_grad, stacked = finish(
            own, finish_self, (hidden_grad, output)
        )
    return (
        output.reshape(hidden.shape),
        hidden_grad.reshape(hidden.shape),
        text_grad.reshape(text_states.shape),
        stacked[0],
        stacked[1],
        sq_grad,
        sk_grad,
        sv_grad,
        so_grad,
        stacked[2],
        stacked[3],
        cq_grad,
        ck_grad,
        cv_grad,
        co_grad,
        stacked[4],
        stacked[5],
        up_grad,
        down_grad,
    )


def solution(mesh):
    rows = P("dp", None, None)
    column, row = P(None, "tensor"), P("tensor", None)
    in_specs = (
        *(rows, rows, P("dp"), P(), P(), column, column, column, row),
        *(P(), P(), column, column, column, row),
        *(P(), P(), column, row, rows),
    )
    vector, down, across = P("dp"), P("dp", "tensor"), P("tensor", "dp")
    out_specs = (
        *(rows, rows, rows, vector, vector, down, down, down, across),
        *(vector, vector, down, down, down, across),
        *(vector, vector, down, across),
    )
    return jax.shard_map(body, mesh=mesh, in_specs=in_specs, out_specs=out_specs, check_vma=False)
```

```python
import functools

import jax
import jax.numpy as jnp
import numpy as np
from jax import lax
from jax.experimental import pallas as pl
from jax.experimental.pallas import tpu as pltpu
from jax.sharding import PartitionSpec as P

HD = 64
EPS = 1e-05
NEG = -1e30
SCALE = HD ** (-0.5)
BF = jnp.bfloat16
F32 = jnp.float32
PAIR = 2 * HD

FLIPS = WEIGHT = {"y": 1, "a": 2, "m": 4}

CORE, PEER, Y, LABEL, TABLE = 0, 1, 2, 3, 8


def index_table(dp_size):
    rows = []
    for me in range(dp_size):
        for t in range(4):
            row = [t & 1, 1 - (t & 1), me & 1, me & 3, 0, 0, 0, 0]
            row += [(me ^ i) if dp_size == 8 else i for i in range(8)]
            rows.append(row)
    return np.array(rows, np.int32)


def dot(left, right):
    return lax.dot_general(left, right, (((1,), (0,)), ((), ())), preferred_element_type=F32)


def against(left, right):
    return lax.dot_general(left, right, (((1,), (1,)), ((), ())), preferred_element_type=F32)


def over_rows(left, right):
    return lax.dot_general(left, right, (((0,), (0,)), ((), ())), preferred_element_type=F32)


def swap(value, axis, size, flip):
    return lax.ppermute(value, axis, [(i, i ^ flip) for i in range(size)])


def core_swap(value):
    return swap(value, "tensor", 4, 1)


def x_swap(value):
    return swap(value, "tensor", 4, 2)


def cross_swap(value):
    return swap(value, "tensor", 4, 3)


def after(value, *others):
    return lax.optimization_barrier((value, *others))[0]


def full(shape):
    return pl.BlockSpec(shape, lambda *_: (0,) * len(shape))


def launch(body, info, args, in_specs, outs, out_specs, grid=(1,), scratch=(), flops=0, exps=0, grant=20, cost=0):
    specs = [full(a.shape) if s is None else s for a, s in zip(args, in_specs)]
    ospecs = [full(o.shape) if s is None else s for o, s in zip(outs, out_specs)]
    return pl.pallas_call(
        body,
        out_shape=list(outs),
        grid_spec=pltpu.PrefetchScalarGridSpec(
            num_scalar_prefetch=1,
            grid=grid,
            in_specs=specs,
            out_specs=ospecs,
            scratch_shapes=list(scratch),
        ),
        compiler_params=pltpu.CompilerParams(vmem_limit_bytes=min(grant, 12) << 20),
        cost_estimate=pl.CostEstimate(
            flops=1 + cost * 10**9, bytes_accessed=1, transcendentals=0
        ),
        name=body.__name__ if hasattr(body, "__name__") else body.func.__name__,
    )(info, *args)


def arr(shape, dtype=F32):
    return jax.ShapeDtypeStruct(shape, dtype)


def normed(values):
    centred = values - jnp.mean(values, -1, keepdims=True)
    inverse = lax.rsqrt(jnp.mean(centred * centred, -1, keepdims=True) + EPS)
    return centred * inverse, inverse


def norm_back(grad, scaled, inverse, gain):
    weighted = grad * gain
    first = jnp.mean(weighted, -1, keepdims=True)
    second = jnp.mean(weighted * scaled, -1, keepdims=True)
    return inverse * (weighted - first - scaled * second)


def head_lanes(odd, dtype):
    lane = lax.broadcasted_iota(jnp.int32, (1, PAIR), 1)
    return ((lane // HD) == odd).astype(dtype)


def norm_project(info, hid, gain, bias, wq, wk, wv, a1, q, k, v):
    scaled, _ = normed(hid[...].astype(F32))
    low = (scaled * gain[...] + bias[...]).astype(BF)
    a1[...] = low
    q[...] = (dot(low, wq[...]) * SCALE).astype(BF)
    k[...] = dot(low, wk[...]).astype(BF)
    v[...] = dot(low, wv[...]).astype(BF)


def text_project(info, text, wk, wv, k, v):
    k[...] = dot(text[...], wk[...]).astype(BF)
    v[...] = dot(text[...], wv[...]).astype(BF)


def blocks_of(rows, step=256):
    return [(s, min(step, rows - s)) for s in range(0, rows, step)]


def causal(scores):
    key = lax.broadcasted_iota(jnp.int32, scores.shape, 0)
    query = lax.broadcasted_iota(jnp.int32, scores.shape, 1)
    return jnp.where(key <= query, scores, NEG)


def self_forward(info, q, k, v, keep, send, total, mixed):
    rows = q.shape[0]
    half = rows // 2
    odd = lax.rem(pl.program_id(0), 2)
    lanes = head_lanes(odd, BF)
    lanes_on = head_lanes(odd, F32) > 0
    for start, size in blocks_of(rows):
        here = slice(start, start + size)
        query = q[here, :] * lanes
        near = causal(against(k[here, :], query))
        top = jnp.max(near, 0, keepdims=True)
        if start:
            far = against(k[:start, :], query)
            top = jnp.maximum(top, jnp.max(far, 0, keepdims=True))
        near = jnp.exp(near - top)
        count = jnp.sum(near, 0, keepdims=True)
        if start:
            far = jnp.exp(far - top)
            count = count + jnp.sum(far, 0, keepdims=True)
        scale = 1.0 / count
        out = over_rows(v[here, :], (near * scale).astype(BF))
        if start:
            out = out + over_rows(v[:start, :], (far * scale).astype(BF))
        total[0, :, here] = top + jnp.log(count)
        mixed[here, :] = jnp.where(lanes_on, out.T, mixed[here, :])

    @pl.when(odd == 1)
    def _():
        keep[...] = mixed[pl.ds(pl.multiple_of(info[CORE] * half, 8), half), :]
        send[...] = mixed[pl.ds(pl.multiple_of(info[PEER] * half, 8), half), :]


def prepare(info, so, co, cq, own, first, later):
    own[0:256, :] = so[...].astype(F32)
    own[256:512, :] = co[...].astype(F32)
    own[512:768, :] = cq[...].astype(F32).T
    first[0:128, :] = own[pl.ds(pl.multiple_of(info[Y] * 128, 8), 128), :]
    at = pl.multiple_of(256 + info[LABEL] * 64, 8)
    first[128:192, :] = own[pl.ds(at, 64), :]
    later[...] = own[pl.ds(at + 256, 64), :]


def stack_two(info, one, two, out):
    rows = one.shape[0]
    out[:rows, :] = one[...]
    out[rows:, :] = two[...]


def mix(info, one, two, w_one, w_two, out):
    out[...] = dot(one[...].astype(BF), w_one[...].astype(BF)) + dot(
        two[...].astype(BF), w_two[...].astype(BF)
    )


def gather_halves(info, far, weights):
    for s in range(2):
        for p in range(2):

            @pl.when(info[Y] == p)
            def _(s=s, p=p):
                weights[s * 256 + p * 128 : s * 256 + p * 128 + 128, :] = far[2 * s][
                    :128, :
                ].astype(BF)

            @pl.when(info[Y] != p)
            def _(s=s, p=p):
                weights[s * 256 + p * 128 : s * 256 + p * 128 + 128, :] = far[2 * s + 1][
                    :128, :
                ].astype(BF)


def gather_quarters(info, far, weights):
    per = len(far) // 2
    for s in range(2):
        refs = far[per * s : per * s + per]
        if per == 3:
            pieces = [refs[0][128:192, :], refs[1][128:192, :]]
        else:
            pieces = [refs[0][:64, :], refs[0][64:, :]]
        pieces += [refs[-1][:64, :], refs[-1][64:, :]]
        for j, piece in enumerate(pieces):
            at = pl.multiple_of(s * 256 + (info[LABEL] ^ j) * 64, 64)
            weights[pl.ds(at, 64), :] = piece.astype(BF)


def mix_far(info, pre, one, two, far, weights, which):
    if which is None:
        gather_halves(info, far, weights)
    else:
        gather_quarters(info, far, weights)
    far_part = dot(one[...].astype(BF), weights[:256, :]) + dot(
        two[...].astype(BF), weights[256:, :]
    )
    return pre[...] + far_part


def mix_norm(which, info, base, pre, one, two, *refs):
    n = 6 if which is None else 5
    far, (gain, bias, resid, low, *packs, weights) = refs[:-n], refs[-n:]
    for pack in packs:
        for j in range(2):
            pack[j * 64 : j * 64 + 64, :] = far[2 + j][128:192, :]
    part = mix_far(info, pre, one, two, far, weights, which)
    total = base[...].astype(F32) + part
    resid[...] = total
    scaled, _ = normed(total)
    low[...] = scaled * gain[...] + bias[...]


def mix_norm_back(info, pre, one, two, *refs):
    far, (gain, resid, e_in, e_out, grads, weights) = refs[:-6], refs[-6:]
    grad = mix_far(info, pre, one, two, far, weights, 64)
    scaled, inverse = normed(resid[...])
    e_out[...] = e_in[...] + norm_back(grad, scaled, inverse, gain[...])
    grads[0:1, :] = jnp.sum(grad * scaled, 0, keepdims=True) * 0.5
    grads[1:2, :] = jnp.sum(grad, 0, keepdims=True) * 0.5


def sum_norm_back(info, mine, far, gain, resid, e_in, e_out, grads):
    grad = mine[...] + far[...]
    scaled, inverse = normed(resid[...])
    e_out[...] = e_in[...].astype(F32) + norm_back(grad, scaled, inverse, gain[...])
    grads[0:1, :] = jnp.sum(grad * scaled, 0, keepdims=True) * 0.5
    grads[1:2, :] = jnp.sum(grad, 0, keepdims=True) * 0.5


def sum_first_grads(info, mine, recv, hid, out, grads):
    grad = mine[...] + recv[...]
    out[...] = grad
    scaled, _ = normed(hid[...].astype(F32))
    grads[0:1, :] = jnp.sum(grad * scaled, 0, keepdims=True)
    grads[1:2, :] = jnp.sum(grad, 0, keepdims=True)


def last_norm_back(info, mine, far, gain, hid, e_in, out):
    grad = mine[...] + far[...]
    scaled, inverse = normed(hid[...].astype(F32))
    out[...] = e_in[...] + norm_back(grad, scaled, inverse, gain[...])


def cross_forward(info, length, a2, wq, k, v, q, mixed, total):
    query_rows = (dot(a2[...].astype(BF), wq[...]) * SCALE).astype(BF)
    q[...] = query_rows
    for pair in range(2):
        cols = slice(pair * PAIR, (pair + 1) * PAIR)
        pair_out = None
        for odd in range(2):
            query = query_rows[:, cols] * head_lanes(odd, BF)
            scores = against(k[:, cols], query)
            slot = lax.broadcasted_iota(jnp.int32, scores.shape, 0)
            scores = jnp.where(slot < length[0], scores, NEG)
            top = jnp.max(scores, 0, keepdims=True)
            scores = jnp.exp(scores - top)
            count = jnp.sum(scores, 0, keepdims=True)
            out = over_rows(v[:, cols], (scores * (1.0 / count)).astype(BF)).T
            total[pair * 2 + odd] = top + jnp.log(count)
            pair_out = out if odd == 0 else jnp.where(head_lanes(1, F32) > 0, out, pair_out)
        mixed[:, cols] = pair_out


def feed_forward(info, a3, cot, up, down, g, du, da3):
    n = pl.program_id(0)
    u = dot(a3[...].astype(BF), up[...])
    cdf = 0.5 + 0.5 * lax.erf(u * (0.5**0.5))
    g[...] = (u * cdf).astype(BF)
    slope = cdf + u * jnp.exp(-0.5 * u * u) * (1.0 / (2.0 * np.pi) ** 0.5)
    dg = against(cot[...], down[...]).astype(BF).astype(F32)
    low = (dg * slope).astype(BF)
    du[...] = low
    part = against(low, up[...])

    @pl.when(n == 0)
    def _():
        da3[...] = part

    @pl.when(n > 0)
    def _():
        da3[...] += part


def stack_rows(info, one, two, three, out):
    for i, ref in enumerate((one, two, three)):
        out[2 * i : 2 * i + 2, :] = ref[...]
    out[6:, :] = jnp.zeros((2, out.shape[1]), F32)


def add_two(info, one, two, out):
    out[...] = one[...] + two[...]


def down_project(info, own, sib, down, out_own, out_sib):
    out_own[...] = dot(own[...], down[...])
    out_sib[...] = dot(sib[...], down[...])


def cross_backward(second, info, length, e1, wo, q, k, v, total, *rest):
    if second:
        dk_in, dv_in, dq, dk_out, dv_out = rest
    else:
        dq, dk_out, dv_out = rest
    mixed_grad = against(e1[...].astype(BF), wo[...]).astype(BF)
    for pair in range(2):
        cols = slice(pair * PAIR, (pair + 1) * PAIR)
        dk = dk_in[:, cols] if second else None
        dv = dv_in[:, cols] if second else None
        pair_dq = None
        for odd in range(2):
            lanes = head_lanes(odd, BF)
            query = q[:, cols] * lanes
            grad = mixed_grad[:, cols] * lanes
            scores = against(k[:, cols], query)
            slot = lax.broadcasted_iota(jnp.int32, scores.shape, 0)
            scores = jnp.where(slot < length[0], scores, NEG)
            probs = jnp.exp(scores - total[pair * 2 + odd])
            prob_grad = against(v[:, cols], grad)
            part = dot(probs.astype(BF), grad)
            dv = part if dv is None else dv + part
            delta = jnp.sum(probs * prob_grad, 0, keepdims=True)
            low = (probs * (prob_grad - delta)).astype(BF)
            part = dot(low, query)
            dk = part if dk is None else dk + part
            out = over_rows(k[:, cols], low).T
            pair_dq = out if odd == 0 else jnp.where(head_lanes(1, F32) > 0, out, pair_dq)
        dq[:, cols] = pair_dq * SCALE
        dk_out[:, cols] = dk.astype(dk_out.dtype)
        dv_out[:, cols] = dv.astype(dv_out.dtype)


def text_back(info, dk, dv, wk, wv, own, send, scratch):
    half = own.shape[0]
    scratch[...] = against(dk[...], wk[...]) + against(dv[...], wv[...])
    own[...] = scratch[pl.ds(pl.multiple_of(info[CORE] * half, 8), half), :]
    send[...] = scratch[pl.ds(pl.multiple_of(info[PEER] * half, 8), half), :]


def mixed_back(info, own, sib, wo, out):
    half = own.shape[0]
    out[pl.ds(pl.multiple_of(info[CORE] * half, 16), half), :] = against(
        own[...].astype(BF), wo[...]
    ).astype(BF)
    out[pl.ds(pl.multiple_of(info[PEER] * half, 16), half), :] = against(
        sib[...].astype(BF), wo[...]
    ).astype(BF)


def self_backward(info, q, k, v, grad_in, total, dq, dk, dv, dq_sum, dk_sum, dv_sum):
    rows = q.shape[0]
    odd = lax.rem(pl.program_id(0), 2)
    lanes = head_lanes(odd, BF)
    lanes_on = head_lanes(odd, F32) > 0

    @pl.when(odd == 0)
    def _():
        dk_sum[...] = jnp.zeros_like(dk_sum)
        dv_sum[...] = jnp.zeros_like(dv_sum)

    for start, size in blocks_of(rows):
        here = slice(start, start + size)
        query = q[here, :] * lanes
        grad = grad_in[here, :] * lanes
        level = total[0, :, here]
        near = jnp.exp(causal(against(k[here, :], query)) - level)
        near_grad = against(v[here, :], grad)
        delta = jnp.sum(near * near_grad, 0, keepdims=True)
        dv_sum[here, :] += dot(near.astype(BF), grad)
        if start:
            far = jnp.exp(against(k[:start, :], query) - level)
            far_grad = against(v[:start, :], grad)
            delta = delta + jnp.sum(far * far_grad, 0, keepdims=True)
            dv_sum[:start, :] += dot(far.astype(BF), grad)
        near_low = (near * (near_grad - delta)).astype(BF)
        dk_sum[here, :] += dot(near_low, query)
        out = over_rows(k[here, :], near_low)
        if start:
            far_low = (far * (far_grad - delta)).astype(BF)
            dk_sum[:start, :] += dot(far_low, query)
            out = out + over_rows(k[:start, :], far_low)
        dq_sum[here, :] = jnp.where(lanes_on, out.T * SCALE, dq_sum[here, :])

    @pl.when(odd == 1)
    def _():
        dq[...] = dq_sum[...].astype(BF)
        dk[...] = dk_sum[...].astype(BF)
        dv[...] = dv_sum[...].astype(BF)


def first_back(info, dq, dk, dv, wq, wk, wv, own, send):
    half = own.shape[0]
    for at, out in ((PEER, send), (CORE, own)):
        here = pl.ds(pl.multiple_of(info[at] * half, 16), half)
        out[...] = (
            against(dq[here, :], wq[...])
            + against(dk[here, :], wk[...])
            + against(dv[here, :], wv[...])
        )


def weight_grad(plan, shapes, n_v, info, *refs):
    at = 0
    groups = []
    for n_left, n_right in shapes:
        groups.append((refs[at : at + n_left], refs[at + n_left : at + n_left + n_right]))
        at += n_left + n_right
    vectors = refs[at : at + n_v]
    outs = refs[at + n_v : at + n_v + 2 * len(plan)]
    lhs, rhs = refs[-2:]
    for g, (lefts, rights) in enumerate(groups):
        row = 0
        per = len(rights) // len(lefts)
        for i, left in enumerate(lefts):
            rows = left.shape[0]
            for j in range(8):
                block = left[:, pl.ds(pl.multiple_of(info[TABLE + j] * 128, 128), 128)]
                lhs[row : row + rows, j * 128 : (j + 1) * 128] = block.astype(BF)
            col = 0
            for right in rights[i * per : (i + 1) * per]:
                rhs[row : row + rows, col : col + right.shape[1]] = right[...].astype(BF)
                col += right.shape[1]
            row += rows
        for s, (order, segments) in enumerate(plan):
            put = 0
            for group, first, width in segments:
                if group == g:
                    for half in range(2):
                        value = over_rows(
                            lhs[:row, half * 512 : half * 512 + 512],
                            rhs[:row, first : first + width],
                        )
                        for q in range(4):
                            j = half * 4 + q
                            sent, pos = spot(order, j)
                            outs[2 * s + sent][pos, :128, put : put + width] = value[
                                q * 128 : (q + 1) * 128, :
                            ]
                put += width
    if n_v:
        for j in range(8):
            sent, pos = spot(plan[-1][0], j)
            out = outs[2 * len(plan) - 2 + sent]
            out[pos, 128:, :] = jnp.zeros((8, out.shape[2]), F32)
            block = vectors[0][:, pl.ds(pl.multiple_of(info[TABLE + j] * 128, 128), 128)]
            out[pos, 128:, :128] = block


def spot(order, j):
    bits = [(j // WEIGHT[name]) & 1 for name in order]
    return bits[0], bits[1] * 2 + bits[2]


def weight_grads(info, groups, plan, vectors=()):
    args, specs, shapes = [], [], []
    for lefts, rights in groups:
        flat = [r for group in rights for r in group]
        for left in lefts:
            array, spec = left if isinstance(left, tuple) else (left, None)
            args.append(array)
            specs.append(spec)
        args += flat
        specs += [None] * len(flat)
        shapes.append((len(lefts), len(flat)))
    args += vectors
    specs += [None] * len(vectors)
    outs = []
    for s, (order, segments) in enumerate(plan):
        tall = 136 if vectors and s == len(plan) - 1 else 128
        outs += [arr((4, tall, sum(w for _, _, w in segments)))] * 2
    rows = max(sum(group[0].shape[0] for group in rights) for _, rights in groups)
    wide = max(sum(r.shape[1] for r in rights[0]) for _, rights in groups)
    return launch(
        functools.partial(weight_grad, plan, tuple(shapes), len(vectors)),
        info,
        tuple(args),
        specs,
        outs,
        [None] * len(outs),
        scratch=[pltpu.VMEM((rows, 1024), BF), pltpu.VMEM((rows, wide), BF)],
        grant=40,
    )


def scatter_sum(keep, send):
    value = jnp.concatenate([keep, send])
    value = value.reshape(-1, value.shape[-1])
    return lax.psum_scatter(value, "dp", scatter_dimension=0, tiled=True)


def fold(info, *refs):
    for i in range(2):
        keep, got = refs[2 * i : 2 * i + 2]
        keep_out, send_out = refs[4 + 2 * i : 6 + 2 * i]
        n = keep_out.shape[0]
        keep_out[...] = keep[:n] + got[:n]
        send_out[...] = keep[n:] + got[n:]


def fold_one(info, keep, got, keep_out, send_out):
    keep_out[...] = keep[0] + got[0]
    send_out[...] = keep[1] + got[1]


def fold_last(info, *refs):
    keep_out, send_out = refs[4:]
    col = 0
    for i in range(2):
        keep, got = refs[2 * i : 2 * i + 2]
        rows, wide = keep.shape[1:]
        keep_out[:rows, col : col + wide] = keep[0] + got[0]
        send_out[:rows, col : col + wide] = keep[1] + got[1]
        col += wide


def finish_ffn(info, keep, got, up, down):
    wide = up.shape[1]
    up[...] = keep[:, :wide] + got[:, :wide]
    down[...] = (keep[:, wide:] + got[:, wide:]).T


def finish_cross(info, keep, got, co, ck, cv, cq):
    co[...] = (keep[:, :256] + got[:, :256]).T
    for i, out in enumerate((ck, cv, cq)):
        here = slice(256 * i + 256, 256 * i + 512)
        out[...] = keep[:, here] + got[:, here]


def finish_self(info, keep, got, so, sk, sv, sq, vectors):
    so[...] = (keep[:128, :256] + got[:128, :256]).T
    for i, out in enumerate((sk, sv, sq)):
        here = slice(256 * i + 256, 256 * i + 512)
        out[...] = keep[:128, here] + got[:128, here]
    vectors[...] = keep[128:, 768:896] + got[128:, 768:896]


FINISH = {
    finish_ffn: [(128, 1024), (1024, 128)],
    finish_cross: [(256, 128), (128, 256), (128, 256), (128, 256)],
    finish_self: [(256, 128), (128, 256), (128, 256), (128, 256), (8, 128)],
}


def exchange(streams, orders, step, first=None, cost=10, ready=()):
    args = []
    for i, ((keep, send), order) in enumerate(zip(streams, orders)):
        got = ready[i] if ready else swap(send, "dp", 8, FLIPS[order[step]])
        args += [keep, got if first is None else after(got, first)]
    none = jnp.zeros((1,), jnp.int32)
    if step == 1:
        shape = (max(a.shape[1] for a in args), args[0].shape[2] + args[2].shape[2])
        return launch(
            fold_last, none, args, [None] * 4, [arr(shape)] * 2, [None] * 2, cost=cost
        )
    outs = []
    for keep, _ in streams:
        outs += [arr((keep.shape[0] // 2, *keep.shape[1:]))] * 2
    out = launch(fold, none, args, [None] * 4, outs, [None] * 4, cost=cost)
    return list(zip(out[0::2], out[1::2]))


def fold_stream(pair, name, first, cost=0):
    keep, send = pair
    got = after(swap(send, "dp", 8, FLIPS[name]), first)
    none = jnp.zeros((1,), jnp.int32)
    outs = [arr(keep.shape[1:])] * 2
    return launch(fold_one, none, (keep, got), [None] * 2, outs, [None] * 2, cost=cost)


def finish(pair, body, first=None, cost=10):
    keep, send = pair
    got = swap(send, "dp", 8, FLIPS["m"])
    got = got if first is None else after(got, first)
    outs = [arr(shape) for shape in FINISH[body]]
    none = jnp.zeros((1,), jnp.int32)
    return launch(body, none, (keep, got), [None] * 2, outs, [None] * len(outs), cost=cost)


def sent(streams):
    return [s for _, s in streams]


def out_second(info, own, got, text_own, text_got, out):
    half = own.shape[0]
    out[:half, :] = own[...] + got[...]
    out[half:, :] = text_own[...] + text_got[...]


def out_sum(info, resid, mine, far, out):
    half = resid.shape[0]
    out[:half, :] = resid[...] + (mine[:half, :] + far[:half, :])
    out[half:, :] = mine[half:, :] + far[half:, :]


def out_place(info, own, sib, out, text_out):
    half = out.shape[0] // 2
    text_half = text_out.shape[0] // 2
    for at, ref in ((CORE, own), (PEER, sib)):
        out[pl.ds(pl.multiple_of(info[at] * half, 16), half), :] = ref[:half, :].astype(BF)
        spot = pl.multiple_of(info[at] * text_half, 8)
        text_out[pl.ds(spot, text_half), :] = ref[half:, :]


def place(info, own, sib, out):
    half = out.shape[0] // 2
    for at, ref in ((CORE, own), (PEER, sib)):
        out[pl.ds(pl.multiple_of(info[at] * half, 16), half), :] = ref[...].astype(BF)


def body(
    hidden,
    text_states,
    text_len,
    ln1_gain,
    ln1_bias,
    self_q,
    self_k,
    self_v,
    self_o,
    ln2_gain,
    ln2_bias,
    cross_q,
    cross_k,
    cross_v,
    cross_o,
    ln3_gain,
    ln3_bias,
    ffn_up,
    ffn_down,
    cotangent,
):
    dp_size = lax.axis_size("dp")
    frames, width = hidden.shape[1:]
    text_rows = text_states.shape[1]
    cols = self_q.shape[1]
    inner = ffn_up.shape[1]
    half = frames // 2
    device = lax.axis_index("dp") * 4 + lax.axis_index("tensor")
    table = jnp.asarray(index_table(dp_size))
    info = lax.dynamic_index_in_dim(table, device, 0, keepdims=False)
    hid = hidden.reshape(frames, width)
    cot = cotangent.reshape(frames, width)
    text = text_states.reshape(text_rows, width)
    gain1, bias1 = ln1_gain.reshape(1, width), ln1_bias.reshape(1, width)
    gain2, bias2 = ln2_gain.reshape(1, width), ln2_bias.reshape(1, width)
    gain3, bias3 = ln3_gain.reshape(1, width), ln3_bias.reshape(1, width)
    own_rows = pl.BlockSpec((half, width), lambda i, table: (table[CORE], 0))
    sib_rows = pl.BlockSpec((half, width), lambda i, table: (table[PEER], 0))
    half_mm = 2 * half * width
    whole = dp_size == 8
    orders = ("yam", "aym") if whole else ("may",) * 2
    order_one, order_two = orders

    own3, first, later = launch(
        prepare,
        info,
        (self_o, cross_o, cross_q),
        [None] * 3,
        [arr((3 * cols, width)), arr((3 * cols // 4, width)), arr((cols // 4, width))],
        [None] * 3,
        flops=1 << 20,
    )
    far_one = cross_swap(first)
    far_later = cross_swap(later)
    sib3 = core_swap(own3)

    def weight_at(i):
        return pl.BlockSpec((cols, width), lambda *_: (i, 0))

    step = frames // 4
    a1, q1, k1, v1 = launch(
        norm_project,
        info,
        (after(hid, first), gain1, bias1, self_q, self_k, self_v),
        [pl.BlockSpec((step, width), lambda i, _: (i, 0))] + [None] * 5,
        [arr((frames, width), BF)] + [arr((frames, cols), BF)] * 3,
        [pl.BlockSpec((step, width), lambda i, _: (i, 0))]
        + [pl.BlockSpec((step, cols), lambda i, _: (i, 0))] * 3,
        grid=(4,),
        flops=2 * frames * width * cols * 3,
    )
    heads = cols // HD
    pair_in = pl.BlockSpec((frames, PAIR), lambda h, _: (0, h // 2))
    pair_half = pl.BlockSpec((half, PAIR), lambda h, _: (0, h // 2))
    level = pl.BlockSpec((1, 1, frames), lambda h, _: (h, 0, 0))
    o1_own, o1_sib, total1 = launch(
        self_forward,
        info,
        (q1, k1, v1),
        [pair_in] * 3,
        [arr((half, cols))] * 2 + [arr((heads, 1, frames))],
        [pair_half] * 2 + [level],
        grid=(heads,),
        scratch=[pltpu.VMEM((frames, PAIR), F32)],
        flops=heads * frames * frames * 512,
        exps=heads * frames * frames,
    )
    o1_cross = cross_swap(after(o1_sib, far_one))
    o1_core = core_swap(after(o1_sib, sib3))
    o1_x = x_swap(o1_own)
    far_two = swap(after(far_one, o1_own), "dp", dp_size, FLIPS["y"])
    k2, v2 = launch(
        text_project,
        info,
        (after(text, o1_own), cross_k, cross_v),
        [None] * 3,
        [arr((text_rows, cols), BF)] * 2,
        [None] * 2,
        flops=2 * text_rows * width * cols * 2,
    )

    def mixed(one, two, i):
        return launch(
            mix,
            info,
            (one, two, own3, sib3),
            [None] * 2 + [weight_at(i)] * 2,
            [arr((half, width))],
            [None],
            flops=half_mm * 512,
        )[0]

    pre1 = mixed(after(o1_own, k2), o1_core, 0)
    far_one_core = core_swap(after(far_one, o1_core))
    far_two_core = core_swap(after(far_two, o1_x, o1_cross, pre1, far_later))
    far_weights = (far_one_core, far_two_core, far_one, far_two)

    def normed_mix(which, base, spec, pre, one, two, weights, gain, bias, packs=0):
        return launch(
            functools.partial(mix_norm, which),
            info,
            (base, pre, one, two, *weights, gain, bias),
            [spec] + [None] * (5 + len(weights)),
            [arr((half, width))] * 2 + [arr((cols // 2, width))] * packs,
            [None] * (2 + packs),
            scratch=[pltpu.VMEM((2 * cols, width), BF)],
            cost=2,
        )

    h1, a2, pack_co = normed_mix(None, hid, own_rows, pre1, o1_x, o1_cross, far_weights, gain2, bias2, 1)
    a2_sib = core_swap(a2)

    smem = pl.BlockSpec(memory_space=pltpu.SMEM)

    def cross(a):
        return launch(
            cross_forward,
            info,
            (text_len, a, cross_q, k2, v2),
            [smem] + [None] * 4,
            [arr((half, cols), BF), arr((half, cols)), arr((heads, 1, half))],
            [None] * 3,
            flops=half_mm * cols + heads * half * text_rows * 512,
            exps=heads * half * text_rows,
        )

    q2_own, o2_own, total2_own = cross(a2)
    o2_x = x_swap(after(o2_own, o1_x))
    q2_sib, o2_sib, total2_sib = cross(after(a2_sib, q2_own))
    o2_cross = cross_swap(after(o2_sib, o1_cross))
    o2_core = core_swap(o2_sib)
    far_co = swap(pack_co, "dp", dp_size, FLIPS["a"])
    next_later = swap(after(far_later, a2), "dp", dp_size, FLIPS["y"])
    pack_cq = launch(
        stack_two,
        info,
        (far_later, after(next_later, o2_sib)),
        [None] * 2,
        [arr((cols // 2, width))],
        [None],
    )[0]
    far_cq = swap(pack_cq, "dp", dp_size, FLIPS["a"])
    pre2 = mixed(after(o2_own, pack_cq), o2_core, 1)
    far_co_core = core_swap(after(far_co, o2_x, o2_cross, far_cq, pre2))
    co_weights = (
        *(far_one_core, far_two_core, far_co_core),
        *(far_one, far_two, far_co),
    )
    h2, a3 = normed_mix(0, h1, None, pre2, o2_x, o2_cross, co_weights, gain3, bias3)
    a3_sib = core_swap(a3)
    far_cq_core = core_swap(after(far_cq, a3))
    pack_cq_core = core_swap(after(pack_cq, pre2))

    unit = 256

    def feed(a, rows):
        return launch(
            feed_forward,
            info,
            (a, cot, ffn_up, ffn_down),
            [
                None,
                rows,
                pl.BlockSpec((width, unit), lambda i, _: (0, i)),
                pl.BlockSpec((unit, width), lambda i, _: (i, 0)),
            ],
            [arr((half, inner), BF)] * 2 + [arr((half, width))],
            [pl.BlockSpec((half, unit), lambda i, _: (0, i))] * 2 + [None],
            grid=(inner // unit,),
            flops=half_mm * inner * 3,
            exps=half * inner * 2,
        )

    g_own, du_own, da3_own = feed(a3, own_rows)
    g_sib, du_sib, da3_sib = feed(after(a3_sib, g_own, far_cq_core), sib_rows)
    da3_sum = launch(
        add_two,
        info,
        (da3_own, core_swap(da3_sib)),
        [None] * 2,
        [arr((half, width))],
        [None],
    )[0]
    da3_far = x_swap(after(da3_sum, o2_x))
    ffn_plan = (
        (order_one, ((0, 0, 1024),)),
        (order_two, ((1, 0, 1024),)),
    )
    ffn = weight_grads(
        info,
        [
            ([after(a3, da3_sum), a3_sib], [[du_own], [du_sib]]),
            ([(cot, own_rows), (cot, sib_rows)], [[g_own], [g_sib]]),
        ],
        ffn_plan,
    )
    out_own, out_sib = launch(
        down_project,
        info,
        (after(g_own, *ffn[1::2]), g_sib, ffn_down),
        [None, None, pl.BlockSpec((inner, 512), lambda i, _: (0, i))],
        [arr((half, width))] * 2,
        [pl.BlockSpec((half, 512), lambda i, _: (0, i))] * 2,
        grid=(width // 512,),
        flops=2 * half_mm * inner,
    )
    out_got = core_swap(out_sib)
    e1, grads3 = launch(
        sum_norm_back,
        info,
        (da3_sum, after(da3_far, out_own), gain3, h2, cot),
        [None] * 4 + [own_rows],
        [arr((half, width)), arr((2, width))],
        [None] * 2,
    )
    e1_sib = core_swap(e1)
    def cross_back(e, q, total, sums):
        last = bool(sums)
        return launch(
            functools.partial(cross_backward, last),
            info,
            (text_len, e, cross_o, q, k2, v2, total, *sums),
            [smem] + [None] * (6 + len(sums)),
            [arr((half, cols))] + [arr((text_rows, cols), BF if last else F32)] * 2,
            [None] * 3,
        )

    dq2_own, *sums = cross_back(after(e1, out_got), q2_own, total2_own, ())
    dq2_sib, dk2, dv2 = cross_back(e1_sib, q2_sib, total2_sib, tuple(sums))
    dq2_cross = cross_swap(dq2_sib)
    dq2_core = core_swap(dq2_sib)
    dq2_x = x_swap(after(dq2_own, da3_far))
    pre3 = mixed(dq2_own, dq2_core, 2)
    cq_weights = (pack_cq_core, far_cq_core, pack_cq, far_cq)

    text_half = text_rows // 2
    text_own, text_send = launch(
        text_back,
        info,
        (dk2, dv2, cross_k, cross_v),
        [None] * 4,
        [arr((text_half, width))] * 2,
        [None] * 2,
        scratch=[pltpu.VMEM((text_rows, width), F32)],
        flops=2 * text_rows * width * cols * 2,
    )
    text_got = core_swap(text_send)
    out_two = launch(
        out_second,
        info,
        (out_own, out_got, text_own, text_got),
        [None] * 4,
        [arr((half + text_half, width))],
        [None],
    )[0]
    cross_plan = (
        (order_one, ((0, 0, 256), (2, 0, 512))),
        (order_two, ((1, 0, 256),)),
    )
    cross = weight_grads(
        info,
        [
            ([e1, e1_sib], [[o2_own], [o2_sib]]),
            ([a2, a2_sib], [[dq2_own], [dq2_sib]]),
            ([text], [[dk2, dv2]]),
        ],
        cross_plan,
    )
    pins = [out_two]
    if whole:
        ffn = exchange(list(zip(ffn[0::2], ffn[1::2])), orders, 0, cross[0], 12)
        pins += sent(ffn)
    e0, grads2 = launch(
        mix_norm_back,
        info,
        (after(pre3, *pins), dq2_x, dq2_cross, *cq_weights, gain2, h1, e1),
        [None] * (6 + len(cq_weights)),
        [arr((half, width)), arr((2, width))],
        [None] * 2,
        scratch=[pltpu.VMEM((2 * cols, width), BF)],
        cost=0,
    )
    out_far_two = x_swap(after(out_two, dq2_x))
    e0_sib = core_swap(e0)
    do1 = launch(
        mixed_back,
        info,
        (e0, e0_sib, self_o),
        [None] * 3,
        [arr((frames, cols), BF)],
        [None],
    )[0]
    dq1, dk1, dv1 = launch(
        self_backward,
        info,
        (q1, k1, v1, do1, total1),
        [pair_in] * 4 + [level],
        [arr((frames, cols), BF)] * 3,
        [pair_in] * 3,
        grid=(heads,),
        scratch=[pltpu.VMEM((frames, PAIR), F32)] * 3,
        flops=heads * frames * frames * 256 * 5,
        exps=heads * frames * frames,
    )
    da1_own, da1_send = launch(
        first_back,
        info,
        (dq1, dk1, dv1, self_q, self_k, self_v),
        [None] * 6,
        [arr((half, width))] * 2,
        [None] * 2,
        flops=2 * half_mm * 3 * cols,
    )
    pins = []
    if whole:
        ffn = exchange(ffn, orders, 1, da1_own, 4)
        pins = [ffn[1]]
        cross = [(k, after(c, ffn[1])) for k, c in zip(cross[0::2], cross[1::2])]
    da1_sum, grads1 = launch(
        sum_first_grads,
        info,
        (da1_own, after(core_swap(da1_send), *pins), hid),
        [None] * 2 + [own_rows],
        [arr((half, width)), arr((2, width))],
        [None] * 2,
    )

    vectors = (grads1, grads2, grads3)
    if whole:
        stacked = launch(stack_rows, info, vectors, [None] * 3, [arr((8, width))], [None])[0]
        for flip in (1, 3):
            stacked = launch(
                add_two,
                info,
                (stacked, swap(stacked, "tensor", 4, flip)),
                [None] * 2,
                [arr((8, width))],
                [None],
            )[0]
        vectors = (stacked,)
    if not whole:
        stacked = lax.psum(jnp.concatenate(vectors), "tensor")
        stacked = lax.psum_scatter(stacked, "dp", scatter_dimension=1, tiled=True)
        vectors = ()
    self_plan = (
        (order_one, ((0, 0, 256), (1, 256, 512))),
        (order_two, ((1, 0, 256),)),
    )
    own = weight_grads(
        info,
        [
            ([after(e0, da1_sum), e0_sib], [[o1_own], [o1_sib]]),
            ([a1], [[dq1, dk1, dv1]]),
        ],
        self_plan,
        vectors,
    )
    pins = [own[0]]
    if whole:
        own = list(zip(own[0::2], own[1::2]))
    out_final = launch(
        out_sum,
        info,
        (h2, out_two, after(out_far_two, *pins)),
        [None] * 3,
        [arr((half + text_half, width))],
        [None],
        cost=0,
    )[0]
    da1_far = x_swap(after(da1_sum, out_final))
    output, text_grad = launch(
        out_place,
        info,
        (out_final, core_swap(out_final)),
        [None] * 2,
        [arr((frames, width), BF), arr((text_rows, width))],
        [None] * 2,
    )
    pins = []
    if not whole:
        ffn, cross, own = (
            [scatter_sum(*p) for p in zip(g[0::2], g[1::2])] for g in (ffn, cross, own)
        )
        up_grad, down_grad = ffn[0], ffn[1].T
        co_grad, cq_grad = cross[0][:, :256].T, cross[1]
        ck_grad, cv_grad = cross[0][:, 256:512], cross[0][:, 512:]
        so_grad, sq_grad = own[0][:, :256].T, own[1]
        sk_grad, sv_grad = own[0][:, 256:512], own[0][:, 512:]
    if whole:
        cross = exchange(cross, orders, 0, own[0][0], 0)
        ready = (
            swap(cross[0][1], "dp", 8, FLIPS["a"]),
            swap(cross[1][1], "dp", 8, FLIPS["y"]),
        )
        own = [(own[0][0], after(own[0][1], ready[1])), (own[1][0], after(own[1][1], cross[0][1]))]
        up_grad, down_grad = finish(ffn, finish_ffn, cross[0][0], 1)
        cross = exchange(cross, orders, 1, up_grad, 10, ready)
        pins = [cross[1]]
    last = launch(
        last_norm_back,
        info,
        (da1_sum, after(da1_far, *pins), gain1, hid, e0),
        [None] * 3 + [own_rows, None],
        [arr((half, width))],
        [None],
        flops=half_mm * 8,
    )[0]
    if whole:
        own = exchange(own, orders, 0, last)
        cross = (cross[0], after(cross[1], up_grad))
        co_grad, ck_grad, cv_grad, cq_grad = finish(cross, finish_cross, own[0][1])
        own = exchange(own, orders, 1, co_grad)
    hidden_grad = launch(
        place,
        info,
        (last, core_swap(last)),
        [None] * 2,
        [arr((frames, width), BF)],
        [None],
    )[0]
    if whole:
        so_grad, sk_grad, sv_grad, sq_grad, stacked = finish(
            own, finish_self, (hidden_grad, output)
        )
    return (
        output.reshape(hidden.shape),
        hidden_grad.reshape(hidden.shape),
        text_grad.reshape(text_states.shape),
        stacked[0],
        stacked[1],
        sq_grad,
        sk_grad,
        sv_grad,
        so_grad,
        stacked[2],
        stacked[3],
        cq_grad,
        ck_grad,
        cv_grad,
        co_grad,
        stacked[4],
        stacked[5],
        up_grad,
        down_grad,
    )


def solution(mesh):
    rows = P("dp", None, None)
    column, row = P(None, "tensor"), P("tensor", None)
    in_specs = (
        *(rows, rows, P("dp"), P(), P(), column, column, column, row),
        *(P(), P(), column, column, column, row),
        *(P(), P(), column, row, rows),
    )
    vector, down, across = P("dp"), P("dp", "tensor"), P("tensor", "dp")
    out_specs = (
        *(rows, rows, rows, vector, vector, down, down, down, across),
        *(vector, vector, down, down, down, across),
        *(vector, vector, down, across),
    )
    return jax.shard_map(body, mesh=mesh, in_specs=in_specs, out_specs=out_specs, check_vma=False)
```

```python
import functools

import jax
import jax.numpy as jnp
import numpy as np
from jax import lax
from jax.experimental import pallas as pl
from jax.experimental.pallas import tpu as pltpu
from jax.sharding import PartitionSpec as P

HD = 64
EPS = 1e-05
NEG = -1e30
SCALE = HD ** (-0.5)
BF = jnp.bfloat16
F32 = jnp.float32
PAIR = 2 * HD

FLIPS = WEIGHT = {"y": 1, "a": 2, "m": 4}

CORE, PEER, Y, LABEL, TABLE = 0, 1, 2, 3, 8


def index_table(dp_size):
    rows = []
    for me in range(dp_size):
        for t in range(4):
            row = [t & 1, 1 - (t & 1), me & 1, me & 3, 0, 0, 0, 0]
            row += [(me ^ i) if dp_size == 8 else i for i in range(8)]
            rows.append(row)
    return np.array(rows, np.int32)


def dot(left, right):
    return lax.dot_general(left, right, (((1,), (0,)), ((), ())), preferred_element_type=F32)


def against(left, right):
    return lax.dot_general(left, right, (((1,), (1,)), ((), ())), preferred_element_type=F32)


def over_rows(left, right):
    return lax.dot_general(left, right, (((0,), (0,)), ((), ())), preferred_element_type=F32)


def swap(value, axis, size, flip):
    return lax.ppermute(value, axis, [(i, i ^ flip) for i in range(size)])


def core_swap(value):
    return swap(value, "tensor", 4, 1)


def x_swap(value):
    return swap(value, "tensor", 4, 2)


def cross_swap(value):
    return swap(value, "tensor", 4, 3)


def after(value, *others):
    return lax.optimization_barrier((value, *others))[0]


def full(shape):
    return pl.BlockSpec(shape, lambda *_: (0,) * len(shape))


def launch(body, info, args, in_specs, outs, out_specs, grid=(1,), scratch=(), flops=0, exps=0, grant=20, cost=0):
    specs = [full(a.shape) if s is None else s for a, s in zip(args, in_specs)]
    ospecs = [full(o.shape) if s is None else s for o, s in zip(outs, out_specs)]
    return pl.pallas_call(
        body,
        out_shape=list(outs),
        grid_spec=pltpu.PrefetchScalarGridSpec(
            num_scalar_prefetch=1,
            grid=grid,
            in_specs=specs,
            out_specs=ospecs,
            scratch_shapes=list(scratch),
        ),
        compiler_params=pltpu.CompilerParams(vmem_limit_bytes=min(grant, 12) << 20),
        cost_estimate=pl.CostEstimate(
            flops=1 + cost * 10**9, bytes_accessed=1, transcendentals=0
        ),
        name=body.__name__ if hasattr(body, "__name__") else body.func.__name__,
    )(info, *args)


def arr(shape, dtype=F32):
    return jax.ShapeDtypeStruct(shape, dtype)


def normed(values):
    centred = values - jnp.mean(values, -1, keepdims=True)
    inverse = lax.rsqrt(jnp.mean(centred * centred, -1, keepdims=True) + EPS)
    return centred * inverse, inverse


def norm_back(grad, scaled, inverse, gain):
    weighted = grad * gain
    first = jnp.mean(weighted, -1, keepdims=True)
    second = jnp.mean(weighted * scaled, -1, keepdims=True)
    return inverse * (weighted - first - scaled * second)


def head_lanes(odd, dtype):
    lane = lax.broadcasted_iota(jnp.int32, (1, PAIR), 1)
    return ((lane // HD) == odd).astype(dtype)


def norm_project(info, hid, gain, bias, wq, wk, wv, a1, q, k, v):
    scaled, _ = normed(hid[...].astype(F32))
    low = (scaled * gain[...] + bias[...]).astype(BF)
    a1[...] = low
    q[...] = (dot(low, wq[...]) * SCALE).astype(BF)
    k[...] = dot(low, wk[...]).astype(BF)
    v[...] = dot(low, wv[...]).astype(BF)


def text_project(info, text, wk, wv, k, v):
    k[...] = dot(text[...], wk[...]).astype(BF)
    v[...] = dot(text[...], wv[...]).astype(BF)


def blocks_of(rows, step=256):
    return [(s, min(step, rows - s)) for s in range(0, rows, step)]


def causal(scores):
    key = lax.broadcasted_iota(jnp.int32, scores.shape, 0)
    query = lax.broadcasted_iota(jnp.int32, scores.shape, 1)
    return jnp.where(key <= query, scores, NEG)


def self_forward(info, q, k, v, keep, send, total, mixed):
    rows = q.shape[0]
    half = rows // 2
    odd = lax.rem(pl.program_id(0), 2)
    lanes = head_lanes(odd, BF)
    lanes_on = head_lanes(odd, F32) > 0
    for start, size in blocks_of(rows):
        here = slice(start, start + size)
        query = q[here, :] * lanes
        near = causal(against(k[here, :], query))
        top = jnp.max(near, 0, keepdims=True)
        if start:
            far = against(k[:start, :], query)
            top = jnp.maximum(top, jnp.max(far, 0, keepdims=True))
        near = jnp.exp(near - top)
        count = jnp.sum(near, 0, keepdims=True)
        if start:
            far = jnp.exp(far - top)
            count = count + jnp.sum(far, 0, keepdims=True)
        scale = 1.0 / count
        out = over_rows(v[here, :], (near * scale).astype(BF))
        if start:
            out = out + over_rows(v[:start, :], (far * scale).astype(BF))
        total[0, :, here] = top + jnp.log(count)
        mixed[here, :] = jnp.where(lanes_on, out.T, mixed[here, :])

    @pl.when(odd == 1)
    def _():
        keep[...] = mixed[pl.ds(pl.multiple_of(info[CORE] * half, 8), half), :]
        send[...] = mixed[pl.ds(pl.multiple_of(info[PEER] * half, 8), half), :]


def prepare(info, so, co, cq, own, first, later):
    own[0:256, :] = so[...].astype(F32)
    own[256:512, :] = co[...].astype(F32)
    own[512:768, :] = cq[...].astype(F32).T
    first[0:128, :] = own[pl.ds(pl.multiple_of(info[Y] * 128, 8), 128), :]
    at = pl.multiple_of(256 + info[LABEL] * 64, 8)
    first[128:192, :] = own[pl.ds(at, 64), :]
    later[...] = own[pl.ds(at + 256, 64), :]


def stack_two(info, one, two, out):
    rows = one.shape[0]
    out[:rows, :] = one[...]
    out[rows:, :] = two[...]


def mix(info, one, two, w_one, w_two, out):
    out[...] = dot(one[...].astype(BF), w_one[...].astype(BF)) + dot(
        two[...].astype(BF), w_two[...].astype(BF)
    )


def gather_halves(info, far, weights):
    for s in range(2):
        for p in range(2):

            @pl.when(info[Y] == p)
            def _(s=s, p=p):
                weights[s * 256 + p * 128 : s * 256 + p * 128 + 128, :] = far[2 * s][
                    :128, :
                ].astype(BF)

            @pl.when(info[Y] != p)
            def _(s=s, p=p):
                weights[s * 256 + p * 128 : s * 256 + p * 128 + 128, :] = far[2 * s + 1][
                    :128, :
                ].astype(BF)


def gather_quarters(info, far, weights):
    per = len(far) // 2
    for s in range(2):
        refs = far[per * s : per * s + per]
        if per == 3:
            pieces = [refs[0][128:192, :], refs[1][128:192, :]]
        else:
            pieces = [refs[0][:64, :], refs[0][64:, :]]
        pieces += [refs[-1][:64, :], refs[-1][64:, :]]
        for j, piece in enumerate(pieces):
            at = pl.multiple_of(s * 256 + (info[LABEL] ^ j) * 64, 64)
            weights[pl.ds(at, 64), :] = piece.astype(BF)


def mix_far(info, pre, one, two, far, weights, which):
    if which is None:
        gather_halves(info, far, weights)
    else:
        gather_quarters(info, far, weights)
    far_part = dot(one[...].astype(BF), weights[:256, :]) + dot(
        two[...].astype(BF), weights[256:, :]
    )
    return pre[...] + far_part


def mix_norm(which, info, base, pre, one, two, *refs):
    n = 6 if which is None else 5
    far, (gain, bias, resid, low, *packs, weights) = refs[:-n], refs[-n:]
    for pack in packs:
        for j in range(2):
            pack[j * 64 : j * 64 + 64, :] = far[2 + j][128:192, :]
    part = mix_far(info, pre, one, two, far, weights, which)
    total = base[...].astype(F32) + part
    resid[...] = total
    scaled, _ = normed(total)
    low[...] = scaled * gain[...] + bias[...]


def mix_norm_back(info, pre, one, two, *refs):
    far, (gain, resid, e_in, e_out, grads, weights) = refs[:-6], refs[-6:]
    grad = mix_far(info, pre, one, two, far, weights, 64)
    scaled, inverse = normed(resid[...])
    e_out[...] = e_in[...] + norm_back(grad, scaled, inverse, gain[...])
    grads[0:1, :] = jnp.sum(grad * scaled, 0, keepdims=True) * 0.5
    grads[1:2, :] = jnp.sum(grad, 0, keepdims=True) * 0.5


def sum_norm_back(info, mine, far, gain, resid, e_in, e_out, grads):
    grad = mine[...] + far[...]
    scaled, inverse = normed(resid[...])
    e_out[...] = e_in[...].astype(F32) + norm_back(grad, scaled, inverse, gain[...])
    grads[0:1, :] = jnp.sum(grad * scaled, 0, keepdims=True) * 0.5
    grads[1:2, :] = jnp.sum(grad, 0, keepdims=True) * 0.5


def sum_first_grads(info, mine, recv, hid, out, grads):
    grad = mine[...] + recv[...]
    out[...] = grad
    scaled, _ = normed(hid[...].astype(F32))
    grads[0:1, :] = jnp.sum(grad * scaled, 0, keepdims=True)
    grads[1:2, :] = jnp.sum(grad, 0, keepdims=True)


def last_norm_back(info, mine, far, gain, hid, e_in, out):
    grad = mine[...] + far[...]
    scaled, inverse = normed(hid[...].astype(F32))
    out[...] = e_in[...] + norm_back(grad, scaled, inverse, gain[...])


def cross_forward(info, length, a2, wq, k, v, q, mixed, total):
    query_rows = (dot(a2[...].astype(BF), wq[...]) * SCALE).astype(BF)
    q[...] = query_rows
    for pair in range(2):
        cols = slice(pair * PAIR, (pair + 1) * PAIR)
        pair_out = None
        for odd in range(2):
            query = query_rows[:, cols] * head_lanes(odd, BF)
            scores = against(k[:, cols], query)
            slot = lax.broadcasted_iota(jnp.int32, scores.shape, 0)
            scores = jnp.where(slot < length[0], scores, NEG)
            top = jnp.max(scores, 0, keepdims=True)
            scores = jnp.exp(scores - top)
            count = jnp.sum(scores, 0, keepdims=True)
            out = over_rows(v[:, cols], (scores * (1.0 / count)).astype(BF)).T
            total[pair * 2 + odd] = top + jnp.log(count)
            pair_out = out if odd == 0 else jnp.where(head_lanes(1, F32) > 0, out, pair_out)
        mixed[:, cols] = pair_out


def feed_forward(info, a3, cot, up, down, g, du, da3):
    n = pl.program_id(0)
    u = dot(a3[...].astype(BF), up[...])
    cdf = 0.5 + 0.5 * lax.erf(u * (0.5**0.5))
    g[...] = (u * cdf).astype(BF)
    slope = cdf + u * jnp.exp(-0.5 * u * u) * (1.0 / (2.0 * np.pi) ** 0.5)
    dg = against(cot[...], down[...]).astype(BF).astype(F32)
    low = (dg * slope).astype(BF)
    du[...] = low
    part = against(low, up[...])

    @pl.when(n == 0)
    def _():
        da3[...] = part

    @pl.when(n > 0)
    def _():
        da3[...] += part


def stack_rows(info, one, two, three, out):
    for i, ref in enumerate((one, two, three)):
        out[2 * i : 2 * i + 2, :] = ref[...]
    out[6:, :] = jnp.zeros((2, out.shape[1]), F32)


def add_two(info, one, two, out):
    out[...] = one[...] + two[...]


def down_project(info, own, sib, down, out_own, out_sib):
    out_own[...] = dot(own[...], down[...])
    out_sib[...] = dot(sib[...], down[...])


def cross_backward(second, info, length, e1, wo, q, k, v, total, *rest):
    if second:
        dk_in, dv_in, dq, dk_out, dv_out = rest
    else:
        dq, dk_out, dv_out = rest
    mixed_grad = against(e1[...].astype(BF), wo[...]).astype(BF)
    for pair in range(2):
        cols = slice(pair * PAIR, (pair + 1) * PAIR)
        dk = dk_in[:, cols] if second else None
        dv = dv_in[:, cols] if second else None
        pair_dq = None
        for odd in range(2):
            lanes = head_lanes(odd, BF)
            query = q[:, cols] * lanes
            grad = mixed_grad[:, cols] * lanes
            scores = against(k[:, cols], query)
            slot = lax.broadcasted_iota(jnp.int32, scores.shape, 0)
            scores = jnp.where(slot < length[0], scores, NEG)
            probs = jnp.exp(scores - total[pair * 2 + odd])
            prob_grad = against(v[:, cols], grad)
            part = dot(probs.astype(BF), grad)
            dv = part if dv is None else dv + part
            delta = jnp.sum(probs * prob_grad, 0, keepdims=True)
            low = (probs * (prob_grad - delta)).astype(BF)
            part = dot(low, query)
            dk = part if dk is None else dk + part
            out = over_rows(k[:, cols], low).T
            pair_dq = out if odd == 0 else jnp.where(head_lanes(1, F32) > 0, out, pair_dq)
        dq[:, cols] = pair_dq * SCALE
        dk_out[:, cols] = dk.astype(dk_out.dtype)
        dv_out[:, cols] = dv.astype(dv_out.dtype)


def text_back(info, dk, dv, wk, wv, own, send, scratch):
    half = own.shape[0]
    scratch[...] = against(dk[...], wk[...]) + against(dv[...], wv[...])
    own[...] = scratch[pl.ds(pl.multiple_of(info[CORE] * half, 8), half), :]
    send[...] = scratch[pl.ds(pl.multiple_of(info[PEER] * half, 8), half), :]


def mixed_back(info, own, sib, wo, out):
    half = own.shape[0]
    out[pl.ds(pl.multiple_of(info[CORE] * half, 16), half), :] = against(
        own[...].astype(BF), wo[...]
    ).astype(BF)
    out[pl.ds(pl.multiple_of(info[PEER] * half, 16), half), :] = against(
        sib[...].astype(BF), wo[...]
    ).astype(BF)


def self_backward(info, q, k, v, grad_in, total, dq, dk, dv, dq_sum, dk_sum, dv_sum):
    rows = q.shape[0]
    odd = lax.rem(pl.program_id(0), 2)
    lanes = head_lanes(odd, BF)
    lanes_on = head_lanes(odd, F32) > 0

    @pl.when(odd == 0)
    def _():
        dk_sum[...] = jnp.zeros_like(dk_sum)
        dv_sum[...] = jnp.zeros_like(dv_sum)

    for start, size in blocks_of(rows):
        here = slice(start, start + size)
        query = q[here, :] * lanes
        grad = grad_in[here, :] * lanes
        level = total[0, :, here]
        near = jnp.exp(causal(against(k[here, :], query)) - level)
        near_grad = against(v[here, :], grad)
        delta = jnp.sum(near * near_grad, 0, keepdims=True)
        dv_sum[here, :] += dot(near.astype(BF), grad)
        if start:
            far = jnp.exp(against(k[:start, :], query) - level)
            far_grad = against(v[:start, :], grad)
            delta = delta + jnp.sum(far * far_grad, 0, keepdims=True)
            dv_sum[:start, :] += dot(far.astype(BF), grad)
        near_low = (near * (near_grad - delta)).astype(BF)
        dk_sum[here, :] += dot(near_low, query)
        out = over_rows(k[here, :], near_low)
        if start:
            far_low = (far * (far_grad - delta)).astype(BF)
            dk_sum[:start, :] += dot(far_low, query)
            out = out + over_rows(k[:start, :], far_low)
        dq_sum[here, :] = jnp.where(lanes_on, out.T * SCALE, dq_sum[here, :])

    @pl.when(odd == 1)
    def _():
        dq[...] = dq_sum[...].astype(BF)
        dk[...] = dk_sum[...].astype(BF)
        dv[...] = dv_sum[...].astype(BF)


def first_back(info, dq, dk, dv, wq, wk, wv, own, send):
    half = own.shape[0]
    for at, out in ((PEER, send), (CORE, own)):
        here = pl.ds(pl.multiple_of(info[at] * half, 16), half)
        out[...] = (
            against(dq[here, :], wq[...])
            + against(dk[here, :], wk[...])
            + against(dv[here, :], wv[...])
        )


def weight_grad(plan, shapes, n_v, info, *refs):
    at = 0
    groups = []
    for n_left, n_right in shapes:
        groups.append((refs[at : at + n_left], refs[at + n_left : at + n_left + n_right]))
        at += n_left + n_right
    vectors = refs[at : at + n_v]
    outs = refs[at + n_v : at + n_v + 2 * len(plan)]
    lhs, rhs = refs[-2:]
    for g, (lefts, rights) in enumerate(groups):
        row = 0
        per = len(rights) // len(lefts)
        for i, left in enumerate(lefts):
            rows = left.shape[0]
            for j in range(8):
                block = left[:, pl.ds(pl.multiple_of(info[TABLE + j] * 128, 128), 128)]
                lhs[row : row + rows, j * 128 : (j + 1) * 128] = block.astype(BF)
            col = 0
            for right in rights[i * per : (i + 1) * per]:
                rhs[row : row + rows, col : col + right.shape[1]] = right[...].astype(BF)
                col += right.shape[1]
            row += rows
        for s, (order, segments) in enumerate(plan):
            put = 0
            for group, first, width in segments:
                if group == g:
                    for half in range(2):
                        value = over_rows(
                            lhs[:row, half * 512 : half * 512 + 512],
                            rhs[:row, first : first + width],
                        )
                        for q in range(4):
                            j = half * 4 + q
                            sent, pos = spot(order, j)
                            outs[2 * s + sent][pos, :128, put : put + width] = value[
                                q * 128 : (q + 1) * 128, :
                            ]
                put += width
    if n_v:
        for j in range(8):
            sent, pos = spot(plan[-1][0], j)
            out = outs[2 * len(plan) - 2 + sent]
            out[pos, 128:, :] = jnp.zeros((8, out.shape[2]), F32)
            block = vectors[0][:, pl.ds(pl.multiple_of(info[TABLE + j] * 128, 128), 128)]
            out[pos, 128:, :128] = block


def spot(order, j):
    bits = [(j // WEIGHT[name]) & 1 for name in order]
    return bits[0], bits[1] * 2 + bits[2]


def weight_grads(info, groups, plan, vectors=()):
    args, specs, shapes = [], [], []
    for lefts, rights in groups:
        flat = [r for group in rights for r in group]
        for left in lefts:
            array, spec = left if isinstance(left, tuple) else (left, None)
            args.append(array)
            specs.append(spec)
        args += flat
        specs += [None] * len(flat)
        shapes.append((len(lefts), len(flat)))
    args += vectors
    specs += [None] * len(vectors)
    outs = []
    for s, (order, segments) in enumerate(plan):
        tall = 136 if vectors and s == len(plan) - 1 else 128
        outs += [arr((4, tall, sum(w for _, _, w in segments)))] * 2
    rows = max(sum(group[0].shape[0] for group in rights) for _, rights in groups)
    wide = max(sum(r.shape[1] for r in rights[0]) for _, rights in groups)
    return launch(
        functools.partial(weight_grad, plan, tuple(shapes), len(vectors)),
        info,
        tuple(args),
        specs,
        outs,
        [None] * len(outs),
        scratch=[pltpu.VMEM((rows, 1024), BF), pltpu.VMEM((rows, wide), BF)],
        grant=40,
    )


def scatter_sum(keep, send):
    value = jnp.concatenate([keep, send])
    value = value.reshape(-1, value.shape[-1])
    return lax.psum_scatter(value, "dp", scatter_dimension=0, tiled=True)


def fold(info, *refs):
    for i in range(2):
        keep, got = refs[2 * i : 2 * i + 2]
        keep_out, send_out = refs[4 + 2 * i : 6 + 2 * i]
        n = keep_out.shape[0]
        keep_out[...] = keep[:n] + got[:n]
        send_out[...] = keep[n:] + got[n:]


def fold_one(info, keep, got, keep_out, send_out):
    keep_out[...] = keep[0] + got[0]
    send_out[...] = keep[1] + got[1]


def fold_last(info, *refs):
    keep_out, send_out = refs[4:]
    col = 0
    for i in range(2):
        keep, got = refs[2 * i : 2 * i + 2]
        rows, wide = keep.shape[1:]
        keep_out[:rows, col : col + wide] = keep[0] + got[0]
        send_out[:rows, col : col + wide] = keep[1] + got[1]
        col += wide


def finish_ffn(info, keep, got, up, down):
    wide = up.shape[1]
    up[...] = keep[:, :wide] + got[:, :wide]
    down[...] = (keep[:, wide:] + got[:, wide:]).T


def finish_cross(info, keep, got, co, ck, cv, cq):
    co[...] = (keep[:, :256] + got[:, :256]).T
    for i, out in enumerate((ck, cv, cq)):
        here = slice(256 * i + 256, 256 * i + 512)
        out[...] = keep[:, here] + got[:, here]


def finish_self(info, keep, got, so, sk, sv, sq, vectors):
    so[...] = (keep[:128, :256] + got[:128, :256]).T
    for i, out in enumerate((sk, sv, sq)):
        here = slice(256 * i + 256, 256 * i + 512)
        out[...] = keep[:128, here] + got[:128, here]
    vectors[...] = keep[128:, 768:896] + got[128:, 768:896]


FINISH = {
    finish_ffn: [(128, 1024), (1024, 128)],
    finish_cross: [(256, 128), (128, 256), (128, 256), (128, 256)],
    finish_self: [(256, 128), (128, 256), (128, 256), (128, 256), (8, 128)],
}


def exchange(streams, orders, step, first=None, cost=10, ready=()):
    args = []
    for i, ((keep, send), order) in enumerate(zip(streams, orders)):
        got = ready[i] if ready else swap(send, "dp", 8, FLIPS[order[step]])
        args += [keep, got if first is None else after(got, first)]
    none = jnp.zeros((1,), jnp.int32)
    if step == 1:
        shape = (max(a.shape[1] for a in args), args[0].shape[2] + args[2].shape[2])
        return launch(
            fold_last, none, args, [None] * 4, [arr(shape)] * 2, [None] * 2, cost=cost
        )
    outs = []
    for keep, _ in streams:
        outs += [arr((keep.shape[0] // 2, *keep.shape[1:]))] * 2
    out = launch(fold, none, args, [None] * 4, outs, [None] * 4, cost=cost)
    return list(zip(out[0::2], out[1::2]))


def fold_stream(pair, name, first, cost=0):
    keep, send = pair
    got = after(swap(send, "dp", 8, FLIPS[name]), first)
    none = jnp.zeros((1,), jnp.int32)
    outs = [arr(keep.shape[1:])] * 2
    return launch(fold_one, none, (keep, got), [None] * 2, outs, [None] * 2, cost=cost)


def finish(pair, body, first=None, cost=10):
    keep, send = pair
    got = swap(send, "dp", 8, FLIPS["m"])
    got = got if first is None else after(got, first)
    outs = [arr(shape) for shape in FINISH[body]]
    none = jnp.zeros((1,), jnp.int32)
    return launch(body, none, (keep, got), [None] * 2, outs, [None] * len(outs), cost=cost)


def sent(streams):
    return [s for _, s in streams]


def out_second(info, own, got, text_own, text_got, out):
    half = own.shape[0]
    out[:half, :] = own[...] + got[...]
    out[half:, :] = text_own[...] + text_got[...]


def out_sum(info, resid, mine, far, out):
    half = resid.shape[0]
    out[:half, :] = resid[...] + (mine[:half, :] + far[:half, :])
    out[half:, :] = mine[half:, :] + far[half:, :]


def out_place(info, own, sib, out, text_out):
    half = out.shape[0] // 2
    text_half = text_out.shape[0] // 2
    for at, ref in ((CORE, own), (PEER, sib)):
        out[pl.ds(pl.multiple_of(info[at] * half, 16), half), :] = ref[:half, :].astype(BF)
        spot = pl.multiple_of(info[at] * text_half, 8)
        text_out[pl.ds(spot, text_half), :] = ref[half:, :]


def place(info, own, sib, out):
    half = out.shape[0] // 2
    for at, ref in ((CORE, own), (PEER, sib)):
        out[pl.ds(pl.multiple_of(info[at] * half, 16), half), :] = ref[...].astype(BF)


def body(
    hidden,
    text_states,
    text_len,
    ln1_gain,
    ln1_bias,
    self_q,
    self_k,
    self_v,
    self_o,
    ln2_gain,
    ln2_bias,
    cross_q,
    cross_k,
    cross_v,
    cross_o,
    ln3_gain,
    ln3_bias,
    ffn_up,
    ffn_down,
    cotangent,
):
    dp_size = lax.axis_size("dp")
    frames, width = hidden.shape[1:]
    text_rows = text_states.shape[1]
    cols = self_q.shape[1]
    inner = ffn_up.shape[1]
    half = frames // 2
    device = lax.axis_index("dp") * 4 + lax.axis_index("tensor")
    table = jnp.asarray(index_table(dp_size))
    info = lax.dynamic_index_in_dim(table, device, 0, keepdims=False)
    hid = hidden.reshape(frames, width)
    cot = cotangent.reshape(frames, width)
    text = text_states.reshape(text_rows, width)
    gain1, bias1 = ln1_gain.reshape(1, width), ln1_bias.reshape(1, width)
    gain2, bias2 = ln2_gain.reshape(1, width), ln2_bias.reshape(1, width)
    gain3, bias3 = ln3_gain.reshape(1, width), ln3_bias.reshape(1, width)
    own_rows = pl.BlockSpec((half, width), lambda i, table: (table[CORE], 0))
    sib_rows = pl.BlockSpec((half, width), lambda i, table: (table[PEER], 0))
    half_mm = 2 * half * width
    whole = dp_size == 8
    orders = ("yam", "aym") if whole else ("may",) * 2
    order_one, order_two = orders

    own3, first, later = launch(
        prepare,
        info,
        (self_o, cross_o, cross_q),
        [None] * 3,
        [arr((3 * cols, width)), arr((3 * cols // 4, width)), arr((cols // 4, width))],
        [None] * 3,
        flops=1 << 20,
    )
    far_one = cross_swap(first)
    far_later = cross_swap(later)
    sib3 = core_swap(own3)

    def weight_at(i):
        return pl.BlockSpec((cols, width), lambda *_: (i, 0))

    step = frames // 4
    a1, q1, k1, v1 = launch(
        norm_project,
        info,
        (after(hid, first), gain1, bias1, self_q, self_k, self_v),
        [pl.BlockSpec((step, width), lambda i, _: (i, 0))] + [None] * 5,
        [arr((frames, width), BF)] + [arr((frames, cols), BF)] * 3,
        [pl.BlockSpec((step, width), lambda i, _: (i, 0))]
        + [pl.BlockSpec((step, cols), lambda i, _: (i, 0))] * 3,
        grid=(4,),
        flops=2 * frames * width * cols * 3,
    )
    heads = cols // HD
    pair_in = pl.BlockSpec((frames, PAIR), lambda h, _: (0, h // 2))
    pair_half = pl.BlockSpec((half, PAIR), lambda h, _: (0, h // 2))
    level = pl.BlockSpec((1, 1, frames), lambda h, _: (h, 0, 0))
    o1_own, o1_sib, total1 = launch(
        self_forward,
        info,
        (q1, k1, v1),
        [pair_in] * 3,
        [arr((half, cols))] * 2 + [arr((heads, 1, frames))],
        [pair_half] * 2 + [level],
        grid=(heads,),
        scratch=[pltpu.VMEM((frames, PAIR), F32)],
        flops=heads * frames * frames * 512,
        exps=heads * frames * frames,
    )
    o1_cross = cross_swap(after(o1_sib, far_one))
    o1_core = core_swap(after(o1_sib, sib3))
    o1_x = x_swap(o1_own)
    far_two = swap(after(far_one, o1_own), "dp", dp_size, FLIPS["y"])
    k2, v2 = launch(
        text_project,
        info,
        (after(text, o1_own), cross_k, cross_v),
        [None] * 3,
        [arr((text_rows, cols), BF)] * 2,
        [None] * 2,
        flops=2 * text_rows * width * cols * 2,
    )

    def mixed(one, two, i):
        return launch(
            mix,
            info,
            (one, two, own3, sib3),
            [None] * 2 + [weight_at(i)] * 2,
            [arr((half, width))],
            [None],
            flops=half_mm * 512,
        )[0]

    pre1 = mixed(after(o1_own, k2), o1_core, 0)
    far_one_core = core_swap(after(far_one, o1_core))
    far_two_core = core_swap(after(far_two, o1_x, o1_cross, pre1, far_later))
    far_weights = (far_one_core, far_two_core, far_one, far_two)

    def normed_mix(which, base, spec, pre, one, two, weights, gain, bias, packs=0):
        return launch(
            functools.partial(mix_norm, which),
            info,
            (base, pre, one, two, *weights, gain, bias),
            [spec] + [None] * (5 + len(weights)),
            [arr((half, width))] * 2 + [arr((cols // 2, width))] * packs,
            [None] * (2 + packs),
            scratch=[pltpu.VMEM((2 * cols, width), BF)],
            cost=2,
        )

    h1, a2, pack_co = normed_mix(None, hid, own_rows, pre1, o1_x, o1_cross, far_weights, gain2, bias2, 1)
    a2_sib = core_swap(a2)

    smem = pl.BlockSpec(memory_space=pltpu.SMEM)

    def cross(a):
        return launch(
            cross_forward,
            info,
            (text_len, a, cross_q, k2, v2),
            [smem] + [None] * 4,
            [arr((half, cols), BF), arr((half, cols)), arr((heads, 1, half))],
            [None] * 3,
            flops=half_mm * cols + heads * half * text_rows * 512,
            exps=heads * half * text_rows,
        )

    q2_own, o2_own, total2_own = cross(a2)
    o2_x = x_swap(after(o2_own, o1_x))
    q2_sib, o2_sib, total2_sib = cross(after(a2_sib, q2_own))
    o2_cross = cross_swap(after(o2_sib, o1_cross))
    o2_core = core_swap(o2_sib)
    far_co = swap(pack_co, "dp", dp_size, FLIPS["a"])
    next_later = swap(after(far_later, a2), "dp", dp_size, FLIPS["y"])
    pack_cq = launch(
        stack_two,
        info,
        (far_later, after(next_later, o2_sib)),
        [None] * 2,
        [arr((cols // 2, width))],
        [None],
    )[0]
    far_cq = swap(pack_cq, "dp", dp_size, FLIPS["a"])
    pre2 = mixed(after(o2_own, pack_cq), o2_core, 1)
    far_co_core = core_swap(after(far_co, o2_x, o2_cross, far_cq, pre2))
    co_weights = (
        *(far_one_core, far_two_core, far_co_core),
        *(far_one, far_two, far_co),
    )
    h2, a3 = normed_mix(0, h1, None, pre2, o2_x, o2_cross, co_weights, gain3, bias3)
    a3_sib = core_swap(a3)
    far_cq_core = core_swap(after(far_cq, a3))
    pack_cq_core = core_swap(after(pack_cq, pre2))

    unit = 256

    def feed(a, rows):
        return launch(
            feed_forward,
            info,
            (a, cot, ffn_up, ffn_down),
            [
                None,
                rows,
                pl.BlockSpec((width, unit), lambda i, _: (0, i)),
                pl.BlockSpec((unit, width), lambda i, _: (i, 0)),
            ],
            [arr((half, inner), BF)] * 2 + [arr((half, width))],
            [pl.BlockSpec((half, unit), lambda i, _: (0, i))] * 2 + [None],
            grid=(inner // unit,),
            flops=half_mm * inner * 3,
            exps=half * inner * 2,
        )

    g_own, du_own, da3_own = feed(a3, own_rows)
    g_sib, du_sib, da3_sib = feed(after(a3_sib, g_own, far_cq_core), sib_rows)
    da3_sum = launch(
        add_two,
        info,
        (da3_own, core_swap(da3_sib)),
        [None] * 2,
        [arr((half, width))],
        [None],
    )[0]
    da3_far = x_swap(after(da3_sum, o2_x))
    ffn_plan = (
        (order_one, ((0, 0, 1024),)),
        (order_two, ((1, 0, 1024),)),
    )
    ffn = weight_grads(
        info,
        [
            ([after(a3, da3_sum), a3_sib], [[du_own], [du_sib]]),
            ([(cot, own_rows), (cot, sib_rows)], [[g_own], [g_sib]]),
        ],
        ffn_plan,
    )
    out_own, out_sib = launch(
        down_project,
        info,
        (after(g_own, *ffn[1::2]), g_sib, ffn_down),
        [None, None, pl.BlockSpec((inner, 512), lambda i, _: (0, i))],
        [arr((half, width))] * 2,
        [pl.BlockSpec((half, 512), lambda i, _: (0, i))] * 2,
        grid=(width // 512,),
        flops=2 * half_mm * inner,
    )
    out_got = core_swap(out_sib)
    e1, grads3 = launch(
        sum_norm_back,
        info,
        (da3_sum, after(da3_far, out_own), gain3, h2, cot),
        [None] * 4 + [own_rows],
        [arr((half, width)), arr((2, width))],
        [None] * 2,
    )
    e1_sib = core_swap(e1)
    def cross_back(e, q, total, sums):
        last = bool(sums)
        return launch(
            functools.partial(cross_backward, last),
            info,
            (text_len, e, cross_o, q, k2, v2, total, *sums),
            [smem] + [None] * (6 + len(sums)),
            [arr((half, cols))] + [arr((text_rows, cols), BF if last else F32)] * 2,
            [None] * 3,
        )

    dq2_own, *sums = cross_back(after(e1, out_got), q2_own, total2_own, ())
    dq2_sib, dk2, dv2 = cross_back(e1_sib, q2_sib, total2_sib, tuple(sums))
    dq2_cross = cross_swap(dq2_sib)
    dq2_core = core_swap(dq2_sib)
    dq2_x = x_swap(after(dq2_own, da3_far))
    pre3 = mixed(dq2_own, dq2_core, 2)
    cq_weights = (pack_cq_core, far_cq_core, pack_cq, far_cq)

    text_half = text_rows // 2
    text_own, text_send = launch(
        text_back,
        info,
        (dk2, dv2, cross_k, cross_v),
        [None] * 4,
        [arr((text_half, width))] * 2,
        [None] * 2,
        scratch=[pltpu.VMEM((text_rows, width), F32)],
        flops=2 * text_rows * width * cols * 2,
    )
    text_got = core_swap(text_send)
    out_two = launch(
        out_second,
        info,
        (out_own, out_got, text_own, text_got),
        [None] * 4,
        [arr((half + text_half, width))],
        [None],
    )[0]
    cross_plan = (
        (order_one, ((0, 0, 256), (2, 0, 512))),
        (order_two, ((1, 0, 256),)),
    )
    cross = weight_grads(
        info,
        [
            ([e1, e1_sib], [[o2_own], [o2_sib]]),
            ([a2, a2_sib], [[dq2_own], [dq2_sib]]),
            ([text], [[dk2, dv2]]),
        ],
        cross_plan,
    )
    pins = [out_two]
    if whole:
        ffn = exchange(list(zip(ffn[0::2], ffn[1::2])), orders, 0, cross[0], 12)
        pins += sent(ffn)
    e0, grads2 = launch(
        mix_norm_back,
        info,
        (after(pre3, *pins), dq2_x, dq2_cross, *cq_weights, gain2, h1, e1),
        [None] * (6 + len(cq_weights)),
        [arr((half, width)), arr((2, width))],
        [None] * 2,
        scratch=[pltpu.VMEM((2 * cols, width), BF)],
        cost=0,
    )
    out_far_two = x_swap(after(out_two, dq2_x))
    e0_sib = core_swap(e0)
    do1 = launch(
        mixed_back,
        info,
        (e0, e0_sib, self_o),
        [None] * 3,
        [arr((frames, cols), BF)],
        [None],
    )[0]
    dq1, dk1, dv1 = launch(
        self_backward,
        info,
        (q1, k1, v1, do1, total1),
        [pair_in] * 4 + [level],
        [arr((frames, cols), BF)] * 3,
        [pair_in] * 3,
        grid=(heads,),
        scratch=[pltpu.VMEM((frames, PAIR), F32)] * 3,
        flops=heads * frames * frames * 256 * 5,
        exps=heads * frames * frames,
    )
    da1_own, da1_send = launch(
        first_back,
        info,
        (dq1, dk1, dv1, self_q, self_k, self_v),
        [None] * 6,
        [arr((half, width))] * 2,
        [None] * 2,
        flops=2 * half_mm * 3 * cols,
    )
    pins = []
    if whole:
        ffn = exchange(ffn, orders, 1, da1_own, 4)
        pins = [ffn[1]]
        cross = [(k, after(c, ffn[1])) for k, c in zip(cross[0::2], cross[1::2])]
    da1_sum, grads1 = launch(
        sum_first_grads,
        info,
        (da1_own, after(core_swap(da1_send), *pins), hid),
        [None] * 2 + [own_rows],
        [arr((half, width)), arr((2, width))],
        [None] * 2,
    )

    vectors = (grads1, grads2, grads3)
    if whole:
        stacked = launch(stack_rows, info, vectors, [None] * 3, [arr((8, width))], [None])[0]
        for flip in (1, 3):
            stacked = launch(
                add_two,
                info,
                (stacked, swap(stacked, "tensor", 4, flip)),
                [None] * 2,
                [arr((8, width))],
                [None],
            )[0]
        vectors = (stacked,)
    if not whole:
        stacked = lax.psum(jnp.concatenate(vectors), "tensor")
        stacked = lax.psum_scatter(stacked, "dp", scatter_dimension=1, tiled=True)
        vectors = ()
    self_plan = (
        (order_one, ((0, 0, 256), (1, 256, 512))),
        (order_two, ((1, 0, 256),)),
    )
    own = weight_grads(
        info,
        [
            ([after(e0, da1_sum), e0_sib], [[o1_own], [o1_sib]]),
            ([a1], [[dq1, dk1, dv1]]),
        ],
        self_plan,
        vectors,
    )
    pins = [own[0]]
    if whole:
        own = list(zip(own[0::2], own[1::2]))
    out_final = launch(
        out_sum,
        info,
        (h2, out_two, after(out_far_two, *pins)),
        [None] * 3,
        [arr((half + text_half, width))],
        [None],
        cost=0,
    )[0]
    da1_far = x_swap(after(da1_sum, out_final))
    output, text_grad = launch(
        out_place,
        info,
        (out_final, core_swap(out_final)),
        [None] * 2,
        [arr((frames, width), BF), arr((text_rows, width))],
        [None] * 2,
    )
    pins = []
    if not whole:
        ffn, cross, own = (
            [scatter_sum(*p) for p in zip(g[0::2], g[1::2])] for g in (ffn, cross, own)
        )
        up_grad, down_grad = ffn[0], ffn[1].T
        co_grad, cq_grad = cross[0][:, :256].T, cross[1]
        ck_grad, cv_grad = cross[0][:, 256:512], cross[0][:, 512:]
        so_grad, sq_grad = own[0][:, :256].T, own[1]
        sk_grad, sv_grad = own[0][:, 256:512], own[0][:, 512:]
    if whole:
        cross = exchange(cross, orders, 0, own[0][0], 0)
        ready = (
            swap(cross[0][1], "dp", 8, FLIPS["a"]),
            swap(cross[1][1], "dp", 8, FLIPS["y"]),
        )
        own = [(own[0][0], after(own[0][1], cross[0][1])), (own[1][0], after(own[1][1], cross[0][1]))]
        up_grad, down_grad = finish(ffn, finish_ffn, cross[0][0], 1)
        cross = exchange(cross, orders, 1, up_grad, 14, ready)
        pins = [cross[1]]
    last = launch(
        last_norm_back,
        info,
        (da1_sum, after(da1_far, *pins), gain1, hid, e0),
        [None] * 3 + [own_rows, None],
        [arr((half, width))],
        [None],
        flops=half_mm * 8,
    )[0]
    if whole:
        own = exchange(own, orders, 0, last)
        cross = (cross[0], after(cross[1], up_grad))
        co_grad, ck_grad, cv_grad, cq_grad = finish(cross, finish_cross, own[0][1])
        own = exchange(own, orders, 1, co_grad)
    hidden_grad = launch(
        place,
        info,
        (last, core_swap(last)),
        [None] * 2,
        [arr((frames, width), BF)],
        [None],
    )[0]
    if whole:
        so_grad, sk_grad, sv_grad, sq_grad, stacked = finish(
            own, finish_self, (hidden_grad, output)
        )
    return (
        output.reshape(hidden.shape),
        hidden_grad.reshape(hidden.shape),
        text_grad.reshape(text_states.shape),
        stacked[0],
        stacked[1],
        sq_grad,
        sk_grad,
        sv_grad,
        so_grad,
        stacked[2],
        stacked[3],
        cq_grad,
        ck_grad,
        cv_grad,
        co_grad,
        stacked[4],
        stacked[5],
        up_grad,
        down_grad,
    )


def solution(mesh):
    rows = P("dp", None, None)
    column, row = P(None, "tensor"), P("tensor", None)
    in_specs = (
        *(rows, rows, P("dp"), P(), P(), column, column, column, row),
        *(P(), P(), column, column, column, row),
        *(P(), P(), column, row, rows),
    )
    vector, down, across = P("dp"), P("dp", "tensor"), P("tensor", "dp")
    out_specs = (
        *(rows, rows, rows, vector, vector, down, down, down, across),
        *(vector, vector, down, down, down, across),
        *(vector, vector, down, across),
    )
    return jax.shard_map(body, mesh=mesh, in_specs=in_specs, out_specs=out_specs, check_vma=False)
```
